32 devices in a mesh: grp: 4 (over x, core), rep: 8 (over z, y).
Axes of the slice: x: 2, y: 2, z: 4, core: 2. Of those that a mesh axis runs over, the one named last changes fastest.
Arguments:
- query_input: bfloat16 [64, 32, 768], P(('grp', 'rep')), may hold values from -6 to 6
- passage_input: bfloat16 [64, 256, 768], P(('grp', 'rep')), may hold values from -6 to 6
- query_length: int32 [64], P(('grp', 'rep')), may hold values from 2 to 30
- passage_length: int32 [64], P(('grp', 'rep')), may hold values from 32 to 200
- cluster_index: int32 [64], replicated, may hold values from 0 to 1
- margin_bin: int32 [64], P(('grp', 'rep')), may hold values from 0 to 9
- positive_index: int32 [64], P(('grp', 'rep')), may hold values from 0 to 63, each once
- query_cotangent: bfloat16 [64, 32, 768], P(('grp', 'rep')), may hold values from -0.29882812 to 0.29882812
- passage_cotangent: bfloat16 [64, 256, 768], P(('grp', 'rep')), may hold values from -0.29882812 to 0.29882812
- query_weight: bfloat16 [2, 768, 768], replicated, may hold values from -0.21875 to 0.21875
- query_bias: bfloat16 [2, 768], replicated, may hold values from -3 to 3
- key_weight: bfloat16 [2, 768, 768], replicated, may hold values from -0.21875 to 0.21875
- value_weight: bfloat16 [2, 768, 768], replicated, may hold values from -0.21875 to 0.21875
- value_bias: bfloat16 [2, 768], replicated, may hold values from -2 to 2
- mix_weight: bfloat16 [2, 768, 768], replicated, may hold values from -0.875 to 0.875
- mix_bias: bfloat16 [2, 768], replicated, may hold values from -2 to 2
- norm_gain: bfloat16 [2, 768], replicated, may hold values from 0.5 to 1.5
- norm_shift: bfloat16 [2, 768], replicated, may hold values from -1.1953125 to 1.1953125
- expand_weight: bfloat16 [2, 768, 3072], replicated, may hold values from -0.21875 to 0.21875
- expand_bias: bfloat16 [2, 3072], replicated, may hold values from -3 to 3
- reduce_weight: bfloat16 [2, 3072, 768], replicated, may hold values from -0.109375 to 0.109375
- reduce_bias: bfloat16 [2, 768], replicated, may hold values from -2 to 2
- final_gain: bfloat16 [2, 768], replicated, may hold values from 0.5 to 1.5
- final_shift: bfloat16 [2, 768], replicated, may hold values from -1.1953125 to 1.1953125
Outputs:
- query_output: bfloat16 [64, 32, 768], P(('grp', 'rep'))
- passage_output: bfloat16 [64, 256, 768], P(('grp', 'rep'))
- query_loss: float32 [64], P(('grp', 'rep'))
- query_input_gradient: float32 [64, 32, 768], P(('grp', 'rep'))
- passage_input_gradient: float32 [64, 256, 768], P(('grp', 'rep'))
- query_weight_gradient: float32 [2, 768, 768], P(None, 'grp')
- query_bias_gradient: float32 [2, 768], P(None, 'grp')
- key_weight_gradient: float32 [2, 768, 768], P(None, 'grp')
- value_weight_gradient: float32 [2, 768, 768], P(None, 'grp')
- value_bias_gradient: float32 [2, 768], P(None, 'grp')
- mix_weight_gradient: float32 [2, 768, 768], P(None, 'grp')
- mix_bias_gradient: float32 [2, 768], P(None, 'grp')
- norm_gain_gradient: float32 [2, 768], P(None, 'grp')
- norm_shift_gradient: float32 [2, 768], P(None, 'grp')
- expand_weight_gradient: float32 [2, 768, 3072], P(None, 'grp')
- expand_bias_gradient: float32 [2, 3072], P(None, 'grp')
- reduce_weight_gradient: float32 [2, 3072, 768], P(None, 'grp')
- reduce_bias_gradient: float32 [2, 768], P(None, 'grp')
- final_gain_gradient: float32 [2, 768], P(None, 'grp')
- final_shift_gradient: float32 [2, 768], P(None, 'grp')
The draws below stay inside these ranges and needn't reach their ends.
Inputs may be any that keep to these rules, and one draw needn't show every extreme that they name: `positive_index`: each passage is the positive of exactly one query.
All inputs are finite; a program needn't handle non-finite values.
Results may differ from the reference program's by a relative error of at most 0.028.
Values may be sent and summed in bfloat16 or wider, within the bound.
A program may use at most 256 MiB of HBM per device.

```python
import math
import jax
import jax.numpy as jnp
from jax import lax

D = 768
HEADS = 12
DH = 64
FF = 3072
LAYERS = 2
QB = 2
QLEN = 32
PLEN = 256
NBINS = 10
QUERIES = 64
NCLUST = 2
N_GRP = 4
N_REP = 8


def place_ends(drawn, own_key, low, largest):
    dims = drawn.shape
    place = [jax.random.randint(jax.random.fold_in(own_key, axis), (), 0, dims[axis]) for axis in range(len(dims))]
    drawn = drawn.at[tuple(place)].set(low)
    longest = dims.index(max(dims))
    place[longest] = (place[longest] + 1) % dims[longest]
    return drawn.at[tuple(place)].set(largest)


def shard_levels(key, shape, split, smallest, largest):
    gain, own = 1.0, jax.random.fold_in(key, 6)
    for position, parts in split:
        draws = jnp.exp(jax.random.uniform(jax.random.fold_in(own, position), (parts,), jnp.float32, smallest / len(split), largest / len(split)))
        gain = gain * jnp.repeat(draws, shape[position] // parts).reshape([-1 if axis == position else 1 for axis in range(len(shape))])
    return gain


def gaussian(own_key, dims, deviation, most, split=(), dtype=jnp.bfloat16):
    drawn = jax.random.normal(own_key, dims, jnp.float32) * deviation
    if len(split) > 0:
        drawn = shard_levels(own_key, dims, split, -0.22, 0.18) * drawn
    return jnp.clip(drawn, min=-most, max=most).astype(dtype)


def setup_inputs(seed: int = 0) -> dict:
    streams_of = jax.random.split(jax.random.key(seed), 25)
    query_input = gaussian(streams_of[0], (QUERIES, QLEN, D), 1.0, 6.0, ((0, 32),))
    passage_input = gaussian(streams_of[1], (QUERIES, PLEN, D), 1.0, 6.0, ((0, 32),))
    query_length = place_ends(jax.random.randint(streams_of[2], (QUERIES,), 2, QLEN * 15 // 16 + 1), jax.random.fold_in(streams_of[2], 1), 2, (QLEN * 15 // 16 + 1) - 1).astype(jnp.int32)
    passage_length = place_ends(jax.random.randint(streams_of[3], (QUERIES,), PLEN // 8, PLEN * 25 // 32 + 1), jax.random.fold_in(streams_of[3], 1), PLEN // 8, (PLEN * 25 // 32 + 1) - 1).astype(jnp.int32)
    cluster_index = place_ends(jax.random.randint(streams_of[4], (QUERIES,), 0, NCLUST), jax.random.fold_in(streams_of[4], 1), 0, NCLUST - 1).astype(jnp.int32)
    margin_bin = place_ends(jax.random.randint(streams_of[5], (QUERIES,), 0, NBINS), jax.random.fold_in(streams_of[5], 1), 0, NBINS - 1).astype(jnp.int32)
    positive_index = jax.random.permutation(streams_of[6], QUERIES).astype(jnp.int32)
    query_cotangent = gaussian(streams_of[7], (QUERIES, QLEN, D), 0.05, 0.29882812, ((0, 32),))
    passage_cotangent = gaussian(streams_of[8], (QUERIES, PLEN, D), 0.05, 0.29882812, ((0, 32),))
    query_weight = gaussian(streams_of[9], (LAYERS, D, D), D ** -0.5, 0.21875)
    query_bias = gaussian(streams_of[10], (LAYERS, D), 0.5, 3.0)
    key_weight = gaussian(streams_of[11], (LAYERS, D, D), D ** -0.5, 0.21875)
    value_weight = gaussian(streams_of[12], (LAYERS, D, D), D ** -0.5, 0.21875)
    value_bias = gaussian(streams_of[13], (LAYERS, D), 0.3, 2.0)
    mix_weight = gaussian(streams_of[14], (LAYERS, D, D), (D // 16) ** -0.5, 0.875)
    mix_bias = gaussian(streams_of[15], (LAYERS, D), 0.3, 2.0)
    norm_gain = jnp.clip(1.0 + 0.1 * jax.random.normal(streams_of[16], (LAYERS, D), jnp.float32), 0.5, 1.5).astype(jnp.bfloat16)
    norm_shift = gaussian(streams_of[17], (LAYERS, D), 0.2, 1.1953125)
    expand_weight = gaussian(streams_of[18], (LAYERS, D, FF), D ** -0.5, 0.21875)
    expand_bias = gaussian(streams_of[19], (LAYERS, FF), 0.5, 3.0)
    reduce_weight = gaussian(streams_of[20], (LAYERS, FF, D), FF ** -0.5, 0.109375)
    reduce_bias = gaussian(streams_of[21], (LAYERS, D), 0.3, 2.0)
    final_gain = jnp.clip(1.0 + 0.1 * jax.random.normal(streams_of[22], (LAYERS, D), jnp.float32), 0.5, 1.5).astype(jnp.bfloat16)
    final_shift = gaussian(streams_of[23], (LAYERS, D), 0.2, 1.1953125)
    return dict(query_input=query_input, passage_input=passage_input, query_length=query_length, passage_length=passage_length, cluster_index=cluster_index, margin_bin=margin_bin, positive_index=positive_index, query_cotangent=query_cotangent, passage_cotangent=passage_cotangent, query_weight=query_weight, query_bias=query_bias, key_weight=key_weight, value_weight=value_weight, value_bias=value_bias, mix_weight=mix_weight, mix_bias=mix_bias, norm_gain=norm_gain, norm_shift=norm_shift, expand_weight=expand_weight, expand_bias=expand_bias, reduce_weight=reduce_weight, reduce_bias=reduce_bias, final_gain=final_gain, final_shift=final_shift)


@jax.custom_vjp
def low(v):
    return lax.optimization_barrier(v.astype(jnp.bfloat16)).astype(jnp.float32)

@jax.custom_vjp
def low_back(v):
    return v

def low_keep(v):
    return (low(v), None)

def low_pass(kept, grad):
    return (grad,)

def back_keep(v):
    return (v, None)

def back_low(kept, grad):
    return (low(grad),)
low.defvjp(low_keep, low_pass)
low_back.defvjp(back_keep, back_low)

def precise_product(former, latter):
    return jnp.dot(former, latter, precision=lax.Precision.HIGHEST, preferred_element_type=jnp.float32)

def precise_einsum(form, former, latter):
    return jnp.einsum(form, former, latter, precision=lax.Precision.HIGHEST, preferred_element_type=jnp.float32)

def normalize(summed, gain_vector, shift_vector):
    average = lax.optimization_barrier(jnp.mean(summed, axis=-1, keepdims=True))
    centred = summed - average
    variance = lax.optimization_barrier(jnp.mean(centred * centred, axis=-1, keepdims=True))
    return centred * lax.rsqrt(variance + 1e-12) * gain_vector + shift_vector

def attend(hidden, keep_mask, params):
    query_weight, query_bias, key_weight, value_weight, value_bias, mix_weight, mix_bias, norm_gain, norm_shift, expand_weight, expand_bias, reduce_weight, reduce_bias, final_gain, final_shift = params
    batch_size, seq_length, model_width = hidden.shape
    flat = low(hidden).reshape(batch_size * seq_length, model_width)
    query_heads = low_back(low(precise_product(flat, query_weight) + query_bias)).reshape(batch_size, seq_length, HEADS, DH)
    key_heads = low_back(low(precise_product(flat, key_weight))).reshape(batch_size, seq_length, HEADS, DH)
    value_heads = low_back(low(precise_product(flat, value_weight) + value_bias)).reshape(batch_size, seq_length, HEADS, DH)
    scores = low_back(precise_einsum('bqhd,bkhd->bhqk', query_heads, key_heads) * 0.125)
    scores = jnp.where(keep_mask[:, None, None, :], scores, -1e+30)
    attention = low(jax.nn.softmax(scores, axis=-1))
    context = low_back(low(precise_einsum('bhqk,bkhd->bqhd', attention, value_heads)))
    context = context.reshape(batch_size * seq_length, model_width)
    mixed = low_back(precise_product(context, mix_weight) + mix_bias)
    middle = low(normalize(flat + mixed, norm_gain, norm_shift))
    expanded = low_back(precise_product(middle, expand_weight) + expand_bias)
    active = low(jax.nn.gelu(expanded, approximate=False))
    branch = low_back(precise_product(active, reduce_weight) + reduce_bias)
    result = low(normalize(middle + branch, final_gain, final_shift))
    return result.reshape(batch_size, seq_length, model_width)

def encode(hidden, keep_mask, weights):
    for layer_index in range(LAYERS):
        hidden = attend(hidden, keep_mask, tuple((array[layer_index] for array in weights)))
    return hidden

def encode_all(inputs, lengths, weights, block_size):
    seq_total, seq_length, model_width = inputs.shape
    keep_mask = jnp.arange(seq_length)[None, :] < lengths[:, None]
    block_count = seq_total // block_size

    def block_step(block_pair):
        return encode(block_pair[0], block_pair[1], weights)
    outputs = lax.map(jax.checkpoint(block_step), (inputs.reshape(block_count, block_size, seq_length, model_width), keep_mask.reshape(block_count, block_size, seq_length)))
    return outputs.reshape(seq_total, seq_length, model_width)

def reference(query_input, passage_input, query_length, passage_length, cluster_index, margin_bin, positive_index, query_cotangent, passage_cotangent, query_weight, query_bias, key_weight, value_weight, value_bias, mix_weight, mix_bias, norm_gain, norm_shift, expand_weight, expand_bias, reduce_weight, reduce_bias, final_gain, final_shift):
    weights = tuple((array.astype(jnp.float32) for array in (query_weight, query_bias, key_weight, value_weight, value_bias, mix_weight, mix_bias, norm_gain, norm_shift, expand_weight, expand_bias, reduce_weight, reduce_bias, final_gain, final_shift)))
    query_block = QB * N_GRP * min(8, N_REP)
    passage_block = QB * N_GRP
    score_scale = 2.0 / math.sqrt(D)
    columns = jnp.arange(QUERIES)
    allowed = (cluster_index[:, None] == cluster_index[None, :]) | (columns[None, :] == positive_index[:, None])
    margin_weight = (margin_bin + 1).astype(jnp.float32) / NBINS

    def forward(query_start, passage_start, weight_set):
        query_out = encode_all(query_start, query_length, weight_set, query_block)
        passage_out = encode_all(passage_start, passage_length, weight_set, passage_block)
        logits = low_back(precise_product(query_out[:, 0, :], passage_out[:, 0, :].T) * score_scale)
        normalizer = jax.nn.logsumexp(jnp.where(allowed, logits, -1e+30), axis=-1)
        chosen = jnp.take_along_axis(logits, positive_index[:, None], axis=1)[:, 0]
        return (query_out, passage_out, margin_weight * (normalizer - chosen))
    outputs, pullback = jax.vjp(forward, query_input.astype(jnp.float32), passage_input.astype(jnp.float32), weights)
    query_grad, passage_grad, weight_grads = pullback((query_cotangent.astype(jnp.float32), passage_cotangent.astype(jnp.float32), jnp.ones((QUERIES,), jnp.float32)))
    return (outputs[0].astype(jnp.bfloat16), outputs[1].astype(jnp.bfloat16), outputs[2], query_grad, passage_grad, weight_grads[0], weight_grads[1], weight_grads[2], weight_grads[3], weight_grads[4], weight_grads[5], weight_grads[6], weight_grads[7], weight_grads[8], weight_grads[9], weight_grads[10], weight_grads[11], weight_grads[12], weight_grads[13], weight_grads[14])
```

```python
import functools
import math

import jax
import jax.numpy as jnp
from jax import lax
from jax.experimental import pallas as pl
from jax.experimental.pallas import tpu as pltpu
from jax.sharding import PartitionSpec as P

HEADS = 12
DH = 64
LAYERS = 2
NBINS = 10


def narrow(values):
    return values.astype(jnp.bfloat16)


def product(former, latter):
    return jnp.dot(former, latter, preferred_element_type=jnp.float32)


def contract_rows(former, latter):
    return lax.dot_general(
        former, latter, (((0,), (0,)), ((), ())), preferred_element_type=jnp.float32
    )


def contract_last(former, latter):
    return lax.dot_general(
        former, latter, (((1,), (1,)), ((), ())), preferred_element_type=jnp.float32
    )


def column_total(values):
    return jnp.sum(values.astype(jnp.float32), axis=0)


def norm_forward(summed, gain_vector, shift_vector):
    average = jnp.mean(summed, axis=-1, keepdims=True)
    centred = summed - average
    scaled = lax.rsqrt(jnp.mean(centred * centred, axis=-1, keepdims=True) + 1e-12)
    unit_rows = centred * scaled
    return (unit_rows * gain_vector + shift_vector, unit_rows, scaled)


def norm_backward(upstream, unit_rows, scaled, gain_vector):
    delta_unit = upstream * gain_vector
    delta_summed = scaled * (
        delta_unit
        - jnp.mean(delta_unit, axis=-1, keepdims=True)
        - unit_rows * jnp.mean(delta_unit * unit_rows, axis=-1, keepdims=True)
    )
    return (delta_summed, jnp.sum(upstream * unit_rows, axis=0), jnp.sum(upstream, axis=0))


def gelu_slope(expanded):
    cumulative = 0.5 * (1.0 + lax.erf(expanded * (1.0 / math.sqrt(2.0))))
    density = jnp.exp(-0.5 * expanded * expanded) * (1.0 / math.sqrt(2.0 * math.pi))
    return cumulative + expanded * density


def split_heads(flat, group_count, length):
    return flat.reshape(group_count, length, HEADS, DH)


def group_spans(layout):
    spans = []
    offset = 0
    for group_count, length in layout:
        spans.append((offset, group_count, length))
        offset = offset + group_count * length
    return spans


def head_scores(query_part, key_part, keep_mask):
    scores = (
        jnp.einsum("bqhd,bkhd->bhqk", query_part, key_part, preferred_element_type=jnp.float32)
        * 0.125
    )
    return jnp.where(keep_mask[:, None, None, :], scores, -1e30)


def attend_forward(query_part, key_part, value_part, keep_mask):
    scores = head_scores(query_part, key_part, keep_mask)
    peak_score = jnp.max(scores, axis=-1, keepdims=True)
    normalizer = peak_score + jnp.log(jnp.sum(jnp.exp(scores - peak_score), axis=-1, keepdims=True))
    attention = narrow(jnp.exp(scores - normalizer))
    context = jnp.einsum(
        "bhqk,bkhd->bqhd", attention, value_part, preferred_element_type=jnp.float32
    )
    return (narrow(context), normalizer)


def attend_backward(query_part, key_part, value_part, keep_mask, normalizer, delta_context):
    scores = head_scores(query_part, key_part, keep_mask)
    attention = jnp.exp(scores - normalizer)
    delta_value = jnp.einsum(
        "bhqk,bqhd->bkhd", narrow(attention), delta_context, preferred_element_type=jnp.float32
    )
    delta_attention = jnp.einsum(
        "bqhd,bkhd->bhqk", delta_context, value_part, preferred_element_type=jnp.float32
    )
    delta_scores = narrow(
        attention * (delta_attention - jnp.sum(attention * delta_attention, axis=-1, keepdims=True))
    )
    delta_query = (
        jnp.einsum("bhqk,bkhd->bqhd", delta_scores, key_part, preferred_element_type=jnp.float32)
        * 0.125
    )
    delta_key = (
        jnp.einsum("bhqk,bqhd->bkhd", delta_scores, query_part, preferred_element_type=jnp.float32)
        * 0.125
    )
    return (delta_query, delta_key, delta_value)


def layer_forward(hidden, keep_masks, layout, params):
    (
        query_weight,
        query_bias,
        key_weight,
        value_weight,
        value_bias,
        mix_weight,
        mix_bias,
        norm_gain,
        norm_shift,
        expand_weight,
        expand_bias,
        reduce_weight,
        reduce_bias,
        final_gain,
        final_shift,
    ) = params
    query_heads = narrow(product(hidden, query_weight) + query_bias)
    key_heads = narrow(product(hidden, key_weight))
    value_heads = narrow(product(hidden, value_weight) + value_bias)
    contexts = []
    normalizers = []
    for keep_mask, (offset, group_count, length) in zip(keep_masks, group_spans(layout)):
        row_span = group_count * length
        pieces = [
            split_heads(array[offset : offset + row_span], group_count, length)
            for array in (query_heads, key_heads, value_heads)
        ]
        context, normalizer = attend_forward(pieces[0], pieces[1], pieces[2], keep_mask)
        contexts.append(context.reshape(row_span, -1))
        normalizers.append(normalizer)
    context = jnp.concatenate(contexts, axis=0)
    summed_one = hidden.astype(jnp.float32) + product(context, mix_weight) + mix_bias
    middle_full, unit_one, scale_one = norm_forward(summed_one, norm_gain, norm_shift)
    middle = narrow(middle_full)
    expanded = product(middle, expand_weight) + expand_bias
    active = narrow(jax.nn.gelu(expanded, approximate=False))
    summed_two = middle.astype(jnp.float32) + product(active, reduce_weight) + reduce_bias
    result_full, unit_two, scale_two = norm_forward(summed_two, final_gain, final_shift)
    stored = (
        hidden,
        query_heads,
        key_heads,
        value_heads,
        normalizers,
        context,
        unit_one,
        scale_one,
        middle,
        expanded,
        active,
        unit_two,
        scale_two,
    )
    return (narrow(result_full), stored)


def layer_backward(upstream, stored, keep_masks, layout, params):
    (
        query_weight,
        query_bias,
        key_weight,
        value_weight,
        value_bias,
        mix_weight,
        mix_bias,
        norm_gain,
        norm_shift,
        expand_weight,
        expand_bias,
        reduce_weight,
        reduce_bias,
        final_gain,
        final_shift,
    ) = params
    (
        hidden,
        query_heads,
        key_heads,
        value_heads,
        normalizers,
        context,
        unit_one,
        scale_one,
        middle,
        expanded,
        active,
        unit_two,
        scale_two,
    ) = stored
    delta_two, delta_final_gain, delta_final_shift = norm_backward(
        upstream, unit_two, scale_two, final_gain
    )
    delta_branch = narrow(delta_two)
    delta_reduce_bias = column_total(delta_branch)
    delta_expanded = narrow(contract_last(delta_branch, reduce_weight) * gelu_slope(expanded))
    delta_expand_bias = column_total(delta_expanded)
    delta_middle = delta_two + contract_last(delta_expanded, expand_weight)
    delta_one, delta_norm_gain, delta_norm_shift = norm_backward(
        delta_middle, unit_one, scale_one, norm_gain
    )
    delta_mix = narrow(delta_one)
    delta_mix_bias = column_total(delta_mix)
    delta_context = narrow(contract_last(delta_mix, mix_weight))
    collected = ([], [], [])
    for keep_mask, normalizer, (offset, group_count, length) in zip(
        keep_masks, normalizers, group_spans(layout)
    ):
        row_span = group_count * length
        pieces = [
            split_heads(array[offset : offset + row_span], group_count, length)
            for array in (query_heads, key_heads, value_heads, delta_context)
        ]
        results = attend_backward(pieces[0], pieces[1], pieces[2], keep_mask, normalizer, pieces[3])
        for bucket, gradient in zip(collected, results):
            bucket.append(narrow(gradient.reshape(row_span, -1)))
    delta_query = jnp.concatenate(collected[0], axis=0)
    delta_key = jnp.concatenate(collected[1], axis=0)
    delta_value = jnp.concatenate(collected[2], axis=0)
    delta_hidden = (
        delta_one
        + contract_last(delta_query, query_weight)
        + contract_last(delta_key, key_weight)
        + contract_last(delta_value, value_weight)
    )
    operands = (
        active,
        delta_branch,
        middle,
        delta_expanded,
        hidden,
        context,
        delta_query,
        delta_key,
        delta_value,
        delta_mix,
    )
    vectors = (
        column_total(delta_query),
        column_total(delta_value),
        delta_mix_bias,
        delta_norm_gain,
        delta_norm_shift,
        delta_expand_bias,
        delta_reduce_bias,
        delta_final_gain,
        delta_final_shift,
    )
    return (delta_hidden, operands, vectors)


CORE_FLIP = [(0, 1), (1, 0), (2, 3), (3, 2)]
SIDE_FLIP = [(0, 2), (2, 0), (1, 3), (3, 1)]


def wide(values):
    return values.astype(jnp.float32)


def pick(array, index):
    return lax.dynamic_index_in_dim(array, index, 0, keepdims=False)


def reduce_chunk(chunk):
    rep_total = lax.axis_size("rep")
    group = lax.axis_index("grp")
    side, core = group // 2, group % 2
    parts = chunk.reshape((2, 2) + chunk.shape[1:])
    got = lax.ppermute(
        lax.dynamic_index_in_dim(parts, 1 - core, 1, keepdims=False), "grp", CORE_FLIP
    )
    mine = lax.dynamic_index_in_dim(parts, core, 1, keepdims=False)
    got = lax.ppermute(
        narrow(wide(pick(mine, 1 - side)) + wide(pick(got, 1 - side))), "grp", SIDE_FLIP
    ), narrow(wide(pick(mine, side)) + wide(pick(got, side)))
    summed = narrow(wide(got[0]) + wide(got[1]))
    rows, columns = summed.shape
    if rep_total != 8:
        part = lax.psum_scatter(summed, "rep", scatter_dimension=0, tiled=True)
        return wide(lax.all_gather(part, "rep", axis=0, tiled=True))
    rep = lax.axis_index("rep")
    deep, near = rep // 2, rep % 2
    flip = [(i, i ^ 1) for i in range(8)]
    shifts = [[(i, (i + 2 * k) % 8) for i in range(8)] for k in range(4)]
    halves = summed.reshape(2, rows // 2, columns)
    got = lax.ppermute(pick(halves, 1 - near), "rep", flip)
    half = narrow(wide(pick(halves, near)) + wide(got)).reshape(4, rows // 8, columns)
    total = wide(pick(half, deep))
    for k in range(1, 4):
        total = total + wide(lax.ppermute(pick(half, (deep + k) % 4), "rep", shifts[k]))
    piece = narrow(total)
    pieces = [piece] + [lax.ppermute(piece, "rep", shifts[k]) for k in range(1, 4)]
    joined = jnp.zeros((4,) + piece.shape, jnp.bfloat16)
    for k in range(4):
        joined = lax.dynamic_update_index_in_dim(joined, pieces[k], (deep - k) % 4, 0)
    other = lax.ppermute(joined, "rep", flip)
    own = joined.reshape(rows // 2, columns)
    other = other.reshape(rows // 2, columns)
    first = jnp.where(near == 0, own, other)
    second = jnp.where(near == 0, other, own)
    return wide(jnp.concatenate([first, second], axis=0))


def reduce_small(small):
    group = lax.axis_index("grp")
    side, core = group // 2, group % 2
    parts = small.reshape(2, 2, -1)
    got = lax.ppermute(
        lax.dynamic_index_in_dim(parts, 1 - core, 1, keepdims=False), "grp", CORE_FLIP
    )
    pair = lax.dynamic_index_in_dim(parts, core, 1, keepdims=False) + got
    total = pick(pair, side) + lax.ppermute(pick(pair, 1 - side), "grp", SIDE_FLIP)
    rep_total = lax.axis_size("rep")
    step = 1
    while step < rep_total:
        total = total + lax.ppermute(total, "rep", [(i, i ^ step) for i in range(rep_total)])
        step = step * 2
    return total


def remote(source, target, send_sem, recv_sem, grp, rep):
    return pltpu.make_async_remote_copy(
        src_ref=source,
        dst_ref=target,
        send_sem=send_sem,
        recv_sem=recv_sem,
        device_id=(grp, rep),
        device_id_type=pl.DeviceIdType.MESH,
    )


def gather_kernel(block_ref, out_ref, send_near, recv_near, send_far, recv_far):
    groups, reps = out_ref.shape[:2]
    grp, rep = lax.axis_index("grp"), lax.axis_index("rep")
    barrier = pltpu.get_barrier_semaphore()

    @pl.loop(1, reps)
    def _(k):
        pl.semaphore_signal(
            barrier, inc=1, device_id=(grp, (rep + k) % reps), device_id_type=pl.DeviceIdType.MESH
        )

    for k in range(1, groups):
        pl.semaphore_signal(
            barrier, inc=1, device_id=((grp + k) % groups, rep), device_id_type=pl.DeviceIdType.MESH
        )
    out_ref[grp, rep] = block_ref[...]
    pl.semaphore_wait(barrier, reps + groups - 2)

    def near(k):
        mine = out_ref.at[grp, rep]
        return remote(mine, mine, send_near.at[k], recv_near.at[k], grp, (rep + k) % reps)

    def far(k):
        row = out_ref.at[grp]
        return remote(row, row, send_far.at[k], recv_far.at[k], (grp + k) % groups, rep)

    @pl.loop(1, reps)
    def _(k):
        near(k).start()

    @pl.loop(1, reps)
    def _(k):
        near(k).wait_recv()

    for k in range(1, groups):
        far(k).start()
    for k in range(1, groups):
        far(k).wait_recv()

    @pl.loop(1, reps)
    def _(k):
        near(k).wait_send()

    for k in range(1, groups):
        far(k).wait_send()


def gather_blocks(block):
    groups, reps = lax.axis_size("grp"), lax.axis_size("rep")
    return pl.pallas_call(
        gather_kernel,
        out_shape=jax.ShapeDtypeStruct((groups, reps) + block.shape, block.dtype),
        in_specs=[pl.BlockSpec(memory_space=pltpu.VMEM)],
        out_specs=pl.BlockSpec(memory_space=pltpu.VMEM),
        scratch_shapes=[
            pltpu.SemaphoreType.DMA((reps,)),
            pltpu.SemaphoreType.DMA((reps,)),
            pltpu.SemaphoreType.DMA((groups,)),
            pltpu.SemaphoreType.DMA((groups,)),
        ],
        compiler_params=pltpu.CompilerParams(collective_id=1, has_side_effects=True),
    )(block)


CHUNKS = 12
OPERANDS = 10


def exchange_kernel(*refs):
    operands = refs[: 2 * OPERANDS]
    (
        small_ref,
        out_ref,
        small_out,
        big,
        slim,
        buf,
        keep,
        side_out,
        core_in,
        side_in,
        near_in,
        deep_in,
        piece,
        small_buf,
        small_core,
        small_side,
        small_near,
        small_deep,
        load_sem,
        core_sem,
        side_sem,
        near_sem,
        deep_send,
        deep_recv,
        back_send,
        back_recv,
        local_sem,
        last_sem,
        small_sem,
        small_send,
        small_recv,
    ) = refs[2 * OPERANDS :]
    depth = deep_in.shape[1] + 1
    width = keep.shape[2]
    quarter = width // 4
    rows = keep.shape[1]
    half_rows = rows // 2
    piece_rows = half_rows // depth
    grp, rep = lax.axis_index("grp"), lax.axis_index("rep")
    side, core = grp // 2, grp % 2
    deep, near = rep // 2, rep % 2
    sibling = (2 * side + (1 - core), rep)
    across = (2 * (1 - side) + core, rep)
    beside = (grp, 2 * deep + (1 - near))

    def behind(k):
        return (grp, 2 * ((deep + k) % depth) + near)

    peers = [sibling, across, beside] + [behind(k) for k in range(1, depth)]
    barrier = pltpu.get_barrier_semaphore()
    for peer in peers:
        pl.semaphore_signal(barrier, inc=1, device_id=peer, device_id_type=pl.DeviceIdType.MESH)

    def loads(group):
        slot = group % 2
        layer = operands[OPERANDS * (group // 3) : OPERANDS * (group // 3 + 1)]
        active, branch, middle, expanded, hidden, context, query, key, value, mix = layer
        whole = pl.ds(0, 4 * width)
        if group % 3 == 0:
            pairs = [(active, big, whole), (branch, slim, pl.ds(0, width))]
        elif group % 3 == 1:
            pairs = [(expanded, big, whole), (middle, slim, pl.ds(0, width))]
        else:
            pairs = [
                (array, big, pl.ds(place * width, width))
                for place, array in enumerate((query, key, value, mix))
            ]
            pairs += [(hidden, slim, pl.ds(0, width)), (context, slim, pl.ds(width, width))]
        return [
            pltpu.make_async_copy(array, target.at[slot, :, columns], load_sem.at[slot, place])
            for place, (array, target, columns) in enumerate(pairs)
        ]

    for copy in loads(0):
        copy.start()
    pl.semaphore_wait(barrier, len(peers))

    def core_copy(t):
        return remote(
            buf.at[t % 2, :, 1 - core], core_in.at[t], core_sem.at[0, t], core_sem.at[1, t], *sibling
        )

    def side_copy(t):
        return remote(
            side_out.at[t % 3], side_in.at[t], side_sem.at[0, t], side_sem.at[1, t], *across
        )

    def near_copy(t):
        far_half = keep.at[t, pl.ds(pl.multiple_of((1 - near) * half_rows, 16), half_rows)]
        return remote(far_half, near_in.at[t], near_sem.at[0, t], near_sem.at[1, t], *beside)

    def piece_of(position):
        return pl.ds(pl.multiple_of(near * half_rows + position * piece_rows, 16), piece_rows)

    def deep_copy(t, k):
        return remote(
            keep.at[t, piece_of((deep + k) % depth)],
            deep_in.at[t, k - 1],
            deep_send.at[k - 1, t],
            deep_recv.at[k - 1, t],
            *behind(k),
        )

    def back_copy(t, k):
        return remote(
            piece.at[t],
            out_ref.at[t, piece_of(deep)],
            back_send.at[k - 1, t],
            back_recv.at[k - 1, t],
            *behind(k),
        )

    def local_copy(t):
        return pltpu.make_async_copy(piece.at[t], out_ref.at[t, piece_of(deep)], local_sem.at[t])

    def last_copy(t):
        half = out_ref.at[t, pl.ds(pl.multiple_of(near * half_rows, 16), half_rows)]
        return remote(half, half, last_sem.at[0, t], last_sem.at[1, t], *beside)

    def add_rows(target, first, second, total):
        step = 48

        @pl.loop(0, total // step)
        def _(i):
            at = pl.ds(pl.multiple_of(i * step, 16), step)
            target(at, narrow(wide(first(at)) + wide(second(at))))

    def make_terms(t):
        group, part = t // 2, t % 2
        slot = group % 2

        @pl.when(part == 0)
        def _():
            for static in range(CHUNKS // 2):

                @pl.when(group == static)
                def _():
                    for copy in loads(static):
                        copy.wait()
                    if static + 1 < CHUNKS // 2:
                        for copy in loads(static + 1):
                            copy.start()

        tall = group % 3 == 0

        @pl.when(tall)
        def _():
            @pl.loop(0, 4)
            def _(i):
                columns = pl.ds(pl.multiple_of(i * width + part * rows, 128), rows)
                terms = contract_rows(big[slot, :, columns], slim[slot, :, pl.ds(0, width)])
                buf[t % 2, i // 2, i % 2] = narrow(terms)

        @pl.when(jnp.logical_not(tall))
        def _():
            @pl.loop(0, 4)
            def _(i):
                unit, half = i // 2, i % 2
                mixing = jnp.where((group % 3 == 2) & (part == 1) & (unit == 1), width, 0)
                rows_at = pl.ds(pl.multiple_of(mixing + half * (2 * quarter), 128), 2 * quarter)
                columns = pl.ds(pl.multiple_of((2 * part + unit) * width, 128), width)
                terms = narrow(contract_rows(slim[slot, :, rows_at], big[slot, :, columns]))
                place = pl.ds(pl.multiple_of(unit * quarter, 16), quarter)
                buf[t % 2, half, 0, place] = terms[:quarter]
                buf[t % 2, half, 1, place] = terms[quarter:]

        core_copy(t).start()

    def after_core(t):
        core_copy(t).wait()

        def to_side(at, values):
            side_out[t % 3, at] = values

        add_rows(
            to_side,
            lambda at: buf[t % 2, 1 - side, core, at],
            lambda at: core_in[t, 1 - side, at],
            rows,
        )
        side_copy(t).start()

        def to_keep(at, values):
            keep[t, at] = values

        add_rows(
            to_keep,
            lambda at: buf[t % 2, side, core, at],
            lambda at: core_in[t, side, at],
            rows,
        )

    def after_side(t):
        side_copy(t).wait()
        for half in (1 - near, near):

            def shifted(at):
                return pl.ds(pl.multiple_of(half * half_rows + at.start, 16), at.size)

            def to_keep(at, values):
                keep[t, shifted(at)] = values

            add_rows(
                to_keep,
                lambda at: keep[t, shifted(at)],
                lambda at: side_in[t, shifted(at)],
                half_rows,
            )
            if half is not near:
                near_copy(t).start()

    def after_near(t):
        near_copy(t).wait()

        def shifted(at):
            return pl.ds(pl.multiple_of(near * half_rows + at.start, 16), at.size)

        def to_keep(at, values):
            keep[t, shifted(at)] = values

        add_rows(
            to_keep, lambda at: keep[t, shifted(at)], lambda at: near_in[t, at], half_rows
        )
        for k in range(1, depth):
            deep_copy(t, k).start()

    def after_deep(t):
        total = wide(keep[t, piece_of(deep)])
        for k in range(1, depth):
            deep_copy(t, k).wait_recv()
        for k in range(1, depth):
            total = total + wide(deep_in[t, k - 1])
        piece[t] = narrow(total)
        local_copy(t).start()
        for k in range(1, depth):
            back_copy(t, k).start()

    def after_back(t):
        local_copy(t).wait()
        for k in range(1, depth):
            back_copy(t, k).wait_recv()
        last_copy(t).start()

    def small_to_core():
        return remote(
            small_ref.at[:, 1 - core], small_core, small_sem.at[0], small_sem.at[1], *sibling
        )

    def small_to_side():
        return remote(
            small_buf.at[1 - side], small_side, small_sem.at[2], small_sem.at[3], *across
        )

    def small_to_near():
        return remote(small_buf.at[side], small_near, small_sem.at[4], small_sem.at[5], *beside)

    def small_to_deep(k):
        own = small_deep.at[deep]
        return remote(own, own, small_send.at[k - 1], small_recv.at[k - 1], *behind(k))

    small_to_core().start()

    @pl.loop(0, CHUNKS + 5)
    def _(t):
        @pl.when(t < CHUNKS)
        def _():
            make_terms(t)

        for lag, stage in enumerate((after_core, after_side, after_near, after_deep, after_back)):

            @pl.when((t > lag) & (t < CHUNKS + lag + 1))
            def _():
                stage(t - lag - 1)

        @pl.when(t == 0)
        def _():
            small_to_core().wait()
            for half in range(2):
                small_buf[half] = small_ref[half, core] + small_core[half]
            small_to_side().start()

        @pl.when(t == 1)
        def _():
            small_to_side().wait()
            small_buf[side] = small_buf[side] + small_side[...]
            small_to_near().start()

        @pl.when(t == 2)
        def _():
            small_to_near().wait()
            small_deep[deep] = small_buf[side] + small_near[...]
            for k in range(1, depth):
                small_to_deep(k).start()

        @pl.when(t == 3)
        def _():
            for k in range(1, depth):
                small_to_deep(k).wait()
            total = small_deep[0]
            for k in range(1, depth):
                total = total + small_deep[k]
            small_out[...] = total

    @pl.loop(0, CHUNKS)
    def _(t):
        for k in range(1, depth):
            deep_copy(t, k).wait_send()
            back_copy(t, k).wait_send()
        last_copy(t).wait()


def exchange(layers, small):
    tokens, width = layers[0][1].shape
    depth = lax.axis_size("rep") // 2
    rows = width // 2
    bf16, f32 = jnp.bfloat16, jnp.float32
    dma = pltpu.SemaphoreType.DMA
    piece_rows = rows // 2 // depth
    small_shape = small.shape[2:]
    return pl.pallas_call(
        exchange_kernel,
        out_shape=(
            jax.ShapeDtypeStruct((CHUNKS, rows, width), bf16),
            jax.ShapeDtypeStruct(small_shape, f32),
        ),
        in_specs=[pl.BlockSpec(memory_space=pl.ANY)] * (2 * OPERANDS)
        + [pl.BlockSpec(memory_space=pltpu.VMEM)],
        out_specs=(pl.BlockSpec(memory_space=pl.ANY), pl.BlockSpec(memory_space=pltpu.VMEM)),
        scratch_shapes=[
            pltpu.VMEM((2, tokens, 4 * width), bf16),
            pltpu.VMEM((2, tokens, 2 * width), bf16),
            pltpu.VMEM((2, 2, 2, rows, width), bf16),
            pltpu.VMEM((CHUNKS, rows, width), bf16),
            pltpu.VMEM((3, rows, width), bf16),
            pltpu.VMEM((CHUNKS, 2, rows, width), bf16),
            pltpu.VMEM((CHUNKS, rows, width), bf16),
            pltpu.VMEM((CHUNKS, rows // 2, width), bf16),
            pltpu.VMEM((CHUNKS, depth - 1, piece_rows, width), bf16),
            pltpu.VMEM((CHUNKS, piece_rows, width), bf16),
            pltpu.VMEM((2,) + small_shape, f32),
            pltpu.VMEM((2,) + small_shape, f32),
            pltpu.VMEM(small_shape, f32),
            pltpu.VMEM(small_shape, f32),
            pltpu.VMEM((depth,) + small_shape, f32),
            dma((2, 6)),
            dma((2, CHUNKS)),
            dma((2, CHUNKS)),
            dma((2, CHUNKS)),
            dma((depth - 1, CHUNKS)),
            dma((depth - 1, CHUNKS)),
            dma((depth - 1, CHUNKS)),
            dma((depth - 1, CHUNKS)),
            dma((CHUNKS,)),
            dma((2, CHUNKS)),
            dma((6,)),
            dma((depth - 1,)),
            dma((depth - 1,)),
        ],
        compiler_params=pltpu.CompilerParams(
            collective_id=0, has_side_effects=True, vmem_limit_bytes=60 * 1024 * 1024
        ),
    )(*layers[0], *layers[1], small)


def reduce_plain(layers):
    results = []
    for active, branch, middle, expanded, hidden, context, query, key, value, mix in layers:
        quarter = lambda former, latter: (
            lambda matrix: narrow(matrix).reshape(4, matrix.shape[0] // 4, matrix.shape[1])
        )(contract_rows(former, latter))
        square = jnp.concatenate(
            [
                quarter(hidden, query),
                quarter(hidden, key),
                quarter(hidden, value),
                quarter(context, mix),
            ],
            axis=1,
        )
        square = reduce_chunk(square)
        height = square.shape[0] // 4
        results.append(
            [square[place * height : (place + 1) * height] for place in range(4)]
            + [reduce_chunk(quarter(middle, expanded)), reduce_chunk(quarter(active, branch))]
        )
    return [jnp.stack([results[1][i], results[0][i]]) for i in range(6)]


def reduce_matrices(layers, small):
    if lax.axis_size("rep") != 8:
        return reduce_plain(layers), reduce_small(small)
    size = small.shape[1]
    small_rows = -(-size // 1024) * 8
    padded = jnp.pad(small, ((0, 0), (0, small_rows * 128 - size)))
    out, small_sum = exchange(layers, padded.reshape(2, 2, small_rows, 128))
    width = out.shape[2]
    out = wide(out).reshape(2, 12, width // 4, width)[::-1]
    reduce_part = out[:, 0:4].reshape(2, width, width)
    expand_part = jnp.swapaxes(out[:, 4:8], 1, 2).reshape(2, width // 4, 4 * width)
    square = [out[:, 8 + place] for place in range(4)]
    return square + [expand_part, reduce_part], small_sum.reshape(-1)[:size]


SMALL = (1, 4, 6, 7, 8, 10, 12, 13, 14)
MATRICES = (0, 2, 3, 5, 9, 11)


def per_device(
    query_input,
    passage_input,
    query_length,
    passage_length,
    cluster_index,
    margin_bin,
    positive_index,
    query_cotangent,
    passage_cotangent,
    query_weight,
    query_bias,
    key_weight,
    value_weight,
    value_bias,
    mix_weight,
    mix_bias,
    norm_gain,
    norm_shift,
    expand_weight,
    expand_bias,
    reduce_weight,
    reduce_bias,
    final_gain,
    final_shift,
):
    params = (
        query_weight,
        query_bias,
        key_weight,
        value_weight,
        value_bias,
        mix_weight,
        mix_bias,
        norm_gain,
        norm_shift,
        expand_weight,
        expand_bias,
        reduce_weight,
        reduce_bias,
        final_gain,
        final_shift,
    )
    batch_size, query_len, model_width = query_input.shape
    passage_len = passage_input.shape[1]
    layout = ((batch_size, query_len), (batch_size, passage_len))
    keep_masks = (
        lax.broadcasted_iota(jnp.int32, (batch_size, query_len), 1) < query_length[:, None],
        lax.broadcasted_iota(jnp.int32, (batch_size, passage_len), 1) < passage_length[:, None],
    )
    query_span = batch_size * query_len
    hidden = jnp.concatenate(
        [
            query_input.reshape(query_span, model_width),
            passage_input.reshape(batch_size * passage_len, model_width),
        ],
        axis=0,
    )
    stored_layers = []
    for layer_index in range(LAYERS):
        layer_params = tuple((array[layer_index] for array in params))
        hidden, stored = layer_forward(hidden, keep_masks, layout, layer_params)
        stored_layers.append(stored)
    query_output = hidden[:query_span].reshape(batch_size, query_len, model_width)
    passage_output = hidden[query_span:].reshape(batch_size, passage_len, model_width)
    query_first = query_output[:, 0, :]
    passage_first = passage_output[:, 0, :]
    facts = jnp.concatenate(
        [margin_bin, positive_index // 128, positive_index % 128], axis=0
    ).astype(jnp.bfloat16)
    facts = jnp.pad(facts, (0, model_width - facts.shape[0]))
    block = jnp.concatenate([query_first, passage_first, facts[None, :]], axis=0)
    block = jnp.pad(block, ((0, 8 - block.shape[0]), (0, 0)))
    total = cluster_index.shape[0]
    every = gather_blocks(block).reshape(-1, 8, model_width)
    every_query = every[:, :batch_size].reshape(total, model_width)
    every_passage = every[:, batch_size : 2 * batch_size].reshape(total, model_width)
    facts = every[:, 2 * batch_size, : 3 * batch_size].astype(jnp.int32)
    facts = facts.reshape(-1, 3, batch_size)
    every_margin = facts[:, 0].reshape(total)
    every_positive = (facts[:, 1] * 128 + facts[:, 2]).reshape(total)
    start_row = lax.axis_index(("grp", "rep")) * batch_size
    score_scale = 2.0 / math.sqrt(model_width)
    logits = contract_last(every_query, every_passage) * score_scale
    columns = lax.broadcasted_iota(jnp.int32, logits.shape, 1)
    chosen_mask = columns == every_positive[:, None]
    allowed = (cluster_index[None, :] == cluster_index[:, None]) | chosen_mask
    masked = jnp.where(allowed, logits, -1e30)
    peak_score = jnp.max(masked, axis=1, keepdims=True)
    normalizer = peak_score + jnp.log(jnp.sum(jnp.exp(masked - peak_score), axis=1, keepdims=True))
    chosen = jnp.sum(jnp.where(chosen_mask, logits, 0.0), axis=1)
    margin_weight = (every_margin + 1).astype(jnp.float32) / NBINS
    every_loss = margin_weight * (normalizer[:, 0] - chosen)
    query_loss = lax.dynamic_slice_in_dim(every_loss, start_row, batch_size)
    delta_logits = narrow(
        margin_weight[:, None]
        * (jnp.where(allowed, jnp.exp(masked - normalizer), 0.0) - chosen_mask.astype(jnp.float32))
    )
    own_rows = lax.dynamic_slice_in_dim(delta_logits, start_row, batch_size, axis=0)
    own_columns = lax.dynamic_slice_in_dim(delta_logits, start_row, batch_size, axis=1)
    delta_query_first = product(own_rows, every_passage) * score_scale
    delta_passage_first = contract_rows(own_columns, every_query) * score_scale
    query_upstream = query_cotangent.astype(jnp.float32).at[:, 0, :].add(delta_query_first)
    passage_upstream = passage_cotangent.astype(jnp.float32).at[:, 0, :].add(delta_passage_first)
    upstream = jnp.concatenate(
        [
            query_upstream.reshape(query_span, model_width),
            passage_upstream.reshape(batch_size * passage_len, model_width),
        ],
        axis=0,
    )
    operands = []
    small = []
    for layer_index in reversed(range(LAYERS)):
        layer_params = tuple((array[layer_index] for array in params))
        upstream, layer_operands, vectors = layer_backward(
            upstream, stored_layers[layer_index], keep_masks, layout, layer_params
        )
        operands.append(layer_operands)
        small.append([vector.reshape(4, -1) for vector in vectors])
    small = small[::-1]
    matrices, flat = reduce_matrices(operands, jnp.concatenate(small[0] + small[1], axis=1))
    reduced = [None] * 15
    for slot, matrix in zip(MATRICES, matrices):
        reduced[slot] = matrix
    flat = flat.reshape(LAYERS, -1)
    offset = 0
    for slot, vector in zip(SMALL, small[0]):
        size = vector.shape[1]
        reduced[slot] = flat[:, offset : offset + size]
        offset = offset + size
    query_input_gradient = upstream[:query_span].reshape(batch_size, query_len, model_width)
    passage_input_gradient = upstream[query_span:].reshape(batch_size, passage_len, model_width)
    return (
        query_output,
        passage_output,
        query_loss,
        query_input_gradient,
        passage_input_gradient,
        reduced[0],
        reduced[1],
        reduced[2],
        reduced[3],
        reduced[4],
        reduced[5],
        reduced[6],
        reduced[7],
        reduced[8],
        reduced[9],
        reduced[10],
        reduced[11],
        reduced[12],
        reduced[13],
        reduced[14],
    )


def solution(mesh):
    placed = (
        P(("grp", "rep"), None, None),
        P(("grp", "rep"), None, None),
        P(("grp", "rep")),
        P(("grp", "rep")),
        P(),
        P(("grp", "rep")),
        P(("grp", "rep")),
        P(("grp", "rep"), None, None),
        P(("grp", "rep"), None, None),
        P(),
        P(),
        P(),
        P(),
        P(),
        P(),
        P(),
        P(),
        P(),
        P(),
        P(),
        P(),
        P(),
        P(),
        P(),
    )
    return jax.shard_map(
        per_device,
        mesh=mesh,
        in_specs=placed,
        out_specs=(
            P(("grp", "rep"), None, None),
            P(("grp", "rep"), None, None),
            P(("grp", "rep")),
            P(("grp", "rep"), None, None),
            P(("grp", "rep"), None, None),
            P(None, "grp", None),
            P(None, "grp"),
            P(None, "grp", None),
            P(None, "grp", None),
            P(None, "grp"),
            P(None, "grp", None),
            P(None, "grp"),
            P(None, "grp"),
            P(None, "grp"),
            P(None, "grp", None),
            P(None, "grp"),
            P(None, "grp", None),
            P(None, "grp"),
            P(None, "grp"),
            P(None, "grp"),
        ),
        check_vma=False,
    )
```

```python
import functools
import math

import jax
import jax.numpy as jnp
from jax import lax
from jax.experimental import pallas as pl
from jax.experimental.pallas import tpu as pltpu
from jax.sharding import PartitionSpec as P

HEADS = 12
DH = 64
LAYERS = 2
NBINS = 10


def narrow(values):
    return values.astype(jnp.bfloat16)


def product(former, latter):
    return jnp.dot(former, latter, preferred_element_type=jnp.float32)


def contract_rows(former, latter):
    return lax.dot_general(
        former, latter, (((0,), (0,)), ((), ())), preferred_element_type=jnp.float32
    )


def contract_last(former, latter):
    return lax.dot_general(
        former, latter, (((1,), (1,)), ((), ())), preferred_element_type=jnp.float32
    )


def column_total(values):
    return jnp.sum(values.astype(jnp.float32), axis=0)


def norm_forward(summed, gain_vector, shift_vector):
    average = jnp.mean(summed, axis=-1, keepdims=True)
    centred = summed - average
    scaled = lax.rsqrt(jnp.mean(centred * centred, axis=-1, keepdims=True) + 1e-12)
    unit_rows = centred * scaled
    return (unit_rows * gain_vector + shift_vector, unit_rows, scaled)


def norm_backward(upstream, unit_rows, scaled, gain_vector):
    delta_unit = upstream * gain_vector
    delta_summed = scaled * (
        delta_unit
        - jnp.mean(delta_unit, axis=-1, keepdims=True)
        - unit_rows * jnp.mean(delta_unit * unit_rows, axis=-1, keepdims=True)
    )
    return (delta_summed, jnp.sum(upstream * unit_rows, axis=0), jnp.sum(upstream, axis=0))


def split_heads(flat, group_count, length):
    return flat.reshape(group_count, length, HEADS, DH)


def group_spans(layout):
    spans = []
    offset = 0
    for group_count, length in layout:
        spans.append((offset, group_count, length))
        offset = offset + group_count * length
    return spans


def attend_backward(query_part, key_part, value_part, shares, delta_context):
    attention = wide(shares)
    delta_value = jnp.einsum(
        "bhqk,bqhd->bkhd", narrow(attention), delta_context, preferred_element_type=jnp.float32
    )
    delta_attention = jnp.einsum(
        "bqhd,bkhd->bhqk", delta_context, value_part, preferred_element_type=jnp.float32
    )
    delta_scores = narrow(
        attention * (delta_attention - jnp.sum(attention * delta_attention, axis=-1, keepdims=True))
    )
    delta_query = (
        jnp.einsum("bhqk,bkhd->bqhd", delta_scores, key_part, preferred_element_type=jnp.float32)
        * 0.125
    )
    delta_key = (
        jnp.einsum("bhqk,bqhd->bkhd", delta_scores, query_part, preferred_element_type=jnp.float32)
        * 0.125
    )
    return (delta_query, delta_key, delta_value)


def layer_backward(upstream, stored, layout, params):
    (
        query_weight,
        query_bias,
        key_weight,
        value_weight,
        value_bias,
        mix_weight,
        mix_bias,
        norm_gain,
        norm_shift,
        expand_weight,
        expand_bias,
        reduce_weight,
        reduce_bias,
        final_gain,
        final_shift,
    ) = params
    (
        hidden,
        query_heads,
        key_heads,
        value_heads,
        shares,
        query_shares,
        context,
        unit_one,
        middle,
        slope,
        active,
        unit_two,
        scales,
    ) = stored
    scale_one, scale_two = scales[:, 0:1], scales[:, 1:2]
    unit_one, unit_two = wide(unit_one), wide(unit_two)
    (count, query_len), (_, passage_len) = layout
    pair_shares = shares.reshape(count, HEADS // 2, passage_len, 2, passage_len)
    pair_shares = pair_shares.transpose(0, 1, 3, 4, 2).reshape(
        count, HEADS, passage_len, passage_len
    )
    head_shares = query_shares.reshape(count, query_len, HEADS, count, query_len)
    head_shares = jnp.stack([head_shares[i, :, :, i] for i in range(count)])
    all_shares = (head_shares.transpose(0, 2, 3, 1), pair_shares)
    delta_two, delta_final_gain, delta_final_shift = norm_backward(
        upstream, unit_two, scale_two, final_gain
    )
    delta_branch = narrow(delta_two)
    delta_reduce_bias = column_total(delta_branch)
    delta_expanded = narrow(contract_last(delta_branch, reduce_weight) * wide(slope))
    delta_expand_bias = column_total(delta_expanded)
    delta_middle = delta_two + contract_last(delta_expanded, expand_weight)
    delta_one, delta_norm_gain, delta_norm_shift = norm_backward(
        delta_middle, unit_one, scale_one, norm_gain
    )
    delta_mix = narrow(delta_one)
    delta_mix_bias = column_total(delta_mix)
    delta_context = narrow(contract_last(delta_mix, mix_weight))
    collected = ([], [], [])
    for part_shares, (offset, group_count, length) in zip(all_shares, group_spans(layout)):
        row_span = group_count * length
        pieces = [
            split_heads(array[offset : offset + row_span], group_count, length)
            for array in (query_heads, key_heads, value_heads, delta_context)
        ]
        results = attend_backward(pieces[0], pieces[1], pieces[2], part_shares, pieces[3])
        for bucket, gradient in zip(collected, results):
            bucket.append(narrow(gradient.reshape(row_span, -1)))
    delta_query = jnp.concatenate(collected[0], axis=0)
    delta_key = jnp.concatenate(collected[1], axis=0)
    delta_value = jnp.concatenate(collected[2], axis=0)
    delta_hidden = (
        delta_one
        + contract_last(delta_query, query_weight)
        + contract_last(delta_key, key_weight)
        + contract_last(delta_value, value_weight)
    )
    operands = (
        active,
        delta_branch,
        middle,
        delta_expanded,
        hidden,
        context,
        delta_query,
        delta_key,
        delta_value,
        delta_mix,
    )
    vectors = (
        column_total(delta_query),
        column_total(delta_value),
        delta_mix_bias,
        delta_norm_gain,
        delta_norm_shift,
        delta_expand_bias,
        delta_reduce_bias,
        delta_final_gain,
        delta_final_shift,
    )
    return (delta_hidden, operands, vectors)


CORE_FLIP = [(0, 1), (1, 0), (2, 3), (3, 2)]
SIDE_FLIP = [(0, 2), (2, 0), (1, 3), (3, 1)]


def wide(values):
    return values.astype(jnp.float32)


def pick(array, index):
    return lax.dynamic_index_in_dim(array, index, 0, keepdims=False)


def reduce_chunk(chunk):
    rep_total = lax.axis_size("rep")
    group = lax.axis_index("grp")
    side, core = group // 2, group % 2
    parts = chunk.reshape((2, 2) + chunk.shape[1:])
    got = lax.ppermute(
        lax.dynamic_index_in_dim(parts, 1 - core, 1, keepdims=False), "grp", CORE_FLIP
    )
    mine = lax.dynamic_index_in_dim(parts, core, 1, keepdims=False)
    got = lax.ppermute(
        narrow(wide(pick(mine, 1 - side)) + wide(pick(got, 1 - side))), "grp", SIDE_FLIP
    ), narrow(wide(pick(mine, side)) + wide(pick(got, side)))
    summed = narrow(wide(got[0]) + wide(got[1]))
    rows, columns = summed.shape
    if rep_total != 8:
        part = lax.psum_scatter(summed, "rep", scatter_dimension=0, tiled=True)
        return wide(lax.all_gather(part, "rep", axis=0, tiled=True))
    rep = lax.axis_index("rep")
    deep, near = rep // 2, rep % 2
    flip = [(i, i ^ 1) for i in range(8)]
    shifts = [[(i, (i + 2 * k) % 8) for i in range(8)] for k in range(4)]
    halves = summed.reshape(2, rows // 2, columns)
    got = lax.ppermute(pick(halves, 1 - near), "rep", flip)
    half = narrow(wide(pick(halves, near)) + wide(got)).reshape(4, rows // 8, columns)
    total = wide(pick(half, deep))
    for k in range(1, 4):
        total = total + wide(lax.ppermute(pick(half, (deep + k) % 4), "rep", shifts[k]))
    piece = narrow(total)
    pieces = [piece] + [lax.ppermute(piece, "rep", shifts[k]) for k in range(1, 4)]
    joined = jnp.zeros((4,) + piece.shape, jnp.bfloat16)
    for k in range(4):
        joined = lax.dynamic_update_index_in_dim(joined, pieces[k], (deep - k) % 4, 0)
    other = lax.ppermute(joined, "rep", flip)
    own = joined.reshape(rows // 2, columns)
    other = other.reshape(rows // 2, columns)
    first = jnp.where(near == 0, own, other)
    second = jnp.where(near == 0, other, own)
    return wide(jnp.concatenate([first, second], axis=0))


def reduce_small(small):
    group = lax.axis_index("grp")
    side, core = group // 2, group % 2
    parts = small.reshape(2, 2, -1)
    got = lax.ppermute(
        lax.dynamic_index_in_dim(parts, 1 - core, 1, keepdims=False), "grp", CORE_FLIP
    )
    pair = lax.dynamic_index_in_dim(parts, core, 1, keepdims=False) + got
    total = pick(pair, side) + lax.ppermute(pick(pair, 1 - side), "grp", SIDE_FLIP)
    rep_total = lax.axis_size("rep")
    step = 1
    while step < rep_total:
        total = total + lax.ppermute(total, "rep", [(i, i ^ step) for i in range(rep_total)])
        step = step * 2
    return total


def remote(source, target, send_sem, recv_sem, grp, rep):
    return pltpu.make_async_remote_copy(
        src_ref=source,
        dst_ref=target,
        send_sem=send_sem,
        recv_sem=recv_sem,
        device_id=(grp, rep),
        device_id_type=pl.DeviceIdType.MESH,
    )


def gather_kernel(block_ref, out_ref, send_near, recv_near, send_far, recv_far):
    groups, reps = out_ref.shape[:2]
    grp, rep = lax.axis_index("grp"), lax.axis_index("rep")
    barrier = pltpu.get_barrier_semaphore()

    @pl.loop(1, reps)
    def _(k):
        pl.semaphore_signal(
            barrier, inc=1, device_id=(grp, (rep + k) % reps), device_id_type=pl.DeviceIdType.MESH
        )

    for k in range(1, groups):
        pl.semaphore_signal(
            barrier, inc=1, device_id=((grp + k) % groups, rep), device_id_type=pl.DeviceIdType.MESH
        )
    out_ref[grp, rep] = block_ref[...]
    pl.semaphore_wait(barrier, reps + groups - 2)

    def near(k):
        mine = out_ref.at[grp, rep]
        return remote(mine, mine, send_near.at[k], recv_near.at[k], grp, (rep + k) % reps)

    def far(k):
        row = out_ref.at[grp]
        return remote(row, row, send_far.at[k], recv_far.at[k], (grp + k) % groups, rep)

    @pl.loop(1, reps)
    def _(k):
        near(k).start()

    @pl.loop(1, reps)
    def _(k):
        near(k).wait_recv()

    for k in range(1, groups):
        far(k).start()
    for k in range(1, groups):
        far(k).wait_recv()

    @pl.loop(1, reps)
    def _(k):
        near(k).wait_send()

    for k in range(1, groups):
        far(k).wait_send()


def gather_blocks(block):
    groups, reps = lax.axis_size("grp"), lax.axis_size("rep")
    return pl.pallas_call(
        gather_kernel,
        out_shape=jax.ShapeDtypeStruct((groups, reps) + block.shape, block.dtype),
        in_specs=[pl.BlockSpec(memory_space=pltpu.VMEM)],
        out_specs=pl.BlockSpec(memory_space=pltpu.VMEM),
        scratch_shapes=[
            pltpu.SemaphoreType.DMA((reps,)),
            pltpu.SemaphoreType.DMA((reps,)),
            pltpu.SemaphoreType.DMA((groups,)),
            pltpu.SemaphoreType.DMA((groups,)),
        ],
        compiler_params=pltpu.CompilerParams(collective_id=1, has_side_effects=True),
    )(block)


def reduce_plain(layers):
    results = []
    for active, branch, middle, expanded, hidden, context, query, key, value, mix in layers:
        quarter = lambda former, latter: (
            lambda matrix: narrow(matrix).reshape(4, matrix.shape[0] // 4, matrix.shape[1])
        )(contract_rows(former, latter))
        square = jnp.concatenate(
            [
                quarter(hidden, query),
                quarter(hidden, key),
                quarter(hidden, value),
                quarter(context, mix),
            ],
            axis=1,
        )
        square = reduce_chunk(square)
        height = square.shape[0] // 4
        results.append(
            [square[place * height : (place + 1) * height] for place in range(4)]
            + [reduce_chunk(quarter(middle, expanded)), reduce_chunk(quarter(active, branch))]
        )
    return [jnp.stack([results[1][i], results[0][i]]) for i in range(6)]


SMALL = (1, 4, 6, 7, 8, 10, 12, 13, 14)
MATRICES = (0, 2, 3, 5, 9, 11)


LOG2E = 1.4426950408889634
V_QUERY, V_VALUE, V_MIX, V_GAIN, V_SHIFT, V_REDUCE, V_LAST_GAIN, V_LAST_SHIFT, V_EXPAND = range(9)
VECTOR_ROWS = 16
TILE = 256


def lane_masks(rows):
    lane = lax.broadcasted_iota(jnp.int32, (rows, 2 * DH), 1)
    return ((lane < DH).astype(jnp.float32).astype(jnp.bfloat16),
            (lane >= DH).astype(jnp.float32).astype(jnp.bfloat16))


def head_mask(head, width):
    lane = lax.broadcasted_iota(jnp.int32, (1, width), 1)
    return ((lane >= head * DH) & (lane < (head + 1) * DH))


def lanes(start, size=TILE):
    return pl.ds(pl.multiple_of(start, 128), size)


def sublanes(start, size):
    return pl.ds(pl.multiple_of(start, 16), size)


def softmax_rows(scores, bias):
    scaled = scores * (0.125 * LOG2E) + bias
    grown = jnp.exp2(scaled - jnp.max(scaled, axis=0, keepdims=True))
    return narrow(grown * (1.0 / jnp.sum(grown, axis=0, keepdims=True)))


def forward_kernel(
    lengths_ref,
    query_in,
    passage_in,
    wq_in,
    wk_in,
    wv_in,
    wm_in,
    we_in,
    wr_in,
    vec_ref,
    query_out,
    passage_out,
    hidden_out,
    q_out,
    k_out,
    v_out,
    pt_out,
    ptq_out,
    c_out,
    u1_out,
    m_out,
    slope_out,
    f_out,
    u2_out,
    r_out,
    wq,
    wk,
    wv,
    wm,
    we,
    wr,
    x,
    q,
    k,
    v,
    pt,
    ptq,
    c,
    u1,
    m,
    slope,
    f,
    u2,
    r,
    z,
    stack,
    weight_sem,
    in_sem,
    out_sem,
):
    width = x.shape[1]
    total = x.shape[0]
    sequences = lengths_ref.shape[0] // 2
    query_rows = query_in.shape[0]
    query_len = query_rows // sequences
    passage_len = (total - query_rows) // sequences
    pairs = width // (2 * DH)

    weights = ((wq_in, wq), (wk_in, wk), (wv_in, wv), (wm_in, wm), (we_in, we), (wr_in, wr))

    def weight_copy(which, layer):
        source, target = weights[which]
        return pltpu.make_async_copy(
            source.at[layer], target.at[layer], weight_sem.at[which, layer]
        )

    stored = (
        (x, hidden_out),
        (q, q_out),
        (k, k_out),
        (v, v_out),
        (pt, pt_out),
        (ptq, ptq_out),
        (c, c_out),
        (u1, u1_out),
        (m, m_out),
        (slope, slope_out),
        (f, f_out),
        (u2, u2_out),
        (r, r_out),
    )
    X, Q, K, V, PT, PTQ, C, U1, M, SLOPE, F, U2, R = range(13)

    def store(which, layer):
        source, target = stored[which]
        return pltpu.make_async_copy(source, target.at[layer], out_sem.at[which])

    def reuse(which, layer):
        @pl.when(layer > 0)
        def _():
            store(which, layer - 1).wait()

    first = pltpu.make_async_copy(query_in, x.at[pl.ds(0, query_rows)], in_sem.at[0])
    rest = pltpu.make_async_copy(
        passage_in, x.at[pl.ds(query_rows, total - query_rows)], in_sem.at[1]
    )
    first.start()
    rest.start()
    for layer in range(LAYERS):
        for which in range(6):
            weight_copy(which, layer).start()
    first.wait()
    rest.wait()

    def project(source, weight, layer, bias_row, target):
        @pl.loop(0, width // TILE)
        def _(i):
            value = product(source[...], weight[layer, :, lanes(i * TILE)])
            if bias_row is not None:
                value = value + vec_ref[layer, pl.ds(bias_row, 1), lanes(i * TILE)]
            target[:, lanes(i * TILE)] = narrow(value)

    def norm(layer, gain_row, shift_row, unit, target, scale_lane):
        step = 96
        gain = vec_ref[layer, pl.ds(gain_row, 1), :]
        shift = vec_ref[layer, pl.ds(shift_row, 1), :]

        @pl.loop(0, total // step)
        def _(i):
            at = sublanes(i * step, step)
            full, unit_rows, scaled = norm_forward(z[at, :], gain, shift)
            unit[at, :] = narrow(unit_rows)
            target[at, :] = narrow(full)
            r[at, scale_lane : scale_lane + 1] = scaled

    @pl.loop(0, LAYERS)
    def _(layer):
        store(X, layer).start()
        weight_copy(0, layer).wait()
        reuse(Q, layer)
        project(x, wq, layer, V_QUERY, q)
        store(Q, layer).start()
        weight_copy(1, layer).wait()
        reuse(K, layer)
        project(x, wk, layer, None, k)
        store(K, layer).start()
        weight_copy(2, layer).wait()
        reuse(V, layer)
        project(x, wv, layer, V_VALUE, v)
        store(V, layer).start()

        reuse(PT, layer)
        reuse(PTQ, layer)
        reuse(C, layer)

        for head in range(HEADS):
            mask = head_mask(head, width).astype(jnp.float32).astype(jnp.bfloat16)
            stack[head * query_rows : (head + 1) * query_rows, :] = q[:query_rows, :] * mask
        scores = contract_last(k[:query_rows, :], stack[...])
        key_slot = lax.broadcasted_iota(jnp.int32, scores.shape, 0)
        query_slot = lax.broadcasted_iota(jnp.int32, scores.shape, 1) % query_rows
        live = jnp.zeros(scores.shape, jnp.bool_)
        for s in range(sequences):
            low = s * query_len
            live = live | (
                (key_slot >= low)
                & (key_slot < low + lengths_ref[s])
                & (query_slot >= low)
                & (query_slot < low + query_len)
            )
        shares = softmax_rows(scores, jnp.where(live, 0.0, -1e30))
        ptq[...] = shares
        spread = contract_rows(shares, v[:query_rows, :])
        context = jnp.zeros((query_rows, width), jnp.float32)
        for head in range(HEADS):
            context = context + jnp.where(
                head_mask(head, width), spread[head * query_rows : (head + 1) * query_rows, :], 0.0
            )
        c[:query_rows, :] = narrow(context)

        @pl.loop(0, sequences * pairs)
        def _(i):
            s, pair = i // pairs, i % pairs
            rows = sublanes(query_rows + s * passage_len, passage_len)
            at = lanes(pair * 2 * DH, 2 * DH)
            even, odd = lane_masks(passage_len)
            q2, k2, v2 = q[rows, at], k[rows, at], v[rows, at]
            scores = contract_last(k2, jnp.concatenate([q2 * even, q2 * odd], axis=0))
            slot = lax.broadcasted_iota(jnp.int32, (passage_len, 1), 0)
            shares = softmax_rows(
                scores, jnp.where(slot < lengths_ref[sequences + s], 0.0, -1e30)
            )
            pt[i] = shares
            shares = jnp.concatenate([shares[:, :passage_len], shares[:, passage_len:]], axis=0)
            spread = contract_rows(jnp.concatenate([v2 * even, v2 * odd], axis=0), shares)
            c[rows, at] = narrow(spread.T)

        store(PT, layer).start()
        store(PTQ, layer).start()
        store(C, layer).start()

        weight_copy(3, layer).wait()

        @pl.loop(0, width // TILE)
        def _(i):
            at = lanes(i * TILE)
            z[:, at] = (
                wide(x[:, at])
                + product(c[...], wm[layer, :, at])
                + vec_ref[layer, pl.ds(V_MIX, 1), at]
            )

        reuse(U1, layer)
        reuse(M, layer)
        reuse(R, layer)
        norm(layer, V_GAIN, V_SHIFT, u1, m, 0)
        store(U1, layer).start()
        store(M, layer).start()

        weight_copy(4, layer).wait()
        reuse(SLOPE, layer)
        reuse(F, layer)

        @pl.loop(0, 4 * width // TILE)
        def _(i):
            at = lanes(i * TILE)
            tiles = width // TILE
            bias = vec_ref[layer, pl.ds(V_EXPAND + i // tiles, 1), lanes((i % tiles) * TILE)]
            value = product(m[...], we[layer, :, at]) + bias
            share = 0.5 * (1.0 + lax.erf(value * (1.0 / math.sqrt(2.0))))
            density = jnp.exp2(value * value * (-0.5 * LOG2E)) * (1.0 / math.sqrt(2.0 * math.pi))
            f[:, at] = narrow(value * share)
            slope[:, at] = narrow(share + value * density)

        store(SLOPE, layer).start()
        store(F, layer).start()

        weight_copy(5, layer).wait()

        @pl.loop(0, width // TILE)
        def _(i):
            at = lanes(i * TILE)
            z[:, at] = (
                wide(m[:, at])
                + product(f[...], wr[layer, :, at])
                + vec_ref[layer, pl.ds(V_REDUCE, 1), at]
            )

        store(X, layer).wait()
        reuse(U2, layer)
        norm(layer, V_LAST_GAIN, V_LAST_SHIFT, u2, x, 1)
        store(U2, layer).start()
        store(R, layer).start()

    last = LAYERS - 1
    first = pltpu.make_async_copy(x.at[pl.ds(0, query_rows)], query_out, in_sem.at[0])
    rest = pltpu.make_async_copy(
        x.at[pl.ds(query_rows, total - query_rows)], passage_out, in_sem.at[1]
    )
    first.start()
    rest.start()
    for which in range(1, 13):
        store(which, last).wait()
    first.wait()
    rest.wait()


def run_forward(lengths, query_input, passage_input, matrices, vectors):
    sequences, query_len, width = query_input.shape
    passage_len = passage_input.shape[1]
    query_rows, passage_rows = sequences * query_len, sequences * passage_len
    total = query_rows + passage_rows
    pairs = width // (2 * DH)
    bf16, f32 = jnp.bfloat16, jnp.float32
    arrays = (
        ((total, width), bf16),
        ((total, width), bf16),
        ((total, width), bf16),
        ((total, width), bf16),
        ((sequences * pairs, passage_len, 2 * passage_len), bf16),
        ((query_rows, HEADS * query_rows), bf16),
        ((total, width), bf16),
        ((total, width), bf16),
        ((total, width), bf16),
        ((total, 4 * width), bf16),
        ((total, 4 * width), bf16),
        ((total, width), bf16),
        ((total, 128), f32),
    )
    anywhere = pl.BlockSpec(memory_space=pl.ANY)
    return pl.pallas_call(
        forward_kernel,
        out_shape=(
            jax.ShapeDtypeStruct((query_rows, width), bf16),
            jax.ShapeDtypeStruct((passage_rows, width), bf16),
        )
        + tuple(jax.ShapeDtypeStruct((LAYERS,) + shape, dtype) for shape, dtype in arrays),
        in_specs=[pl.BlockSpec(memory_space=pltpu.SMEM)]
        + [anywhere] * 8
        + [pl.BlockSpec(memory_space=pltpu.VMEM)],
        out_specs=[anywhere] * 15,
        scratch_shapes=[pltpu.VMEM(matrix.shape, bf16) for matrix in matrices]
        + [pltpu.VMEM(shape, dtype) for shape, dtype in arrays]
        + [
            pltpu.VMEM((total, width), f32),
            pltpu.VMEM((HEADS * query_rows, width), bf16),
            pltpu.SemaphoreType.DMA((6, LAYERS)),
            pltpu.SemaphoreType.DMA((2,)),
            pltpu.SemaphoreType.DMA((13,)),
        ],
        compiler_params=pltpu.CompilerParams(vmem_limit_bytes=60 * 1024 * 1024),
    )(
        lengths,
        query_input.reshape(query_rows, width),
        passage_input.reshape(passage_rows, width),
        *matrices,
        vectors,
    )


def pack_vectors(query_bias, value_bias, mix_bias, norm_gain, norm_shift, reduce_bias, final_gain, final_shift, expand_bias):
    width = query_bias.shape[1]
    rows = [query_bias, value_bias, mix_bias, norm_gain, norm_shift, reduce_bias, final_gain, final_shift]
    packed = jnp.concatenate(
        [jnp.stack(rows, axis=1), expand_bias.reshape(LAYERS, -1, width)], axis=1
    )
    packed = jnp.pad(packed, ((0, 0), (0, VECTOR_ROWS - packed.shape[1]), (0, 0)))
    return packed.astype(jnp.float32)


CHUNKS = 12
PARTS = 6
S_QUERY, S_VALUE, S_MIX, S_GAIN, S_SHIFT, S_REDUCE, S_LAST_GAIN, S_LAST_SHIFT, S_EXPAND = range(9)
CORE_SLOTS, SIDE_SLOTS, NEAR_SLOTS, KEEP_SLOTS = 3, 4, 4, 6
BLOCK = 16


def one_hot(shape, hit):
    row = lax.broadcasted_iota(jnp.int32, shape, 0)
    column = lax.broadcasted_iota(jnp.int32, shape, 1)
    return narrow(jnp.where(hit(row, column), 1.0, 0.0))


def backward_kernel(
    margin_ref,
    positive_ref,
    cluster_row,
    cluster_column,
    vec_ref,
    query_out,
    passage_out,
    query_cot,
    passage_cot,
    wq_in,
    wk_in,
    wv_in,
    wm_in,
    we_in,
    wr_in,
    hidden_in,
    q_in,
    k_in,
    v_in,
    pt_in,
    ptq_in,
    c_in,
    u1_in,
    m_in,
    slope_in,
    f_in,
    u2_in,
    r_in,
    out_ref,
    small_out,
    loss_out,
    query_grad,
    passage_grad,
    buf,
    keep,
    side_out,
    core_in,
    side_in,
    near_in,
    deep_in,
    piece,
    small,
    small_core,
    small_side,
    small_near,
    small_deep,
    first,
    blocks,
    dz,
    dy,
    du,
    quad,
    pair_in,
    middle,
    unit,
    active,
    dc,
    pt,
    ptq,
    stack,
    r,
    w,
    gather_near,
    gather_far,
    first_sem,
    load_sem,
    weight_sem,
    core_sem,
    side_sem,
    near_sem,
    deep_send,
    deep_recv,
    back_send,
    back_recv,
    local_sem,
    last_sem,
    small_sem,
    small_send,
    small_recv,
    core_free,
    side_free,
    near_free,
):
    groups, reps = blocks.shape[:2]
    depth = reps // 2
    rows, width = keep.shape[1:]
    quarter = width // 4
    half_rows = rows // 2
    piece_rows = half_rows // depth
    total = dz.shape[0]
    sequences = margin_ref.shape[0]
    query_rows = query_out.shape[0]
    query_len = query_rows // sequences
    passage_len = (total - query_rows) // sequences
    pairs = width // (2 * DH)
    passage_rows = pl.ds(query_rows, total - query_rows)
    everyone = cluster_row.shape[1]

    grp, rep = lax.axis_index("grp"), lax.axis_index("rep")
    side, core = grp // 2, grp % 2
    deep, near = rep // 2, rep % 2
    sibling = (2 * side + (1 - core), rep)
    across = (2 * (1 - side) + core, rep)
    beside = (grp, 2 * deep + (1 - near))

    def behind(k):
        return (grp, 2 * ((deep + k) % depth) + near)

    def signal(semaphore, peer):
        pl.semaphore_signal(
            semaphore, inc=1, device_id=peer, device_id_type=pl.DeviceIdType.MESH
        )

    barrier = pltpu.get_barrier_semaphore()
    for k in range(1, reps):
        signal(barrier, (grp, (rep + k) % reps))
    for k in range(1, groups):
        signal(barrier, ((grp + k) % groups, rep))

    firsts = [
        pltpu.make_async_copy(
            source.at[pl.ds(s * length, BLOCK)],
            first.at[pl.ds((place * sequences + s) * BLOCK, BLOCK)],
            first_sem.at[place * sequences + s],
        )
        for place, (source, length) in enumerate(
            ((query_out, query_len), (passage_out, passage_len))
        )
        for s in range(sequences)
    ]
    for copy in firsts:
        copy.start()

    loaded = {
        "f": (f_in, active),
        "u2": (u2_in, unit.at[0]),
        "slope": (slope_in, du),
        "m": (m_in, middle),
        "u1": (u1_in, unit.at[1]),
        "c": (c_in, pair_in.at[1]),
        "q": (q_in, quad.at[0]),
        "k": (k_in, quad.at[1]),
        "v": (v_in, quad.at[2]),
        "pt": (pt_in, pt),
        "ptq": (ptq_in, ptq),
        "x": (hidden_in, pair_in.at[0]),
    }
    places = {name: place for place, name in enumerate(loaded)}

    def load(name, layer):
        source, target = loaded[name]
        return pltpu.make_async_copy(source.at[layer], target, load_sem.at[places[name]])

    def weight_loads(kind, layer, slot):
        squares = []
        for j in range(4):
            block = pl.ds(j * width, width)
            if kind == 0:
                source = wr_in.at[layer, block]
            elif kind == 1:
                source = we_in.at[layer, :, block]
            else:
                source = (wq_in, wk_in, wv_in, wm_in)[j].at[layer]
            squares.append(
                pltpu.make_async_copy(source, w.at[slot, j], weight_sem.at[slot, j])
            )
        return squares

    def start_weights(kind, layer, slot):
        for copy in weight_loads(kind, layer, slot):
            copy.start()

    def wait_weights(kind, layer, slot):
        for copy in weight_loads(kind, layer, slot):
            copy.wait()

    last = LAYERS - 1
    cots = [
        pltpu.make_async_copy(query_cot, dy.at[pl.ds(0, query_rows)], first_sem.at[4]),
        pltpu.make_async_copy(passage_cot, dy.at[passage_rows], first_sem.at[5]),
        pltpu.make_async_copy(r_in, r, first_sem.at[6]),
    ]
    for copy in cots:
        copy.start()
    for name in ("u2", "f"):
        load(name, last).start()
    start_weights(0, last, 0)
    for name in ("slope", "m", "u1", "c", "q", "k", "v", "pt", "ptq", "x"):
        load(name, last).start()
    start_weights(1, last, 1)

    for copy in firsts:
        copy.wait()
    chosen_rows = product(
        one_hot((BLOCK, first.shape[0]), lambda i, j: j == i * BLOCK), first[...]
    )
    row = lax.broadcasted_iota(jnp.int32, chosen_rows.shape, 0)
    lane = lax.broadcasted_iota(jnp.int32, chosen_rows.shape, 1)
    for s in range(sequences):
        positive = positive_ref[s]
        facts = (margin_ref[s], positive // 128, positive % 128)
        for place, fact in enumerate(facts):
            at = (row == 2 * sequences) & (lane == place * sequences + s)
            chosen_rows = jnp.where(at, fact.astype(jnp.float32), chosen_rows)
    blocks[grp, rep] = narrow(chosen_rows)

    def to_near(k):
        mine = blocks.at[grp, rep]
        return remote(
            mine, mine, gather_near.at[0, k], gather_near.at[1, k], grp, (rep + k) % reps
        )

    def to_far(k):
        line = blocks.at[grp]
        return remote(
            line, line, gather_far.at[0, k], gather_far.at[1, k], (grp + k) % groups, rep
        )

    pl.semaphore_wait(barrier, reps + groups - 2)

    @pl.loop(1, reps)
    def _(k):
        to_near(k).start()

    for copy in cots:
        copy.wait()
    small[...] = jnp.zeros_like(small)

    @pl.loop(0, total // 96)
    def _(i):
        at = sublanes(i * 96, 96)
        dz[at, :] = wide(dy[at, :])

    @pl.loop(1, reps)
    def _(k):
        to_near(k).wait_recv()

    for k in range(1, groups):
        to_far(k).start()
    for k in range(1, groups):
        to_far(k).wait_recv()

    gathered = blocks[...].reshape(groups * reps * BLOCK, width)

    def taken(offset):
        return product(
            one_hot(
                (everyone, gathered.shape[0]),
                lambda i, j: j == BLOCK * (i // sequences) + offset(i),
            ),
            gathered,
        )

    every_query = narrow(taken(lambda i: i % sequences))
    every_passage = narrow(taken(lambda i: sequences + i % sequences))
    facts = taken(lambda i: 2 * sequences)[:, :128]
    query_at = lax.broadcasted_iota(jnp.int32, facts.shape, 0) % sequences
    lane_at = lax.broadcasted_iota(jnp.int32, facts.shape, 1)

    def fact(place):
        hit = lane_at == place * sequences + query_at
        return jnp.sum(jnp.where(hit, facts, 0.0), axis=1, keepdims=True)

    margin_weight = (fact(0) + 1.0) / NBINS
    every_positive = fact(1) * 128.0 + fact(2)
    score_scale = 2.0 / math.sqrt(width)
    logits = contract_last(every_query, every_passage) * score_scale
    columns = lax.broadcasted_iota(jnp.int32, logits.shape, 1).astype(jnp.float32)
    chosen_mask = columns == every_positive
    allowed = (cluster_row[...] == cluster_column[...]) | chosen_mask
    masked = jnp.where(allowed, logits, -1e30)
    peak = jnp.max(masked, axis=1, keepdims=True)
    normalizer = peak + jnp.log(jnp.sum(jnp.exp(masked - peak), axis=1, keepdims=True))
    chosen = jnp.sum(jnp.where(chosen_mask, logits, 0.0), axis=1, keepdims=True)
    loss = margin_weight * (normalizer - chosen)
    share = jnp.where(allowed, jnp.exp(masked - normalizer), 0.0)
    delta_logits = narrow(margin_weight * (share - jnp.where(chosen_mask, 1.0, 0.0)))
    start = (grp * reps + rep) * sequences
    loss_row = lax.broadcasted_iota(jnp.int32, (everyone, 128), 0)
    loss_lane = lax.broadcasted_iota(jnp.int32, (everyone, 128), 1)
    loss_out[...] = jnp.broadcast_to(
        jnp.sum(jnp.where(loss_row == start + loss_lane, loss, 0.0), axis=0, keepdims=True),
        loss_out.shape,
    )
    own = one_hot((BLOCK, everyone), lambda i, j: (j == start + i) & (i < sequences))
    own_rows = narrow(product(own, delta_logits))
    own_columns = narrow(contract_last(own, delta_logits))
    delta_firsts = (
        product(own_rows, every_passage) * score_scale,
        product(own_columns, every_query) * score_scale,
    )
    eight = lax.broadcasted_iota(jnp.int32, (8, width), 0)
    for place, (base, length) in enumerate(((0, query_len), (query_rows, passage_len))):
        for s in range(sequences):
            at = pl.ds(base + s * length, 8)
            dz[at, :] = dz[at, :] + jnp.where(
                eight == 0, delta_firsts[place][s : s + 1, :], 0.0
            )

    def core_copy(t):
        return remote(
            buf.at[t % 2, :, 1 - core],
            core_in.at[t % CORE_SLOTS],
            core_sem.at[0, t],
            core_sem.at[1, t],
            *sibling,
        )

    def side_copy(t):
        return remote(
            side_out.at[t % 3],
            side_in.at[t % SIDE_SLOTS],
            side_sem.at[0, t],
            side_sem.at[1, t],
            *across,
        )

    def near_copy(t):
        return remote(
            keep.at[t % KEEP_SLOTS, sublanes((1 - near) * half_rows, half_rows)],
            near_in.at[t % NEAR_SLOTS],
            near_sem.at[0, t],
            near_sem.at[1, t],
            *beside,
        )

    def piece_of(position):
        return sublanes(near * half_rows + position * piece_rows, piece_rows)

    def deep_copy(t, k):
        return remote(
            keep.at[t % KEEP_SLOTS, piece_of((deep + k) % depth)],
            deep_in.at[t, k - 1],
            deep_send.at[k - 1, t],
            deep_recv.at[k - 1, t],
            *behind(k),
        )

    def chunk_place(t):
        step, part = t // PARTS, t % PARTS
        return (part // 2) * 4 + (last - step) * 2 + part % 2

    def back_copy(t, k):
        return remote(
            piece.at[t],
            out_ref.at[chunk_place(t), piece_of(deep)],
            back_send.at[k - 1, t],
            back_recv.at[k - 1, t],
            *behind(k),
        )

    def local_copy(t):
        return pltpu.make_async_copy(
            piece.at[t], out_ref.at[chunk_place(t), piece_of(deep)], local_sem.at[t]
        )

    def last_copy(t):
        half = out_ref.at[chunk_place(t), sublanes(near * half_rows, half_rows)]
        return remote(half, half, last_sem.at[0, t], last_sem.at[1, t], *beside)

    def add_rows(target, former, latter, count):
        step = 48

        @pl.loop(0, count // step)
        def _(i):
            def at(first_row):
                return sublanes(first_row + i * step, step)

            (to, to_row), (one, one_row), (two, two_row) = target, former, latter
            to[at(to_row), :] = narrow(wide(one[at(one_row), :]) + wide(two[at(two_row), :]))

    def after_core(t):
        core_copy(t).wait()
        slot = t % CORE_SLOTS
        add_rows(
            (side_out.at[t % 3], 0),
            (buf.at[t % 2, 1 - side, core], 0),
            (core_in.at[slot, 1 - side], 0),
            rows,
        )

        @pl.when(t >= SIDE_SLOTS)
        def _():
            pl.semaphore_wait(side_free, 1)

        side_copy(t).start()
        add_rows(
            (keep.at[t % KEEP_SLOTS], 0),
            (buf.at[t % 2, side, core], 0),
            (core_in.at[slot, side], 0),
            rows,
        )

        @pl.when(t + CORE_SLOTS < CHUNKS)
        def _():
            signal(core_free, sibling)

    def after_side(t):
        side_copy(t).wait()
        kept = keep.at[t % KEEP_SLOTS]
        came = side_in.at[t % SIDE_SLOTS]
        there, here = (1 - near) * half_rows, near * half_rows
        add_rows((kept, there), (kept, there), (came, there), half_rows)

        @pl.when(t >= NEAR_SLOTS)
        def _():
            pl.semaphore_wait(near_free, 1)

        near_copy(t).start()
        add_rows((kept, here), (kept, here), (came, here), half_rows)

        @pl.when(t + SIDE_SLOTS < CHUNKS)
        def _():
            signal(side_free, across)

    def after_near(t):
        near_copy(t).wait()
        kept = keep.at[t % KEEP_SLOTS]
        here = near * half_rows
        add_rows((kept, here), (kept, here), (near_in.at[t % NEAR_SLOTS], 0), half_rows)

        @pl.when(t + NEAR_SLOTS < CHUNKS)
        def _():
            signal(near_free, beside)

        for k in range(1, depth):
            deep_copy(t, k).start()

    def after_deep(t):
        summed = wide(keep[t % KEEP_SLOTS, piece_of(deep), :])
        for k in range(1, depth):
            deep_copy(t, k).wait()
        for k in range(1, depth):
            summed = summed + wide(deep_in[t, k - 1])
        piece[t] = narrow(summed)
        local_copy(t).start()
        for k in range(1, depth):
            back_copy(t, k).start()

    def after_back(t):
        local_copy(t).wait()
        for k in range(1, depth):
            back_copy(t, k).wait_recv()
        last_copy(t).start()

    def tally(layer, row_at, columns, values):
        at = (layer, pl.ds(row_at, 1), columns)
        small[at] = small[at] + jnp.sum(values, axis=0, keepdims=True)

    every_lane = pl.ds(0, width)

    def norm_back(layer, unit_at, scale_lane, gain_row, target, gain_to, shift_to, bias_to):
        step = 48
        gain = vec_ref[layer, pl.ds(gain_row, 1), :]

        @pl.loop(0, total // step)
        def _(i):
            at = sublanes(i * step, step)
            upstream = dz[at, :]
            unit_rows = wide(unit[unit_at, at, :])
            scaled = r[layer, at, scale_lane : scale_lane + 1]
            delta_unit = upstream * gain
            delta = scaled * (
                delta_unit
                - jnp.mean(delta_unit, axis=-1, keepdims=True)
                - unit_rows * jnp.mean(delta_unit * unit_rows, axis=-1, keepdims=True)
            )
            dz[at, :] = delta
            rounded = narrow(delta)
            target[at, :] = rounded
            tally(layer, gain_to, every_lane, upstream * unit_rows)
            tally(layer, shift_to, every_lane, upstream)
            tally(layer, bias_to, every_lane, wide(rounded))

    def expand_back(layer, slot):
        tiles = width // TILE

        @pl.loop(0, 4 * tiles)
        def _(i):
            at = lanes(i * TILE)
            block, tile = i // tiles, i % tiles
            weight = w[slot, block, sublanes(tile * TILE, TILE), :]
            value = narrow(contract_last(dy[...], weight) * wide(du[:, at]))
            du[:, at] = value
            tally(layer, S_EXPAND + block, lanes(tile * TILE), wide(value))

    def middle_back(slot):
        @pl.loop(0, width // TILE)
        def _(i):
            at = lanes(i * TILE)
            value = dz[:, at]
            for block in range(4):
                weight = w[slot, block, sublanes(i * TILE, TILE), :]
                value = value + contract_last(du[:, block * width : (block + 1) * width], weight)
            dz[:, at] = value

    def context_back(slot):
        @pl.loop(0, width // TILE)
        def _(i):
            weight = w[slot, 3, sublanes(i * TILE, TILE), :]
            dc[:, lanes(i * TILE)] = narrow(contract_last(quad[3], weight))

    def hidden_back(slot):
        @pl.loop(0, width // TILE)
        def _(i):
            at = lanes(i * TILE)
            value = dz[:, at]
            for place in range(3):
                weight = w[slot, place, sublanes(i * TILE, TILE), :]
                value = value + contract_last(quad[place], weight)
            dz[:, at] = value

    def score_back(shares, delta):
        shares = wide(shares)
        weighed = shares * delta
        return narrow(weighed - shares * jnp.sum(weighed, axis=0, keepdims=True))

    def attention_back(layer):
        query_span = pl.ds(0, query_rows)
        q2, k2, v2 = quad[0, query_span, :], quad[1, query_span, :], quad[2, query_span, :]

        def fill(rows_of):
            for head in range(HEADS):
                mask = narrow(jnp.where(head_mask(head, width), 1.0, 0.0))
                stack[head * query_rows : (head + 1) * query_rows, :] = rows_of * mask

        fill(dc[query_span, :])
        delta_value = narrow(product(ptq[...], stack[...]))
        delta_scores = score_back(ptq[...], contract_last(v2, stack[...]))
        fill(q2)
        delta_key = narrow(product(delta_scores, stack[...]) * 0.125)
        stack[...] = narrow(contract_rows(delta_scores, k2) * 0.125)
        delta_query = jnp.zeros((query_rows, width), jnp.float32)
        for head in range(HEADS):
            delta_query = delta_query + jnp.where(
                head_mask(head, width),
                wide(stack[head * query_rows : (head + 1) * query_rows, :]),
                0.0,
            )
        delta_query = narrow(delta_query)
        quad[0, query_span, :] = delta_query
        quad[1, query_span, :] = delta_key
        quad[2, query_span, :] = delta_value
        tally(layer, S_QUERY, every_lane, wide(delta_query))
        tally(layer, S_VALUE, every_lane, wide(delta_value))

        @pl.loop(0, sequences * pairs)
        def _(i):
            s, pair = i // pairs, i % pairs
            at_rows = sublanes(query_rows + s * passage_len, passage_len)
            at = lanes(pair * 2 * DH, 2 * DH)
            even, odd = lane_masks(passage_len)
            q2, k2, v2 = quad[0, at_rows, at], quad[1, at_rows, at], quad[2, at_rows, at]
            d2 = dc[at_rows, at]
            shares = pt[i]
            deltas = jnp.concatenate([d2 * even, d2 * odd], axis=0)
            delta_value = narrow(product(shares, deltas))
            delta_scores = score_back(shares, contract_last(v2, deltas))
            queries = jnp.concatenate([q2 * even, q2 * odd], axis=0)
            delta_key = narrow(product(delta_scores, queries) * 0.125)
            keys = jnp.concatenate([k2 * even, k2 * odd], axis=0)
            piled = jnp.concatenate(
                [delta_scores[:, :passage_len], delta_scores[:, passage_len:]], axis=0
            )
            delta_query = narrow((contract_rows(keys, piled) * 0.125).T)
            quad[0, at_rows, at] = delta_query
            quad[1, at_rows, at] = delta_key
            quad[2, at_rows, at] = delta_value
            tally(layer, S_QUERY, at, wide(delta_query))
            tally(layer, S_VALUE, at, wide(delta_value))

    def make_terms(t, part):
        tall = part < 2

        @pl.when(tall)
        def _():
            @pl.loop(0, 4)
            def _(i):
                columns = lanes(i * width + part * rows, rows)
                buf[t % 2, i // 2, i % 2] = narrow(contract_rows(active[:, columns], dy[...]))

        def split(i, terms):
            unit_at, half = i // 2, i % 2
            place = sublanes(unit_at * quarter, quarter)
            terms = narrow(terms)
            buf[t % 2, half, 0, place, :] = terms[:quarter]
            buf[t % 2, half, 1, place, :] = terms[quarter:]

        @pl.when((part == 2) | (part == 3))
        def _():
            @pl.loop(0, 4)
            def _(i):
                columns = lanes((2 * (part - 2) + i // 2) * width, width)
                split(
                    i,
                    contract_rows(
                        middle[:, lanes((i % 2) * 2 * quarter, 2 * quarter)], du[:, columns]
                    ),
                )

        @pl.when(part >= 4)
        def _():
            @pl.loop(0, 4)
            def _(i):
                which = 2 * (part - 4) + i // 2
                split(
                    i,
                    contract_rows(
                        pair_in[which // 3, :, lanes((i % 2) * 2 * quarter, 2 * quarter)],
                        quad[which],
                    ),
                )

        @pl.when(t >= CORE_SLOTS)
        def _():
            pl.semaphore_wait(core_free, 1)

        core_copy(t).start()

    def small_move(place, target, peer):
        return remote(
            small, target, small_sem.at[2 * place], small_sem.at[2 * place + 1], *peer
        )

    def small_to_deep(k):
        line = small_deep.at[deep]
        return remote(line, line, small_send.at[k - 1], small_recv.at[k - 1], *behind(k))

    def gradients_out():
        return (
            pltpu.make_async_copy(dz.at[pl.ds(0, query_rows)], query_grad, first_sem.at[4]),
            pltpu.make_async_copy(dz.at[passage_rows], passage_grad, first_sem.at[5]),
        )

    @pl.loop(0, CHUNKS + 5)
    def _(t):
        step, part = t // PARTS, t % PARTS
        layer = last - step
        slot = (3 * step) % 2
        busy = t < CHUNKS
        more = busy & (step < LAYERS - 1)

        @pl.when((t > 0) & (t <= CHUNKS))
        def _():
            after_core(t - 1)

        @pl.when(busy & (part == 0))
        def _():
            @pl.when(step > 0)
            def _():
                for name in ("c", "q", "k", "v", "x"):
                    load(name, layer).start()

            load("u2", layer).wait()
            norm_back(layer, 0, 1, V_LAST_GAIN, dy, S_LAST_GAIN, S_LAST_SHIFT, S_REDUCE)
            load("f", layer).wait()

        @pl.when(busy & (part == 4))
        def _():
            @pl.when(more)
            def _():
                for name in ("slope", "m", "u1"):
                    load(name, layer - 1).start()

            for name in ("c", "q", "k", "v", "pt", "ptq", "x"):
                load(name, layer).wait()
            attention_back(layer)

        @pl.when(busy & (part == 2))
        def _():
            load("m", layer).wait()

        @pl.when(busy)
        def _():
            make_terms(t, part)

        @pl.when(busy & (part == 1))
        def _():
            @pl.when(more)
            def _():
                for name in ("u2", "f"):
                    load(name, layer - 1).start()

            load("slope", layer).wait()
            wait_weights(0, layer, slot)
            expand_back(layer, slot)
            start_weights(2, layer, slot)

        @pl.when(busy & (part == 3))
        def _():
            wait_weights(1, layer, 1 - slot)
            middle_back(1 - slot)

            @pl.when(more)
            def _():
                start_weights(0, layer - 1, 1 - slot)

            load("u1", layer).wait()
            norm_back(layer, 1, 0, V_GAIN, quad.at[3], S_GAIN, S_SHIFT, S_MIX)
            wait_weights(2, layer, slot)
            context_back(slot)

        @pl.when(busy & (part == 5))
        def _():
            @pl.when(more)
            def _():
                for name in ("pt", "ptq"):
                    load(name, layer - 1).start()

            hidden_back(slot)

            @pl.when(more)
            def _():
                start_weights(1, layer - 1, slot)

            @pl.when(step == LAYERS - 1)
            def _():
                for copy in gradients_out():
                    copy.start()

        for lag, stage in enumerate((after_side, after_near, after_deep, after_back)):

            @pl.when((t > lag + 1) & (t < CHUNKS + lag + 2))
            def _():
                stage(t - lag - 2)

        for place, (target, peer, came) in enumerate(
            (
                (small_core, sibling, small_core),
                (small_side, across, small_side),
                (small_near, beside, small_near),
            )
        ):

            @pl.when(t == CHUNKS - 1 + place)
            def _():
                small_move(place, target, peer).start()

            @pl.when(t == CHUNKS + place)
            def _():
                small_move(place, target, peer).wait()
                small[...] = small[...] + came[...]

        @pl.when(t == CHUNKS + 2)
        def _():
            small_deep[deep] = small[...]
            for k in range(1, depth):
                small_to_deep(k).start()

        @pl.when(t == CHUNKS + 4)
        def _():
            for k in range(1, depth):
                small_to_deep(k).wait()
            summed = small_deep[0]
            for k in range(1, depth):
                summed = summed + small_deep[k]
            small_out[...] = summed

    @pl.loop(0, CHUNKS)
    def _(t):
        for k in range(1, depth):
            back_copy(t, k).wait_send()
        last_copy(t).wait()

    for copy in gradients_out():
        copy.wait()

    @pl.loop(1, reps)
    def _(k):
        to_near(k).wait_send()

    for k in range(1, groups):
        to_far(k).wait_send()


def run_backward(
    margin_bin,
    positive_index,
    cluster_index,
    vectors,
    query_output,
    passage_output,
    query_cotangent,
    passage_cotangent,
    matrices,
    stored,
):
    query_rows, width = query_output.shape
    passage_rows = passage_output.shape[0]
    total = query_rows + passage_rows
    sequences = margin_bin.shape[0]
    everyone = cluster_index.shape[0]
    groups, reps = lax.axis_size("grp"), lax.axis_size("rep")
    depth = reps // 2
    rows = width // 2
    piece_rows = rows // 2 // depth
    bf16, f32 = jnp.bfloat16, jnp.float32
    dma = pltpu.SemaphoreType.DMA
    anywhere = pl.BlockSpec(memory_space=pl.ANY)
    vmem = pl.BlockSpec(memory_space=pltpu.VMEM)
    smem = pl.BlockSpec(memory_space=pltpu.SMEM)
    small_shape = (LAYERS, 16, width)
    pt_shape, ptq_shape = stored[4].shape[1:], stored[5].shape[1:]
    return pl.pallas_call(
        backward_kernel,
        out_shape=(
            jax.ShapeDtypeStruct((CHUNKS, rows, width), bf16),
            jax.ShapeDtypeStruct(small_shape, f32),
            jax.ShapeDtypeStruct((8, 128), f32),
            jax.ShapeDtypeStruct((query_rows, width), f32),
            jax.ShapeDtypeStruct((passage_rows, width), f32),
        ),
        in_specs=[smem, smem, vmem, vmem, vmem] + [anywhere] * 23,
        out_specs=(anywhere, vmem, vmem, anywhere, anywhere),
        scratch_shapes=[
            pltpu.VMEM((2, 2, 2, rows, width), bf16),
            pltpu.VMEM((KEEP_SLOTS, rows, width), bf16),
            pltpu.VMEM((3, rows, width), bf16),
            pltpu.VMEM((CORE_SLOTS, 2, rows, width), bf16),
            pltpu.VMEM((SIDE_SLOTS, rows, width), bf16),
            pltpu.VMEM((NEAR_SLOTS, rows // 2, width), bf16),
            pltpu.VMEM((CHUNKS, depth - 1, piece_rows, width), bf16),
            pltpu.VMEM((CHUNKS, piece_rows, width), bf16),
            pltpu.VMEM(small_shape, f32),
            pltpu.VMEM(small_shape, f32),
            pltpu.VMEM(small_shape, f32),
            pltpu.VMEM(small_shape, f32),
            pltpu.VMEM((depth,) + small_shape, f32),
            pltpu.VMEM((2 * sequences * BLOCK, width), bf16),
            pltpu.VMEM((groups, reps, BLOCK, width), bf16),
            pltpu.VMEM((total, width), f32),
            pltpu.VMEM((total, width), bf16),
            pltpu.VMEM((total, 4 * width), bf16),
            pltpu.VMEM((4, total, width), bf16),
            pltpu.VMEM((2, total, width), bf16),
            pltpu.VMEM((total, width), bf16),
            pltpu.VMEM((2, total, width), bf16),
            pltpu.VMEM((total, 4 * width), bf16),
            pltpu.VMEM((total, width), bf16),
            pltpu.VMEM(pt_shape, bf16),
            pltpu.VMEM(ptq_shape, bf16),
            pltpu.VMEM((HEADS * query_rows, width), bf16),
            pltpu.VMEM((LAYERS, total, 128), f32),
            pltpu.VMEM((2, 4, width, width), bf16),
            dma((2, reps)),
            dma((2, groups)),
            dma((7,)),
            dma((12,)),
            dma((2, 4)),
            dma((2, CHUNKS)),
            dma((2, CHUNKS)),
            dma((2, CHUNKS)),
            dma((depth - 1, CHUNKS)),
            dma((depth - 1, CHUNKS)),
            dma((depth - 1, CHUNKS)),
            dma((depth - 1, CHUNKS)),
            dma((CHUNKS,)),
            dma((2, CHUNKS)),
            dma((6,)),
            dma((depth - 1,)),
            dma((depth - 1,)),
            pltpu.SemaphoreType.REGULAR,
            pltpu.SemaphoreType.REGULAR,
            pltpu.SemaphoreType.REGULAR,
        ],
        compiler_params=pltpu.CompilerParams(
            collective_id=0, has_side_effects=True, vmem_limit_bytes=62 * 1024 * 1024
        ),
    )(
        margin_bin,
        positive_index,
        cluster_index.reshape(1, everyone),
        cluster_index.reshape(everyone, 1),
        vectors,
        query_output,
        passage_output,
        query_cotangent.reshape(query_rows, width),
        passage_cotangent.reshape(passage_rows, width),
        *matrices,
        *stored,
    )


def backward_plain(
    query_output,
    passage_output,
    cluster_index,
    margin_bin,
    positive_index,
    query_cotangent,
    passage_cotangent,
    stored,
    params,
):
    batch_size, query_len, model_width = query_output.shape
    passage_len = passage_output.shape[1]
    layout = ((batch_size, query_len), (batch_size, passage_len))
    query_span = batch_size * query_len
    stored_layers = [tuple(array[layer_index] for array in stored) for layer_index in range(LAYERS)]
    query_first = query_output[:, 0, :]
    passage_first = passage_output[:, 0, :]
    facts = jnp.concatenate(
        [margin_bin, positive_index // 128, positive_index % 128], axis=0
    ).astype(jnp.bfloat16)
    facts = jnp.pad(facts, (0, model_width - facts.shape[0]))
    block = jnp.concatenate([query_first, passage_first, facts[None, :]], axis=0)
    block = jnp.pad(block, ((0, 8 - block.shape[0]), (0, 0)))
    total = cluster_index.shape[0]
    every = gather_blocks(block).reshape(-1, 8, model_width)
    every_query = every[:, :batch_size].reshape(total, model_width)
    every_passage = every[:, batch_size : 2 * batch_size].reshape(total, model_width)
    facts = every[:, 2 * batch_size, : 3 * batch_size].astype(jnp.int32)
    facts = facts.reshape(-1, 3, batch_size)
    every_margin = facts[:, 0].reshape(total)
    every_positive = (facts[:, 1] * 128 + facts[:, 2]).reshape(total)
    start_row = lax.axis_index(("grp", "rep")) * batch_size
    score_scale = 2.0 / math.sqrt(model_width)
    logits = contract_last(every_query, every_passage) * score_scale
    columns = lax.broadcasted_iota(jnp.int32, logits.shape, 1)
    chosen_mask = columns == every_positive[:, None]
    allowed = (cluster_index[None, :] == cluster_index[:, None]) | chosen_mask
    masked = jnp.where(allowed, logits, -1e30)
    peak_score = jnp.max(masked, axis=1, keepdims=True)
    normalizer = peak_score + jnp.log(jnp.sum(jnp.exp(masked - peak_score), axis=1, keepdims=True))
    chosen = jnp.sum(jnp.where(chosen_mask, logits, 0.0), axis=1)
    margin_weight = (every_margin + 1).astype(jnp.float32) / NBINS
    every_loss = margin_weight * (normalizer[:, 0] - chosen)
    query_loss = lax.dynamic_slice_in_dim(every_loss, start_row, batch_size)
    delta_logits = narrow(
        margin_weight[:, None]
        * (jnp.where(allowed, jnp.exp(masked - normalizer), 0.0) - chosen_mask.astype(jnp.float32))
    )
    own_rows = lax.dynamic_slice_in_dim(delta_logits, start_row, batch_size, axis=0)
    own_columns = lax.dynamic_slice_in_dim(delta_logits, start_row, batch_size, axis=1)
    delta_query_first = product(own_rows, every_passage) * score_scale
    delta_passage_first = contract_rows(own_columns, every_query) * score_scale
    query_upstream = query_cotangent.astype(jnp.float32).at[:, 0, :].add(delta_query_first)
    passage_upstream = passage_cotangent.astype(jnp.float32).at[:, 0, :].add(delta_passage_first)
    upstream = jnp.concatenate(
        [
            query_upstream.reshape(query_span, model_width),
            passage_upstream.reshape(batch_size * passage_len, model_width),
        ],
        axis=0,
    )
    operands = []
    small = []
    for layer_index in reversed(range(LAYERS)):
        layer_params = tuple(array[layer_index] for array in params)
        upstream, layer_operands, vectors = layer_backward(
            upstream, stored_layers[layer_index], layout, layer_params
        )
        operands.append(layer_operands)
        small.append([vector.reshape(4, -1) for vector in vectors])
    small = small[::-1]
    matrices = reduce_plain(operands)
    flat = reduce_small(jnp.concatenate(small[0] + small[1], axis=1))
    reduced = [None] * 15
    for slot, matrix in zip(MATRICES, matrices):
        reduced[slot] = matrix
    flat = flat.reshape(LAYERS, -1)
    offset = 0
    for slot, vector in zip(SMALL, small[0]):
        size = vector.shape[1]
        reduced[slot] = flat[:, offset : offset + size]
        offset = offset + size
    return query_loss, upstream[:query_span], upstream[query_span:], reduced


def unpack_gradients(out, small):
    width = out.shape[2]
    quarter = width // 4
    blocks = out.reshape(3, LAYERS, 4, quarter, width)
    reduced = [None] * 15
    reduced[11] = wide(blocks[0].reshape(LAYERS, width, width))
    reduced[9] = wide(jnp.swapaxes(blocks[1], 1, 2).reshape(LAYERS, quarter, 4 * width))
    for place, slot in enumerate((0, 2, 3, 5)):
        reduced[slot] = wide(blocks[2, :, place])
    group = lax.axis_index("grp")
    narrow_rows = lax.dynamic_slice_in_dim(small[:, :8], group * quarter, quarter, axis=2)
    for place, slot in enumerate((1, 4, 6, 7, 8, 12, 13, 14)):
        reduced[slot] = narrow_rows[:, place]
    reduced[10] = lax.dynamic_index_in_dim(small, S_EXPAND + group, 1, keepdims=False)
    return reduced


def per_device(
    query_input,
    passage_input,
    query_length,
    passage_length,
    cluster_index,
    margin_bin,
    positive_index,
    query_cotangent,
    passage_cotangent,
    query_weight,
    query_bias,
    key_weight,
    value_weight,
    value_bias,
    mix_weight,
    mix_bias,
    norm_gain,
    norm_shift,
    expand_weight,
    expand_bias,
    reduce_weight,
    reduce_bias,
    final_gain,
    final_shift,
):
    params = (
        query_weight,
        query_bias,
        key_weight,
        value_weight,
        value_bias,
        mix_weight,
        mix_bias,
        norm_gain,
        norm_shift,
        expand_weight,
        expand_bias,
        reduce_weight,
        reduce_bias,
        final_gain,
        final_shift,
    )
    batch_size, query_len, model_width = query_input.shape
    passage_len = passage_input.shape[1]
    matrices = (query_weight, key_weight, value_weight, mix_weight, expand_weight, reduce_weight)
    vectors = pack_vectors(
        query_bias,
        value_bias,
        mix_bias,
        norm_gain,
        norm_shift,
        reduce_bias,
        final_gain,
        final_shift,
        expand_bias,
    )
    results = run_forward(
        jnp.concatenate([query_length, passage_length]),
        query_input,
        passage_input,
        matrices,
        vectors,
    )
    query_output = results[0].reshape(batch_size, query_len, model_width)
    passage_output = results[1].reshape(batch_size, passage_len, model_width)
    if lax.axis_size("rep") != 8:
        query_loss, query_gradient, passage_gradient, reduced = backward_plain(
            query_output,
            passage_output,
            cluster_index,
            margin_bin,
            positive_index,
            query_cotangent,
            passage_cotangent,
            results[2:],
            params,
        )
    else:
        out, small, loss, query_gradient, passage_gradient = run_backward(
            margin_bin,
            positive_index,
            cluster_index,
            vectors,
            results[0],
            results[1],
            query_cotangent,
            passage_cotangent,
            matrices,
            results[2:],
        )
        query_loss = loss[0, :batch_size]
        reduced = unpack_gradients(out, small)
    return (
        query_output,
        passage_output,
        query_loss,
        query_gradient.reshape(batch_size, query_len, model_width),
        passage_gradient.reshape(batch_size, passage_len, model_width),
        reduced[0],
        reduced[1],
        reduced[2],
        reduced[3],
        reduced[4],
        reduced[5],
        reduced[6],
        reduced[7],
        reduced[8],
        reduced[9],
        reduced[10],
        reduced[11],
        reduced[12],
        reduced[13],
        reduced[14],
    )


def solution(mesh):
    placed = (
        P(("grp", "rep"), None, None),
        P(("grp", "rep"), None, None),
        P(("grp", "rep")),
        P(("grp", "rep")),
        P(),
        P(("grp", "rep")),
        P(("grp", "rep")),
        P(("grp", "rep"), None, None),
        P(("grp", "rep"), None, None),
        P(),
        P(),
        P(),
        P(),
        P(),
        P(),
        P(),
        P(),
        P(),
        P(),
        P(),
        P(),
        P(),
        P(),
        P(),
    )
    return jax.shard_map(
        per_device,
        mesh=mesh,
        in_specs=placed,
        out_specs=(
            P(("grp", "rep"), None, None),
            P(("grp", "rep"), None, None),
            P(("grp", "rep")),
            P(("grp", "rep"), None, None),
            P(("grp", "rep"), None, None),
            P(None, "grp", None),
            P(None, "grp"),
            P(None, "grp", None),
            P(None, "grp", None),
            P(None, "grp"),
            P(None, "grp", None),
            P(None, "grp"),
            P(None, "grp"),
            P(None, "grp"),
            P(None, "grp", None),
            P(None, "grp"),
            P(None, "grp", None),
            P(None, "grp"),
            P(None, "grp"),
            P(None, "grp"),
        ),
        check_vma=False,
    )
```

```python
import functools
import math

import jax
import jax.numpy as jnp
from jax import lax
from jax.experimental import pallas as pl
from jax.experimental.pallas import tpu as pltpu
from jax.sharding import PartitionSpec as P

HEADS = 12
DH = 64
LAYERS = 2
NBINS = 10


def narrow(values):
    return values.astype(jnp.bfloat16)


def product(former, latter):
    return jnp.dot(former, latter, preferred_element_type=jnp.float32)


def contract_rows(former, latter):
    return lax.dot_general(
        former, latter, (((0,), (0,)), ((), ())), preferred_element_type=jnp.float32
    )


def contract_last(former, latter):
    return lax.dot_general(
        former, latter, (((1,), (1,)), ((), ())), preferred_element_type=jnp.float32
    )


def column_total(values):
    return jnp.sum(values.astype(jnp.float32), axis=0)


def norm_forward(summed, gain_vector, shift_vector):
    average = jnp.mean(summed, axis=-1, keepdims=True)
    centred = summed - average
    scaled = lax.rsqrt(jnp.mean(centred * centred, axis=-1, keepdims=True) + 1e-12)
    unit_rows = centred * scaled
    return (unit_rows * gain_vector + shift_vector, unit_rows, scaled)


def norm_backward(upstream, unit_rows, scaled, gain_vector):
    delta_unit = upstream * gain_vector
    delta_summed = scaled * (
        delta_unit
        - jnp.mean(delta_unit, axis=-1, keepdims=True)
        - unit_rows * jnp.mean(delta_unit * unit_rows, axis=-1, keepdims=True)
    )
    return (delta_summed, jnp.sum(upstream * unit_rows, axis=0), jnp.sum(upstream, axis=0))


def split_heads(flat, group_count, length):
    return flat.reshape(group_count, length, HEADS, DH)


def group_spans(layout):
    spans = []
    offset = 0
    for group_count, length in layout:
        spans.append((offset, group_count, length))
        offset = offset + group_count * length
    return spans


def attend_backward(query_part, key_part, value_part, shares, delta_context):
    attention = wide(shares)
    delta_value = jnp.einsum(
        "bhqk,bqhd->bkhd", narrow(attention), delta_context, preferred_element_type=jnp.float32
    )
    delta_attention = jnp.einsum(
        "bqhd,bkhd->bhqk", delta_context, value_part, preferred_element_type=jnp.float32
    )
    delta_scores = narrow(
        attention * (delta_attention - jnp.sum(attention * delta_attention, axis=-1, keepdims=True))
    )
    delta_query = (
        jnp.einsum("bhqk,bkhd->bqhd", delta_scores, key_part, preferred_element_type=jnp.float32)
        * 0.125
    )
    delta_key = (
        jnp.einsum("bhqk,bqhd->bkhd", delta_scores, query_part, preferred_element_type=jnp.float32)
        * 0.125
    )
    return (delta_query, delta_key, delta_value)


def layer_backward(upstream, stored, layout, params):
    (
        query_weight,
        query_bias,
        key_weight,
        value_weight,
        value_bias,
        mix_weight,
        mix_bias,
        norm_gain,
        norm_shift,
        expand_weight,
        expand_bias,
        reduce_weight,
        reduce_bias,
        final_gain,
        final_shift,
    ) = params
    (
        hidden,
        query_heads,
        key_heads,
        value_heads,
        shares,
        query_shares,
        context,
        unit_one,
        middle,
        slope,
        active,
        unit_two,
        scales,
    ) = stored
    scale_one, scale_two = scales[:, 0:1], scales[:, 1:2]
    unit_one, unit_two = wide(unit_one), wide(unit_two)
    (count, query_len), (_, passage_len) = layout
    pair_shares = shares.reshape(count, HEADS // 2, passage_len, 2, passage_len)
    pair_shares = pair_shares.transpose(0, 1, 3, 4, 2).reshape(
        count, HEADS, passage_len, passage_len
    )
    head_shares = query_shares.reshape(count, query_len, HEADS, count, query_len)
    head_shares = jnp.stack([head_shares[i, :, :, i] for i in range(count)])
    all_shares = (head_shares.transpose(0, 2, 3, 1), pair_shares)
    delta_two, delta_final_gain, delta_final_shift = norm_backward(
        upstream, unit_two, scale_two, final_gain
    )
    delta_branch = narrow(delta_two)
    delta_reduce_bias = column_total(delta_branch)
    delta_expanded = narrow(contract_last(delta_branch, reduce_weight) * wide(slope))
    delta_expand_bias = column_total(delta_expanded)
    delta_middle = delta_two + contract_last(delta_expanded, expand_weight)
    delta_one, delta_norm_gain, delta_norm_shift = norm_backward(
        delta_middle, unit_one, scale_one, norm_gain
    )
    delta_mix = narrow(delta_one)
    delta_mix_bias = column_total(delta_mix)
    delta_context = narrow(contract_last(delta_mix, mix_weight))
    collected = ([], [], [])
    for part_shares, (offset, group_count, length) in zip(all_shares, group_spans(layout)):
        row_span = group_count * length
        pieces = [
            split_heads(array[offset : offset + row_span], group_count, length)
            for array in (query_heads, key_heads, value_heads, delta_context)
        ]
        results = attend_backward(pieces[0], pieces[1], pieces[2], part_shares, pieces[3])
        for bucket, gradient in zip(collected, results):
            bucket.append(narrow(gradient.reshape(row_span, -1)))
    delta_query = jnp.concatenate(collected[0], axis=0)
    delta_key = jnp.concatenate(collected[1], axis=0)
    delta_value = jnp.concatenate(collected[2], axis=0)
    delta_hidden = (
        delta_one
        + contract_last(delta_query, query_weight)
        + contract_last(delta_key, key_weight)
        + contract_last(delta_value, value_weight)
    )
    operands = (
        active,
        delta_branch,
        middle,
        delta_expanded,
        hidden,
        context,
        delta_query,
        delta_key,
        delta_value,
        delta_mix,
    )
    vectors = (
        column_total(delta_query),
        column_total(delta_value),
        delta_mix_bias,
        delta_norm_gain,
        delta_norm_shift,
        delta_expand_bias,
        delta_reduce_bias,
        delta_final_gain,
        delta_final_shift,
    )
    return (delta_hidden, operands, vectors)


CORE_FLIP = [(0, 1), (1, 0), (2, 3), (3, 2)]
SIDE_FLIP = [(0, 2), (2, 0), (1, 3), (3, 1)]


def wide(values):
    return values.astype(jnp.float32)


def pick(array, index):
    return lax.dynamic_index_in_dim(array, index, 0, keepdims=False)


def reduce_chunk(chunk):
    rep_total = lax.axis_size("rep")
    group = lax.axis_index("grp")
    side, core = group // 2, group % 2
    parts = chunk.reshape((2, 2) + chunk.shape[1:])
    got = lax.ppermute(
        lax.dynamic_index_in_dim(parts, 1 - core, 1, keepdims=False), "grp", CORE_FLIP
    )
    mine = lax.dynamic_index_in_dim(parts, core, 1, keepdims=False)
    got = lax.ppermute(
        narrow(wide(pick(mine, 1 - side)) + wide(pick(got, 1 - side))), "grp", SIDE_FLIP
    ), narrow(wide(pick(mine, side)) + wide(pick(got, side)))
    summed = narrow(wide(got[0]) + wide(got[1]))
    rows, columns = summed.shape
    if rep_total != 8:
        part = lax.psum_scatter(summed, "rep", scatter_dimension=0, tiled=True)
        return wide(lax.all_gather(part, "rep", axis=0, tiled=True))
    rep = lax.axis_index("rep")
    deep, near = rep // 2, rep % 2
    flip = [(i, i ^ 1) for i in range(8)]
    shifts = [[(i, (i + 2 * k) % 8) for i in range(8)] for k in range(4)]
    halves = summed.reshape(2, rows // 2, columns)
    got = lax.ppermute(pick(halves, 1 - near), "rep", flip)
    half = narrow(wide(pick(halves, near)) + wide(got)).reshape(4, rows // 8, columns)
    total = wide(pick(half, deep))
    for k in range(1, 4):
        total = total + wide(lax.ppermute(pick(half, (deep + k) % 4), "rep", shifts[k]))
    piece = narrow(total)
    pieces = [piece] + [lax.ppermute(piece, "rep", shifts[k]) for k in range(1, 4)]
    joined = jnp.zeros((4,) + piece.shape, jnp.bfloat16)
    for k in range(4):
        joined = lax.dynamic_update_index_in_dim(joined, pieces[k], (deep - k) % 4, 0)
    other = lax.ppermute(joined, "rep", flip)
    own = joined.reshape(rows // 2, columns)
    other = other.reshape(rows // 2, columns)
    first = jnp.where(near == 0, own, other)
    second = jnp.where(near == 0, other, own)
    return wide(jnp.concatenate([first, second], axis=0))


def reduce_small(small):
    group = lax.axis_index("grp")
    side, core = group // 2, group % 2
    parts = small.reshape(2, 2, -1)
    got = lax.ppermute(
        lax.dynamic_index_in_dim(parts, 1 - core, 1, keepdims=False), "grp", CORE_FLIP
    )
    pair = lax.dynamic_index_in_dim(parts, core, 1, keepdims=False) + got
    total = pick(pair, side) + lax.ppermute(pick(pair, 1 - side), "grp", SIDE_FLIP)
    rep_total = lax.axis_size("rep")
    step = 1
    while step < rep_total:
        total = total + lax.ppermute(total, "rep", [(i, i ^ step) for i in range(rep_total)])
        step = step * 2
    return total


def remote(source, target, send_sem, recv_sem, grp, rep):
    return pltpu.make_async_remote_copy(
        src_ref=source,
        dst_ref=target,
        send_sem=send_sem,
        recv_sem=recv_sem,
        device_id=(grp, rep),
        device_id_type=pl.DeviceIdType.MESH,
    )


def gather_kernel(block_ref, out_ref, send_near, recv_near, send_far, recv_far):
    groups, reps = out_ref.shape[:2]
    grp, rep = lax.axis_index("grp"), lax.axis_index("rep")
    barrier = pltpu.get_barrier_semaphore()

    @pl.loop(1, reps)
    def _(k):
        pl.semaphore_signal(
            barrier, inc=1, device_id=(grp, (rep + k) % reps), device_id_type=pl.DeviceIdType.MESH
        )

    for k in range(1, groups):
        pl.semaphore_signal(
            barrier, inc=1, device_id=((grp + k) % groups, rep), device_id_type=pl.DeviceIdType.MESH
        )
    out_ref[grp, rep] = block_ref[...]
    pl.semaphore_wait(barrier, reps + groups - 2)

    def near(k):
        mine = out_ref.at[grp, rep]
        return remote(mine, mine, send_near.at[k], recv_near.at[k], grp, (rep + k) % reps)

    def far(k):
        row = out_ref.at[grp]
        return remote(row, row, send_far.at[k], recv_far.at[k], (grp + k) % groups, rep)

    @pl.loop(1, reps)
    def _(k):
        near(k).start()

    @pl.loop(1, reps)
    def _(k):
        near(k).wait_recv()

    for k in range(1, groups):
        far(k).start()
    for k in range(1, groups):
        far(k).wait_recv()

    @pl.loop(1, reps)
    def _(k):
        near(k).wait_send()

    for k in range(1, groups):
        far(k).wait_send()


def gather_blocks(block):
    groups, reps = lax.axis_size("grp"), lax.axis_size("rep")
    return pl.pallas_call(
        gather_kernel,
        out_shape=jax.ShapeDtypeStruct((groups, reps) + block.shape, block.dtype),
        in_specs=[pl.BlockSpec(memory_space=pltpu.VMEM)],
        out_specs=pl.BlockSpec(memory_space=pltpu.VMEM),
        scratch_shapes=[
            pltpu.SemaphoreType.DMA((reps,)),
            pltpu.SemaphoreType.DMA((reps,)),
            pltpu.SemaphoreType.DMA((groups,)),
            pltpu.SemaphoreType.DMA((groups,)),
        ],
        compiler_params=pltpu.CompilerParams(collective_id=1, has_side_effects=True),
    )(block)


def reduce_plain(layers):
    results = []
    for active, branch, middle, expanded, hidden, context, query, key, value, mix in layers:
        quarter = lambda former, latter: (
            lambda matrix: narrow(matrix).reshape(4, matrix.shape[0] // 4, matrix.shape[1])
        )(contract_rows(former, latter))
        square = jnp.concatenate(
            [
                quarter(hidden, query),
                quarter(hidden, key),
                quarter(hidden, value),
                quarter(context, mix),
            ],
            axis=1,
        )
        square = reduce_chunk(square)
        height = square.shape[0] // 4
        results.append(
            [square[place * height : (place + 1) * height] for place in range(4)]
            + [reduce_chunk(quarter(middle, expanded)), reduce_chunk(quarter(active, branch))]
        )
    return [jnp.stack([results[1][i], results[0][i]]) for i in range(6)]


SMALL = (1, 4, 6, 7, 8, 10, 12, 13, 14)
MATRICES = (0, 2, 3, 5, 9, 11)


LOG2E = 1.4426950408889634
V_QUERY, V_VALUE, V_MIX, V_GAIN, V_SHIFT, V_REDUCE, V_LAST_GAIN, V_LAST_SHIFT, V_EXPAND = range(9)
VECTOR_ROWS = 16
TILE = 256


def lane_masks(rows):
    lane = lax.broadcasted_iota(jnp.int32, (rows, 2 * DH), 1)
    return ((lane < DH).astype(jnp.float32).astype(jnp.bfloat16),
            (lane >= DH).astype(jnp.float32).astype(jnp.bfloat16))


def head_mask(head, width):
    lane = lax.broadcasted_iota(jnp.int32, (1, width), 1)
    return ((lane >= head * DH) & (lane < (head + 1) * DH))


def lanes(start, size=TILE):
    return pl.ds(pl.multiple_of(start, 128), size)


def sublanes(start, size):
    return pl.ds(pl.multiple_of(start, 16), size)


def softmax_rows(scores, bias):
    scaled = scores * (0.125 * LOG2E) + bias
    grown = jnp.exp2(scaled - jnp.max(scaled, axis=0, keepdims=True))
    return narrow(grown * (1.0 / jnp.sum(grown, axis=0, keepdims=True)))


def forward_kernel(
    query_lengths,
    passage_lengths,
    query_in,
    passage_in,
    wq_in,
    wk_in,
    wv_in,
    wm_in,
    we_in,
    wr_in,
    query_bias,
    value_bias,
    mix_bias,
    norm_gain,
    norm_shift,
    reduce_bias,
    final_gain,
    final_shift,
    expand_bias,
    query_out,
    passage_out,
    hidden_out,
    q_out,
    k_out,
    v_out,
    pt_out,
    ptq_out,
    c_out,
    u1_out,
    m_out,
    slope_out,
    f_out,
    u2_out,
    r_out,
    wq,
    wk,
    wv,
    wm,
    we,
    wr,
    x,
    q,
    k,
    v,
    pt,
    ptq,
    c,
    u1,
    m,
    slope,
    f,
    u2,
    r,
    z,
    stack,
    vec_ref,
    weight_sem,
    in_sem,
    out_sem,
):
    width = x.shape[1]
    total = x.shape[0]
    sequences = query_lengths.shape[0]
    query_rows = query_in.shape[0]
    query_len = query_rows // sequences
    passage_len = (total - query_rows) // sequences
    pairs = width // (2 * DH)

    weights = ((wq_in, wq), (wk_in, wk), (wv_in, wv), (wm_in, wm), (we_in, we), (wr_in, wr))

    def weight_copy(which, layer):
        source, target = weights[which]
        return pltpu.make_async_copy(
            source.at[layer], target.at[layer], weight_sem.at[which, layer]
        )

    stored = (
        (x, hidden_out),
        (q, q_out),
        (k, k_out),
        (v, v_out),
        (pt, pt_out),
        (ptq, ptq_out),
        (c, c_out),
        (u1, u1_out),
        (m, m_out),
        (slope, slope_out),
        (f, f_out),
        (u2, u2_out),
        (r, r_out),
    )
    X, Q, K, V, PT, PTQ, C, U1, M, SLOPE, F, U2, R = range(13)

    def store(which, layer):
        source, target = stored[which]
        return pltpu.make_async_copy(source, target.at[layer], out_sem.at[which])

    def reuse(which, layer):
        @pl.when(layer > 0)
        def _():
            store(which, layer - 1).wait()

    first = pltpu.make_async_copy(query_in, x.at[pl.ds(0, query_rows)], in_sem.at[0])
    rest = pltpu.make_async_copy(
        passage_in, x.at[pl.ds(query_rows, total - query_rows)], in_sem.at[1]
    )
    first.start()
    rest.start()
    for layer in range(LAYERS):
        for which in range(6):
            weight_copy(which, layer).start()
    vectors = (
        query_bias,
        value_bias,
        mix_bias,
        norm_gain,
        norm_shift,
        reduce_bias,
        final_gain,
        final_shift,
    )
    for layer in range(LAYERS):
        for place, vector in enumerate(vectors):
            vec_ref[layer, place : place + 1, :] = wide(vector[layer : layer + 1, :])
        for j in range(4):
            vec_ref[layer, V_EXPAND + j : V_EXPAND + j + 1, :] = wide(
                expand_bias[layer : layer + 1, j * width : (j + 1) * width]
            )
    first.wait()
    rest.wait()

    def project(source, weight, layer, bias_row, target):
        @pl.loop(0, width // TILE)
        def _(i):
            value = product(source[...], weight[layer, :, lanes(i * TILE)])
            if bias_row is not None:
                value = value + vec_ref[layer, pl.ds(bias_row, 1), lanes(i * TILE)]
            target[:, lanes(i * TILE)] = narrow(value)

    def norm(layer, gain_row, shift_row, unit, target, scale_lane):
        step = 96
        gain = vec_ref[layer, pl.ds(gain_row, 1), :]
        shift = vec_ref[layer, pl.ds(shift_row, 1), :]

        @pl.loop(0, total // step)
        def _(i):
            at = sublanes(i * step, step)
            full, unit_rows, scaled = norm_forward(z[at, :], gain, shift)
            unit[at, :] = narrow(unit_rows)
            target[at, :] = narrow(full)
            r[at, scale_lane : scale_lane + 1] = scaled

    @pl.loop(0, LAYERS)
    def _(layer):
        store(X, layer).start()
        weight_copy(0, layer).wait()
        reuse(Q, layer)
        project(x, wq, layer, V_QUERY, q)
        store(Q, layer).start()
        weight_copy(1, layer).wait()
        reuse(K, layer)
        project(x, wk, layer, None, k)
        store(K, layer).start()
        weight_copy(2, layer).wait()
        reuse(V, layer)
        project(x, wv, layer, V_VALUE, v)
        store(V, layer).start()

        reuse(PT, layer)
        reuse(PTQ, layer)
        reuse(C, layer)

        for head in range(HEADS):
            mask = head_mask(head, width).astype(jnp.float32).astype(jnp.bfloat16)
            stack[head * query_rows : (head + 1) * query_rows, :] = q[:query_rows, :] * mask
        scores = contract_last(k[:query_rows, :], stack[...])
        key_slot = lax.broadcasted_iota(jnp.int32, scores.shape, 0)
        query_slot = lax.broadcasted_iota(jnp.int32, scores.shape, 1) % query_rows
        live = jnp.zeros(scores.shape, jnp.bool_)
        for s in range(sequences):
            low = s * query_len
            live = live | (
                (key_slot >= low)
                & (key_slot < low + query_lengths[s])
                & (query_slot >= low)
                & (query_slot < low + query_len)
            )
        shares = softmax_rows(scores, jnp.where(live, 0.0, -1e30))
        ptq[...] = shares
        spread = contract_rows(shares, v[:query_rows, :])
        context = jnp.zeros((query_rows, width), jnp.float32)
        for head in range(HEADS):
            context = context + jnp.where(
                head_mask(head, width), spread[head * query_rows : (head + 1) * query_rows, :], 0.0
            )
        c[:query_rows, :] = narrow(context)

        @pl.loop(0, sequences * pairs)
        def _(i):
            s, pair = i // pairs, i % pairs
            rows = sublanes(query_rows + s * passage_len, passage_len)
            at = lanes(pair * 2 * DH, 2 * DH)
            even, odd = lane_masks(passage_len)
            q2, k2, v2 = q[rows, at], k[rows, at], v[rows, at]
            scores = contract_last(k2, jnp.concatenate([q2 * even, q2 * odd], axis=0))
            slot = lax.broadcasted_iota(jnp.int32, (passage_len, 1), 0)
            shares = softmax_rows(
                scores, jnp.where(slot < passage_lengths[s], 0.0, -1e30)
            )
            pt[i] = shares
            shares = jnp.concatenate([shares[:, :passage_len], shares[:, passage_len:]], axis=0)
            spread = contract_rows(jnp.concatenate([v2 * even, v2 * odd], axis=0), shares)
            c[rows, at] = narrow(spread.T)

        store(PT, layer).start()
        store(PTQ, layer).start()
        store(C, layer).start()

        weight_copy(3, layer).wait()

        @pl.loop(0, width // TILE)
        def _(i):
            at = lanes(i * TILE)
            z[:, at] = (
                wide(x[:, at])
                + product(c[...], wm[layer, :, at])
                + vec_ref[layer, pl.ds(V_MIX, 1), at]
            )

        reuse(U1, layer)
        reuse(M, layer)
        reuse(R, layer)
        norm(layer, V_GAIN, V_SHIFT, u1, m, 0)
        store(U1, layer).start()
        store(M, layer).start()

        weight_copy(4, layer).wait()
        reuse(SLOPE, layer)
        reuse(F, layer)

        @pl.loop(0, 4 * width // TILE)
        def _(i):
            at = lanes(i * TILE)
            tiles = width // TILE
            bias = vec_ref[layer, pl.ds(V_EXPAND + i // tiles, 1), lanes((i % tiles) * TILE)]
            value = product(m[...], we[layer, :, at]) + bias
            share = 0.5 * (1.0 + lax.erf(value * (1.0 / math.sqrt(2.0))))
            density = jnp.exp2(value * value * (-0.5 * LOG2E)) * (1.0 / math.sqrt(2.0 * math.pi))
            f[:, at] = narrow(value * share)
            slope[:, at] = narrow(share + value * density)

        store(SLOPE, layer).start()
        store(F, layer).start()

        weight_copy(5, layer).wait()

        @pl.loop(0, width // TILE)
        def _(i):
            at = lanes(i * TILE)
            z[:, at] = (
                wide(m[:, at])
                + product(f[...], wr[layer, :, at])
                + vec_ref[layer, pl.ds(V_REDUCE, 1), at]
            )

        store(X, layer).wait()
        reuse(U2, layer)
        norm(layer, V_LAST_GAIN, V_LAST_SHIFT, u2, x, 1)
        store(U2, layer).start()
        store(R, layer).start()

    last = LAYERS - 1
    first = pltpu.make_async_copy(x.at[pl.ds(0, query_rows)], query_out, in_sem.at[0])
    rest = pltpu.make_async_copy(
        x.at[pl.ds(query_rows, total - query_rows)], passage_out, in_sem.at[1]
    )
    first.start()
    rest.start()
    for which in range(1, 13):
        store(which, last).wait()
    first.wait()
    rest.wait()


def run_forward(query_length, passage_length, query_input, passage_input, matrices, vectors):
    sequences, query_len, width = query_input.shape
    passage_len = passage_input.shape[1]
    query_rows, passage_rows = sequences * query_len, sequences * passage_len
    total = query_rows + passage_rows
    pairs = width // (2 * DH)
    bf16, f32 = jnp.bfloat16, jnp.float32
    arrays = (
        ((total, width), bf16),
        ((total, width), bf16),
        ((total, width), bf16),
        ((total, width), bf16),
        ((sequences * pairs, passage_len, 2 * passage_len), bf16),
        ((query_rows, HEADS * query_rows), bf16),
        ((total, width), bf16),
        ((total, width), bf16),
        ((total, width), bf16),
        ((total, 4 * width), bf16),
        ((total, 4 * width), bf16),
        ((total, width), bf16),
        ((total, 128), f32),
    )
    anywhere = pl.BlockSpec(memory_space=pl.ANY)
    return pl.pallas_call(
        forward_kernel,
        out_shape=(
            jax.ShapeDtypeStruct((query_rows, width), bf16),
            jax.ShapeDtypeStruct((passage_rows, width), bf16),
        )
        + tuple(jax.ShapeDtypeStruct((LAYERS,) + shape, dtype) for shape, dtype in arrays),
        in_specs=[pl.BlockSpec(memory_space=pltpu.SMEM)] * 2
        + [anywhere] * 8
        + [pl.BlockSpec(memory_space=pltpu.VMEM)] * 9,
        out_specs=[anywhere] * 15,
        scratch_shapes=[pltpu.VMEM(matrix.shape, bf16) for matrix in matrices]
        + [pltpu.VMEM(shape, dtype) for shape, dtype in arrays]
        + [
            pltpu.VMEM((total, width), f32),
            pltpu.VMEM((HEADS * query_rows, width), bf16),
            pltpu.VMEM((LAYERS, VECTOR_ROWS, width), f32),
            pltpu.SemaphoreType.DMA((6, LAYERS)),
            pltpu.SemaphoreType.DMA((2,)),
            pltpu.SemaphoreType.DMA((13,)),
        ],
        compiler_params=pltpu.CompilerParams(vmem_limit_bytes=60 * 1024 * 1024),
    )(
        query_length,
        passage_length,
        query_input.reshape(query_rows, width),
        passage_input.reshape(passage_rows, width),
        *matrices,
        *vectors,
    )


CHUNKS = 24
PARTS = 12
S_QUERY, S_VALUE, S_MIX, S_GAIN, S_SHIFT, S_REDUCE, S_LAST_GAIN, S_LAST_SHIFT, S_EXPAND = range(9)
CORE_SLOTS, SIDE_SLOTS, NEAR_SLOTS, KEEP_SLOTS, SENT_SLOTS = 4, 4, 4, 6, 3
LAGS = (2, 3, 4, 5, 6)
BLOCK = 16
SMALL_AT = 21


def one_hot(shape, hit):
    row = lax.broadcasted_iota(jnp.int32, shape, 0)
    column = lax.broadcasted_iota(jnp.int32, shape, 1)
    return narrow(jnp.where(hit(row, column), 1.0, 0.0))


def backward_kernel(
    margin_ref,
    positive_ref,
    cluster_row,
    norm_gain,
    final_gain,
    query_out,
    passage_out,
    query_cot,
    passage_cot,
    wq_in,
    wk_in,
    wv_in,
    wm_in,
    we_in,
    wr_in,
    hidden_in,
    q_in,
    k_in,
    v_in,
    pt_in,
    ptq_in,
    c_in,
    u1_in,
    m_in,
    slope_in,
    f_in,
    u2_in,
    r_in,
    out_ref,
    small_out,
    loss_out,
    query_grad,
    passage_grad,
    buf,
    keep,
    side_out,
    core_in,
    side_in,
    near_in,
    deep_in,
    piece,
    small,
    small_core,
    small_side,
    small_near,
    small_deep,
    first,
    blocks,
    gains,
    dz,
    dy,
    du,
    quad,
    pair_in,
    middle,
    unit,
    active,
    dc,
    pt,
    ptq,
    stack,
    r,
    w,
    gather_near,
    gather_far,
    first_sem,
    load_sem,
    weight_sem,
    core_sem,
    side_sem,
    near_sem,
    deep_send,
    deep_recv,
    back_sem,
    local_sem,
    small_sem,
    small_send,
    small_recv,
    core_free,
    side_free,
    near_free,
):
    groups, reps = blocks.shape[:2]
    depth = reps // 2
    rows, columns = keep.shape[1:]
    width = dz.shape[1]
    quarter = width // 4
    half_rows = rows // 2
    piece_rows = half_rows // depth
    total = dz.shape[0]
    sequences = margin_ref.shape[0]
    query_rows = query_out.shape[0]
    query_len = query_rows // sequences
    passage_len = (total - query_rows) // sequences
    pairs = width // (2 * DH)
    passage_rows = pl.ds(query_rows, total - query_rows)
    everyone = cluster_row.shape[1]

    grp, rep = lax.axis_index("grp"), lax.axis_index("rep")
    side, core = grp // 2, grp % 2
    deep, near = rep // 2, rep % 2
    sibling = (2 * side + (1 - core), rep)
    across = (2 * (1 - side) + core, rep)
    beside = (grp, 2 * deep + (1 - near))

    def behind(k):
        return (grp, 2 * ((deep + k) % depth) + near)

    deep_low, deep_high = deep % 2, deep // 2
    beyond = (grp, 2 * (deep + 2 - 4 * deep_high) + near)
    next_to = (grp, 2 * (deep + 1 - 2 * deep_low) + near)

    def signal(semaphore, peer):
        pl.semaphore_signal(
            semaphore, inc=1, device_id=peer, device_id_type=pl.DeviceIdType.MESH
        )

    barrier = pltpu.get_barrier_semaphore()
    for k in range(1, reps):
        signal(barrier, (grp, (rep + k) % reps))
    for k in range(1, groups):
        signal(barrier, ((grp + k) % groups, rep))

    firsts = [
        pltpu.make_async_copy(
            source.at[pl.ds(s * length, BLOCK)],
            first.at[pl.ds((place * sequences + s) * BLOCK, BLOCK)],
            first_sem.at[place * sequences + s],
        )
        for place, (source, length) in enumerate(
            ((query_out, query_len), (passage_out, passage_len))
        )
        for s in range(sequences)
    ]
    for copy in firsts:
        copy.start()

    loaded = {
        "f": (f_in, active),
        "u2": (u2_in, unit.at[0]),
        "slope": (slope_in, du),
        "m": (m_in, middle),
        "u1": (u1_in, unit.at[1]),
        "c": (c_in, pair_in.at[1]),
        "q": (q_in, quad.at[0]),
        "k": (k_in, quad.at[1]),
        "v": (v_in, quad.at[2]),
        "pt": (pt_in, pt),
        "ptq": (ptq_in, ptq),
        "x": (hidden_in, pair_in.at[0]),
    }
    places = {name: place for place, name in enumerate(loaded)}

    def load(name, layer):
        source, target = loaded[name]
        return pltpu.make_async_copy(source.at[layer], target, load_sem.at[places[name]])

    def weight_loads(kind, layer, slot):
        squares = []
        for j in range(4):
            block = pl.ds(j * width, width)
            if kind == 0:
                source = wr_in.at[layer, block]
            elif kind == 1:
                source = we_in.at[layer, :, block]
            else:
                source = (wq_in, wk_in, wv_in, wm_in)[j].at[layer]
            squares.append(
                pltpu.make_async_copy(source, w.at[slot, j], weight_sem.at[slot, j])
            )
        return squares

    def start_weights(kind, layer, slot):
        for copy in weight_loads(kind, layer, slot):
            copy.start()

    def wait_weights(kind, layer, slot):
        for copy in weight_loads(kind, layer, slot):
            copy.wait()

    last = LAYERS - 1
    cots = [
        pltpu.make_async_copy(query_cot, dy.at[pl.ds(0, query_rows)], first_sem.at[4]),
        pltpu.make_async_copy(passage_cot, dy.at[passage_rows], first_sem.at[5]),
        pltpu.make_async_copy(r_in, r, first_sem.at[6]),
    ]
    for copy in cots:
        copy.start()
    for name in ("u2", "f"):
        load(name, last).start()

    def tally(layer, row_at, lanes_at, values):
        at = (layer, pl.ds(row_at, 1), lanes_at)
        small[at] = small[at] + jnp.sum(values, axis=0, keepdims=True)

    every_lane = pl.ds(0, width)

    norm_step = 48

    def norm_back_rows(
        layer, unit_at, scale_lane, gain_row, target, gain_to, shift_to, bias_to, tile
    ):
        gain = gains[layer, pl.ds(gain_row, 1), :]
        at = sublanes(tile * norm_step, norm_step)
        upstream = dz[at, :]
        unit_rows = wide(unit[unit_at, at, :])
        scaled = r[layer, at, scale_lane : scale_lane + 1]
        delta_unit = upstream * gain
        delta = scaled * (
            delta_unit
            - jnp.mean(delta_unit, axis=-1, keepdims=True)
            - unit_rows * jnp.mean(delta_unit * unit_rows, axis=-1, keepdims=True)
        )
        dz[at, :] = delta
        rounded = narrow(delta)
        target[at, :] = rounded
        tally(layer, gain_to, every_lane, upstream * unit_rows)
        tally(layer, shift_to, every_lane, upstream)
        tally(layer, bias_to, every_lane, wide(rounded))

    def last_norm_back(layer, tile):
        norm_back_rows(
            layer, 0, 1, 1, dy, S_LAST_GAIN, S_LAST_SHIFT, S_REDUCE, tile
        )

    def first_norm_back(layer, tile):
        norm_back_rows(layer, 1, 0, 0, quad.at[3], S_GAIN, S_SHIFT, S_MIX, tile)

    for copy in firsts:
        copy.wait()
    firsts_count = 2 * sequences
    segments = width // TILE
    packed = jnp.zeros((BLOCK, TILE), jnp.float32)
    for j in range(segments):
        low = j * firsts_count
        packed = packed + product(
            one_hot(
                (BLOCK, first.shape[0]),
                lambda i, k: (k == (i - low) * BLOCK) & (i >= low) & (i < low + firsts_count),
            ),
            first[:, j * TILE : (j + 1) * TILE],
        )
    row = lax.broadcasted_iota(jnp.int32, packed.shape, 0)
    lane = lax.broadcasted_iota(jnp.int32, packed.shape, 1)
    for s in range(sequences):
        positive = positive_ref[s]
        facts = (margin_ref[s], positive // 128, positive % 128)
        for place, fact in enumerate(facts):
            at = (row == segments * firsts_count) & (lane == place * sequences + s)
            packed = jnp.where(at, fact.astype(jnp.float32), packed)
    blocks[grp, rep] = narrow(packed)

    def to_near(k):
        mine = blocks.at[grp, rep]
        return remote(
            mine, mine, gather_near.at[0, k], gather_near.at[1, k], grp, (rep + k) % reps
        )

    def to_far(k):
        line = blocks.at[grp]
        return remote(
            line, line, gather_far.at[0, k], gather_far.at[1, k], (grp + k) % groups, rep
        )

    pl.semaphore_wait(barrier, reps + groups - 2)

    @pl.loop(1, reps)
    def _(k):
        to_near(k).start()

    start_weights(0, last, 0)
    for name in ("slope", "m", "u1", "c", "q", "k", "v", "pt", "ptq", "x"):
        load(name, last).start()
    start_weights(1, last, 1)

    for copy in cots:
        copy.wait()
    small[...] = jnp.zeros_like(small)
    for layer in range(LAYERS):
        gains[layer, 0:1, :] = wide(norm_gain[layer : layer + 1, :])
        gains[layer, 1:2, :] = wide(final_gain[layer : layer + 1, :])

    @pl.loop(0, total // 96)
    def _(i):
        at = sublanes(i * 96, 96)
        dz[at, :] = wide(dy[at, :])

    first_at = [s * query_len for s in range(sequences)]
    first_at += [query_rows + s * passage_len for s in range(sequences)]
    late = sorted({at // norm_step for at in first_at})
    spans = [span for span in zip([-1] + late, late + [total // norm_step])]
    load("u2", last).wait()

    def early_norm(low, high):
        @pl.loop(low, high)
        def _(tile):
            last_norm_back(last, tile)

    for low, high in spans[: len(spans) // 2]:
        if low + 1 < high:
            early_norm(low + 1, high)

    @pl.loop(1, reps)
    def _(k):
        to_near(k).wait_recv()

    for k in range(1, groups):
        to_far(k).start()

    for low, high in spans[len(spans) // 2 :]:
        if low + 1 < high:
            early_norm(low + 1, high)

    for k in range(1, groups):
        to_far(k).wait_recv()

    gathered = blocks[...].reshape(groups * reps * BLOCK, TILE)

    def taken(offset):
        return product(
            one_hot(
                (everyone, gathered.shape[0]),
                lambda i, j: j == BLOCK * (i // sequences) + offset(i),
            ),
            gathered,
        )

    def taken_rows(base):
        return narrow(
            jnp.concatenate(
                [
                    taken(lambda i: j * firsts_count + base + i % sequences)
                    for j in range(segments)
                ],
                axis=1,
            )
        )

    every_query = taken_rows(0)
    every_passage = taken_rows(sequences)
    facts = taken(lambda i: segments * firsts_count)[:, :128]
    query_at = lax.broadcasted_iota(jnp.int32, facts.shape, 0) % sequences
    lane_at = lax.broadcasted_iota(jnp.int32, facts.shape, 1)

    def fact(place):
        hit = lane_at == place * sequences + query_at
        return jnp.sum(jnp.where(hit, facts, 0.0), axis=1, keepdims=True)

    margin_weight = (fact(0) + 1.0) / NBINS
    every_positive = fact(1) * 128.0 + fact(2)
    score_scale = 2.0 / math.sqrt(width)
    logits = contract_last(every_query, every_passage) * score_scale
    passage_at = lax.broadcasted_iota(jnp.int32, logits.shape, 1).astype(jnp.float32)
    chosen_mask = passage_at == every_positive
    clusters = jnp.broadcast_to(cluster_row[...], (everyone, everyone))
    on_diagonal = lax.broadcasted_iota(jnp.int32, clusters.shape, 0) == (
        lax.broadcasted_iota(jnp.int32, clusters.shape, 1)
    )
    own_clusters = jnp.sum(
        jnp.where(on_diagonal, clusters.astype(jnp.float32), 0.0), axis=1, keepdims=True
    )
    allowed = (clusters.astype(jnp.float32) == own_clusters) | chosen_mask
    masked = jnp.where(allowed, logits, -1e30)
    peak = jnp.max(masked, axis=1, keepdims=True)
    normalizer = peak + jnp.log(jnp.sum(jnp.exp(masked - peak), axis=1, keepdims=True))
    chosen = jnp.sum(jnp.where(chosen_mask, logits, 0.0), axis=1, keepdims=True)
    loss = margin_weight * (normalizer - chosen)
    share = jnp.where(allowed, jnp.exp(masked - normalizer), 0.0)
    delta_logits = narrow(margin_weight * (share - jnp.where(chosen_mask, 1.0, 0.0)))
    start = (grp * reps + rep) * sequences
    loss_row = lax.broadcasted_iota(jnp.int32, (everyone, 128), 0)
    loss_lane = lax.broadcasted_iota(jnp.int32, (everyone, 128), 1)
    loss_out[...] = jnp.broadcast_to(
        jnp.sum(jnp.where(loss_row == start + loss_lane, loss, 0.0), axis=0, keepdims=True),
        loss_out.shape,
    )
    own = one_hot((BLOCK, everyone), lambda i, j: (j == start + i) & (i < sequences))
    own_rows = narrow(product(own, delta_logits))
    own_columns = narrow(contract_last(own, delta_logits))
    delta_firsts = (
        product(own_rows, every_passage) * score_scale,
        product(own_columns, every_query) * score_scale,
    )
    eight = lax.broadcasted_iota(jnp.int32, (8, width), 0)
    for place, (base, length) in enumerate(((0, query_len), (query_rows, passage_len))):
        for s in range(sequences):
            at = pl.ds(base + s * length, 8)
            dz[at, :] = dz[at, :] + jnp.where(
                eight == 0, delta_firsts[place][s : s + 1, :], 0.0
            )

    for tile in late:
        last_norm_back(last, tile)

    def core_copy(t):
        return remote(
            buf.at[t % 2, :, 1 - core],
            core_in.at[t % CORE_SLOTS],
            core_sem.at[0, t],
            core_sem.at[1, t],
            *sibling,
        )

    def side_copy(t):
        return remote(
            side_out.at[t % SENT_SLOTS],
            side_in.at[t % SIDE_SLOTS],
            side_sem.at[0, t],
            side_sem.at[1, t],
            *across,
        )

    def near_copy(t):
        return remote(
            keep.at[t % KEEP_SLOTS, sublanes((1 - near) * half_rows, half_rows)],
            near_in.at[t % NEAR_SLOTS],
            near_sem.at[0, t],
            near_sem.at[1, t],
            *beside,
        )

    def piece_of(place):
        order = 2 * (place % 2) + place // 2
        return sublanes(near * half_rows + order * piece_rows, piece_rows)

    def deep_copy(t, k):
        return remote(
            keep.at[t % KEEP_SLOTS, piece_of((deep + k) % depth)],
            deep_in.at[t, k - 1],
            deep_send.at[k - 1, t],
            deep_recv.at[k - 1, t],
            *behind(k),
        )

    def chunk_place(t):
        step, part = t // PARTS, t % PARTS
        return (part // 4) * 8 + (last - step) * 4 + part % 4

    def own_piece(t):
        return out_ref.at[
            chunk_place(t), near, deep_low, sublanes(deep_high * piece_rows, piece_rows)
        ]

    def local_copy(t):
        return pltpu.make_async_copy(piece.at[t], own_piece(t), local_sem.at[t])

    def back_copy(stage, source, peer, t, target=None):
        return remote(
            source,
            source if target is None else target,
            back_sem.at[0, stage, t],
            back_sem.at[1, stage, t],
            *peer,
        )

    def back_high(t):
        return back_copy(0, piece.at[t], beyond, t, own_piece(t))

    def even_second(t):
        return back_copy(1, out_ref.at[chunk_place(t), near, deep_low], next_to, t)

    def even_third(t):
        return back_copy(2, out_ref.at[chunk_place(t), near], beside, t)

    def odd_second(t):
        return back_copy(1, out_ref.at[chunk_place(t), near, deep_low], beside, t)

    def odd_third(t):
        return back_copy(2, out_ref.at[chunk_place(t), :, deep_low], next_to, t)

    def by_parity(t, even, odd):
        @pl.when(t % 2 == 0)
        def _():
            even(t)

        @pl.when(t % 2 == 1)
        def _():
            odd(t)

    def add_rows(target, former, latter, count):
        step = 48

        @pl.loop(0, count // step)
        def _(i):
            def at(first_row):
                return sublanes(first_row + i * step, step)

            (to, to_row), (one, one_row), (two, two_row) = target, former, latter
            to[at(to_row), :] = narrow(wide(one[at(one_row), :]) + wide(two[at(two_row), :]))

    def after_core(t):
        core_copy(t).wait()
        slot = t % CORE_SLOTS
        add_rows(
            (side_out.at[t % SENT_SLOTS], 0),
            (buf.at[t % 2, 1 - side, core], 0),
            (core_in.at[slot, 1 - side], 0),
            rows,
        )

        @pl.when(t >= SIDE_SLOTS)
        def _():
            pl.semaphore_wait(side_free, 1)

        side_copy(t).start()
        add_rows(
            (keep.at[t % KEEP_SLOTS], 0),
            (buf.at[t % 2, side, core], 0),
            (core_in.at[slot, side], 0),
            rows,
        )

        @pl.when(t + CORE_SLOTS < CHUNKS)
        def _():
            signal(core_free, sibling)

    def after_side(t):
        side_copy(t).wait()
        kept = keep.at[t % KEEP_SLOTS]
        came = side_in.at[t % SIDE_SLOTS]
        there, here = (1 - near) * half_rows, near * half_rows
        add_rows((kept, there), (kept, there), (came, there), half_rows)

        @pl.when(t >= NEAR_SLOTS)
        def _():
            pl.semaphore_wait(near_free, 1)

        near_copy(t).start()
        add_rows((kept, here), (kept, here), (came, here), half_rows)

        @pl.when(t + SIDE_SLOTS < CHUNKS)
        def _():
            signal(side_free, across)

    def after_near(t):
        near_copy(t).wait()
        kept = keep.at[t % KEEP_SLOTS]
        here = near * half_rows
        add_rows((kept, here), (kept, here), (near_in.at[t % NEAR_SLOTS], 0), half_rows)

        @pl.when(t + NEAR_SLOTS < CHUNKS)
        def _():
            signal(near_free, beside)

        for k in range(1, depth):
            deep_copy(t, k).start()

    def after_deep(t):
        summed = wide(keep[t % KEEP_SLOTS, piece_of(deep), :])
        for k in range(1, depth):
            deep_copy(t, k).wait()
        for k in range(1, depth):
            summed = summed + wide(deep_in[t, k - 1])
        piece[t] = narrow(summed)
        local_copy(t).start()
        back_high(t).start()

    def after_high(t):
        local_copy(t).wait()
        back_high(t).wait()
        by_parity(t, lambda t: even_second(t).start(), lambda t: odd_second(t).start())

    def after_second(t):
        def even(t):
            even_second(t).wait()
            even_third(t).start()

        def odd(t):
            odd_second(t).wait()
            odd_third(t).start()

        by_parity(t, even, odd)

    def expand_back(layer, slot):
        tiles = width // TILE

        @pl.loop(0, 4 * tiles)
        def _(i):
            at = lanes(i * TILE)
            block, tile = i // tiles, i % tiles
            weight = w[slot, block, sublanes(tile * TILE, TILE), :]
            value = narrow(contract_last(dy[...], weight) * wide(du[:, at]))
            du[:, at] = value
            tally(layer, S_EXPAND + block, lanes(tile * TILE), wide(value))

    def middle_back(slot):
        @pl.loop(0, width // TILE)
        def _(i):
            at = lanes(i * TILE)
            value = dz[:, at]
            for block in range(4):
                weight = w[slot, block, sublanes(i * TILE, TILE), :]
                value = value + contract_last(du[:, block * width : (block + 1) * width], weight)
            dz[:, at] = value

    def context_back(slot):
        @pl.loop(0, width // TILE)
        def _(i):
            weight = w[slot, 3, sublanes(i * TILE, TILE), :]
            dc[:, lanes(i * TILE)] = narrow(contract_last(quad[3], weight))

    def hidden_back(slot):
        @pl.loop(0, width // TILE)
        def _(i):
            at = lanes(i * TILE)
            value = dz[:, at]
            for place in range(3):
                weight = w[slot, place, sublanes(i * TILE, TILE), :]
                value = value + contract_last(quad[place], weight)
            dz[:, at] = value

    def score_back(shares, delta):
        shares = wide(shares)
        weighed = shares * delta
        return narrow(weighed - shares * jnp.sum(weighed, axis=0, keepdims=True))

    def query_attention_back(layer):
        query_span = pl.ds(0, query_rows)
        q2, k2, v2 = quad[0, query_span, :], quad[1, query_span, :], quad[2, query_span, :]

        def fill(rows_of):
            for head in range(HEADS):
                mask = narrow(jnp.where(head_mask(head, width), 1.0, 0.0))
                stack[head * query_rows : (head + 1) * query_rows, :] = rows_of * mask

        fill(dc[query_span, :])
        delta_value = narrow(product(ptq[...], stack[...]))
        delta_scores = score_back(ptq[...], contract_last(v2, stack[...]))
        fill(q2)
        delta_key = narrow(product(delta_scores, stack[...]) * 0.125)
        stack[...] = narrow(contract_rows(delta_scores, k2) * 0.125)
        delta_query = jnp.zeros((query_rows, width), jnp.float32)
        for head in range(HEADS):
            delta_query = delta_query + jnp.where(
                head_mask(head, width),
                wide(stack[head * query_rows : (head + 1) * query_rows, :]),
                0.0,
            )
        delta_query = narrow(delta_query)
        quad[0, query_span, :] = delta_query
        quad[1, query_span, :] = delta_key
        quad[2, query_span, :] = delta_value
        tally(layer, S_QUERY, every_lane, wide(delta_query))
        tally(layer, S_VALUE, every_lane, wide(delta_value))

    def passage_attention_back(layer, low, high):
        @pl.loop(low, high)
        def _(i):
            s, pair = i // pairs, i % pairs
            at_rows = sublanes(query_rows + s * passage_len, passage_len)
            at = lanes(pair * 2 * DH, 2 * DH)
            even, odd = lane_masks(passage_len)
            q2, k2, v2 = quad[0, at_rows, at], quad[1, at_rows, at], quad[2, at_rows, at]
            d2 = dc[at_rows, at]
            shares = pt[i]
            deltas = jnp.concatenate([d2 * even, d2 * odd], axis=0)
            delta_value = narrow(product(shares, deltas))
            delta_scores = score_back(shares, contract_last(v2, deltas))
            queries = jnp.concatenate([q2 * even, q2 * odd], axis=0)
            delta_key = narrow(product(delta_scores, queries) * 0.125)
            keys = jnp.concatenate([k2 * even, k2 * odd], axis=0)
            piled = jnp.concatenate(
                [delta_scores[:, :passage_len], delta_scores[:, passage_len:]], axis=0
            )
            delta_query = narrow((contract_rows(keys, piled) * 0.125).T)
            quad[0, at_rows, at] = delta_query
            quad[1, at_rows, at] = delta_key
            quad[2, at_rows, at] = delta_value
            tally(layer, S_QUERY, at, wide(delta_query))
            tally(layer, S_VALUE, at, wide(delta_value))

    def make_terms(t, part):
        pair, half = (part % 4) // 2, lanes((part % 2) * columns, columns)

        @pl.when(part < 4)
        def _():
            @pl.loop(0, 4)
            def _(i):
                taller = active[:, lanes(i * width + pair * rows, rows)]
                buf[t % 2, i // 2, i % 2] = narrow(contract_rows(taller, dy[:, half]))

        def split(i, terms):
            place = sublanes((i // 2) * quarter, quarter)
            terms = narrow(terms)
            buf[t % 2, i % 2, 0, place, :] = terms[:quarter]
            buf[t % 2, i % 2, 1, place, :] = terms[quarter:]

        def two_quarters(i):
            return lanes((i % 2) * 2 * quarter, 2 * quarter)

        @pl.when((part >= 4) & (part < 8))
        def _():
            @pl.loop(0, 4)
            def _(i):
                wider = du[:, lanes((2 * pair + i // 2) * width + (part % 2) * columns, columns)]
                split(i, contract_rows(middle[:, two_quarters(i)], wider))

        @pl.when(part >= 8)
        def _():
            @pl.loop(0, 4)
            def _(i):
                which = 2 * pair + i // 2
                split(
                    i,
                    contract_rows(
                        pair_in[which // 3, :, two_quarters(i)], quad[which, :, half]
                    ),
                )

        @pl.when(t >= CORE_SLOTS)
        def _():
            pl.semaphore_wait(core_free, 1)

        core_copy(t).start()

    def small_move(place, target, peer):
        return remote(
            small, target, small_sem.at[2 * place], small_sem.at[2 * place + 1], *peer
        )

    def small_to_deep(k):
        line = small_deep.at[deep]
        return remote(line, line, small_send.at[k - 1], small_recv.at[k - 1], *behind(k))

    def gradients_out():
        return (
            pltpu.make_async_copy(dz.at[pl.ds(0, query_rows)], query_grad, first_sem.at[4]),
            pltpu.make_async_copy(dz.at[passage_rows], passage_grad, first_sem.at[5]),
        )

    @pl.loop(0, CHUNKS + LAGS[-1])
    def _(t):
        step, part = t // PARTS, t % PARTS
        layer = last - step
        slot = (3 * step) % 2
        busy = t < CHUNKS
        more = busy & (step < LAYERS - 1)

        @pl.when((t > 0) & (t <= CHUNKS))
        def _():
            after_core(t - 1)

        @pl.when(busy & (part == 0))
        def _():
            @pl.when(step > 0)
            def _():
                for name in ("c", "q", "k", "v", "x"):
                    load(name, layer).start()

                load("u2", layer).wait()

                @pl.loop(0, total // norm_step)
                def _(tile):
                    last_norm_back(layer, tile)

            load("f", layer).wait()

        @pl.when(busy & (part == 4))
        def _():
            load("m", layer).wait()

        @pl.when(busy & (part == 8))
        def _():
            for name in ("c", "x"):
                load(name, layer).wait()

        @pl.when(busy)
        def _():
            make_terms(t, part)

        @pl.when(busy & (part == 1))
        def _():
            @pl.when(more)
            def _():
                load("u2", layer - 1).start()

            load("slope", layer).wait()
            wait_weights(0, layer, slot)
            expand_back(layer, slot)
            start_weights(2, layer, slot)

        @pl.when(busy & (part == 2))
        def _():
            wait_weights(1, layer, 1 - slot)
            middle_back(1 - slot)

            @pl.when(more)
            def _():
                start_weights(0, layer - 1, 1 - slot)

        @pl.when(busy & (part == 3))
        def _():
            load("u1", layer).wait()

            @pl.loop(0, total // norm_step)
            def _(tile):
                first_norm_back(layer, tile)

            wait_weights(2, layer, slot)
            context_back(slot)

            @pl.when(more)
            def _():
                for name in ("f", "u1"):
                    load(name, layer - 1).start()

        @pl.when(busy & (part == 4))
        def _():
            for name in ("q", "k", "v", "pt", "ptq"):
                load(name, layer).wait()
            query_attention_back(layer)

        passages = sequences * pairs

        @pl.when(busy & (part == 5))
        def _():
            passage_attention_back(layer, 0, passages // 3)

        @pl.when(busy & (part == 6))
        def _():
            passage_attention_back(layer, passages // 3, 2 * passages // 3)

        @pl.when(busy & (part == 7))
        def _():
            passage_attention_back(layer, 2 * passages // 3, passages)

        @pl.when(busy & (part == 8))
        def _():
            @pl.when(more)
            def _():
                for name in ("pt", "ptq", "slope", "m"):
                    load(name, layer - 1).start()

            hidden_back(slot)

            @pl.when(more)
            def _():
                start_weights(1, layer - 1, slot)

            @pl.when(step == LAYERS - 1)
            def _():
                for copy in gradients_out():
                    copy.start()

        for lag, stage in zip(LAGS, (after_side, after_near, after_deep, after_high, after_second)):

            @pl.when((t >= lag) & (t < CHUNKS + lag))
            def _():
                stage(t - lag)

        for place, (target, peer, came) in enumerate(
            (
                (small_core, sibling, small_core),
                (small_side, across, small_side),
                (small_near, beside, small_near),
            )
        ):

            @pl.when(t == SMALL_AT + place)
            def _():
                small_move(place, target, peer).start()

            @pl.when(t == SMALL_AT + 1 + place)
            def _():
                small_move(place, target, peer).wait()
                small[...] = small[...] + came[...]

        @pl.when(t == SMALL_AT + 3)
        def _():
            small_deep[deep] = small[...]
            for k in range(1, depth):
                small_to_deep(k).start()

        @pl.when(t == SMALL_AT + 5)
        def _():
            for k in range(1, depth):
                small_to_deep(k).wait()
            summed = small_deep[0]
            for k in range(1, depth):
                summed = summed + small_deep[k]
            small_out[...] = summed

    @pl.loop(0, CHUNKS)
    def _(t):
        by_parity(t, lambda t: even_third(t).wait(), lambda t: odd_third(t).wait())

    for copy in gradients_out():
        copy.wait()

    @pl.loop(1, reps)
    def _(k):
        to_near(k).wait_send()

    for k in range(1, groups):
        to_far(k).wait_send()


def run_backward(
    margin_bin,
    positive_index,
    cluster_index,
    norm_gain,
    final_gain,
    query_output,
    passage_output,
    query_cotangent,
    passage_cotangent,
    matrices,
    stored,
):
    query_rows, width = query_output.shape
    passage_rows = passage_output.shape[0]
    total = query_rows + passage_rows
    sequences = margin_bin.shape[0]
    everyone = cluster_index.shape[0]
    groups, reps = lax.axis_size("grp"), lax.axis_size("rep")
    depth = reps // 2
    rows = width // 2
    piece_rows = rows // 2 // depth
    bf16, f32 = jnp.bfloat16, jnp.float32
    dma = pltpu.SemaphoreType.DMA
    anywhere = pl.BlockSpec(memory_space=pl.ANY)
    vmem = pl.BlockSpec(memory_space=pltpu.VMEM)
    smem = pl.BlockSpec(memory_space=pltpu.SMEM)
    small_shape = (LAYERS, 16, width)
    pt_shape, ptq_shape = stored[4].shape[1:], stored[5].shape[1:]
    columns = width // 2
    return pl.pallas_call(
        backward_kernel,
        out_shape=(
            jax.ShapeDtypeStruct((CHUNKS, 2, 2, rows // 4, columns), bf16),
            jax.ShapeDtypeStruct(small_shape, f32),
            jax.ShapeDtypeStruct((8, 128), f32),
            jax.ShapeDtypeStruct((query_rows, width), f32),
            jax.ShapeDtypeStruct((passage_rows, width), f32),
        ),
        in_specs=[smem, smem, vmem, vmem, vmem] + [anywhere] * 23,
        out_specs=(anywhere, vmem, vmem, anywhere, anywhere),
        scratch_shapes=[
            pltpu.VMEM((2, 2, 2, rows, columns), bf16),
            pltpu.VMEM((KEEP_SLOTS, rows, columns), bf16),
            pltpu.VMEM((SENT_SLOTS, rows, columns), bf16),
            pltpu.VMEM((CORE_SLOTS, 2, rows, columns), bf16),
            pltpu.VMEM((SIDE_SLOTS, rows, columns), bf16),
            pltpu.VMEM((NEAR_SLOTS, rows // 2, columns), bf16),
            pltpu.VMEM((CHUNKS, depth - 1, piece_rows, columns), bf16),
            pltpu.VMEM((CHUNKS, piece_rows, columns), bf16),
            pltpu.VMEM(small_shape, f32),
            pltpu.VMEM(small_shape, f32),
            pltpu.VMEM(small_shape, f32),
            pltpu.VMEM(small_shape, f32),
            pltpu.VMEM((depth,) + small_shape, f32),
            pltpu.VMEM((2 * sequences * BLOCK, width), bf16),
            pltpu.VMEM((groups, reps, BLOCK, TILE), bf16),
            pltpu.VMEM((LAYERS, 8, width), f32),
            pltpu.VMEM((total, width), f32),
            pltpu.VMEM((total, width), bf16),
            pltpu.VMEM((total, 4 * width), bf16),
            pltpu.VMEM((4, total, width), bf16),
            pltpu.VMEM((2, total, width), bf16),
            pltpu.VMEM((total, width), bf16),
            pltpu.VMEM((2, total, width), bf16),
            pltpu.VMEM((total, 4 * width), bf16),
            pltpu.VMEM((total, width), bf16),
            pltpu.VMEM(pt_shape, bf16),
            pltpu.VMEM(ptq_shape, bf16),
            pltpu.VMEM((HEADS * query_rows, width), bf16),
            pltpu.VMEM((LAYERS, total, 128), f32),
            pltpu.VMEM((2, 4, width, width), bf16),
            dma((2, reps)),
            dma((2, groups)),
            dma((7,)),
            dma((12,)),
            dma((2, 4)),
            dma((2, CHUNKS)),
            dma((2, CHUNKS)),
            dma((2, CHUNKS)),
            dma((depth - 1, CHUNKS)),
            dma((depth - 1, CHUNKS)),
            dma((2, 3, CHUNKS)),
            dma((CHUNKS,)),
            dma((6,)),
            dma((depth - 1,)),
            dma((depth - 1,)),
            pltpu.SemaphoreType.REGULAR,
            pltpu.SemaphoreType.REGULAR,
            pltpu.SemaphoreType.REGULAR,
        ],
        compiler_params=pltpu.CompilerParams(
            collective_id=0, has_side_effects=True, vmem_limit_bytes=62 * 1024 * 1024
        ),
    )(
        margin_bin,
        positive_index,
        cluster_index.reshape(1, everyone),
        norm_gain,
        final_gain,
        query_output,
        passage_output,
        query_cotangent.reshape(query_rows, width),
        passage_cotangent.reshape(passage_rows, width),
        *matrices,
        *stored,
    )


def backward_plain(
    query_output,
    passage_output,
    cluster_index,
    margin_bin,
    positive_index,
    query_cotangent,
    passage_cotangent,
    stored,
    params,
):
    batch_size, query_len, model_width = query_output.shape
    passage_len = passage_output.shape[1]
    layout = ((batch_size, query_len), (batch_size, passage_len))
    query_span = batch_size * query_len
    stored_layers = [tuple(array[layer_index] for array in stored) for layer_index in range(LAYERS)]
    query_first = query_output[:, 0, :]
    passage_first = passage_output[:, 0, :]
    facts = jnp.concatenate(
        [margin_bin, positive_index // 128, positive_index % 128], axis=0
    ).astype(jnp.bfloat16)
    facts = jnp.pad(facts, (0, model_width - facts.shape[0]))
    block = jnp.concatenate([query_first, passage_first, facts[None, :]], axis=0)
    block = jnp.pad(block, ((0, 8 - block.shape[0]), (0, 0)))
    total = cluster_index.shape[0]
    every = gather_blocks(block).reshape(-1, 8, model_width)
    every_query = every[:, :batch_size].reshape(total, model_width)
    every_passage = every[:, batch_size : 2 * batch_size].reshape(total, model_width)
    facts = every[:, 2 * batch_size, : 3 * batch_size].astype(jnp.int32)
    facts = facts.reshape(-1, 3, batch_size)
    every_margin = facts[:, 0].reshape(total)
    every_positive = (facts[:, 1] * 128 + facts[:, 2]).reshape(total)
    start_row = lax.axis_index(("grp", "rep")) * batch_size
    score_scale = 2.0 / math.sqrt(model_width)
    logits = contract_last(every_query, every_passage) * score_scale
    columns = lax.broadcasted_iota(jnp.int32, logits.shape, 1)
    chosen_mask = columns == every_positive[:, None]
    allowed = (cluster_index[None, :] == cluster_index[:, None]) | chosen_mask
    masked = jnp.where(allowed, logits, -1e30)
    peak_score = jnp.max(masked, axis=1, keepdims=True)
    normalizer = peak_score + jnp.log(jnp.sum(jnp.exp(masked - peak_score), axis=1, keepdims=True))
    chosen = jnp.sum(jnp.where(chosen_mask, logits, 0.0), axis=1)
    margin_weight = (every_margin + 1).astype(jnp.float32) / NBINS
    every_loss = margin_weight * (normalizer[:, 0] - chosen)
    query_loss = lax.dynamic_slice_in_dim(every_loss, start_row, batch_size)
    delta_logits = narrow(
        margin_weight[:, None]
        * (jnp.where(allowed, jnp.exp(masked - normalizer), 0.0) - chosen_mask.astype(jnp.float32))
    )
    own_rows = lax.dynamic_slice_in_dim(delta_logits, start_row, batch_size, axis=0)
    own_columns = lax.dynamic_slice_in_dim(delta_logits, start_row, batch_size, axis=1)
    delta_query_first = product(own_rows, every_passage) * score_scale
    delta_passage_first = contract_rows(own_columns, every_query) * score_scale
    query_upstream = query_cotangent.astype(jnp.float32).at[:, 0, :].add(delta_query_first)
    passage_upstream = passage_cotangent.astype(jnp.float32).at[:, 0, :].add(delta_passage_first)
    upstream = jnp.concatenate(
        [
            query_upstream.reshape(query_span, model_width),
            passage_upstream.reshape(batch_size * passage_len, model_width),
        ],
        axis=0,
    )
    operands = []
    small = []
    for layer_index in reversed(range(LAYERS)):
        layer_params = tuple(array[layer_index] for array in params)
        upstream, layer_operands, vectors = layer_backward(
            upstream, stored_layers[layer_index], layout, layer_params
        )
        operands.append(layer_operands)
        small.append([vector.reshape(4, -1) for vector in vectors])
    small = small[::-1]
    matrices = reduce_plain(operands)
    flat = reduce_small(jnp.concatenate(small[0] + small[1], axis=1))
    reduced = [None] * 15
    for slot, matrix in zip(MATRICES, matrices):
        reduced[slot] = matrix
    flat = flat.reshape(LAYERS, -1)
    offset = 0
    for slot, vector in zip(SMALL, small[0]):
        size = vector.shape[1]
        reduced[slot] = flat[:, offset : offset + size]
        offset = offset + size
    return query_loss, upstream[:query_span], upstream[query_span:], reduced


def finish_kernel(
    out_ref,
    small_in,
    loss_in,
    query_in,
    passage_in,
    reduce_out,
    expand_out,
    *rest,
):
    square_outs = rest[:4]
    vector_outs = rest[4:12]
    expand_bias_out, query_out, passage_out, loss_out = rest[12:16]
    sums, tall, flat, squares, query, passage, small_ref, loss, in_sem, out_sem = rest[16:]
    rows, columns = sums.shape[1:]
    quarter = rows // 2
    width = 2 * columns
    each = sums.shape[0] // (3 * LAYERS)
    moves = [
        pltpu.make_async_copy(query_in, query, in_sem.at[3 * LAYERS]),
        pltpu.make_async_copy(passage_in, passage, in_sem.at[3 * LAYERS + 1]),
    ]
    little = [
        pltpu.make_async_copy(small_in, small_ref, in_sem.at[3 * LAYERS + 2]),
        pltpu.make_async_copy(loss_in, loss, in_sem.at[3 * LAYERS + 3]),
    ]
    loads = []
    for i in range(3 * LAYERS):
        span = pl.ds(i * each, each)
        loads.append(pltpu.make_async_copy(out_ref.at[span], sums.at[span], in_sem.at[i]))
    for copy in little + loads + moves:
        copy.start()
    for copy in little:
        copy.wait()
    for i in range(loss_out.shape[0]):
        loss_out[i] = jnp.sum(loss[0:1, i : i + 1])
    group = lax.axis_index("grp")
    vectors = small_ref[:, :8, 0:quarter]
    expand_bias = small_ref[:, S_EXPAND, :]
    for g in range(1, 4):
        vectors = jnp.where(
            group == g, small_ref[:, :8, g * quarter : (g + 1) * quarter], vectors
        )
        expand_bias = jnp.where(group == g, small_ref[:, S_EXPAND + g, :], expand_bias)
    for i in range(8):
        vector_outs[i][...] = vectors[:, i, :]
    expand_bias_out[...] = expand_bias
    stores = []

    def store(source, target):
        copy = pltpu.make_async_copy(source, target, out_sem.at[len(stores)])
        stores.append(copy)
        copy.start()

    for layer in range(LAYERS):
        loads[layer].wait()
        for part in range(4):
            at = pl.ds((part // 2) * rows, rows), pl.ds((part % 2) * columns, columns)
            tall[layer, at[0], at[1]] = wide(sums[layer * each + part])
        store(tall.at[layer], reduce_out.at[layer])
    for move, (source, target) in zip(moves, ((query, query_out), (passage, passage_out))):
        move.wait()
        store(source, target)
    for layer in range(LAYERS):
        loads[LAYERS + layer].wait()
        for part in range(4):
            value = wide(sums[(LAYERS + layer) * each + part])
            for unit in range(2):
                start = (2 * (part // 2) + unit) * width + (part % 2) * columns
                flat[layer, :, start : start + columns] = value[
                    unit * quarter : (unit + 1) * quarter
                ]
        store(flat.at[layer], expand_out.at[layer])
    for layer in range(LAYERS):
        loads[2 * LAYERS + layer].wait()
        for part in range(4):
            value = wide(sums[(2 * LAYERS + layer) * each + part])
            for unit in range(2):
                at = pl.ds((part % 2) * columns, columns)
                squares[2 * (part // 2) + unit, layer, :, at] = value[
                    unit * quarter : (unit + 1) * quarter
                ]
        for which in range(4):
            store(squares.at[which, layer], square_outs[which].at[layer])
    for copy in stores:
        copy.wait()


def finish(out, small, loss, query_gradient, passage_gradient, sequences):
    out = out.reshape(out.shape[0], -1, out.shape[-1])
    rows, columns = out.shape[1:]
    quarter, width = rows // 2, 2 * columns
    f32 = jnp.float32
    anywhere = pl.BlockSpec(memory_space=pl.ANY)
    vmem = pl.BlockSpec(memory_space=pltpu.VMEM)
    tall, flat = (LAYERS, width, width), (LAYERS, quarter, 4 * width)
    square, vector = (LAYERS, quarter, width), (LAYERS, quarter)
    results = pl.pallas_call(
        finish_kernel,
        out_shape=[
            jax.ShapeDtypeStruct(shape, f32)
            for shape in [tall, flat]
            + [square] * 4
            + [vector] * 8
            + [(LAYERS, width), query_gradient.shape, passage_gradient.shape, (sequences,)]
        ],
        in_specs=[anywhere] * 5,
        out_specs=[anywhere] * 6
        + [vmem] * 9
        + [anywhere] * 2
        + [pl.BlockSpec(memory_space=pltpu.SMEM)],
        scratch_shapes=[
            pltpu.VMEM(out.shape, jnp.bfloat16),
            pltpu.VMEM(tall, f32),
            pltpu.VMEM(flat, f32),
            pltpu.VMEM((4,) + square, f32),
            pltpu.VMEM(query_gradient.shape, f32),
            pltpu.VMEM(passage_gradient.shape, f32),
            pltpu.VMEM(small.shape, f32),
            pltpu.VMEM(loss.shape, f32),
            pltpu.SemaphoreType.DMA((3 * LAYERS + 4,)),
            pltpu.SemaphoreType.DMA((6 * LAYERS + 2,)),
        ],
        compiler_params=pltpu.CompilerParams(vmem_limit_bytes=60 * 1024 * 1024),
    )(out, small, loss, query_gradient, passage_gradient)
    reduced = [None] * 15
    reduced[11], reduced[9] = results[0], results[1]
    for place, slot in enumerate((0, 2, 3, 5)):
        reduced[slot] = results[2 + place]
    for place, slot in enumerate((1, 4, 6, 7, 8, 12, 13, 14)):
        reduced[slot] = results[6 + place]
    reduced[10] = results[14]
    return results[15], results[16], results[17], reduced


def per_device(
    query_input,
    passage_input,
    query_length,
    passage_length,
    cluster_index,
    margin_bin,
    positive_index,
    query_cotangent,
    passage_cotangent,
    query_weight,
    query_bias,
    key_weight,
    value_weight,
    value_bias,
    mix_weight,
    mix_bias,
    norm_gain,
    norm_shift,
    expand_weight,
    expand_bias,
    reduce_weight,
    reduce_bias,
    final_gain,
    final_shift,
):
    params = (
        query_weight,
        query_bias,
        key_weight,
        value_weight,
        value_bias,
        mix_weight,
        mix_bias,
        norm_gain,
        norm_shift,
        expand_weight,
        expand_bias,
        reduce_weight,
        reduce_bias,
        final_gain,
        final_shift,
    )
    batch_size, query_len, model_width = query_input.shape
    passage_len = passage_input.shape[1]
    matrices = (query_weight, key_weight, value_weight, mix_weight, expand_weight, reduce_weight)
    vectors = (
        query_bias,
        value_bias,
        mix_bias,
        norm_gain,
        norm_shift,
        reduce_bias,
        final_gain,
        final_shift,
        expand_bias,
    )
    results = run_forward(
        query_length,
        passage_length,
        query_input,
        passage_input,
        matrices,
        vectors,
    )
    query_output = results[0].reshape(batch_size, query_len, model_width)
    passage_output = results[1].reshape(batch_size, passage_len, model_width)
    if lax.axis_size("rep") != 8:
        query_loss, query_gradient, passage_gradient, reduced = backward_plain(
            query_output,
            passage_output,
            cluster_index,
            margin_bin,
            positive_index,
            query_cotangent,
            passage_cotangent,
            results[2:],
            params,
        )
    else:
        out, small, loss, query_gradient, passage_gradient = run_backward(
            margin_bin,
            positive_index,
            cluster_index,
            norm_gain,
            final_gain,
            results[0],
            results[1],
            query_cotangent,
            passage_cotangent,
            matrices,
            results[2:],
        )
        query_gradient, passage_gradient, query_loss, reduced = finish(
            out, small, loss, query_gradient, passage_gradient, batch_size
        )
    return (
        query_output,
        passage_output,
        query_loss,
        query_gradient.reshape(batch_size, query_len, model_width),
        passage_gradient.reshape(batch_size, passage_len, model_width),
        reduced[0],
        reduced[1],
        reduced[2],
        reduced[3],
        reduced[4],
        reduced[5],
        reduced[6],
        reduced[7],
        reduced[8],
        reduced[9],
        reduced[10],
        reduced[11],
        reduced[12],
        reduced[13],
        reduced[14],
    )


def solution(mesh):
    placed = (
        P(("grp", "rep"), None, None),
        P(("grp", "rep"), None, None),
        P(("grp", "rep")),
        P(("grp", "rep")),
        P(),
        P(("grp", "rep")),
        P(("grp", "rep")),
        P(("grp", "rep"), None, None),
        P(("grp", "rep"), None, None),
        P(),
        P(),
        P(),
        P(),
        P(),
        P(),
        P(),
        P(),
        P(),
        P(),
        P(),
        P(),
        P(),
        P(),
        P(),
    )
    return jax.shard_map(
        per_device,
        mesh=mesh,
        in_specs=placed,
        out_specs=(
            P(("grp", "rep"), None, None),
            P(("grp", "rep"), None, None),
            P(("grp", "rep")),
            P(("grp", "rep"), None, None),
            P(("grp", "rep"), None, None),
            P(None, "grp", None),
            P(None, "grp"),
            P(None, "grp", None),
            P(None, "grp", None),
            P(None, "grp"),
            P(None, "grp", None),
            P(None, "grp"),
            P(None, "grp"),
            P(None, "grp"),
            P(None, "grp", None),
            P(None, "grp"),
            P(None, "grp", None),
            P(None, "grp"),
            P(None, "grp"),
            P(None, "grp"),
        ),
        check_vma=False,
    )
```

```python
import functools
import math

import jax
import jax.numpy as jnp
from jax import lax
from jax.experimental import pallas as pl
from jax.experimental.pallas import tpu as pltpu
from jax.sharding import PartitionSpec as P

HEADS = 12
DH = 64
LAYERS = 2
NBINS = 10


def narrow(values):
    return values.astype(jnp.bfloat16)


def product(former, latter):
    return jnp.dot(former, latter, preferred_element_type=jnp.float32)


def contract_rows(former, latter):
    return lax.dot_general(
        former, latter, (((0,), (0,)), ((), ())), preferred_element_type=jnp.float32
    )


def contract_last(former, latter):
    return lax.dot_general(
        former, latter, (((1,), (1,)), ((), ())), preferred_element_type=jnp.float32
    )


def column_total(values):
    return jnp.sum(values.astype(jnp.float32), axis=0)


def norm_forward(summed, gain_vector, shift_vector):
    average = jnp.mean(summed, axis=-1, keepdims=True)
    centred = summed - average
    scaled = lax.rsqrt(jnp.mean(centred * centred, axis=-1, keepdims=True) + 1e-12)
    unit_rows = centred * scaled
    return (unit_rows * gain_vector + shift_vector, unit_rows, scaled)


def norm_backward(upstream, unit_rows, scaled, gain_vector):
    delta_unit = upstream * gain_vector
    delta_summed = scaled * (
        delta_unit
        - jnp.mean(delta_unit, axis=-1, keepdims=True)
        - unit_rows * jnp.mean(delta_unit * unit_rows, axis=-1, keepdims=True)
    )
    return (delta_summed, jnp.sum(upstream * unit_rows, axis=0), jnp.sum(upstream, axis=0))


def split_heads(flat, group_count, length):
    return flat.reshape(group_count, length, HEADS, DH)


def group_spans(layout):
    spans = []
    offset = 0
    for group_count, length in layout:
        spans.append((offset, group_count, length))
        offset = offset + group_count * length
    return spans


def attend_backward(query_part, key_part, value_part, shares, delta_context):
    attention = wide(shares)
    delta_value = jnp.einsum(
        "bhqk,bqhd->bkhd", narrow(attention), delta_context, preferred_element_type=jnp.float32
    )
    delta_attention = jnp.einsum(
        "bqhd,bkhd->bhqk", delta_context, value_part, preferred_element_type=jnp.float32
    )
    delta_scores = narrow(
        attention * (delta_attention - jnp.sum(attention * delta_attention, axis=-1, keepdims=True))
    )
    delta_query = (
        jnp.einsum("bhqk,bkhd->bqhd", delta_scores, key_part, preferred_element_type=jnp.float32)
        * 0.125
    )
    delta_key = (
        jnp.einsum("bhqk,bqhd->bkhd", delta_scores, query_part, preferred_element_type=jnp.float32)
        * 0.125
    )
    return (delta_query, delta_key, delta_value)


def layer_backward(upstream, stored, layout, params):
    (
        query_weight,
        query_bias,
        key_weight,
        value_weight,
        value_bias,
        mix_weight,
        mix_bias,
        norm_gain,
        norm_shift,
        expand_weight,
        expand_bias,
        reduce_weight,
        reduce_bias,
        final_gain,
        final_shift,
    ) = params
    (
        hidden,
        query_heads,
        key_heads,
        value_heads,
        shares,
        query_shares,
        context,
        unit_one,
        middle,
        slope,
        active,
        unit_two,
        scales,
    ) = stored
    scale_one, scale_two = scales[:, 0:1], scales[:, 1:2]
    unit_one, unit_two = wide(unit_one), wide(unit_two)
    (count, query_len), (_, passage_len) = layout
    pair_shares = jnp.pad(shares, ((0, 0), (0, passage_len - shares.shape[1]), (0, 0)))
    pair_shares = pair_shares.reshape(count, HEADS // 2, passage_len, 2, passage_len)
    pair_shares = pair_shares.transpose(0, 1, 3, 4, 2).reshape(
        count, HEADS, passage_len, passage_len
    )
    head_shares = query_shares.reshape(count, query_len, HEADS, count, query_len)
    head_shares = jnp.stack([head_shares[i, :, :, i] for i in range(count)])
    all_shares = (head_shares.transpose(0, 2, 3, 1), pair_shares)
    delta_two, delta_final_gain, delta_final_shift = norm_backward(
        upstream, unit_two, scale_two, final_gain
    )
    delta_branch = narrow(delta_two)
    delta_reduce_bias = column_total(delta_branch)
    delta_expanded = narrow(contract_last(delta_branch, reduce_weight) * wide(slope))
    delta_expand_bias = column_total(delta_expanded)
    delta_middle = delta_two + contract_last(delta_expanded, expand_weight)
    delta_one, delta_norm_gain, delta_norm_shift = norm_backward(
        delta_middle, unit_one, scale_one, norm_gain
    )
    delta_mix = narrow(delta_one)
    delta_mix_bias = column_total(delta_mix)
    delta_context = narrow(contract_last(delta_mix, mix_weight))
    collected = ([], [], [])
    for part_shares, (offset, group_count, length) in zip(all_shares, group_spans(layout)):
        row_span = group_count * length
        pieces = [
            split_heads(array[offset : offset + row_span], group_count, length)
            for array in (query_heads, key_heads, value_heads, delta_context)
        ]
        results = attend_backward(pieces[0], pieces[1], pieces[2], part_shares, pieces[3])
        for bucket, gradient in zip(collected, results):
            bucket.append(narrow(gradient.reshape(row_span, -1)))
    delta_query = jnp.concatenate(collected[0], axis=0)
    delta_key = jnp.concatenate(collected[1], axis=0)
    delta_value = jnp.concatenate(collected[2], axis=0)
    delta_hidden = (
        delta_one
        + contract_last(delta_query, query_weight)
        + contract_last(delta_key, key_weight)
        + contract_last(delta_value, value_weight)
    )
    operands = (
        active,
        delta_branch,
        middle,
        delta_expanded,
        hidden,
        context,
        delta_query,
        delta_key,
        delta_value,
        delta_mix,
    )
    vectors = (
        column_total(delta_query),
        column_total(delta_value),
        delta_mix_bias,
        delta_norm_gain,
        delta_norm_shift,
        delta_expand_bias,
        delta_reduce_bias,
        delta_final_gain,
        delta_final_shift,
    )
    return (delta_hidden, operands, vectors)


CORE_FLIP = [(0, 1), (1, 0), (2, 3), (3, 2)]
SIDE_FLIP = [(0, 2), (2, 0), (1, 3), (3, 1)]


def wide(values):
    return values.astype(jnp.float32)


def pick(array, index):
    return lax.dynamic_index_in_dim(array, index, 0, keepdims=False)


def reduce_chunk(chunk):
    rep_total = lax.axis_size("rep")
    group = lax.axis_index("grp")
    side, core = group // 2, group % 2
    parts = chunk.reshape((2, 2) + chunk.shape[1:])
    got = lax.ppermute(
        lax.dynamic_index_in_dim(parts, 1 - core, 1, keepdims=False), "grp", CORE_FLIP
    )
    mine = lax.dynamic_index_in_dim(parts, core, 1, keepdims=False)
    got = lax.ppermute(
        narrow(wide(pick(mine, 1 - side)) + wide(pick(got, 1 - side))), "grp", SIDE_FLIP
    ), narrow(wide(pick(mine, side)) + wide(pick(got, side)))
    summed = narrow(wide(got[0]) + wide(got[1]))
    rows, columns = summed.shape
    if rep_total != 8:
        part = lax.psum_scatter(summed, "rep", scatter_dimension=0, tiled=True)
        return wide(lax.all_gather(part, "rep", axis=0, tiled=True))
    rep = lax.axis_index("rep")
    deep, near = rep // 2, rep % 2
    flip = [(i, i ^ 1) for i in range(8)]
    shifts = [[(i, (i + 2 * k) % 8) for i in range(8)] for k in range(4)]
    halves = summed.reshape(2, rows // 2, columns)
    got = lax.ppermute(pick(halves, 1 - near), "rep", flip)
    half = narrow(wide(pick(halves, near)) + wide(got)).reshape(4, rows // 8, columns)
    total = wide(pick(half, deep))
    for k in range(1, 4):
        total = total + wide(lax.ppermute(pick(half, (deep + k) % 4), "rep", shifts[k]))
    piece = narrow(total)
    pieces = [piece] + [lax.ppermute(piece, "rep", shifts[k]) for k in range(1, 4)]
    joined = jnp.zeros((4,) + piece.shape, jnp.bfloat16)
    for k in range(4):
        joined = lax.dynamic_update_index_in_dim(joined, pieces[k], (deep - k) % 4, 0)
    other = lax.ppermute(joined, "rep", flip)
    own = joined.reshape(rows // 2, columns)
    other = other.reshape(rows // 2, columns)
    first = jnp.where(near == 0, own, other)
    second = jnp.where(near == 0, other, own)
    return wide(jnp.concatenate([first, second], axis=0))


def reduce_small(small):
    group = lax.axis_index("grp")
    side, core = group // 2, group % 2
    parts = small.reshape(2, 2, -1)
    got = lax.ppermute(
        lax.dynamic_index_in_dim(parts, 1 - core, 1, keepdims=False), "grp", CORE_FLIP
    )
    pair = lax.dynamic_index_in_dim(parts, core, 1, keepdims=False) + got
    total = pick(pair, side) + lax.ppermute(pick(pair, 1 - side), "grp", SIDE_FLIP)
    rep_total = lax.axis_size("rep")
    step = 1
    while step < rep_total:
        total = total + lax.ppermute(total, "rep", [(i, i ^ step) for i in range(rep_total)])
        step = step * 2
    return total


def remote(source, target, send_sem, recv_sem, grp, rep):
    return pltpu.make_async_remote_copy(
        src_ref=source,
        dst_ref=target,
        send_sem=send_sem,
        recv_sem=recv_sem,
        device_id=(grp, rep),
        device_id_type=pl.DeviceIdType.MESH,
    )


def gather_kernel(block_ref, out_ref, send_near, recv_near, send_far, recv_far):
    groups, reps = out_ref.shape[:2]
    grp, rep = lax.axis_index("grp"), lax.axis_index("rep")
    barrier = pltpu.get_barrier_semaphore()

    @pl.loop(1, reps)
    def _(k):
        pl.semaphore_signal(
            barrier, inc=1, device_id=(grp, (rep + k) % reps), device_id_type=pl.DeviceIdType.MESH
        )

    for k in range(1, groups):
        pl.semaphore_signal(
            barrier, inc=1, device_id=((grp + k) % groups, rep), device_id_type=pl.DeviceIdType.MESH
        )
    out_ref[grp, rep] = block_ref[...]
    pl.semaphore_wait(barrier, reps + groups - 2)

    def near(k):
        mine = out_ref.at[grp, rep]
        return remote(mine, mine, send_near.at[k], recv_near.at[k], grp, (rep + k) % reps)

    def far(k):
        row = out_ref.at[grp]
        return remote(row, row, send_far.at[k], recv_far.at[k], (grp + k) % groups, rep)

    @pl.loop(1, reps)
    def _(k):
        near(k).start()

    @pl.loop(1, reps)
    def _(k):
        near(k).wait_recv()

    for k in range(1, groups):
        far(k).start()
    for k in range(1, groups):
        far(k).wait_recv()

    @pl.loop(1, reps)
    def _(k):
        near(k).wait_send()

    for k in range(1, groups):
        far(k).wait_send()


def gather_blocks(block):
    groups, reps = lax.axis_size("grp"), lax.axis_size("rep")
    return pl.pallas_call(
        gather_kernel,
        out_shape=jax.ShapeDtypeStruct((groups, reps) + block.shape, block.dtype),
        in_specs=[pl.BlockSpec(memory_space=pltpu.VMEM)],
        out_specs=pl.BlockSpec(memory_space=pltpu.VMEM),
        scratch_shapes=[
            pltpu.SemaphoreType.DMA((reps,)),
            pltpu.SemaphoreType.DMA((reps,)),
            pltpu.SemaphoreType.DMA((groups,)),
            pltpu.SemaphoreType.DMA((groups,)),
        ],
        compiler_params=pltpu.CompilerParams(collective_id=1, has_side_effects=True),
    )(block)


def reduce_plain(layers):
    results = []
    for active, branch, middle, expanded, hidden, context, query, key, value, mix in layers:
        quarter = lambda former, latter: (
            lambda matrix: narrow(matrix).reshape(4, matrix.shape[0] // 4, matrix.shape[1])
        )(contract_rows(former, latter))
        square = jnp.concatenate(
            [
                quarter(hidden, query),
                quarter(hidden, key),
                quarter(hidden, value),
                quarter(context, mix),
            ],
            axis=1,
        )
        square = reduce_chunk(square)
        height = square.shape[0] // 4
        results.append(
            [square[place * height : (place + 1) * height] for place in range(4)]
            + [reduce_chunk(quarter(middle, expanded)), reduce_chunk(quarter(active, branch))]
        )
    return [jnp.stack([results[1][i], results[0][i]]) for i in range(6)]


SMALL = (1, 4, 6, 7, 8, 10, 12, 13, 14)
MATRICES = (0, 2, 3, 5, 9, 11)


LOG2E = 1.4426950408889634
V_QUERY, V_VALUE, V_MIX, V_GAIN, V_SHIFT, V_REDUCE, V_LAST_GAIN, V_LAST_SHIFT, V_EXPAND = range(9)
VECTOR_ROWS = 16
TILE = 256


def lane_masks(rows):
    lane = lax.broadcasted_iota(jnp.int32, (rows, 2 * DH), 1)
    return ((lane < DH).astype(jnp.float32).astype(jnp.bfloat16),
            (lane >= DH).astype(jnp.float32).astype(jnp.bfloat16))


def head_mask(head, width):
    lane = lax.broadcasted_iota(jnp.int32, (1, width), 1)
    return ((lane >= head * DH) & (lane < (head + 1) * DH))


def live_keys(passage_len):
    return -(-(passage_len * 25 // 32) // 16) * 16


def lanes(start, size=TILE):
    return pl.ds(pl.multiple_of(start, 128), size)


def sublanes(start, size):
    return pl.ds(pl.multiple_of(start, 16), size)


def softmax_rows(scores, bias):
    scaled = scores * (0.125 * LOG2E) + bias
    grown = jnp.exp2(scaled - jnp.max(scaled, axis=0, keepdims=True))
    return narrow(grown * (1.0 / jnp.sum(grown, axis=0, keepdims=True)))


def forward_kernel(
    query_lengths,
    passage_lengths,
    query_in,
    passage_in,
    wq_in,
    wk_in,
    wv_in,
    wm_in,
    we_in,
    wr_in,
    query_bias,
    value_bias,
    mix_bias,
    norm_gain,
    norm_shift,
    reduce_bias,
    final_gain,
    final_shift,
    expand_bias,
    query_out,
    passage_out,
    hidden_out,
    q_out,
    k_out,
    v_out,
    pt_out,
    ptq_out,
    c_out,
    u1_out,
    m_out,
    slope_out,
    f_out,
    u2_out,
    r_out,
    wq,
    wk,
    wv,
    wm,
    we,
    wr,
    x,
    q,
    k,
    v,
    pt,
    ptq,
    c,
    u1,
    m,
    slope,
    f,
    u2,
    r,
    z,
    stack,
    vec_ref,
    weight_sem,
    in_sem,
    out_sem,
):
    width = x.shape[1]
    total = x.shape[0]
    sequences = query_lengths.shape[0]
    query_rows = query_in.shape[0]
    query_len = query_rows // sequences
    passage_len = (total - query_rows) // sequences
    pairs = width // (2 * DH)
    kept = live_keys(passage_len)

    weights = ((wq_in, wq), (wk_in, wk), (wv_in, wv), (wm_in, wm), (we_in, we), (wr_in, wr))

    def weight_copy(which, layer):
        source, target = weights[which]
        return pltpu.make_async_copy(
            source.at[layer], target.at[layer], weight_sem.at[which, layer]
        )

    stored = (
        (x, hidden_out),
        (q, q_out),
        (k, k_out),
        (v, v_out),
        (pt, pt_out),
        (ptq, ptq_out),
        (c, c_out),
        (u1, u1_out),
        (m, m_out),
        (slope, slope_out),
        (f, f_out),
        (u2, u2_out),
        (r, r_out),
    )
    X, Q, K, V, PT, PTQ, C, U1, M, SLOPE, F, U2, R = range(13)

    def store(which, layer):
        source, target = stored[which]
        return pltpu.make_async_copy(source, target.at[layer], out_sem.at[which])

    def reuse(which, layer):
        @pl.when(layer > 0)
        def _():
            store(which, layer - 1).wait()

    first = pltpu.make_async_copy(query_in, x.at[pl.ds(0, query_rows)], in_sem.at[0])
    rest = pltpu.make_async_copy(
        passage_in, x.at[pl.ds(query_rows, total - query_rows)], in_sem.at[1]
    )
    first.start()
    rest.start()
    for which in range(3):
        weight_copy(which, 0).start()
    vectors = (
        query_bias,
        value_bias,
        mix_bias,
        norm_gain,
        norm_shift,
        reduce_bias,
        final_gain,
        final_shift,
    )
    for layer in range(LAYERS):
        for place, vector in enumerate(vectors):
            vec_ref[layer, place : place + 1, :] = wide(vector[layer : layer + 1, :])
        for j in range(4):
            vec_ref[layer, V_EXPAND + j : V_EXPAND + j + 1, :] = wide(
                expand_bias[layer : layer + 1, j * width : (j + 1) * width]
            )
    first.wait()
    rest.wait()

    def project(source, weight, layer, bias_row, target):
        @pl.loop(0, width // TILE, unroll=3)
        def _(i):
            value = product(source[...], weight[layer, :, lanes(i * TILE)])
            if bias_row is not None:
                value = value + vec_ref[layer, pl.ds(bias_row, 1), lanes(i * TILE)]
            target[:, lanes(i * TILE)] = narrow(value)

    def norm(layer, gain_row, shift_row, unit, target, scale_lane):
        step = 96
        gain = vec_ref[layer, pl.ds(gain_row, 1), :]
        shift = vec_ref[layer, pl.ds(shift_row, 1), :]

        @pl.loop(0, total // step, unroll=2)
        def _(i):
            at = sublanes(i * step, step)
            full, unit_rows, scaled = norm_forward(z[at, :], gain, shift)
            unit[at, :] = narrow(unit_rows)
            target[at, :] = narrow(full)
            r[at, scale_lane : scale_lane + 1] = scaled

    @pl.loop(0, LAYERS)
    def _(layer):
        store(X, layer).start()
        weight_copy(0, layer).wait()

        @pl.when(layer == 0)
        def _():
            for which in range(3, 6):
                weight_copy(which, 0).start()

        reuse(Q, layer)
        project(x, wq, layer, V_QUERY, q)
        store(Q, layer).start()
        weight_copy(1, layer).wait()
        reuse(K, layer)
        project(x, wk, layer, None, k)
        store(K, layer).start()
        weight_copy(2, layer).wait()
        reuse(V, layer)
        project(x, wv, layer, V_VALUE, v)
        store(V, layer).start()

        reuse(PT, layer)
        reuse(PTQ, layer)
        reuse(C, layer)

        for head in range(HEADS):
            mask = head_mask(head, width).astype(jnp.float32).astype(jnp.bfloat16)
            stack[head * query_rows : (head + 1) * query_rows, :] = q[:query_rows, :] * mask
        scores = contract_last(k[:query_rows, :], stack[...])
        key_slot = lax.broadcasted_iota(jnp.int32, scores.shape, 0)
        query_slot = lax.broadcasted_iota(jnp.int32, scores.shape, 1) % query_rows
        live = jnp.zeros(scores.shape, jnp.bool_)
        for s in range(sequences):
            low = s * query_len
            live = live | (
                (key_slot >= low)
                & (key_slot < low + query_lengths[s])
                & (query_slot >= low)
                & (query_slot < low + query_len)
            )
        shares = softmax_rows(scores, jnp.where(live, 0.0, -1e30))
        ptq[...] = shares
        spread = contract_rows(shares, v[:query_rows, :])
        context = jnp.zeros((query_rows, width), jnp.float32)
        for head in range(HEADS):
            context = context + jnp.where(
                head_mask(head, width), spread[head * query_rows : (head + 1) * query_rows, :], 0.0
            )
        c[:query_rows, :] = narrow(context)

        @pl.loop(0, sequences * pairs, unroll=3)
        def _(i):
            s, pair = i // pairs, i % pairs
            rows = sublanes(query_rows + s * passage_len, passage_len)
            at = lanes(pair * 2 * DH, 2 * DH)
            key_rows = sublanes(query_rows + s * passage_len, kept)
            even, odd = lane_masks(passage_len)
            q2, k2, v2 = q[rows, at], k[key_rows, at], v[key_rows, at]
            scores = contract_last(k2, jnp.concatenate([q2 * even, q2 * odd], axis=0))
            even, odd = even[:kept], odd[:kept]
            slot = lax.broadcasted_iota(jnp.int32, (kept, 1), 0)
            shares = softmax_rows(
                scores, jnp.where(slot < passage_lengths[s], 0.0, -1e30)
            )
            pt[i] = shares
            shares = jnp.concatenate([shares[:, :passage_len], shares[:, passage_len:]], axis=0)
            spread = contract_rows(jnp.concatenate([v2 * even, v2 * odd], axis=0), shares)
            c[rows, at] = narrow(spread.T)

        store(PT, layer).start()
        store(PTQ, layer).start()
        store(C, layer).start()

        weight_copy(3, layer).wait()

        @pl.when(layer + 1 < LAYERS)
        def _():
            for which in range(6):
                weight_copy(which, layer + 1).start()

        @pl.loop(0, width // TILE)
        def _(i):
            at = lanes(i * TILE)
            z[:, at] = (
                wide(x[:, at])
                + product(c[...], wm[layer, :, at])
                + vec_ref[layer, pl.ds(V_MIX, 1), at]
            )

        reuse(U1, layer)
        reuse(M, layer)
        reuse(R, layer)
        norm(layer, V_GAIN, V_SHIFT, u1, m, 0)
        store(U1, layer).start()
        store(M, layer).start()

        weight_copy(4, layer).wait()
        reuse(SLOPE, layer)
        reuse(F, layer)

        @pl.loop(0, 4 * width // TILE, unroll=2)
        def _(i):
            at = lanes(i * TILE)
            tiles = width // TILE
            bias = vec_ref[layer, pl.ds(V_EXPAND + i // tiles, 1), lanes((i % tiles) * TILE)]
            value = product(m[...], we[layer, :, at]) + bias
            share = 0.5 * (1.0 + lax.erf(value * (1.0 / math.sqrt(2.0))))
            density = jnp.exp2(value * value * (-0.5 * LOG2E)) * (1.0 / math.sqrt(2.0 * math.pi))
            f[:, at] = narrow(value * share)
            slope[:, at] = narrow(share + value * density)

        store(SLOPE, layer).start()
        store(F, layer).start()

        weight_copy(5, layer).wait()

        @pl.loop(0, width // TILE)
        def _(i):
            at = lanes(i * TILE)
            z[:, at] = (
                wide(m[:, at])
                + product(f[...], wr[layer, :, at])
                + vec_ref[layer, pl.ds(V_REDUCE, 1), at]
            )

        store(X, layer).wait()
        reuse(U2, layer)
        norm(layer, V_LAST_GAIN, V_LAST_SHIFT, u2, x, 1)
        store(U2, layer).start()
        store(R, layer).start()

    last = LAYERS - 1
    first = pltpu.make_async_copy(x.at[pl.ds(0, query_rows)], query_out, in_sem.at[0])
    rest = pltpu.make_async_copy(
        x.at[pl.ds(query_rows, total - query_rows)], passage_out, in_sem.at[1]
    )
    first.start()
    rest.start()
    for which in range(1, 13):
        store(which, last).wait()
    first.wait()
    rest.wait()


def run_forward(query_length, passage_length, query_input, passage_input, matrices, vectors):
    sequences, query_len, width = query_input.shape
    passage_len = passage_input.shape[1]
    query_rows, passage_rows = sequences * query_len, sequences * passage_len
    total = query_rows + passage_rows
    pairs = width // (2 * DH)
    bf16, f32 = jnp.bfloat16, jnp.float32
    arrays = (
        ((total, width), bf16),
        ((total, width), bf16),
        ((total, width), bf16),
        ((total, width), bf16),
        ((sequences * pairs, live_keys(passage_len), 2 * passage_len), bf16),
        ((query_rows, HEADS * query_rows), bf16),
        ((total, width), bf16),
        ((total, width), bf16),
        ((total, width), bf16),
        ((total, 4 * width), bf16),
        ((total, 4 * width), bf16),
        ((total, width), bf16),
        ((total, 128), f32),
    )
    anywhere = pl.BlockSpec(memory_space=pl.ANY)
    return pl.pallas_call(
        forward_kernel,
        out_shape=(
            jax.ShapeDtypeStruct((query_rows, width), bf16),
            jax.ShapeDtypeStruct((passage_rows, width), bf16),
        )
        + tuple(jax.ShapeDtypeStruct((LAYERS,) + shape, dtype) for shape, dtype in arrays),
        in_specs=[pl.BlockSpec(memory_space=pltpu.SMEM)] * 2
        + [anywhere] * 8
        + [pl.BlockSpec(memory_space=pltpu.VMEM)] * 9,
        out_specs=[anywhere] * 15,
        scratch_shapes=[pltpu.VMEM(matrix.shape, bf16) for matrix in matrices]
        + [pltpu.VMEM(shape, dtype) for shape, dtype in arrays]
        + [
            pltpu.VMEM((total, width), f32),
            pltpu.VMEM((HEADS * query_rows, width), bf16),
            pltpu.VMEM((LAYERS, VECTOR_ROWS, width), f32),
            pltpu.SemaphoreType.DMA((6, LAYERS)),
            pltpu.SemaphoreType.DMA((2,)),
            pltpu.SemaphoreType.DMA((13,)),
        ],
        compiler_params=pltpu.CompilerParams(vmem_limit_bytes=60 * 1024 * 1024),
    )(
        query_length,
        passage_length,
        query_input.reshape(query_rows, width),
        passage_input.reshape(passage_rows, width),
        *matrices,
        *vectors,
    )


CHUNKS = 24
PARTS = 12
S_QUERY, S_VALUE, S_MIX, S_GAIN, S_SHIFT, S_REDUCE, S_LAST_GAIN, S_LAST_SHIFT, S_EXPAND = range(9)
CORE_SLOTS, SIDE_SLOTS, NEAR_SLOTS, KEEP_SLOTS, SENT_SLOTS = 4, 4, 4, 6, 3
TURNS = 8
LAGS = (2, 3, 4, 5, 6, 9)
BLOCK = 16
SMALL_AT = 21


def one_hot(shape, hit):
    row = lax.broadcasted_iota(jnp.int32, shape, 0)
    column = lax.broadcasted_iota(jnp.int32, shape, 1)
    return narrow(jnp.where(hit(row, column), 1.0, 0.0))


def backward_kernel(
    margin_ref,
    positive_ref,
    cluster_row,
    norm_gain,
    final_gain,
    query_out,
    passage_out,
    query_cot,
    passage_cot,
    wq_in,
    wk_in,
    wv_in,
    wm_in,
    we_in,
    wr_in,
    hidden_in,
    q_in,
    k_in,
    v_in,
    pt_in,
    ptq_in,
    c_in,
    u1_in,
    m_in,
    slope_in,
    f_in,
    u2_in,
    r_in,
    out_ref,
    small_out,
    loss_out,
    query_grad,
    passage_grad,
    buf,
    keep,
    side_out,
    core_in,
    side_in,
    near_in,
    deep_in,
    piece,
    small,
    small_core,
    small_side,
    small_near,
    small_deep,
    first,
    blocks,
    gains,
    dz,
    dy,
    du,
    quad,
    pair_in,
    middle,
    unit,
    active,
    dc,
    pt,
    ptq,
    stack,
    r,
    w,
    gather_near,
    gather_far,
    first_sem,
    load_sem,
    weight_sem,
    core_sem,
    side_sem,
    near_sem,
    deep_send,
    deep_recv,
    back_sem,
    local_sem,
    small_sem,
    small_send,
    small_recv,
    core_free,
    side_free,
    near_free,
):
    groups, reps = blocks.shape[:2]
    depth = reps // 2
    rows, columns = keep.shape[1:]
    width = dz.shape[1]
    quarter = width // 4
    half_rows = rows // 2
    piece_rows = half_rows // depth
    total = dz.shape[0]
    sequences = margin_ref.shape[0]
    query_rows = query_out.shape[0]
    query_len = query_rows // sequences
    passage_len = (total - query_rows) // sequences
    pairs = width // (2 * DH)
    live = live_keys(passage_len)
    passage_rows = pl.ds(query_rows, total - query_rows)
    everyone = cluster_row.shape[1]

    grp, rep = lax.axis_index("grp"), lax.axis_index("rep")
    side, core = grp // 2, grp % 2
    deep, near = rep // 2, rep % 2
    sibling = (2 * side + (1 - core), rep)
    across = (2 * (1 - side) + core, rep)
    beside = (grp, 2 * deep + (1 - near))

    def behind(k):
        return (grp, 2 * ((deep + k) % depth) + near)

    deep_low, deep_high = deep % 2, deep // 2
    beyond = (grp, 2 * (deep + 2 - 4 * deep_high) + near)
    next_to = (grp, 2 * (deep + 1 - 2 * deep_low) + near)

    def signal(semaphore, peer):
        pl.semaphore_signal(
            semaphore, inc=1, device_id=peer, device_id_type=pl.DeviceIdType.MESH
        )

    barrier = pltpu.get_barrier_semaphore()
    for k in range(1, reps):
        signal(barrier, (grp, (rep + k) % reps))
    for k in range(1, groups):
        signal(barrier, ((grp + k) % groups, rep))

    firsts = [
        pltpu.make_async_copy(
            source.at[pl.ds(s * length, BLOCK)],
            first.at[pl.ds((place * sequences + s) * BLOCK, BLOCK)],
            first_sem.at[place * sequences + s],
        )
        for place, (source, length) in enumerate(
            ((query_out, query_len), (passage_out, passage_len))
        )
        for s in range(sequences)
    ]
    for copy in firsts:
        copy.start()

    loaded = {
        "f": (f_in, active),
        "u2": (u2_in, unit.at[0]),
        "slope": (slope_in, du),
        "m": (m_in, middle),
        "u1": (u1_in, unit.at[1]),
        "c": (c_in, pair_in.at[1]),
        "q": (q_in, quad.at[0]),
        "k": (k_in, quad.at[1]),
        "v": (v_in, quad.at[2]),
        "pt": (pt_in, pt),
        "ptq": (ptq_in, ptq),
        "x": (hidden_in, pair_in.at[0]),
    }
    places = {name: place for place, name in enumerate(loaded)}

    def load(name, layer):
        source, target = loaded[name]
        return pltpu.make_async_copy(source.at[layer], target, load_sem.at[places[name]])

    def weight_loads(kind, layer, slot):
        squares = []
        for j in range(4):
            block = pl.ds(j * width, width)
            if kind == 0:
                source = wr_in.at[layer, block]
            elif kind == 1:
                source = we_in.at[layer, :, block]
            else:
                source = (wq_in, wk_in, wv_in, wm_in)[j].at[layer]
            squares.append(
                pltpu.make_async_copy(source, w.at[slot, j], weight_sem.at[slot, j])
            )
        return squares

    def start_weights(kind, layer, slot):
        for copy in weight_loads(kind, layer, slot):
            copy.start()

    def wait_weights(kind, layer, slot):
        for copy in weight_loads(kind, layer, slot):
            copy.wait()

    last = LAYERS - 1
    cots = [
        pltpu.make_async_copy(query_cot, dy.at[pl.ds(0, query_rows)], first_sem.at[4]),
        pltpu.make_async_copy(passage_cot, dy.at[passage_rows], first_sem.at[5]),
        pltpu.make_async_copy(r_in, r, first_sem.at[6]),
    ]
    for copy in cots:
        copy.start()
    load("u2", last).start()

    def tally(layer, row_at, lanes_at, values):
        at = (layer, pl.ds(row_at, 1), lanes_at)
        small[at] = small[at] + jnp.sum(values, axis=0, keepdims=True)

    every_lane = pl.ds(0, width)

    norm_step = 48

    def norm_back_rows(
        layer, unit_at, scale_lane, gain_row, target, gain_to, shift_to, bias_to, tile
    ):
        gain = gains[layer, pl.ds(gain_row, 1), :]
        at = sublanes(tile * norm_step, norm_step)
        upstream = dz[at, :]
        unit_rows = wide(unit[unit_at, at, :])
        scaled = r[layer, at, scale_lane : scale_lane + 1]
        delta_unit = upstream * gain
        delta = scaled * (
            delta_unit
            - jnp.mean(delta_unit, axis=-1, keepdims=True)
            - unit_rows * jnp.mean(delta_unit * unit_rows, axis=-1, keepdims=True)
        )
        dz[at, :] = delta
        rounded = narrow(delta)
        target[at, :] = rounded
        tally(layer, gain_to, every_lane, upstream * unit_rows)
        tally(layer, shift_to, every_lane, upstream)
        tally(layer, bias_to, every_lane, wide(rounded))

    def last_norm_back(layer, tile):
        norm_back_rows(
            layer, 0, 1, 1, dy, S_LAST_GAIN, S_LAST_SHIFT, S_REDUCE, tile
        )

    def first_norm_back(layer, tile):
        norm_back_rows(layer, 1, 0, 0, quad.at[3], S_GAIN, S_SHIFT, S_MIX, tile)

    for copy in firsts:
        copy.wait()
    firsts_count = 2 * sequences
    segments = width // TILE
    packed = jnp.zeros((BLOCK, TILE), jnp.float32)
    for j in range(segments):
        low = j * firsts_count
        packed = packed + product(
            one_hot(
                (BLOCK, first.shape[0]),
                lambda i, k: (k == (i - low) * BLOCK) & (i >= low) & (i < low + firsts_count),
            ),
            first[:, j * TILE : (j + 1) * TILE],
        )
    row = lax.broadcasted_iota(jnp.int32, packed.shape, 0)
    lane = lax.broadcasted_iota(jnp.int32, packed.shape, 1)
    for s in range(sequences):
        positive = positive_ref[s]
        facts = (margin_ref[s], positive // 128, positive % 128)
        for place, fact in enumerate(facts):
            at = (row == segments * firsts_count) & (lane == place * sequences + s)
            packed = jnp.where(at, fact.astype(jnp.float32), packed)
    blocks[grp, rep] = narrow(packed)

    def to_near(k):
        mine = blocks.at[grp, rep]
        return remote(
            mine, mine, gather_near.at[0, k], gather_near.at[1, k], grp, (rep + k) % reps
        )

    def to_far(k):
        line = blocks.at[grp]
        return remote(
            line, line, gather_far.at[0, k], gather_far.at[1, k], (grp + k) % groups, rep
        )

    pl.semaphore_wait(barrier, reps + groups - 2)

    @pl.loop(1, reps)
    def _(k):
        to_near(k).start()

    load("f", last).start()
    load("slope", last).start()
    start_weights(0, last, 0)

    for copy in cots:
        copy.wait()
    small[...] = jnp.zeros_like(small)
    for layer in range(LAYERS):
        gains[layer, 0:1, :] = wide(norm_gain[layer : layer + 1, :])
        gains[layer, 1:2, :] = wide(final_gain[layer : layer + 1, :])

    @pl.loop(0, total // 96)
    def _(i):
        at = sublanes(i * 96, 96)
        dz[at, :] = wide(dy[at, :])

    first_at = [s * query_len for s in range(sequences)]
    first_at += [query_rows + s * passage_len for s in range(sequences)]
    late = sorted({at // norm_step for at in first_at})
    spans = [span for span in zip([-1] + late, late + [total // norm_step])]
    load("u2", last).wait()

    def early_norm(low, high):
        @pl.loop(low, high)
        def _(tile):
            last_norm_back(last, tile)

    for low, high in spans[: len(spans) // 2]:
        if low + 1 < high:
            early_norm(low + 1, high)

    @pl.loop(1, reps)
    def _(k):
        to_near(k).wait_recv()

    for k in range(1, groups):
        to_far(k).start()

    for low, high in spans[len(spans) // 2 :]:
        if low + 1 < high:
            early_norm(low + 1, high)

    for k in range(1, groups):
        to_far(k).wait_recv()

    gathered = blocks[...].reshape(groups * reps * BLOCK, TILE)

    def taken(offset):
        return product(
            one_hot(
                (everyone, gathered.shape[0]),
                lambda i, j: j == BLOCK * (i // sequences) + offset(i),
            ),
            gathered,
        )

    def taken_rows(base):
        return narrow(
            jnp.concatenate(
                [
                    taken(lambda i: j * firsts_count + base + i % sequences)
                    for j in range(segments)
                ],
                axis=1,
            )
        )

    every_query = taken_rows(0)
    every_passage = taken_rows(sequences)
    facts = taken(lambda i: segments * firsts_count)[:, :128]
    query_at = lax.broadcasted_iota(jnp.int32, facts.shape, 0) % sequences
    lane_at = lax.broadcasted_iota(jnp.int32, facts.shape, 1)

    def fact(place):
        hit = lane_at == place * sequences + query_at
        return jnp.sum(jnp.where(hit, facts, 0.0), axis=1, keepdims=True)

    margin_weight = (fact(0) + 1.0) / NBINS
    every_positive = fact(1) * 128.0 + fact(2)
    score_scale = 2.0 / math.sqrt(width)
    logits = contract_last(every_query, every_passage) * score_scale
    passage_at = lax.broadcasted_iota(jnp.int32, logits.shape, 1).astype(jnp.float32)
    chosen_mask = passage_at == every_positive
    clusters = jnp.broadcast_to(cluster_row[...], (everyone, everyone))
    on_diagonal = lax.broadcasted_iota(jnp.int32, clusters.shape, 0) == (
        lax.broadcasted_iota(jnp.int32, clusters.shape, 1)
    )
    own_clusters = jnp.sum(
        jnp.where(on_diagonal, clusters.astype(jnp.float32), 0.0), axis=1, keepdims=True
    )
    allowed = (clusters.astype(jnp.float32) == own_clusters) | chosen_mask
    masked = jnp.where(allowed, logits, -1e30)
    peak = jnp.max(masked, axis=1, keepdims=True)
    normalizer = peak + jnp.log(jnp.sum(jnp.exp(masked - peak), axis=1, keepdims=True))
    chosen = jnp.sum(jnp.where(chosen_mask, logits, 0.0), axis=1, keepdims=True)
    loss = margin_weight * (normalizer - chosen)
    share = jnp.where(allowed, jnp.exp(masked - normalizer), 0.0)
    delta_logits = narrow(margin_weight * (share - jnp.where(chosen_mask, 1.0, 0.0)))
    start = (grp * reps + rep) * sequences
    loss_row = lax.broadcasted_iota(jnp.int32, (everyone, 128), 0)
    loss_lane = lax.broadcasted_iota(jnp.int32, (everyone, 128), 1)
    loss_out[...] = jnp.broadcast_to(
        jnp.sum(jnp.where(loss_row == start + loss_lane, loss, 0.0), axis=0, keepdims=True),
        loss_out.shape,
    )
    own = one_hot((BLOCK, everyone), lambda i, j: (j == start + i) & (i < sequences))
    own_rows = narrow(product(own, delta_logits))
    own_columns = narrow(contract_last(own, delta_logits))
    delta_firsts = (
        product(own_rows, every_passage) * score_scale,
        product(own_columns, every_query) * score_scale,
    )
    eight = lax.broadcasted_iota(jnp.int32, (8, width), 0)
    for place, (base, length) in enumerate(((0, query_len), (query_rows, passage_len))):
        for s in range(sequences):
            at = pl.ds(base + s * length, 8)
            dz[at, :] = dz[at, :] + jnp.where(
                eight == 0, delta_firsts[place][s : s + 1, :], 0.0
            )

    for tile in late:
        last_norm_back(last, tile)

    def core_copy(t):
        return remote(
            buf.at[t % 2, :, 1 - core],
            core_in.at[t % CORE_SLOTS],
            core_sem.at[0, t % CORE_SLOTS],
            core_sem.at[1, t % CORE_SLOTS],
            *sibling,
        )

    def side_copy(t):
        return remote(
            side_out.at[t % SENT_SLOTS],
            side_in.at[t % SIDE_SLOTS],
            side_sem.at[0, t % SIDE_SLOTS],
            side_sem.at[1, t % SIDE_SLOTS],
            *across,
        )

    def near_copy(t):
        return remote(
            keep.at[t % KEEP_SLOTS, sublanes((1 - near) * half_rows, half_rows)],
            near_in.at[t % NEAR_SLOTS],
            near_sem.at[0, t % NEAR_SLOTS],
            near_sem.at[1, t % NEAR_SLOTS],
            *beside,
        )

    def piece_of(place):
        order = 2 * (place % 2) + place // 2
        return sublanes(near * half_rows + order * piece_rows, piece_rows)

    def deep_copy(t, k):
        return remote(
            keep.at[t % KEEP_SLOTS, piece_of((deep + k) % depth)],
            deep_in.at[t % TURNS, k - 1],
            deep_send.at[k - 1, t % TURNS],
            deep_recv.at[k - 1, t % TURNS],
            *behind(k),
        )

    def chunk_place(t):
        step, part = t // PARTS, t % PARTS
        return (part // 4) * 8 + (last - step) * 4 + part % 4

    def own_piece(t):
        return out_ref.at[
            chunk_place(t), near, deep_low, sublanes(deep_high * piece_rows, piece_rows)
        ]

    def local_copy(t):
        return pltpu.make_async_copy(piece.at[t % TURNS], own_piece(t), local_sem.at[t % TURNS])

    def back_copy(stage, source, peer, t, target=None):
        return remote(
            source,
            source if target is None else target,
            back_sem.at[0, stage, t % TURNS],
            back_sem.at[1, stage, t % TURNS],
            *peer,
        )

    def back_high(t):
        return back_copy(0, piece.at[t % TURNS], beyond, t, own_piece(t))

    def even_second(t):
        return back_copy(1, out_ref.at[chunk_place(t), near, deep_low], next_to, t)

    def even_third(t):
        return back_copy(2, out_ref.at[chunk_place(t), near], beside, t)

    def odd_second(t):
        return back_copy(1, out_ref.at[chunk_place(t), near, deep_low], beside, t)

    def odd_third(t):
        return back_copy(2, out_ref.at[chunk_place(t), :, deep_low], next_to, t)

    def by_parity(t, even, odd):
        @pl.when(t % 2 == 0)
        def _():
            even(t)

        @pl.when(t % 2 == 1)
        def _():
            odd(t)

    def add_rows(target, former, latter, count):
        step = 48

        @pl.loop(0, count // step)
        def _(i):
            def at(first_row):
                return sublanes(first_row + i * step, step)

            (to, to_row), (one, one_row), (two, two_row) = target, former, latter
            to[at(to_row), :] = narrow(wide(one[at(one_row), :]) + wide(two[at(two_row), :]))

    def after_core(t):
        core_copy(t).wait()
        slot = t % CORE_SLOTS
        add_rows(
            (side_out.at[t % SENT_SLOTS], 0),
            (buf.at[t % 2, 1 - side, core], 0),
            (core_in.at[slot, 1 - side], 0),
            rows,
        )

        @pl.when(t >= SIDE_SLOTS)
        def _():
            pl.semaphore_wait(side_free, 1)

        side_copy(t).start()
        add_rows(
            (keep.at[t % KEEP_SLOTS], 0),
            (buf.at[t % 2, side, core], 0),
            (core_in.at[slot, side], 0),
            rows,
        )

        @pl.when(t + CORE_SLOTS < CHUNKS)
        def _():
            signal(core_free, sibling)

    def after_side(t):
        side_copy(t).wait()
        kept = keep.at[t % KEEP_SLOTS]
        came = side_in.at[t % SIDE_SLOTS]
        there, here = (1 - near) * half_rows, near * half_rows
        add_rows((kept, there), (kept, there), (came, there), half_rows)

        @pl.when(t >= NEAR_SLOTS)
        def _():
            pl.semaphore_wait(near_free, 1)

        near_copy(t).start()
        add_rows((kept, here), (kept, here), (came, here), half_rows)

        @pl.when(t + SIDE_SLOTS < CHUNKS)
        def _():
            signal(side_free, across)

    def after_near(t):
        near_copy(t).wait()
        kept = keep.at[t % KEEP_SLOTS]
        here = near * half_rows
        add_rows((kept, here), (kept, here), (near_in.at[t % NEAR_SLOTS], 0), half_rows)

        @pl.when(t + NEAR_SLOTS < CHUNKS)
        def _():
            signal(near_free, beside)

        for k in range(1, depth):
            deep_copy(t, k).start()

    def after_deep(t):
        summed = wide(keep[t % KEEP_SLOTS, piece_of(deep), :])
        for k in range(1, depth):
            deep_copy(t, k).wait()
        for k in range(1, depth):
            summed = summed + wide(deep_in[t % TURNS, k - 1])
        piece[t % TURNS] = narrow(summed)
        local_copy(t).start()
        back_high(t).start()

    def after_high(t):
        local_copy(t).wait()
        back_high(t).wait()
        by_parity(t, lambda t: even_second(t).start(), lambda t: odd_second(t).start())

    def after_second(t):
        def even(t):
            even_second(t).wait()
            even_third(t).start()

        def odd(t):
            odd_second(t).wait()
            odd_third(t).start()

        by_parity(t, even, odd)

    def after_third(t):
        by_parity(t, lambda t: even_third(t).wait(), lambda t: odd_third(t).wait())

    def expand_back(layer, slot):
        tiles = width // TILE

        @pl.loop(0, 4 * tiles)
        def _(i):
            at = lanes(i * TILE)
            block, tile = i // tiles, i % tiles
            weight = w[slot, block, sublanes(tile * TILE, TILE), :]
            value = narrow(contract_last(dy[...], weight) * wide(du[:, at]))
            du[:, at] = value
            tally(layer, S_EXPAND + block, lanes(tile * TILE), wide(value))

    def middle_back(slot):
        @pl.loop(0, width // TILE)
        def _(i):
            at = lanes(i * TILE)
            value = dz[:, at]
            for block in range(4):
                weight = w[slot, block, sublanes(i * TILE, TILE), :]
                value = value + contract_last(du[:, block * width : (block + 1) * width], weight)
            dz[:, at] = value

    def context_back(slot):
        @pl.loop(0, width // TILE)
        def _(i):
            weight = w[slot, 3, sublanes(i * TILE, TILE), :]
            dc[:, lanes(i * TILE)] = narrow(contract_last(quad[3], weight))

    def hidden_back(slot):
        @pl.loop(0, width // TILE)
        def _(i):
            at = lanes(i * TILE)
            value = dz[:, at]
            for place in range(3):
                weight = w[slot, place, sublanes(i * TILE, TILE), :]
                value = value + contract_last(quad[place], weight)
            dz[:, at] = value

    def score_back(shares, delta):
        shares = wide(shares)
        weighed = shares * delta
        return narrow(weighed - shares * jnp.sum(weighed, axis=0, keepdims=True))

    def query_attention_back(layer):
        query_span = pl.ds(0, query_rows)
        q2, k2, v2 = quad[0, query_span, :], quad[1, query_span, :], quad[2, query_span, :]

        def fill(rows_of):
            for head in range(HEADS):
                mask = narrow(jnp.where(head_mask(head, width), 1.0, 0.0))
                stack[head * query_rows : (head + 1) * query_rows, :] = rows_of * mask

        fill(dc[query_span, :])
        delta_value = narrow(product(ptq[...], stack[...]))
        delta_scores = score_back(ptq[...], contract_last(v2, stack[...]))
        fill(q2)
        delta_key = narrow(product(delta_scores, stack[...]) * 0.125)
        stack[...] = narrow(contract_rows(delta_scores, k2) * 0.125)
        delta_query = jnp.zeros((query_rows, width), jnp.float32)
        for head in range(HEADS):
            delta_query = delta_query + jnp.where(
                head_mask(head, width),
                wide(stack[head * query_rows : (head + 1) * query_rows, :]),
                0.0,
            )
        delta_query = narrow(delta_query)
        quad[0, query_span, :] = delta_query
        quad[1, query_span, :] = delta_key
        quad[2, query_span, :] = delta_value
        tally(layer, S_QUERY, every_lane, wide(delta_query))
        tally(layer, S_VALUE, every_lane, wide(delta_value))

    def passage_attention_back(layer, low, high):
        @pl.loop(low, high)
        def _(i):
            s, pair = i // pairs, i % pairs
            at_rows = sublanes(query_rows + s * passage_len, passage_len)
            at = lanes(pair * 2 * DH, 2 * DH)
            live_rows = sublanes(query_rows + s * passage_len, live)
            dead_rows = sublanes(query_rows + s * passage_len + live, passage_len - live)
            even, odd = lane_masks(passage_len)
            q2, k2, v2 = quad[0, at_rows, at], quad[1, live_rows, at], quad[2, live_rows, at]
            d2 = dc[at_rows, at]
            shares = pt[i]
            deltas = jnp.concatenate([d2 * even, d2 * odd], axis=0)
            delta_value = narrow(product(shares, deltas))
            delta_scores = score_back(shares, contract_last(v2, deltas))
            queries = jnp.concatenate([q2 * even, q2 * odd], axis=0)
            delta_key = narrow(product(delta_scores, queries) * 0.125)
            keys = jnp.concatenate([k2 * even[:live], k2 * odd[:live]], axis=0)
            piled = jnp.concatenate(
                [delta_scores[:, :passage_len], delta_scores[:, passage_len:]], axis=0
            )
            delta_query = narrow((contract_rows(keys, piled) * 0.125).T)
            quad[0, at_rows, at] = delta_query
            quad[1, live_rows, at] = delta_key
            quad[2, live_rows, at] = delta_value
            nothing = jnp.zeros((passage_len - live, 2 * DH), jnp.bfloat16)
            quad[1, dead_rows, at] = nothing
            quad[2, dead_rows, at] = nothing
            tally(layer, S_QUERY, at, wide(delta_query))
            tally(layer, S_VALUE, at, wide(delta_value))

    def make_terms(t, part):
        pair, half = (part % 4) // 2, lanes((part % 2) * columns, columns)

        @pl.when(part < 4)
        def _():
            @pl.loop(0, 4)
            def _(i):
                taller = active[:, lanes(i * width + pair * rows, rows)]
                buf[t % 2, i // 2, i % 2] = narrow(contract_rows(taller, dy[:, half]))

        def split(i, terms):
            place = sublanes((i // 2) * quarter, quarter)
            terms = narrow(terms)
            buf[t % 2, i % 2, 0, place, :] = terms[:quarter]
            buf[t % 2, i % 2, 1, place, :] = terms[quarter:]

        def two_quarters(i):
            return lanes((i % 2) * 2 * quarter, 2 * quarter)

        @pl.when((part >= 4) & (part < 8))
        def _():
            @pl.loop(0, 4)
            def _(i):
                wider = du[:, lanes((2 * pair + i // 2) * width + (part % 2) * columns, columns)]
                split(i, contract_rows(middle[:, two_quarters(i)], wider))

        @pl.when(part >= 8)
        def _():
            @pl.loop(0, 4)
            def _(i):
                which = 2 * pair + i // 2
                split(
                    i,
                    contract_rows(
                        pair_in[which // 3, :, two_quarters(i)], quad[which, :, half]
                    ),
                )

        @pl.when(t >= CORE_SLOTS)
        def _():
            pl.semaphore_wait(core_free, 1)

        core_copy(t).start()

    def small_move(place, target, peer):
        return remote(
            small, target, small_sem.at[2 * place], small_sem.at[2 * place + 1], *peer
        )

    def small_to_deep(k):
        line = small_deep.at[deep]
        return remote(line, line, small_send.at[k - 1], small_recv.at[k - 1], *behind(k))

    def gradients_out():
        return (
            pltpu.make_async_copy(dz.at[pl.ds(0, query_rows)], query_grad, first_sem.at[4]),
            pltpu.make_async_copy(dz.at[passage_rows], passage_grad, first_sem.at[5]),
        )

    @pl.loop(0, CHUNKS + LAGS[-1])
    def _(t):
        step, part = t // PARTS, t % PARTS
        layer = last - step
        slot = (3 * step) % 2
        busy = t < CHUNKS
        more = busy & (step < LAYERS - 1)

        @pl.when((t > 0) & (t <= CHUNKS))
        def _():
            after_core(t - 1)

        @pl.when(busy & (part == 0))
        def _():
            @pl.when(step > 0)
            def _():
                load("u2", layer).wait()

                @pl.loop(0, total // norm_step)
                def _(tile):
                    last_norm_back(layer, tile)

            load("f", layer).wait()

            @pl.when(step == 0)
            def _():
                start_weights(1, layer, 1)

        for at, names in ((1, ("u1",)), (2, ("q", "k", "v", "ptq")), (3, ("pt", "m")), (5, ("c", "x"))):

            @pl.when(busy & (part == at))
            def _():
                for name in names:
                    load(name, layer).start()

        @pl.when(busy & (part == 4))
        def _():
            load("m", layer).wait()

        @pl.when(busy & (part == 8))
        def _():
            for name in ("c", "x"):
                load(name, layer).wait()

        @pl.when(busy)
        def _():
            make_terms(t, part)

        @pl.when(busy & (part == 1))
        def _():
            @pl.when(more)
            def _():
                load("u2", layer - 1).start()

            load("slope", layer).wait()
            wait_weights(0, layer, slot)
            expand_back(layer, slot)
            start_weights(2, layer, slot)

        @pl.when(busy & (part == 2))
        def _():
            wait_weights(1, layer, 1 - slot)
            middle_back(1 - slot)

            @pl.when(more)
            def _():
                start_weights(0, layer - 1, 1 - slot)

        @pl.when(busy & (part == 3))
        def _():
            load("u1", layer).wait()

            @pl.loop(0, total // norm_step)
            def _(tile):
                first_norm_back(layer, tile)

            wait_weights(2, layer, slot)
            context_back(slot)

            @pl.when(more)
            def _():
                load("f", layer - 1).start()

        @pl.when(busy & (part == 4))
        def _():
            for name in ("q", "k", "v", "pt", "ptq"):
                load(name, layer).wait()
            query_attention_back(layer)

        passages = sequences * pairs

        @pl.when(busy & (part == 5))
        def _():
            passage_attention_back(layer, 0, passages // 3)

        @pl.when(busy & (part == 6))
        def _():
            passage_attention_back(layer, passages // 3, 2 * passages // 3)

        @pl.when(busy & (part == 7))
        def _():
            passage_attention_back(layer, 2 * passages // 3, passages)

        @pl.when(busy & (part == 8))
        def _():
            @pl.when(more)
            def _():
                load("slope", layer - 1).start()

            hidden_back(slot)

            @pl.when(more)
            def _():
                start_weights(1, layer - 1, slot)

            @pl.when(step == LAYERS - 1)
            def _():
                for copy in gradients_out():
                    copy.start()

        for lag, stage in zip(LAGS, (after_side, after_near, after_deep, after_high, after_second, after_third)):

            @pl.when((t >= lag) & (t < CHUNKS + lag))
            def _():
                stage(t - lag)

        for place, (target, peer, came) in enumerate(
            (
                (small_core, sibling, small_core),
                (small_side, across, small_side),
                (small_near, beside, small_near),
            )
        ):

            @pl.when(t == SMALL_AT + place)
            def _():
                small_move(place, target, peer).start()

            @pl.when(t == SMALL_AT + 1 + place)
            def _():
                small_move(place, target, peer).wait()
                small[...] = small[...] + came[...]

        @pl.when(t == SMALL_AT + 3)
        def _():
            small_deep[deep] = small[...]
            for k in range(1, depth):
                small_to_deep(k).start()

        @pl.when(t == SMALL_AT + 5)
        def _():
            for k in range(1, depth):
                small_to_deep(k).wait()
            summed = small_deep[0]
            for k in range(1, depth):
                summed = summed + small_deep[k]
            small_out[...] = summed

    for copy in gradients_out():
        copy.wait()

    @pl.loop(1, reps)
    def _(k):
        to_near(k).wait_send()

    for k in range(1, groups):
        to_far(k).wait_send()


def run_backward(
    margin_bin,
    positive_index,
    cluster_index,
    norm_gain,
    final_gain,
    query_output,
    passage_output,
    query_cotangent,
    passage_cotangent,
    matrices,
    stored,
):
    query_rows, width = query_output.shape
    passage_rows = passage_output.shape[0]
    total = query_rows + passage_rows
    sequences = margin_bin.shape[0]
    everyone = cluster_index.shape[0]
    groups, reps = lax.axis_size("grp"), lax.axis_size("rep")
    depth = reps // 2
    rows = width // 2
    piece_rows = rows // 2 // depth
    bf16, f32 = jnp.bfloat16, jnp.float32
    dma = pltpu.SemaphoreType.DMA
    anywhere = pl.BlockSpec(memory_space=pl.ANY)
    vmem = pl.BlockSpec(memory_space=pltpu.VMEM)
    smem = pl.BlockSpec(memory_space=pltpu.SMEM)
    small_shape = (LAYERS, 16, width)
    pt_shape, ptq_shape = stored[4].shape[1:], stored[5].shape[1:]
    columns = width // 2
    return pl.pallas_call(
        backward_kernel,
        out_shape=(
            jax.ShapeDtypeStruct((CHUNKS, 2, 2, rows // 4, columns), bf16),
            jax.ShapeDtypeStruct(small_shape, f32),
            jax.ShapeDtypeStruct((8, 128), f32),
            jax.ShapeDtypeStruct((query_rows, width), f32),
            jax.ShapeDtypeStruct((passage_rows, width), f32),
        ),
        in_specs=[smem, smem, vmem, vmem, vmem] + [anywhere] * 23,
        out_specs=(anywhere, vmem, vmem, anywhere, anywhere),
        scratch_shapes=[
            pltpu.VMEM((2, 2, 2, rows, columns), bf16),
            pltpu.VMEM((KEEP_SLOTS, rows, columns), bf16),
            pltpu.VMEM((SENT_SLOTS, rows, columns), bf16),
            pltpu.VMEM((CORE_SLOTS, 2, rows, columns), bf16),
            pltpu.VMEM((SIDE_SLOTS, rows, columns), bf16),
            pltpu.VMEM((NEAR_SLOTS, rows // 2, columns), bf16),
            pltpu.VMEM((TURNS, depth - 1, piece_rows, columns), bf16),
            pltpu.VMEM((TURNS, piece_rows, columns), bf16),
            pltpu.VMEM(small_shape, f32),
            pltpu.VMEM(small_shape, f32),
            pltpu.VMEM(small_shape, f32),
            pltpu.VMEM(small_shape, f32),
            pltpu.VMEM((depth,) + small_shape, f32),
            pltpu.VMEM((2 * sequences * BLOCK, width), bf16),
            pltpu.VMEM((groups, reps, BLOCK, TILE), bf16),
            pltpu.VMEM((LAYERS, 8, width), f32),
            pltpu.VMEM((total, width), f32),
            pltpu.VMEM((total, width), bf16),
            pltpu.VMEM((total, 4 * width), bf16),
            pltpu.VMEM((4, total, width), bf16),
            pltpu.VMEM((2, total, width), bf16),
            pltpu.VMEM((total, width), bf16),
            pltpu.VMEM((2, total, width), bf16),
            pltpu.VMEM((total, 4 * width), bf16),
            pltpu.VMEM((total, width), bf16),
            pltpu.VMEM(pt_shape, bf16),
            pltpu.VMEM(ptq_shape, bf16),
            pltpu.VMEM((HEADS * query_rows, width), bf16),
            pltpu.VMEM((LAYERS, total, 128), f32),
            pltpu.VMEM((2, 4, width, width), bf16),
            dma((2, reps)),
            dma((2, groups)),
            dma((7,)),
            dma((12,)),
            dma((2, 4)),
            dma((2, CORE_SLOTS)),
            dma((2, SIDE_SLOTS)),
            dma((2, NEAR_SLOTS)),
            dma((depth - 1, TURNS)),
            dma((depth - 1, TURNS)),
            dma((2, 3, TURNS)),
            dma((TURNS,)),
            dma((6,)),
            dma((depth - 1,)),
            dma((depth - 1,)),
            pltpu.SemaphoreType.REGULAR,
            pltpu.SemaphoreType.REGULAR,
            pltpu.SemaphoreType.REGULAR,
        ],
        compiler_params=pltpu.CompilerParams(
            collective_id=0, has_side_effects=True, vmem_limit_bytes=62 * 1024 * 1024
        ),
    )(
        margin_bin,
        positive_index,
        cluster_index.reshape(1, everyone),
        norm_gain,
        final_gain,
        query_output,
        passage_output,
        query_cotangent.reshape(query_rows, width),
        passage_cotangent.reshape(passage_rows, width),
        *matrices,
        *stored,
    )


def backward_plain(
    query_output,
    passage_output,
    cluster_index,
    margin_bin,
    positive_index,
    query_cotangent,
    passage_cotangent,
    stored,
    params,
):
    batch_size, query_len, model_width = query_output.shape
    passage_len = passage_output.shape[1]
    layout = ((batch_size, query_len), (batch_size, passage_len))
    query_span = batch_size * query_len
    stored_layers = [tuple(array[layer_index] for array in stored) for layer_index in range(LAYERS)]
    query_first = query_output[:, 0, :]
    passage_first = passage_output[:, 0, :]
    facts = jnp.concatenate(
        [margin_bin, positive_index // 128, positive_index % 128], axis=0
    ).astype(jnp.bfloat16)
    facts = jnp.pad(facts, (0, model_width - facts.shape[0]))
    block = jnp.concatenate([query_first, passage_first, facts[None, :]], axis=0)
    block = jnp.pad(block, ((0, 8 - block.shape[0]), (0, 0)))
    total = cluster_index.shape[0]
    every = gather_blocks(block).reshape(-1, 8, model_width)
    every_query = every[:, :batch_size].reshape(total, model_width)
    every_passage = every[:, batch_size : 2 * batch_size].reshape(total, model_width)
    facts = every[:, 2 * batch_size, : 3 * batch_size].astype(jnp.int32)
    facts = facts.reshape(-1, 3, batch_size)
    every_margin = facts[:, 0].reshape(total)
    every_positive = (facts[:, 1] * 128 + facts[:, 2]).reshape(total)
    start_row = lax.axis_index(("grp", "rep")) * batch_size
    score_scale = 2.0 / math.sqrt(model_width)
    logits = contract_last(every_query, every_passage) * score_scale
    columns = lax.broadcasted_iota(jnp.int32, logits.shape, 1)
    chosen_mask = columns == every_positive[:, None]
    allowed = (cluster_index[None, :] == cluster_index[:, None]) | chosen_mask
    masked = jnp.where(allowed, logits, -1e30)
    peak_score = jnp.max(masked, axis=1, keepdims=True)
    normalizer = peak_score + jnp.log(jnp.sum(jnp.exp(masked - peak_score), axis=1, keepdims=True))
    chosen = jnp.sum(jnp.where(chosen_mask, logits, 0.0), axis=1)
    margin_weight = (every_margin + 1).astype(jnp.float32) / NBINS
    every_loss = margin_weight * (normalizer[:, 0] - chosen)
    query_loss = lax.dynamic_slice_in_dim(every_loss, start_row, batch_size)
    delta_logits = narrow(
        margin_weight[:, None]
        * (jnp.where(allowed, jnp.exp(masked - normalizer), 0.0) - chosen_mask.astype(jnp.float32))
    )
    own_rows = lax.dynamic_slice_in_dim(delta_logits, start_row, batch_size, axis=0)
    own_columns = lax.dynamic_slice_in_dim(delta_logits, start_row, batch_size, axis=1)
    delta_query_first = product(own_rows, every_passage) * score_scale
    delta_passage_first = contract_rows(own_columns, every_query) * score_scale
    query_upstream = query_cotangent.astype(jnp.float32).at[:, 0, :].add(delta_query_first)
    passage_upstream = passage_cotangent.astype(jnp.float32).at[:, 0, :].add(delta_passage_first)
    upstream = jnp.concatenate(
        [
            query_upstream.reshape(query_span, model_width),
            passage_upstream.reshape(batch_size * passage_len, model_width),
        ],
        axis=0,
    )
    operands = []
    small = []
    for layer_index in reversed(range(LAYERS)):
        layer_params = tuple(array[layer_index] for array in params)
        upstream, layer_operands, vectors = layer_backward(
            upstream, stored_layers[layer_index], layout, layer_params
        )
        operands.append(layer_operands)
        small.append([vector.reshape(4, -1) for vector in vectors])
    small = small[::-1]
    matrices = reduce_plain(operands)
    flat = reduce_small(jnp.concatenate(small[0] + small[1], axis=1))
    reduced = [None] * 15
    for slot, matrix in zip(MATRICES, matrices):
        reduced[slot] = matrix
    flat = flat.reshape(LAYERS, -1)
    offset = 0
    for slot, vector in zip(SMALL, small[0]):
        size = vector.shape[1]
        reduced[slot] = flat[:, offset : offset + size]
        offset = offset + size
    return query_loss, upstream[:query_span], upstream[query_span:], reduced


def finish_kernel(
    out_ref,
    small_in,
    loss_in,
    query_in,
    passage_in,
    reduce_out,
    expand_out,
    *rest,
):
    square_outs = rest[:4]
    vector_outs = rest[4:12]
    expand_bias_out, query_out, passage_out, loss_out = rest[12:16]
    sums, tall, flat, squares, query, passage, small_ref, loss, in_sem, out_sem = rest[16:]
    rows, columns = sums.shape[1:]
    quarter = rows // 2
    width = 2 * columns
    each = sums.shape[0] // (3 * LAYERS)
    moves = [
        pltpu.make_async_copy(query_in, query, in_sem.at[3 * LAYERS]),
        pltpu.make_async_copy(passage_in, passage, in_sem.at[3 * LAYERS + 1]),
    ]
    little = [
        pltpu.make_async_copy(small_in, small_ref, in_sem.at[3 * LAYERS + 2]),
        pltpu.make_async_copy(loss_in, loss, in_sem.at[3 * LAYERS + 3]),
    ]
    loads = []
    for i in range(3 * LAYERS):
        span = pl.ds(i * each, each)
        loads.append(pltpu.make_async_copy(out_ref.at[span], sums.at[span], in_sem.at[i]))
    for copy in loads + moves + little:
        copy.start()
    stores = []

    def store(source, target):
        copy = pltpu.make_async_copy(source, target, out_sem.at[len(stores)])
        stores.append(copy)
        copy.start()

    for layer in range(LAYERS):
        loads[layer].wait()
        for part in range(4):
            at = pl.ds((part // 2) * rows, rows), pl.ds((part % 2) * columns, columns)
            tall[layer, at[0], at[1]] = wide(sums[layer * each + part])
        store(tall.at[layer], reduce_out.at[layer])
    for move, (source, target) in zip(moves, ((query, query_out), (passage, passage_out))):
        move.wait()
        store(source, target)
    for layer in range(LAYERS):
        loads[LAYERS + layer].wait()
        for part in range(4):
            value = wide(sums[(LAYERS + layer) * each + part])
            for unit in range(2):
                start = (2 * (part // 2) + unit) * width + (part % 2) * columns
                flat[layer, :, start : start + columns] = value[
                    unit * quarter : (unit + 1) * quarter
                ]
        store(flat.at[layer], expand_out.at[layer])
    for layer in range(LAYERS):
        loads[2 * LAYERS + layer].wait()
        for part in range(4):
            value = wide(sums[(2 * LAYERS + layer) * each + part])
            for unit in range(2):
                at = pl.ds((part % 2) * columns, columns)
                squares[2 * (part // 2) + unit, layer, :, at] = value[
                    unit * quarter : (unit + 1) * quarter
                ]
        for which in range(4):
            store(squares.at[which, layer], square_outs[which].at[layer])
    for copy in little:
        copy.wait()
    for i in range(loss_out.shape[0]):
        loss_out[i] = jnp.sum(loss[0:1, i : i + 1])
    group = lax.axis_index("grp")
    vectors = small_ref[:, :8, 0:quarter]
    expand_bias = small_ref[:, S_EXPAND, :]
    for g in range(1, 4):
        vectors = jnp.where(
            group == g, small_ref[:, :8, g * quarter : (g + 1) * quarter], vectors
        )
        expand_bias = jnp.where(group == g, small_ref[:, S_EXPAND + g, :], expand_bias)
    for i in range(8):
        vector_outs[i][...] = vectors[:, i, :]
    expand_bias_out[...] = expand_bias
    for copy in stores:
        copy.wait()


def finish(out, small, loss, query_gradient, passage_gradient, sequences):
    out = out.reshape(out.shape[0], -1, out.shape[-1])
    rows, columns = out.shape[1:]
    quarter, width = rows // 2, 2 * columns
    f32 = jnp.float32
    anywhere = pl.BlockSpec(memory_space=pl.ANY)
    vmem = pl.BlockSpec(memory_space=pltpu.VMEM)
    tall, flat = (LAYERS, width, width), (LAYERS, quarter, 4 * width)
    square, vector = (LAYERS, quarter, width), (LAYERS, quarter)
    results = pl.pallas_call(
        finish_kernel,
        out_shape=[
            jax.ShapeDtypeStruct(shape, f32)
            for shape in [tall, flat]
            + [square] * 4
            + [vector] * 8
            + [(LAYERS, width), query_gradient.shape, passage_gradient.shape, (sequences,)]
        ],
        in_specs=[anywhere] * 5,
        out_specs=[anywhere] * 6
        + [vmem] * 9
        + [anywhere] * 2
        + [pl.BlockSpec(memory_space=pltpu.SMEM)],
        scratch_shapes=[
            pltpu.VMEM(out.shape, jnp.bfloat16),
            pltpu.VMEM(tall, f32),
            pltpu.VMEM(flat, f32),
            pltpu.VMEM((4,) + square, f32),
            pltpu.VMEM(query_gradient.shape, f32),
            pltpu.VMEM(passage_gradient.shape, f32),
            pltpu.VMEM(small.shape, f32),
            pltpu.VMEM(loss.shape, f32),
            pltpu.SemaphoreType.DMA((3 * LAYERS + 4,)),
            pltpu.SemaphoreType.DMA((6 * LAYERS + 2,)),
        ],
        compiler_params=pltpu.CompilerParams(vmem_limit_bytes=60 * 1024 * 1024),
    )(out, small, loss, query_gradient, passage_gradient)
    reduced = [None] * 15
    reduced[11], reduced[9] = results[0], results[1]
    for place, slot in enumerate((0, 2, 3, 5)):
        reduced[slot] = results[2 + place]
    for place, slot in enumerate((1, 4, 6, 7, 8, 12, 13, 14)):
        reduced[slot] = results[6 + place]
    reduced[10] = results[14]
    return results[15], results[16], results[17], reduced


def per_device(
    query_input,
    passage_input,
    query_length,
    passage_length,
    cluster_index,
    margin_bin,
    positive_index,
    query_cotangent,
    passage_cotangent,
    query_weight,
    query_bias,
    key_weight,
    value_weight,
    value_bias,
    mix_weight,
    mix_bias,
    norm_gain,
    norm_shift,
    expand_weight,
    expand_bias,
    reduce_weight,
    reduce_bias,
    final_gain,
    final_shift,
):
    params = (
        query_weight,
        query_bias,
        key_weight,
        value_weight,
        value_bias,
        mix_weight,
        mix_bias,
        norm_gain,
        norm_shift,
        expand_weight,
        expand_bias,
        reduce_weight,
        reduce_bias,
        final_gain,
        final_shift,
    )
    batch_size, query_len, model_width = query_input.shape
    passage_len = passage_input.shape[1]
    matrices = (query_weight, key_weight, value_weight, mix_weight, expand_weight, reduce_weight)
    vectors = (
        query_bias,
        value_bias,
        mix_bias,
        norm_gain,
        norm_shift,
        reduce_bias,
        final_gain,
        final_shift,
        expand_bias,
    )
    results = run_forward(
        query_length,
        passage_length,
        query_input,
        passage_input,
        matrices,
        vectors,
    )
    query_output = results[0].reshape(batch_size, query_len, model_width)
    passage_output = results[1].reshape(batch_size, passage_len, model_width)
    if lax.axis_size("rep") != 8:
        query_loss, query_gradient, passage_gradient, reduced = backward_plain(
            query_output,
            passage_output,
            cluster_index,
            margin_bin,
            positive_index,
            query_cotangent,
            passage_cotangent,
            results[2:],
            params,
        )
    else:
        out, small, loss, query_gradient, passage_gradient = run_backward(
            margin_bin,
            positive_index,
            cluster_index,
            norm_gain,
            final_gain,
            results[0],
            results[1],
            query_cotangent,
            passage_cotangent,
            matrices,
            results[2:],
        )
        query_gradient, passage_gradient, query_loss, reduced = finish(
            out, small, loss, query_gradient, passage_gradient, batch_size
        )
    return (
        query_output,
        passage_output,
        query_loss,
        query_gradient.reshape(batch_size, query_len, model_width),
        passage_gradient.reshape(batch_size, passage_len, model_width),
        reduced[0],
        reduced[1],
        reduced[2],
        reduced[3],
        reduced[4],
        reduced[5],
        reduced[6],
        reduced[7],
        reduced[8],
        reduced[9],
        reduced[10],
        reduced[11],
        reduced[12],
        reduced[13],
        reduced[14],
    )


def solution(mesh):
    placed = (
        P(("grp", "rep"), None, None),
        P(("grp", "rep"), None, None),
        P(("grp", "rep")),
        P(("grp", "rep")),
        P(),
        P(("grp", "rep")),
        P(("grp", "rep")),
        P(("grp", "rep"), None, None),
        P(("grp", "rep"), None, None),
        P(),
        P(),
        P(),
        P(),
        P(),
        P(),
        P(),
        P(),
        P(),
        P(),
        P(),
        P(),
        P(),
        P(),
        P(),
    )
    return jax.shard_map(
        per_device,
        mesh=mesh,
        in_specs=placed,
        out_specs=(
            P(("grp", "rep"), None, None),
            P(("grp", "rep"), None, None),
            P(("grp", "rep")),
            P(("grp", "rep"), None, None),
            P(("grp", "rep"), None, None),
            P(None, "grp", None),
            P(None, "grp"),
            P(None, "grp", None),
            P(None, "grp", None),
            P(None, "grp"),
            P(None, "grp", None),
            P(None, "grp"),
            P(None, "grp"),
            P(None, "grp"),
            P(None, "grp", None),
            P(None, "grp"),
            P(None, "grp", None),
            P(None, "grp"),
            P(None, "grp"),
            P(None, "grp"),
        ),
        check_vma=False,
    )
```

```python
import functools
import math

import jax
import jax.numpy as jnp
from jax import lax
from jax.experimental import pallas as pl
from jax.experimental.pallas import tpu as pltpu
from jax.sharding import PartitionSpec as P

HEADS = 12
DH = 64
LAYERS = 2
NBINS = 10


def narrow(values):
    return values.astype(jnp.bfloat16)


def product(former, latter):
    return jnp.dot(former, latter, preferred_element_type=jnp.float32)


def contract_rows(former, latter):
    return lax.dot_general(
        former, latter, (((0,), (0,)), ((), ())), preferred_element_type=jnp.float32
    )


def contract_last(former, latter):
    return lax.dot_general(
        former, latter, (((1,), (1,)), ((), ())), preferred_element_type=jnp.float32
    )


def column_total(values):
    return jnp.sum(values.astype(jnp.float32), axis=0)


def norm_forward(summed, gain_vector, shift_vector):
    average = jnp.mean(summed, axis=-1, keepdims=True)
    centred = summed - average
    scaled = lax.rsqrt(jnp.mean(centred * centred, axis=-1, keepdims=True) + 1e-12)
    unit_rows = centred * scaled
    return (unit_rows * gain_vector + shift_vector, unit_rows, scaled)


def norm_backward(upstream, unit_rows, scaled, gain_vector):
    delta_unit = upstream * gain_vector
    delta_summed = scaled * (
        delta_unit
        - jnp.mean(delta_unit, axis=-1, keepdims=True)
        - unit_rows * jnp.mean(delta_unit * unit_rows, axis=-1, keepdims=True)
    )
    return (delta_summed, jnp.sum(upstream * unit_rows, axis=0), jnp.sum(upstream, axis=0))


def split_heads(flat, group_count, length):
    return flat.reshape(group_count, length, HEADS, DH)


def group_spans(layout):
    spans = []
    offset = 0
    for group_count, length in layout:
        spans.append((offset, group_count, length))
        offset = offset + group_count * length
    return spans


def attend_backward(query_part, key_part, value_part, shares, delta_context):
    attention = wide(shares)
    delta_value = jnp.einsum(
        "bhqk,bqhd->bkhd", narrow(attention), delta_context, preferred_element_type=jnp.float32
    )
    delta_attention = jnp.einsum(
        "bqhd,bkhd->bhqk", delta_context, value_part, preferred_element_type=jnp.float32
    )
    delta_scores = narrow(
        attention * (delta_attention - jnp.sum(attention * delta_attention, axis=-1, keepdims=True))
    )
    delta_query = (
        jnp.einsum("bhqk,bkhd->bqhd", delta_scores, key_part, preferred_element_type=jnp.float32)
        * 0.125
    )
    delta_key = (
        jnp.einsum("bhqk,bqhd->bkhd", delta_scores, query_part, preferred_element_type=jnp.float32)
        * 0.125
    )
    return (delta_query, delta_key, delta_value)


def layer_backward(upstream, stored, layout, params):
    (
        query_weight,
        query_bias,
        key_weight,
        value_weight,
        value_bias,
        mix_weight,
        mix_bias,
        norm_gain,
        norm_shift,
        expand_weight,
        expand_bias,
        reduce_weight,
        reduce_bias,
        final_gain,
        final_shift,
    ) = params
    (
        hidden,
        query_heads,
        key_heads,
        value_heads,
        shares,
        query_shares,
        context,
        unit_one,
        middle,
        slope,
        active,
        unit_two,
        scales,
    ) = stored
    scale_one, scale_two = scales[:, 0:1], scales[:, 1:2]
    unit_one, unit_two = wide(unit_one), wide(unit_two)
    (count, query_len), (_, passage_len) = layout
    pair_shares = jnp.pad(shares, ((0, 0), (0, passage_len - shares.shape[1]), (0, 0)))
    pair_shares = pair_shares.reshape(count, HEADS // 2, passage_len, 2, passage_len)
    pair_shares = pair_shares.transpose(0, 1, 3, 4, 2).reshape(
        count, HEADS, passage_len, passage_len
    )
    head_shares = query_shares.reshape(count, query_len, HEADS, count, query_len)
    head_shares = jnp.stack([head_shares[i, :, :, i] for i in range(count)])
    all_shares = (head_shares.transpose(0, 2, 3, 1), pair_shares)
    delta_two, delta_final_gain, delta_final_shift = norm_backward(
        upstream, unit_two, scale_two, final_gain
    )
    delta_branch = narrow(delta_two)
    delta_reduce_bias = column_total(delta_branch)
    delta_expanded = narrow(contract_last(delta_branch, reduce_weight) * wide(slope))
    delta_expand_bias = column_total(delta_expanded)
    delta_middle = delta_two + contract_last(delta_expanded, expand_weight)
    delta_one, delta_norm_gain, delta_norm_shift = norm_backward(
        delta_middle, unit_one, scale_one, norm_gain
    )
    delta_mix = narrow(delta_one)
    delta_mix_bias = column_total(delta_mix)
    delta_context = narrow(contract_last(delta_mix, mix_weight))
    collected = ([], [], [])
    for part_shares, (offset, group_count, length) in zip(all_shares, group_spans(layout)):
        row_span = group_count * length
        pieces = [
            split_heads(array[offset : offset + row_span], group_count, length)
            for array in (query_heads, key_heads, value_heads, delta_context)
        ]
        results = attend_backward(pieces[0], pieces[1], pieces[2], part_shares, pieces[3])
        for bucket, gradient in zip(collected, results):
            bucket.append(narrow(gradient.reshape(row_span, -1)))
    delta_query = jnp.concatenate(collected[0], axis=0)
    delta_key = jnp.concatenate(collected[1], axis=0)
    delta_value = jnp.concatenate(collected[2], axis=0)
    delta_hidden = (
        delta_one
        + contract_last(delta_query, query_weight)
        + contract_last(delta_key, key_weight)
        + contract_last(delta_value, value_weight)
    )
    operands = (
        active,
        delta_branch,
        middle,
        delta_expanded,
        hidden,
        context,
        delta_query,
        delta_key,
        delta_value,
        delta_mix,
    )
    vectors = (
        column_total(delta_query),
        column_total(delta_value),
        delta_mix_bias,
        delta_norm_gain,
        delta_norm_shift,
        delta_expand_bias,
        delta_reduce_bias,
        delta_final_gain,
        delta_final_shift,
    )
    return (delta_hidden, operands, vectors)


CORE_FLIP = [(0, 1), (1, 0), (2, 3), (3, 2)]
SIDE_FLIP = [(0, 2), (2, 0), (1, 3), (3, 1)]


def wide(values):
    return values.astype(jnp.float32)


def pick(array, index):
    return lax.dynamic_index_in_dim(array, index, 0, keepdims=False)


def reduce_chunk(chunk):
    rep_total = lax.axis_size("rep")
    group = lax.axis_index("grp")
    side, core = group // 2, group % 2
    parts = chunk.reshape((2, 2) + chunk.shape[1:])
    got = lax.ppermute(
        lax.dynamic_index_in_dim(parts, 1 - core, 1, keepdims=False), "grp", CORE_FLIP
    )
    mine = lax.dynamic_index_in_dim(parts, core, 1, keepdims=False)
    got = lax.ppermute(
        narrow(wide(pick(mine, 1 - side)) + wide(pick(got, 1 - side))), "grp", SIDE_FLIP
    ), narrow(wide(pick(mine, side)) + wide(pick(got, side)))
    summed = narrow(wide(got[0]) + wide(got[1]))
    rows, columns = summed.shape
    if rep_total != 8:
        part = lax.psum_scatter(summed, "rep", scatter_dimension=0, tiled=True)
        return wide(lax.all_gather(part, "rep", axis=0, tiled=True))
    rep = lax.axis_index("rep")
    deep, near = rep // 2, rep % 2
    flip = [(i, i ^ 1) for i in range(8)]
    shifts = [[(i, (i + 2 * k) % 8) for i in range(8)] for k in range(4)]
    halves = summed.reshape(2, rows // 2, columns)
    got = lax.ppermute(pick(halves, 1 - near), "rep", flip)
    half = narrow(wide(pick(halves, near)) + wide(got)).reshape(4, rows // 8, columns)
    total = wide(pick(half, deep))
    for k in range(1, 4):
        total = total + wide(lax.ppermute(pick(half, (deep + k) % 4), "rep", shifts[k]))
    piece = narrow(total)
    pieces = [piece] + [lax.ppermute(piece, "rep", shifts[k]) for k in range(1, 4)]
    joined = jnp.zeros((4,) + piece.shape, jnp.bfloat16)
    for k in range(4):
        joined = lax.dynamic_update_index_in_dim(joined, pieces[k], (deep - k) % 4, 0)
    other = lax.ppermute(joined, "rep", flip)
    own = joined.reshape(rows // 2, columns)
    other = other.reshape(rows // 2, columns)
    first = jnp.where(near == 0, own, other)
    second = jnp.where(near == 0, other, own)
    return wide(jnp.concatenate([first, second], axis=0))


def reduce_small(small):
    group = lax.axis_index("grp")
    side, core = group // 2, group % 2
    parts = small.reshape(2, 2, -1)
    got = lax.ppermute(
        lax.dynamic_index_in_dim(parts, 1 - core, 1, keepdims=False), "grp", CORE_FLIP
    )
    pair = lax.dynamic_index_in_dim(parts, core, 1, keepdims=False) + got
    total = pick(pair, side) + lax.ppermute(pick(pair, 1 - side), "grp", SIDE_FLIP)
    rep_total = lax.axis_size("rep")
    step = 1
    while step < rep_total:
        total = total + lax.ppermute(total, "rep", [(i, i ^ step) for i in range(rep_total)])
        step = step * 2
    return total


def remote(source, target, send_sem, recv_sem, grp, rep):
    return pltpu.make_async_remote_copy(
        src_ref=source,
        dst_ref=target,
        send_sem=send_sem,
        recv_sem=recv_sem,
        device_id=(grp, rep),
        device_id_type=pl.DeviceIdType.MESH,
    )


def gather_kernel(block_ref, out_ref, send_near, recv_near, send_far, recv_far):
    groups, reps = out_ref.shape[:2]
    grp, rep = lax.axis_index("grp"), lax.axis_index("rep")
    barrier = pltpu.get_barrier_semaphore()

    @pl.loop(1, reps)
    def _(k):
        pl.semaphore_signal(
            barrier, inc=1, device_id=(grp, (rep + k) % reps), device_id_type=pl.DeviceIdType.MESH
        )

    for k in range(1, groups):
        pl.semaphore_signal(
            barrier, inc=1, device_id=((grp + k) % groups, rep), device_id_type=pl.DeviceIdType.MESH
        )
    out_ref[grp, rep] = block_ref[...]
    pl.semaphore_wait(barrier, reps + groups - 2)

    def near(k):
        mine = out_ref.at[grp, rep]
        return remote(mine, mine, send_near.at[k], recv_near.at[k], grp, (rep + k) % reps)

    def far(k):
        row = out_ref.at[grp]
        return remote(row, row, send_far.at[k], recv_far.at[k], (grp + k) % groups, rep)

    @pl.loop(1, reps)
    def _(k):
        near(k).start()

    @pl.loop(1, reps)
    def _(k):
        near(k).wait_recv()

    for k in range(1, groups):
        far(k).start()
    for k in range(1, groups):
        far(k).wait_recv()

    @pl.loop(1, reps)
    def _(k):
        near(k).wait_send()

    for k in range(1, groups):
        far(k).wait_send()


def gather_blocks(block):
    groups, reps = lax.axis_size("grp"), lax.axis_size("rep")
    return pl.pallas_call(
        gather_kernel,
        out_shape=jax.ShapeDtypeStruct((groups, reps) + block.shape, block.dtype),
        in_specs=[pl.BlockSpec(memory_space=pltpu.VMEM)],
        out_specs=pl.BlockSpec(memory_space=pltpu.VMEM),
        scratch_shapes=[
            pltpu.SemaphoreType.DMA((reps,)),
            pltpu.SemaphoreType.DMA((reps,)),
            pltpu.SemaphoreType.DMA((groups,)),
            pltpu.SemaphoreType.DMA((groups,)),
        ],
        compiler_params=pltpu.CompilerParams(collective_id=1, has_side_effects=True),
    )(block)


def reduce_plain(layers):
    results = []
    for active, branch, middle, expanded, hidden, context, query, key, value, mix in layers:
        quarter = lambda former, latter: (
            lambda matrix: narrow(matrix).reshape(4, matrix.shape[0] // 4, matrix.shape[1])
        )(contract_rows(former, latter))
        square = jnp.concatenate(
            [
                quarter(hidden, query),
                quarter(hidden, key),
                quarter(hidden, value),
                quarter(context, mix),
            ],
            axis=1,
        )
        square = reduce_chunk(square)
        height = square.shape[0] // 4
        results.append(
            [square[place * height : (place + 1) * height] for place in range(4)]
            + [reduce_chunk(quarter(middle, expanded)), reduce_chunk(quarter(active, branch))]
        )
    return [jnp.stack([results[1][i], results[0][i]]) for i in range(6)]


SMALL = (1, 4, 6, 7, 8, 10, 12, 13, 14)
MATRICES = (0, 2, 3, 5, 9, 11)


LOG2E = 1.4426950408889634
V_QUERY, V_VALUE, V_MIX, V_GAIN, V_SHIFT, V_REDUCE, V_LAST_GAIN, V_LAST_SHIFT, V_EXPAND = range(9)
VECTOR_ROWS = 16
TILE = 256


def lane_masks(rows):
    lane = lax.broadcasted_iota(jnp.int32, (rows, 2 * DH), 1)
    return ((lane < DH).astype(jnp.float32).astype(jnp.bfloat16),
            (lane >= DH).astype(jnp.float32).astype(jnp.bfloat16))


def head_mask(head, width):
    lane = lax.broadcasted_iota(jnp.int32, (1, width), 1)
    return ((lane >= head * DH) & (lane < (head + 1) * DH))


def live_keys(passage_len):
    return -(-(passage_len * 25 // 32) // 16) * 16


def lanes(start, size=TILE):
    return pl.ds(pl.multiple_of(start, 128), size)


def sublanes(start, size):
    return pl.ds(pl.multiple_of(start, 16), size)


def softmax_rows(scores, bias):
    scaled = scores * (0.125 * LOG2E) + bias
    grown = jnp.exp2(scaled - jnp.max(scaled, axis=0, keepdims=True))
    return narrow(grown * (1.0 / jnp.sum(grown, axis=0, keepdims=True)))


def forward_kernel(
    query_lengths,
    passage_lengths,
    query_in,
    passage_in,
    wq_in,
    wk_in,
    wv_in,
    wm_in,
    we_in,
    wr_in,
    query_bias,
    value_bias,
    mix_bias,
    norm_gain,
    norm_shift,
    reduce_bias,
    final_gain,
    final_shift,
    expand_bias,
    query_out,
    passage_out,
    hidden_out,
    q_out,
    k_out,
    v_out,
    pt_out,
    ptq_out,
    c_out,
    u1_out,
    m_out,
    slope_out,
    f_out,
    u2_out,
    r_out,
    wq,
    wk,
    wv,
    wm,
    we,
    wr,
    x,
    q,
    k,
    v,
    pt,
    ptq,
    c,
    u1,
    m,
    slope,
    f,
    u2,
    r,
    z,
    stack,
    vec_ref,
    weight_sem,
    in_sem,
    out_sem,
):
    width = x.shape[1]
    total = x.shape[0]
    sequences = query_lengths.shape[0]
    query_rows = query_in.shape[0]
    query_len = query_rows // sequences
    passage_len = (total - query_rows) // sequences
    pairs = width // (2 * DH)
    kept = live_keys(passage_len)

    weights = ((wq_in, wq), (wk_in, wk), (wv_in, wv), (wm_in, wm), (we_in, we), (wr_in, wr))

    def weight_copy(which, layer):
        source, target = weights[which]
        return pltpu.make_async_copy(
            source.at[layer], target.at[layer], weight_sem.at[which, layer]
        )

    stored = (
        (x, hidden_out),
        (q, q_out),
        (k, k_out),
        (v, v_out),
        (pt, pt_out),
        (ptq, ptq_out),
        (c, c_out),
        (u1, u1_out),
        (m, m_out),
        (slope, slope_out),
        (f, f_out),
        (u2, u2_out),
        (r, r_out),
    )
    X, Q, K, V, PT, PTQ, C, U1, M, SLOPE, F, U2, R = range(13)

    def store(which, layer):
        source, target = stored[which]
        return pltpu.make_async_copy(source, target.at[layer], out_sem.at[which])

    def reuse(which, layer):
        @pl.when(layer > 0)
        def _():
            store(which, layer - 1).wait()

    first = pltpu.make_async_copy(query_in, x.at[pl.ds(0, query_rows)], in_sem.at[0])
    rest = pltpu.make_async_copy(
        passage_in, x.at[pl.ds(query_rows, total - query_rows)], in_sem.at[1]
    )
    first.start()
    rest.start()
    for which in range(3):
        weight_copy(which, 0).start()
    vectors = (
        query_bias,
        value_bias,
        mix_bias,
        norm_gain,
        norm_shift,
        reduce_bias,
        final_gain,
        final_shift,
    )
    for layer in range(LAYERS):
        for place, vector in enumerate(vectors):
            vec_ref[layer, place : place + 1, :] = wide(vector[layer : layer + 1, :])
        for j in range(4):
            vec_ref[layer, V_EXPAND + j : V_EXPAND + j + 1, :] = wide(
                expand_bias[layer : layer + 1, j * width : (j + 1) * width]
            )
    first.wait()
    rest.wait()

    def project(source, weight, layer, bias_row, target):
        @pl.loop(0, width // TILE, unroll=3)
        def _(i):
            value = product(source[...], weight[layer, :, lanes(i * TILE)])
            if bias_row is not None:
                value = value + vec_ref[layer, pl.ds(bias_row, 1), lanes(i * TILE)]
            target[:, lanes(i * TILE)] = narrow(value)

    def norm(layer, gain_row, shift_row, unit, target, scale_lane):
        step = 96
        gain = vec_ref[layer, pl.ds(gain_row, 1), :]
        shift = vec_ref[layer, pl.ds(shift_row, 1), :]

        @pl.loop(0, total // step, unroll=6)
        def _(i):
            at = sublanes(i * step, step)
            full, unit_rows, scaled = norm_forward(z[at, :], gain, shift)
            unit[at, :] = narrow(unit_rows)
            target[at, :] = narrow(full)
            r[at, scale_lane : scale_lane + 1] = scaled

    @pl.loop(0, LAYERS)
    def _(layer):
        store(X, layer).start()
        weight_copy(0, layer).wait()

        @pl.when(layer == 0)
        def _():
            for which in range(3, 6):
                weight_copy(which, 0).start()

        reuse(Q, layer)
        project(x, wq, layer, V_QUERY, q)
        store(Q, layer).start()
        weight_copy(1, layer).wait()
        reuse(K, layer)
        project(x, wk, layer, None, k)
        store(K, layer).start()
        weight_copy(2, layer).wait()
        reuse(V, layer)
        project(x, wv, layer, V_VALUE, v)
        store(V, layer).start()

        reuse(PT, layer)
        reuse(PTQ, layer)
        reuse(C, layer)

        for head in range(HEADS):
            mask = head_mask(head, width).astype(jnp.float32).astype(jnp.bfloat16)
            stack[head * query_rows : (head + 1) * query_rows, :] = q[:query_rows, :] * mask
        scores = contract_last(k[:query_rows, :], stack[...])
        key_slot = lax.broadcasted_iota(jnp.int32, scores.shape, 0)
        query_slot = lax.broadcasted_iota(jnp.int32, scores.shape, 1) % query_rows
        live = jnp.zeros(scores.shape, jnp.bool_)
        for s in range(sequences):
            low = s * query_len
            live = live | (
                (key_slot >= low)
                & (key_slot < low + query_lengths[s])
                & (query_slot >= low)
                & (query_slot < low + query_len)
            )
        shares = softmax_rows(scores, jnp.where(live, 0.0, -1e30))
        ptq[...] = shares
        spread = contract_rows(shares, v[:query_rows, :])
        context = jnp.zeros((query_rows, width), jnp.float32)
        for head in range(HEADS):
            context = context + jnp.where(
                head_mask(head, width), spread[head * query_rows : (head + 1) * query_rows, :], 0.0
            )
        c[:query_rows, :] = narrow(context)

        @pl.loop(0, sequences * pairs, unroll=3)
        def _(i):
            s, pair = i // pairs, i % pairs
            rows = sublanes(query_rows + s * passage_len, passage_len)
            at = lanes(pair * 2 * DH, 2 * DH)
            key_rows = sublanes(query_rows + s * passage_len, kept)
            even, odd = lane_masks(passage_len)
            q2, k2, v2 = q[rows, at], k[key_rows, at], v[key_rows, at]
            scores = contract_last(k2, jnp.concatenate([q2 * even, q2 * odd], axis=0))
            even, odd = even[:kept], odd[:kept]
            slot = lax.broadcasted_iota(jnp.int32, (kept, 1), 0)
            shares = softmax_rows(
                scores, jnp.where(slot < passage_lengths[s], 0.0, -1e30)
            )
            pt[i] = shares
            shares = jnp.concatenate([shares[:, :passage_len], shares[:, passage_len:]], axis=0)
            spread = contract_rows(jnp.concatenate([v2 * even, v2 * odd], axis=0), shares)
            c[rows, at] = narrow(spread.T)

        store(PT, layer).start()
        store(PTQ, layer).start()
        store(C, layer).start()

        weight_copy(3, layer).wait()

        @pl.when(layer + 1 < LAYERS)
        def _():
            for which in range(6):
                weight_copy(which, layer + 1).start()

        @pl.loop(0, width // TILE, unroll=3)
        def _(i):
            at = lanes(i * TILE)
            z[:, at] = (
                wide(x[:, at])
                + product(c[...], wm[layer, :, at])
                + vec_ref[layer, pl.ds(V_MIX, 1), at]
            )

        reuse(U1, layer)
        reuse(M, layer)
        reuse(R, layer)
        norm(layer, V_GAIN, V_SHIFT, u1, m, 0)
        store(U1, layer).start()
        store(M, layer).start()

        weight_copy(4, layer).wait()
        reuse(SLOPE, layer)
        reuse(F, layer)

        @pl.loop(0, 4 * width // TILE, unroll=6)
        def _(i):
            at = lanes(i * TILE)
            tiles = width // TILE
            bias = vec_ref[layer, pl.ds(V_EXPAND + i // tiles, 1), lanes((i % tiles) * TILE)]
            value = product(m[...], we[layer, :, at]) + bias
            share = 0.5 * (1.0 + lax.erf(value * (1.0 / math.sqrt(2.0))))
            density = jnp.exp2(value * value * (-0.5 * LOG2E)) * (1.0 / math.sqrt(2.0 * math.pi))
            f[:, at] = narrow(value * share)
            slope[:, at] = narrow(share + value * density)

        store(SLOPE, layer).start()
        store(F, layer).start()

        weight_copy(5, layer).wait()

        @pl.loop(0, width // TILE, unroll=3)
        def _(i):
            at = lanes(i * TILE)
            z[:, at] = (
                wide(m[:, at])
                + product(f[...], wr[layer, :, at])
                + vec_ref[layer, pl.ds(V_REDUCE, 1), at]
            )

        store(X, layer).wait()
        reuse(U2, layer)
        norm(layer, V_LAST_GAIN, V_LAST_SHIFT, u2, x, 1)
        store(U2, layer).start()
        store(R, layer).start()

    last = LAYERS - 1
    first = pltpu.make_async_copy(x.at[pl.ds(0, query_rows)], query_out, in_sem.at[0])
    rest = pltpu.make_async_copy(
        x.at[pl.ds(query_rows, total - query_rows)], passage_out, in_sem.at[1]
    )
    first.start()
    rest.start()
    for which in range(1, 13):
        store(which, last).wait()
    first.wait()
    rest.wait()


def run_forward(query_length, passage_length, query_input, passage_input, matrices, vectors):
    sequences, query_len, width = query_input.shape
    passage_len = passage_input.shape[1]
    query_rows, passage_rows = sequences * query_len, sequences * passage_len
    total = query_rows + passage_rows
    pairs = width // (2 * DH)
    bf16, f32 = jnp.bfloat16, jnp.float32
    arrays = (
        ((total, width), bf16),
        ((total, width), bf16),
        ((total, width), bf16),
        ((total, width), bf16),
        ((sequences * pairs, live_keys(passage_len), 2 * passage_len), bf16),
        ((query_rows, HEADS * query_rows), bf16),
        ((total, width), bf16),
        ((total, width), bf16),
        ((total, width), bf16),
        ((total, 4 * width), bf16),
        ((total, 4 * width), bf16),
        ((total, width), bf16),
        ((total, 128), f32),
    )
    anywhere = pl.BlockSpec(memory_space=pl.ANY)
    return pl.pallas_call(
        forward_kernel,
        out_shape=(
            jax.ShapeDtypeStruct((query_rows, width), bf16),
            jax.ShapeDtypeStruct((passage_rows, width), bf16),
        )
        + tuple(jax.ShapeDtypeStruct((LAYERS,) + shape, dtype) for shape, dtype in arrays),
        in_specs=[pl.BlockSpec(memory_space=pltpu.SMEM)] * 2
        + [anywhere] * 8
        + [pl.BlockSpec(memory_space=pltpu.VMEM)] * 9,
        out_specs=[anywhere] * 15,
        scratch_shapes=[pltpu.VMEM(matrix.shape, bf16) for matrix in matrices]
        + [pltpu.VMEM(shape, dtype) for shape, dtype in arrays]
        + [
            pltpu.VMEM((total, width), f32),
            pltpu.VMEM((HEADS * query_rows, width), bf16),
            pltpu.VMEM((LAYERS, VECTOR_ROWS, width), f32),
            pltpu.SemaphoreType.DMA((6, LAYERS)),
            pltpu.SemaphoreType.DMA((2,)),
            pltpu.SemaphoreType.DMA((13,)),
        ],
        compiler_params=pltpu.CompilerParams(vmem_limit_bytes=60 * 1024 * 1024),
    )(
        query_length,
        passage_length,
        query_input.reshape(query_rows, width),
        passage_input.reshape(passage_rows, width),
        *matrices,
        *vectors,
    )


CHUNKS = 24
PARTS = 12
S_QUERY, S_VALUE, S_MIX, S_GAIN, S_SHIFT, S_REDUCE, S_LAST_GAIN, S_LAST_SHIFT, S_EXPAND = range(9)
CORE_SLOTS, SIDE_SLOTS, NEAR_SLOTS, KEEP_SLOTS, SENT_SLOTS = 4, 4, 4, 6, 3
TURNS = 8
LAGS = (2, 3, 4, 5, 6, 9)
BLOCK = 16
SMALL_AT = 21


def one_hot(shape, hit):
    row = lax.broadcasted_iota(jnp.int32, shape, 0)
    column = lax.broadcasted_iota(jnp.int32, shape, 1)
    return narrow(jnp.where(hit(row, column), 1.0, 0.0))


def backward_kernel(
    margin_ref,
    positive_ref,
    cluster_row,
    norm_gain,
    final_gain,
    query_out,
    passage_out,
    query_cot,
    passage_cot,
    wq_in,
    wk_in,
    wv_in,
    wm_in,
    we_in,
    wr_in,
    hidden_in,
    q_in,
    k_in,
    v_in,
    pt_in,
    ptq_in,
    c_in,
    u1_in,
    m_in,
    slope_in,
    f_in,
    u2_in,
    r_in,
    out_ref,
    small_out,
    loss_out,
    query_grad,
    passage_grad,
    buf,
    keep,
    side_out,
    core_in,
    side_in,
    near_in,
    deep_in,
    piece,
    small,
    small_core,
    small_side,
    small_near,
    small_deep,
    first,
    blocks,
    gains,
    dz,
    dy,
    du,
    quad,
    pair_in,
    middle,
    unit,
    active,
    dc,
    pt,
    ptq,
    stack,
    r,
    w,
    gather_near,
    gather_far,
    first_sem,
    load_sem,
    weight_sem,
    core_sem,
    side_sem,
    near_sem,
    deep_send,
    deep_recv,
    back_sem,
    local_sem,
    small_sem,
    small_send,
    small_recv,
    core_free,
    side_free,
    near_free,
):
    groups, reps = blocks.shape[:2]
    depth = reps // 2
    rows, columns = keep.shape[1:]
    width = dz.shape[1]
    quarter = width // 4
    half_rows = rows // 2
    piece_rows = half_rows // depth
    total = dz.shape[0]
    sequences = margin_ref.shape[0]
    query_rows = query_out.shape[0]
    query_len = query_rows // sequences
    passage_len = (total - query_rows) // sequences
    pairs = width // (2 * DH)
    live = live_keys(passage_len)
    passage_rows = pl.ds(query_rows, total - query_rows)
    everyone = cluster_row.shape[1]

    grp, rep = lax.axis_index("grp"), lax.axis_index("rep")
    side, core = grp // 2, grp % 2
    deep, near = rep // 2, rep % 2
    sibling = (2 * side + (1 - core), rep)
    across = (2 * (1 - side) + core, rep)
    beside = (grp, 2 * deep + (1 - near))

    def behind(k):
        return (grp, 2 * ((deep + k) % depth) + near)

    deep_low, deep_high = deep % 2, deep // 2
    beyond = (grp, 2 * (deep + 2 - 4 * deep_high) + near)
    next_to = (grp, 2 * (deep + 1 - 2 * deep_low) + near)

    def signal(semaphore, peer):
        pl.semaphore_signal(
            semaphore, inc=1, device_id=peer, device_id_type=pl.DeviceIdType.MESH
        )

    barrier = pltpu.get_barrier_semaphore()
    for k in range(1, reps):
        signal(barrier, (grp, (rep + k) % reps))
    for k in range(1, groups):
        signal(barrier, ((grp + k) % groups, rep))

    firsts = [
        pltpu.make_async_copy(
            source.at[pl.ds(s * length, BLOCK)],
            first.at[pl.ds((place * sequences + s) * BLOCK, BLOCK)],
            first_sem.at[place * sequences + s],
        )
        for place, (source, length) in enumerate(
            ((query_out, query_len), (passage_out, passage_len))
        )
        for s in range(sequences)
    ]
    for copy in firsts:
        copy.start()

    loaded = {
        "f": (f_in, active),
        "u2": (u2_in, unit.at[0]),
        "slope": (slope_in, du),
        "m": (m_in, middle),
        "u1": (u1_in, unit.at[1]),
        "c": (c_in, pair_in.at[1]),
        "q": (q_in, quad.at[0]),
        "k": (k_in, quad.at[1]),
        "v": (v_in, quad.at[2]),
        "pt": (pt_in, pt),
        "ptq": (ptq_in, ptq),
        "x": (hidden_in, pair_in.at[0]),
    }
    places = {name: place for place, name in enumerate(loaded)}

    def load(name, layer):
        source, target = loaded[name]
        return pltpu.make_async_copy(source.at[layer], target, load_sem.at[places[name]])

    def weight_loads(kind, layer, slot):
        squares = []
        for j in range(4):
            block = pl.ds(j * width, width)
            if kind == 0:
                source = wr_in.at[layer, block]
            elif kind == 1:
                source = we_in.at[layer, :, block]
            else:
                source = (wq_in, wk_in, wv_in, wm_in)[j].at[layer]
            squares.append(
                pltpu.make_async_copy(source, w.at[slot, j], weight_sem.at[slot, j])
            )
        return squares

    def start_weights(kind, layer, slot):
        for copy in weight_loads(kind, layer, slot):
            copy.start()

    def wait_weights(kind, layer, slot):
        for copy in weight_loads(kind, layer, slot):
            copy.wait()

    last = LAYERS - 1
    cots = [
        pltpu.make_async_copy(query_cot, dy.at[pl.ds(0, query_rows)], first_sem.at[4]),
        pltpu.make_async_copy(passage_cot, dy.at[passage_rows], first_sem.at[5]),
        pltpu.make_async_copy(r_in, r, first_sem.at[6]),
    ]
    for copy in cots:
        copy.start()
    load("u2", last).start()

    def tally(layer, row_at, lanes_at, values):
        at = (layer, pl.ds(row_at, 1), lanes_at)
        small[at] = small[at] + jnp.sum(values, axis=0, keepdims=True)

    every_lane = pl.ds(0, width)

    norm_step = 48

    def norm_back_rows(
        layer, unit_at, scale_lane, gain_row, target, gain_to, shift_to, bias_to, tile
    ):
        gain = gains[layer, pl.ds(gain_row, 1), :]
        at = sublanes(tile * norm_step, norm_step)
        upstream = dz[at, :]
        unit_rows = wide(unit[unit_at, at, :])
        scaled = r[layer, at, scale_lane : scale_lane + 1]
        delta_unit = upstream * gain
        delta = scaled * (
            delta_unit
            - jnp.mean(delta_unit, axis=-1, keepdims=True)
            - unit_rows * jnp.mean(delta_unit * unit_rows, axis=-1, keepdims=True)
        )
        dz[at, :] = delta
        rounded = narrow(delta)
        target[at, :] = rounded
        tally(layer, gain_to, every_lane, upstream * unit_rows)
        tally(layer, shift_to, every_lane, upstream)
        tally(layer, bias_to, every_lane, wide(rounded))

    def last_norm_back(layer, tile):
        norm_back_rows(
            layer, 0, 1, 1, dy, S_LAST_GAIN, S_LAST_SHIFT, S_REDUCE, tile
        )

    def first_norm_back(layer, tile):
        norm_back_rows(layer, 1, 0, 0, quad.at[3], S_GAIN, S_SHIFT, S_MIX, tile)

    for copy in firsts:
        copy.wait()
    firsts_count = 2 * sequences
    segments = width // TILE
    packed = jnp.zeros((BLOCK, TILE), jnp.float32)
    for j in range(segments):
        low = j * firsts_count
        packed = packed + product(
            one_hot(
                (BLOCK, first.shape[0]),
                lambda i, k: (k == (i - low) * BLOCK) & (i >= low) & (i < low + firsts_count),
            ),
            first[:, j * TILE : (j + 1) * TILE],
        )
    row = lax.broadcasted_iota(jnp.int32, packed.shape, 0)
    lane = lax.broadcasted_iota(jnp.int32, packed.shape, 1)
    for s in range(sequences):
        positive = positive_ref[s]
        facts = (margin_ref[s], positive // 128, positive % 128)
        for place, fact in enumerate(facts):
            at = (row == segments * firsts_count) & (lane == place * sequences + s)
            packed = jnp.where(at, fact.astype(jnp.float32), packed)
    blocks[grp, rep] = narrow(packed)

    def to_near(k):
        mine = blocks.at[grp, rep]
        return remote(
            mine, mine, gather_near.at[0, k], gather_near.at[1, k], grp, (rep + k) % reps
        )

    def to_far(k):
        line = blocks.at[grp]
        return remote(
            line, line, gather_far.at[0, k], gather_far.at[1, k], (grp + k) % groups, rep
        )

    pl.semaphore_wait(barrier, reps + groups - 2)

    @pl.loop(1, reps)
    def _(k):
        to_near(k).start()

    load("f", last).start()
    load("slope", last).start()
    start_weights(0, last, 0)

    for copy in cots:
        copy.wait()
    small[...] = jnp.zeros_like(small)
    for layer in range(LAYERS):
        gains[layer, 0:1, :] = wide(norm_gain[layer : layer + 1, :])
        gains[layer, 1:2, :] = wide(final_gain[layer : layer + 1, :])

    @pl.loop(0, total // 96)
    def _(i):
        at = sublanes(i * 96, 96)
        dz[at, :] = wide(dy[at, :])

    first_at = [s * query_len for s in range(sequences)]
    first_at += [query_rows + s * passage_len for s in range(sequences)]
    late = sorted({at // norm_step for at in first_at})
    spans = [span for span in zip([-1] + late, late + [total // norm_step])]
    load("u2", last).wait()

    def early_norm(low, high):
        @pl.loop(low, high)
        def _(tile):
            last_norm_back(last, tile)

    for low, high in spans[: len(spans) // 2]:
        if low + 1 < high:
            early_norm(low + 1, high)

    @pl.loop(1, reps)
    def _(k):
        to_near(k).wait_recv()

    for k in range(1, groups):
        to_far(k).start()

    for low, high in spans[len(spans) // 2 :]:
        if low + 1 < high:
            early_norm(low + 1, high)

    for k in range(1, groups):
        to_far(k).wait_recv()

    gathered = blocks[...].reshape(groups * reps * BLOCK, TILE)

    def taken(offset):
        return product(
            one_hot(
                (everyone, gathered.shape[0]),
                lambda i, j: j == BLOCK * (i // sequences) + offset(i),
            ),
            gathered,
        )

    def taken_rows(base):
        return narrow(
            jnp.concatenate(
                [
                    taken(lambda i: j * firsts_count + base + i % sequences)
                    for j in range(segments)
                ],
                axis=1,
            )
        )

    every_query = taken_rows(0)
    every_passage = taken_rows(sequences)
    facts = taken(lambda i: segments * firsts_count)[:, :128]
    query_at = lax.broadcasted_iota(jnp.int32, facts.shape, 0) % sequences
    lane_at = lax.broadcasted_iota(jnp.int32, facts.shape, 1)

    def fact(place):
        hit = lane_at == place * sequences + query_at
        return jnp.sum(jnp.where(hit, facts, 0.0), axis=1, keepdims=True)

    margin_weight = (fact(0) + 1.0) / NBINS
    every_positive = fact(1) * 128.0 + fact(2)
    score_scale = 2.0 / math.sqrt(width)
    logits = contract_last(every_query, every_passage) * score_scale
    passage_at = lax.broadcasted_iota(jnp.int32, logits.shape, 1).astype(jnp.float32)
    chosen_mask = passage_at == every_positive
    clusters = jnp.broadcast_to(cluster_row[...], (everyone, everyone))
    on_diagonal = lax.broadcasted_iota(jnp.int32, clusters.shape, 0) == (
        lax.broadcasted_iota(jnp.int32, clusters.shape, 1)
    )
    own_clusters = jnp.sum(
        jnp.where(on_diagonal, clusters.astype(jnp.float32), 0.0), axis=1, keepdims=True
    )
    allowed = (clusters.astype(jnp.float32) == own_clusters) | chosen_mask
    masked = jnp.where(allowed, logits, -1e30)
    peak = jnp.max(masked, axis=1, keepdims=True)
    normalizer = peak + jnp.log(jnp.sum(jnp.exp(masked - peak), axis=1, keepdims=True))
    chosen = jnp.sum(jnp.where(chosen_mask, logits, 0.0), axis=1, keepdims=True)
    loss = margin_weight * (normalizer - chosen)
    share = jnp.where(allowed, jnp.exp(masked - normalizer), 0.0)
    delta_logits = narrow(margin_weight * (share - jnp.where(chosen_mask, 1.0, 0.0)))
    start = (grp * reps + rep) * sequences
    loss_row = lax.broadcasted_iota(jnp.int32, (everyone, 128), 0)
    loss_lane = lax.broadcasted_iota(jnp.int32, (everyone, 128), 1)
    loss_out[...] = jnp.broadcast_to(
        jnp.sum(jnp.where(loss_row == start + loss_lane, loss, 0.0), axis=0, keepdims=True),
        loss_out.shape,
    )
    own = one_hot((BLOCK, everyone), lambda i, j: (j == start + i) & (i < sequences))
    own_rows = narrow(product(own, delta_logits))
    own_columns = narrow(contract_last(own, delta_logits))
    delta_firsts = (
        product(own_rows, every_passage) * score_scale,
        product(own_columns, every_query) * score_scale,
    )
    eight = lax.broadcasted_iota(jnp.int32, (8, width), 0)
    for place, (base, length) in enumerate(((0, query_len), (query_rows, passage_len))):
        for s in range(sequences):
            at = pl.ds(base + s * length, 8)
            dz[at, :] = dz[at, :] + jnp.where(
                eight == 0, delta_firsts[place][s : s + 1, :], 0.0
            )

    for tile in late:
        last_norm_back(last, tile)

    def core_copy(t):
        return remote(
            buf.at[t % 2, :, 1 - core],
            core_in.at[t % CORE_SLOTS],
            core_sem.at[0, t % CORE_SLOTS],
            core_sem.at[1, t % CORE_SLOTS],
            *sibling,
        )

    def side_copy(t):
        return remote(
            side_out.at[t % SENT_SLOTS],
            side_in.at[t % SIDE_SLOTS],
            side_sem.at[0, t % SIDE_SLOTS],
            side_sem.at[1, t % SIDE_SLOTS],
            *across,
        )

    def near_copy(t):
        return remote(
            keep.at[t % KEEP_SLOTS, sublanes((1 - near) * half_rows, half_rows)],
            near_in.at[t % NEAR_SLOTS],
            near_sem.at[0, t % NEAR_SLOTS],
            near_sem.at[1, t % NEAR_SLOTS],
            *beside,
        )

    def piece_of(place):
        order = 2 * (place % 2) + place // 2
        return sublanes(near * half_rows + order * piece_rows, piece_rows)

    def deep_copy(t, k):
        return remote(
            keep.at[t % KEEP_SLOTS, piece_of((deep + k) % depth)],
            deep_in.at[t % TURNS, k - 1],
            deep_send.at[k - 1, t % TURNS],
            deep_recv.at[k - 1, t % TURNS],
            *behind(k),
        )

    def chunk_place(t):
        step, part = t // PARTS, t % PARTS
        return (part // 4) * 8 + (last - step) * 4 + part % 4

    def own_piece(t):
        return out_ref.at[
            chunk_place(t), near, deep_low, sublanes(deep_high * piece_rows, piece_rows)
        ]

    def local_copy(t):
        return pltpu.make_async_copy(piece.at[t % TURNS], own_piece(t), local_sem.at[t % TURNS])

    def back_copy(stage, source, peer, t, target=None):
        return remote(
            source,
            source if target is None else target,
            back_sem.at[0, stage, t % TURNS],
            back_sem.at[1, stage, t % TURNS],
            *peer,
        )

    def back_high(t):
        return back_copy(0, piece.at[t % TURNS], beyond, t, own_piece(t))

    def even_second(t):
        return back_copy(1, out_ref.at[chunk_place(t), near, deep_low], next_to, t)

    def even_third(t):
        return back_copy(2, out_ref.at[chunk_place(t), near], beside, t)

    def odd_second(t):
        return back_copy(1, out_ref.at[chunk_place(t), near, deep_low], beside, t)

    def odd_third(t):
        return back_copy(2, out_ref.at[chunk_place(t), :, deep_low], next_to, t)

    def by_parity(t, even, odd):
        @pl.when(t % 2 == 0)
        def _():
            even(t)

        @pl.when(t % 2 == 1)
        def _():
            odd(t)

    def add_rows(target, former, latter, count):
        step = 48

        @pl.loop(0, count // step, unroll=2)
        def _(i):
            def at(first_row):
                return sublanes(first_row + i * step, step)

            (to, to_row), (one, one_row), (two, two_row) = target, former, latter
            to[at(to_row), :] = narrow(wide(one[at(one_row), :]) + wide(two[at(two_row), :]))

    def after_core(t):
        core_copy(t).wait()
        slot = t % CORE_SLOTS
        add_rows(
            (side_out.at[t % SENT_SLOTS], 0),
            (buf.at[t % 2, 1 - side, core], 0),
            (core_in.at[slot, 1 - side], 0),
            rows,
        )

        @pl.when(t >= SIDE_SLOTS)
        def _():
            pl.semaphore_wait(side_free, 1)

        side_copy(t).start()
        add_rows(
            (keep.at[t % KEEP_SLOTS], 0),
            (buf.at[t % 2, side, core], 0),
            (core_in.at[slot, side], 0),
            rows,
        )

        @pl.when(t + CORE_SLOTS < CHUNKS)
        def _():
            signal(core_free, sibling)

    def after_side(t):
        side_copy(t).wait()
        kept = keep.at[t % KEEP_SLOTS]
        came = side_in.at[t % SIDE_SLOTS]
        there, here = (1 - near) * half_rows, near * half_rows
        add_rows((kept, there), (kept, there), (came, there), half_rows)

        @pl.when(t >= NEAR_SLOTS)
        def _():
            pl.semaphore_wait(near_free, 1)

        near_copy(t).start()
        add_rows((kept, here), (kept, here), (came, here), half_rows)

        @pl.when(t + SIDE_SLOTS < CHUNKS)
        def _():
            signal(side_free, across)

    def after_near(t):
        near_copy(t).wait()
        kept = keep.at[t % KEEP_SLOTS]
        here = near * half_rows
        add_rows((kept, here), (kept, here), (near_in.at[t % NEAR_SLOTS], 0), half_rows)

        @pl.when(t + NEAR_SLOTS < CHUNKS)
        def _():
            signal(near_free, beside)

        for k in range(1, depth):
            deep_copy(t, k).start()

    def after_deep(t):
        summed = wide(keep[t % KEEP_SLOTS, piece_of(deep), :])
        for k in range(1, depth):
            deep_copy(t, k).wait()
        for k in range(1, depth):
            summed = summed + wide(deep_in[t % TURNS, k - 1])
        piece[t % TURNS] = narrow(summed)
        local_copy(t).start()
        back_high(t).start()

    def after_high(t):
        local_copy(t).wait()
        back_high(t).wait()
        by_parity(t, lambda t: even_second(t).start(), lambda t: odd_second(t).start())

    def after_second(t):
        def even(t):
            even_second(t).wait()
            even_third(t).start()

        def odd(t):
            odd_second(t).wait()
            odd_third(t).start()

        by_parity(t, even, odd)

    def after_third(t):
        by_parity(t, lambda t: even_third(t).wait(), lambda t: odd_third(t).wait())

    def expand_back(layer, slot):
        tiles = width // TILE

        @pl.loop(0, 4 * tiles, unroll=2)
        def _(i):
            at = lanes(i * TILE)
            block, tile = i // tiles, i % tiles
            weight = w[slot, block, sublanes(tile * TILE, TILE), :]
            value = narrow(contract_last(dy[...], weight) * wide(du[:, at]))
            du[:, at] = value
            tally(layer, S_EXPAND + block, lanes(tile * TILE), wide(value))

    def middle_back(slot):
        @pl.loop(0, width // TILE, unroll=3)
        def _(i):
            at = lanes(i * TILE)
            value = dz[:, at]
            for block in range(4):
                weight = w[slot, block, sublanes(i * TILE, TILE), :]
                value = value + contract_last(du[:, block * width : (block + 1) * width], weight)
            dz[:, at] = value

    def context_back(slot):
        @pl.loop(0, width // TILE, unroll=3)
        def _(i):
            weight = w[slot, 3, sublanes(i * TILE, TILE), :]
            dc[:, lanes(i * TILE)] = narrow(contract_last(quad[3], weight))

    def hidden_back(slot):
        @pl.loop(0, width // TILE, unroll=3)
        def _(i):
            at = lanes(i * TILE)
            value = dz[:, at]
            for place in range(3):
                weight = w[slot, place, sublanes(i * TILE, TILE), :]
                value = value + contract_last(quad[place], weight)
            dz[:, at] = value

    def score_back(shares, delta):
        shares = wide(shares)
        weighed = shares * delta
        return narrow(weighed - shares * jnp.sum(weighed, axis=0, keepdims=True))

    def query_attention_back(layer):
        query_span = pl.ds(0, query_rows)
        q2, k2, v2 = quad[0, query_span, :], quad[1, query_span, :], quad[2, query_span, :]

        def fill(rows_of):
            for head in range(HEADS):
                mask = narrow(jnp.where(head_mask(head, width), 1.0, 0.0))
                stack[head * query_rows : (head + 1) * query_rows, :] = rows_of * mask

        fill(dc[query_span, :])
        delta_value = narrow(product(ptq[...], stack[...]))
        delta_scores = score_back(ptq[...], contract_last(v2, stack[...]))
        fill(q2)
        delta_key = narrow(product(delta_scores, stack[...]) * 0.125)
        stack[...] = narrow(contract_rows(delta_scores, k2) * 0.125)
        delta_query = jnp.zeros((query_rows, width), jnp.float32)
        for head in range(HEADS):
            delta_query = delta_query + jnp.where(
                head_mask(head, width),
                wide(stack[head * query_rows : (head + 1) * query_rows, :]),
                0.0,
            )
        delta_query = narrow(delta_query)
        quad[0, query_span, :] = delta_query
        quad[1, query_span, :] = delta_key
        quad[2, query_span, :] = delta_value
        tally(layer, S_QUERY, every_lane, wide(delta_query))
        tally(layer, S_VALUE, every_lane, wide(delta_value))

    def passage_attention_back(layer, low, high):
        @pl.loop(low, high, unroll=2)
        def _(i):
            s, pair = i // pairs, i % pairs
            at_rows = sublanes(query_rows + s * passage_len, passage_len)
            at = lanes(pair * 2 * DH, 2 * DH)
            live_rows = sublanes(query_rows + s * passage_len, live)
            dead_rows = sublanes(query_rows + s * passage_len + live, passage_len - live)
            even, odd = lane_masks(passage_len)
            q2, k2, v2 = quad[0, at_rows, at], quad[1, live_rows, at], quad[2, live_rows, at]
            d2 = dc[at_rows, at]
            shares = pt[i]
            deltas = jnp.concatenate([d2 * even, d2 * odd], axis=0)
            delta_value = narrow(product(shares, deltas))
            delta_scores = score_back(shares, contract_last(v2, deltas))
            queries = jnp.concatenate([q2 * even, q2 * odd], axis=0)
            delta_key = narrow(product(delta_scores, queries) * 0.125)
            keys = jnp.concatenate([k2 * even[:live], k2 * odd[:live]], axis=0)
            piled = jnp.concatenate(
                [delta_scores[:, :passage_len], delta_scores[:, passage_len:]], axis=0
            )
            delta_query = narrow((contract_rows(keys, piled) * 0.125).T)
            quad[0, at_rows, at] = delta_query
            quad[1, live_rows, at] = delta_key
            quad[2, live_rows, at] = delta_value
            nothing = jnp.zeros((passage_len - live, 2 * DH), jnp.bfloat16)
            quad[1, dead_rows, at] = nothing
            quad[2, dead_rows, at] = nothing
            tally(layer, S_QUERY, at, wide(delta_query))
            tally(layer, S_VALUE, at, wide(delta_value))

    def make_terms(t, part):
        pair, half = (part % 4) // 2, lanes((part % 2) * columns, columns)

        @pl.when(part < 4)
        def _():
            @pl.loop(0, 4, unroll=2)
            def _(i):
                taller = active[:, lanes(i * width + pair * rows, rows)]
                buf[t % 2, i // 2, i % 2] = narrow(contract_rows(taller, dy[:, half]))

        def split(i, terms):
            place = sublanes((i // 2) * quarter, quarter)
            terms = narrow(terms)
            buf[t % 2, i % 2, 0, place, :] = terms[:quarter]
            buf[t % 2, i % 2, 1, place, :] = terms[quarter:]

        def two_quarters(i):
            return lanes((i % 2) * 2 * quarter, 2 * quarter)

        @pl.when((part >= 4) & (part < 8))
        def _():
            @pl.loop(0, 4, unroll=2)
            def _(i):
                wider = du[:, lanes((2 * pair + i // 2) * width + (part % 2) * columns, columns)]
                split(i, contract_rows(middle[:, two_quarters(i)], wider))

        @pl.when(part >= 8)
        def _():
            @pl.loop(0, 4, unroll=2)
            def _(i):
                which = 2 * pair + i // 2
                split(
                    i,
                    contract_rows(
                        pair_in[which // 3, :, two_quarters(i)], quad[which, :, half]
                    ),
                )

        @pl.when(t >= CORE_SLOTS)
        def _():
            pl.semaphore_wait(core_free, 1)

        core_copy(t).start()

    def small_move(place, target, peer):
        return remote(
            small, target, small_sem.at[2 * place], small_sem.at[2 * place + 1], *peer
        )

    def small_to_deep(k):
        line = small_deep.at[deep]
        return remote(line, line, small_send.at[k - 1], small_recv.at[k - 1], *behind(k))

    def gradients_out():
        return (
            pltpu.make_async_copy(dz.at[pl.ds(0, query_rows)], query_grad, first_sem.at[4]),
            pltpu.make_async_copy(dz.at[passage_rows], passage_grad, first_sem.at[5]),
        )

    @pl.loop(0, CHUNKS + LAGS[-1])
    def _(t):
        step, part = t // PARTS, t % PARTS
        layer = last - step
        slot = (3 * step) % 2
        busy = t < CHUNKS
        more = busy & (step < LAYERS - 1)

        @pl.when((t > 0) & (t <= CHUNKS))
        def _():
            after_core(t - 1)

        @pl.when(busy & (part == 0))
        def _():
            @pl.when(step > 0)
            def _():
                load("u2", layer).wait()

                @pl.loop(0, total // norm_step)
                def _(tile):
                    last_norm_back(layer, tile)

            load("f", layer).wait()

            @pl.when(step == 0)
            def _():
                start_weights(1, layer, 1)

        for at, names in ((1, ("u1",)), (2, ("q", "k", "v", "ptq")), (3, ("pt", "m")), (5, ("c", "x"))):

            @pl.when(busy & (part == at))
            def _():
                for name in names:
                    load(name, layer).start()

        @pl.when(busy & (part == 4))
        def _():
            load("m", layer).wait()

        @pl.when(busy & (part == 8))
        def _():
            for name in ("c", "x"):
                load(name, layer).wait()

        @pl.when(busy)
        def _():
            make_terms(t, part)

        @pl.when(busy & (part == 1))
        def _():
            @pl.when(more)
            def _():
                load("u2", layer - 1).start()

            load("slope", layer).wait()
            wait_weights(0, layer, slot)
            expand_back(layer, slot)
            start_weights(2, layer, slot)

        @pl.when(busy & (part == 2))
        def _():
            wait_weights(1, layer, 1 - slot)
            middle_back(1 - slot)

            @pl.when(more)
            def _():
                start_weights(0, layer - 1, 1 - slot)

        @pl.when(busy & (part == 3))
        def _():
            load("u1", layer).wait()

            @pl.loop(0, total // norm_step, unroll=2)
            def _(tile):
                first_norm_back(layer, tile)

            wait_weights(2, layer, slot)
            context_back(slot)

            @pl.when(more)
            def _():
                load("f", layer - 1).start()

        @pl.when(busy & (part == 4))
        def _():
            for name in ("q", "k", "v", "pt", "ptq"):
                load(name, layer).wait()
            query_attention_back(layer)

        passages = sequences * pairs

        @pl.when(busy & (part == 5))
        def _():
            passage_attention_back(layer, 0, passages // 3)

        @pl.when(busy & (part == 6))
        def _():
            passage_attention_back(layer, passages // 3, 2 * passages // 3)

        @pl.when(busy & (part == 7))
        def _():
            passage_attention_back(layer, 2 * passages // 3, passages)

        @pl.when(busy & (part == 8))
        def _():
            @pl.when(more)
            def _():
                load("slope", layer - 1).start()

            hidden_back(slot)

            @pl.when(more)
            def _():
                start_weights(1, layer - 1, slot)

            @pl.when(step == LAYERS - 1)
            def _():
                for copy in gradients_out():
                    copy.start()

        for lag, stage in zip(LAGS, (after_side, after_near, after_deep, after_high, after_second, after_third)):

            @pl.when((t >= lag) & (t < CHUNKS + lag))
            def _():
                stage(t - lag)

        for place, (target, peer, came) in enumerate(
            (
                (small_core, sibling, small_core),
                (small_side, across, small_side),
                (small_near, beside, small_near),
            )
        ):

            @pl.when(t == SMALL_AT + place)
            def _():
                small_move(place, target, peer).start()

            @pl.when(t == SMALL_AT + 1 + place)
            def _():
                small_move(place, target, peer).wait()
                small[...] = small[...] + came[...]

        @pl.when(t == SMALL_AT + 3)
        def _():
            small_deep[deep] = small[...]
            for k in range(1, depth):
                small_to_deep(k).start()

        @pl.when(t == SMALL_AT + 5)
        def _():
            for k in range(1, depth):
                small_to_deep(k).wait()
            summed = small_deep[0]
            for k in range(1, depth):
                summed = summed + small_deep[k]
            small_out[...] = summed

    for copy in gradients_out():
        copy.wait()

    @pl.loop(1, reps)
    def _(k):
        to_near(k).wait_send()

    for k in range(1, groups):
        to_far(k).wait_send()


def run_backward(
    margin_bin,
    positive_index,
    cluster_index,
    norm_gain,
    final_gain,
    query_output,
    passage_output,
    query_cotangent,
    passage_cotangent,
    matrices,
    stored,
):
    query_rows, width = query_output.shape
    passage_rows = passage_output.shape[0]
    total = query_rows + passage_rows
    sequences = margin_bin.shape[0]
    everyone = cluster_index.shape[0]
    groups, reps = lax.axis_size("grp"), lax.axis_size("rep")
    depth = reps // 2
    rows = width // 2
    piece_rows = rows // 2 // depth
    bf16, f32 = jnp.bfloat16, jnp.float32
    dma = pltpu.SemaphoreType.DMA
    anywhere = pl.BlockSpec(memory_space=pl.ANY)
    vmem = pl.BlockSpec(memory_space=pltpu.VMEM)
    smem = pl.BlockSpec(memory_space=pltpu.SMEM)
    small_shape = (LAYERS, 16, width)
    pt_shape, ptq_shape = stored[4].shape[1:], stored[5].shape[1:]
    columns = width // 2
    return pl.pallas_call(
        backward_kernel,
        out_shape=(
            jax.ShapeDtypeStruct((CHUNKS, 2, 2, rows // 4, columns), bf16),
            jax.ShapeDtypeStruct(small_shape, f32),
            jax.ShapeDtypeStruct((8, 128), f32),
            jax.ShapeDtypeStruct((query_rows, width), f32),
            jax.ShapeDtypeStruct((passage_rows, width), f32),
        ),
        in_specs=[smem, smem, vmem, vmem, vmem] + [anywhere] * 23,
        out_specs=(anywhere, vmem, vmem, anywhere, anywhere),
        scratch_shapes=[
            pltpu.VMEM((2, 2, 2, rows, columns), bf16),
            pltpu.VMEM((KEEP_SLOTS, rows, columns), bf16),
            pltpu.VMEM((SENT_SLOTS, rows, columns), bf16),
            pltpu.VMEM((CORE_SLOTS, 2, rows, columns), bf16),
            pltpu.VMEM((SIDE_SLOTS, rows, columns), bf16),
            pltpu.VMEM((NEAR_SLOTS, rows // 2, columns), bf16),
            pltpu.VMEM((TURNS, depth - 1, piece_rows, columns), bf16),
            pltpu.VMEM((TURNS, piece_rows, columns), bf16),
            pltpu.VMEM(small_shape, f32),
            pltpu.VMEM(small_shape, f32),
            pltpu.VMEM(small_shape, f32),
            pltpu.VMEM(small_shape, f32),
            pltpu.VMEM((depth,) + small_shape, f32),
            pltpu.VMEM((2 * sequences * BLOCK, width), bf16),
            pltpu.VMEM((groups, reps, BLOCK, TILE), bf16),
            pltpu.VMEM((LAYERS, 8, width), f32),
            pltpu.VMEM((total, width), f32),
            pltpu.VMEM((total, width), bf16),
            pltpu.VMEM((total, 4 * width), bf16),
            pltpu.VMEM((4, total, width), bf16),
            pltpu.VMEM((2, total, width), bf16),
            pltpu.VMEM((total, width), bf16),
            pltpu.VMEM((2, total, width), bf16),
            pltpu.VMEM((total, 4 * width), bf16),
            pltpu.VMEM((total, width), bf16),
            pltpu.VMEM(pt_shape, bf16),
            pltpu.VMEM(ptq_shape, bf16),
            pltpu.VMEM((HEADS * query_rows, width), bf16),
            pltpu.VMEM((LAYERS, total, 128), f32),
            pltpu.VMEM((2, 4, width, width), bf16),
            dma((2, reps)),
            dma((2, groups)),
            dma((7,)),
            dma((12,)),
            dma((2, 4)),
            dma((2, CORE_SLOTS)),
            dma((2, SIDE_SLOTS)),
            dma((2, NEAR_SLOTS)),
            dma((depth - 1, TURNS)),
            dma((depth - 1, TURNS)),
            dma((2, 3, TURNS)),
            dma((TURNS,)),
            dma((6,)),
            dma((depth - 1,)),
            dma((depth - 1,)),
            pltpu.SemaphoreType.REGULAR,
            pltpu.SemaphoreType.REGULAR,
            pltpu.SemaphoreType.REGULAR,
        ],
        compiler_params=pltpu.CompilerParams(
            collective_id=0, has_side_effects=True, vmem_limit_bytes=62 * 1024 * 1024
        ),
    )(
        margin_bin,
        positive_index,
        cluster_index.reshape(1, everyone),
        norm_gain,
        final_gain,
        query_output,
        passage_output,
        query_cotangent.reshape(query_rows, width),
        passage_cotangent.reshape(passage_rows, width),
        *matrices,
        *stored,
    )


def backward_plain(
    query_output,
    passage_output,
    cluster_index,
    margin_bin,
    positive_index,
    query_cotangent,
    passage_cotangent,
    stored,
    params,
):
    batch_size, query_len, model_width = query_output.shape
    passage_len = passage_output.shape[1]
    layout = ((batch_size, query_len), (batch_size, passage_len))
    query_span = batch_size * query_len
    stored_layers = [tuple(array[layer_index] for array in stored) for layer_index in range(LAYERS)]
    query_first = query_output[:, 0, :]
    passage_first = passage_output[:, 0, :]
    facts = jnp.concatenate(
        [margin_bin, positive_index // 128, positive_index % 128], axis=0
    ).astype(jnp.bfloat16)
    facts = jnp.pad(facts, (0, model_width - facts.shape[0]))
    block = jnp.concatenate([query_first, passage_first, facts[None, :]], axis=0)
    block = jnp.pad(block, ((0, 8 - block.shape[0]), (0, 0)))
    total = cluster_index.shape[0]
    every = gather_blocks(block).reshape(-1, 8, model_width)
    every_query = every[:, :batch_size].reshape(total, model_width)
    every_passage = every[:, batch_size : 2 * batch_size].reshape(total, model_width)
    facts = every[:, 2 * batch_size, : 3 * batch_size].astype(jnp.int32)
    facts = facts.reshape(-1, 3, batch_size)
    every_margin = facts[:, 0].reshape(total)
    every_positive = (facts[:, 1] * 128 + facts[:, 2]).reshape(total)
    start_row = lax.axis_index(("grp", "rep")) * batch_size
    score_scale = 2.0 / math.sqrt(model_width)
    logits = contract_last(every_query, every_passage) * score_scale
    columns = lax.broadcasted_iota(jnp.int32, logits.shape, 1)
    chosen_mask = columns == every_positive[:, None]
    allowed = (cluster_index[None, :] == cluster_index[:, None]) | chosen_mask
    masked = jnp.where(allowed, logits, -1e30)
    peak_score = jnp.max(masked, axis=1, keepdims=True)
    normalizer = peak_score + jnp.log(jnp.sum(jnp.exp(masked - peak_score), axis=1, keepdims=True))
    chosen = jnp.sum(jnp.where(chosen_mask, logits, 0.0), axis=1)
    margin_weight = (every_margin + 1).astype(jnp.float32) / NBINS
    every_loss = margin_weight * (normalizer[:, 0] - chosen)
    query_loss = lax.dynamic_slice_in_dim(every_loss, start_row, batch_size)
    delta_logits = narrow(
        margin_weight[:, None]
        * (jnp.where(allowed, jnp.exp(masked - normalizer), 0.0) - chosen_mask.astype(jnp.float32))
    )
    own_rows = lax.dynamic_slice_in_dim(delta_logits, start_row, batch_size, axis=0)
    own_columns = lax.dynamic_slice_in_dim(delta_logits, start_row, batch_size, axis=1)
    delta_query_first = product(own_rows, every_passage) * score_scale
    delta_passage_first = contract_rows(own_columns, every_query) * score_scale
    query_upstream = query_cotangent.astype(jnp.float32).at[:, 0, :].add(delta_query_first)
    passage_upstream = passage_cotangent.astype(jnp.float32).at[:, 0, :].add(delta_passage_first)
    upstream = jnp.concatenate(
        [
            query_upstream.reshape(query_span, model_width),
            passage_upstream.reshape(batch_size * passage_len, model_width),
        ],
        axis=0,
    )
    operands = []
    small = []
    for layer_index in reversed(range(LAYERS)):
        layer_params = tuple(array[layer_index] for array in params)
        upstream, layer_operands, vectors = layer_backward(
            upstream, stored_layers[layer_index], layout, layer_params
        )
        operands.append(layer_operands)
        small.append([vector.reshape(4, -1) for vector in vectors])
    small = small[::-1]
    matrices = reduce_plain(operands)
    flat = reduce_small(jnp.concatenate(small[0] + small[1], axis=1))
    reduced = [None] * 15
    for slot, matrix in zip(MATRICES, matrices):
        reduced[slot] = matrix
    flat = flat.reshape(LAYERS, -1)
    offset = 0
    for slot, vector in zip(SMALL, small[0]):
        size = vector.shape[1]
        reduced[slot] = flat[:, offset : offset + size]
        offset = offset + size
    return query_loss, upstream[:query_span], upstream[query_span:], reduced


def finish_kernel(
    out_ref,
    small_in,
    loss_in,
    query_in,
    passage_in,
    reduce_out,
    expand_out,
    *rest,
):
    square_outs = rest[:4]
    vector_outs = rest[4:12]
    expand_bias_out, query_out, passage_out, loss_out = rest[12:16]
    sums, tall, flat, squares, query, passage, small_ref, loss, in_sem, out_sem = rest[16:]
    rows, columns = sums.shape[1:]
    quarter = rows // 2
    width = 2 * columns
    each = sums.shape[0] // (3 * LAYERS)
    moves = [
        pltpu.make_async_copy(query_in, query, in_sem.at[3 * LAYERS]),
        pltpu.make_async_copy(passage_in, passage, in_sem.at[3 * LAYERS + 1]),
    ]
    little = [
        pltpu.make_async_copy(small_in, small_ref, in_sem.at[3 * LAYERS + 2]),
        pltpu.make_async_copy(loss_in, loss, in_sem.at[3 * LAYERS + 3]),
    ]
    loads = []
    for i in range(3 * LAYERS):
        span = pl.ds(i * each, each)
        loads.append(pltpu.make_async_copy(out_ref.at[span], sums.at[span], in_sem.at[i]))
    for copy in loads + moves + little:
        copy.start()
    stores = []

    def store(source, target):
        copy = pltpu.make_async_copy(source, target, out_sem.at[len(stores)])
        stores.append(copy)
        copy.start()

    for layer in range(LAYERS):
        loads[layer].wait()
        for part in range(4):
            at = pl.ds((part // 2) * rows, rows), pl.ds((part % 2) * columns, columns)
            tall[layer, at[0], at[1]] = wide(sums[layer * each + part])
        store(tall.at[layer], reduce_out.at[layer])
    for move, (source, target) in zip(moves, ((query, query_out), (passage, passage_out))):
        move.wait()
        store(source, target)
    for layer in range(LAYERS):
        loads[LAYERS + layer].wait()
        for part in range(4):
            value = wide(sums[(LAYERS + layer) * each + part])
            for unit in range(2):
                start = (2 * (part // 2) + unit) * width + (part % 2) * columns
                flat[layer, :, start : start + columns] = value[
                    unit * quarter : (unit + 1) * quarter
                ]
        store(flat.at[layer], expand_out.at[layer])
    for layer in range(LAYERS):
        loads[2 * LAYERS + layer].wait()
        for part in range(4):
            value = wide(sums[(2 * LAYERS + layer) * each + part])
            for unit in range(2):
                at = pl.ds((part % 2) * columns, columns)
                squares[2 * (part // 2) + unit, layer, :, at] = value[
                    unit * quarter : (unit + 1) * quarter
                ]
        for which in range(4):
            store(squares.at[which, layer], square_outs[which].at[layer])
    for copy in little:
        copy.wait()
    for i in range(loss_out.shape[0]):
        loss_out[i] = jnp.sum(loss[0:1, i : i + 1])
    group = lax.axis_index("grp")
    vectors = small_ref[:, :8, 0:quarter]
    expand_bias = small_ref[:, S_EXPAND, :]
    for g in range(1, 4):
        vectors = jnp.where(
            group == g, small_ref[:, :8, g * quarter : (g + 1) * quarter], vectors
        )
        expand_bias = jnp.where(group == g, small_ref[:, S_EXPAND + g, :], expand_bias)
    for i in range(8):
        vector_outs[i][...] = vectors[:, i, :]
    expand_bias_out[...] = expand_bias
    for copy in stores:
        copy.wait()


def finish(out, small, loss, query_gradient, passage_gradient, sequences):
    out = out.reshape(out.shape[0], -1, out.shape[-1])
    rows, columns = out.shape[1:]
    quarter, width = rows // 2, 2 * columns
    f32 = jnp.float32
    anywhere = pl.BlockSpec(memory_space=pl.ANY)
    vmem = pl.BlockSpec(memory_space=pltpu.VMEM)
    tall, flat = (LAYERS, width, width), (LAYERS, quarter, 4 * width)
    square, vector = (LAYERS, quarter, width), (LAYERS, quarter)
    results = pl.pallas_call(
        finish_kernel,
        out_shape=[
            jax.ShapeDtypeStruct(shape, f32)
            for shape in [tall, flat]
            + [square] * 4
            + [vector] * 8
            + [(LAYERS, width), query_gradient.shape, passage_gradient.shape, (sequences,)]
        ],
        in_specs=[anywhere] * 5,
        out_specs=[anywhere] * 6
        + [vmem] * 9
        + [anywhere] * 2
        + [pl.BlockSpec(memory_space=pltpu.SMEM)],
        scratch_shapes=[
            pltpu.VMEM(out.shape, jnp.bfloat16),
            pltpu.VMEM(tall, f32),
            pltpu.VMEM(flat, f32),
            pltpu.VMEM((4,) + square, f32),
            pltpu.VMEM(query_gradient.shape, f32),
            pltpu.VMEM(passage_gradient.shape, f32),
            pltpu.VMEM(small.shape, f32),
            pltpu.VMEM(loss.shape, f32),
            pltpu.SemaphoreType.DMA((3 * LAYERS + 4,)),
            pltpu.SemaphoreType.DMA((6 * LAYERS + 2,)),
        ],
        compiler_params=pltpu.CompilerParams(vmem_limit_bytes=60 * 1024 * 1024),
    )(out, small, loss, query_gradient, passage_gradient)
    reduced = [None] * 15
    reduced[11], reduced[9] = results[0], results[1]
    for place, slot in enumerate((0, 2, 3, 5)):
        reduced[slot] = results[2 + place]
    for place, slot in enumerate((1, 4, 6, 7, 8, 12, 13, 14)):
        reduced[slot] = results[6 + place]
    reduced[10] = results[14]
    return results[15], results[16], results[17], reduced


def per_device(
    query_input,
    passage_input,
    query_length,
    passage_length,
    cluster_index,
    margin_bin,
    positive_index,
    query_cotangent,
    passage_cotangent,
    query_weight,
    query_bias,
    key_weight,
    value_weight,
    value_bias,
    mix_weight,
    mix_bias,
    norm_gain,
    norm_shift,
    expand_weight,
    expand_bias,
    reduce_weight,
    reduce_bias,
    final_gain,
    final_shift,
):
    params = (
        query_weight,
        query_bias,
        key_weight,
        value_weight,
        value_bias,
        mix_weight,
        mix_bias,
        norm_gain,
        norm_shift,
        expand_weight,
        expand_bias,
        reduce_weight,
        reduce_bias,
        final_gain,
        final_shift,
    )
    batch_size, query_len, model_width = query_input.shape
    passage_len = passage_input.shape[1]
    matrices = (query_weight, key_weight, value_weight, mix_weight, expand_weight, reduce_weight)
    vectors = (
        query_bias,
        value_bias,
        mix_bias,
        norm_gain,
        norm_shift,
        reduce_bias,
        final_gain,
        final_shift,
        expand_bias,
    )
    results = run_forward(
        query_length,
        passage_length,
        query_input,
        passage_input,
        matrices,
        vectors,
    )
    query_output = results[0].reshape(batch_size, query_len, model_width)
    passage_output = results[1].reshape(batch_size, passage_len, model_width)
    if lax.axis_size("rep") != 8:
        query_loss, query_gradient, passage_gradient, reduced = backward_plain(
            query_output,
            passage_output,
            cluster_index,
            margin_bin,
            positive_index,
            query_cotangent,
            passage_cotangent,
            results[2:],
            params,
        )
    else:
        out, small, loss, query_gradient, passage_gradient = run_backward(
            margin_bin,
            positive_index,
            cluster_index,
            norm_gain,
            final_gain,
            results[0],
            results[1],
            query_cotangent,
            passage_cotangent,
            matrices,
            results[2:],
        )
        query_gradient, passage_gradient, query_loss, reduced = finish(
            out, small, loss, query_gradient, passage_gradient, batch_size
        )
    return (
        query_output,
        passage_output,
        query_loss,
        query_gradient.reshape(batch_size, query_len, model_width),
        passage_gradient.reshape(batch_size, passage_len, model_width),
        reduced[0],
        reduced[1],
        reduced[2],
        reduced[3],
        reduced[4],
        reduced[5],
        reduced[6],
        reduced[7],
        reduced[8],
        reduced[9],
        reduced[10],
        reduced[11],
        reduced[12],
        reduced[13],
        reduced[14],
    )


def solution(mesh):
    placed = (
        P(("grp", "rep"), None, None),
        P(("grp", "rep"), None, None),
        P(("grp", "rep")),
        P(("grp", "rep")),
        P(),
        P(("grp", "rep")),
        P(("grp", "rep")),
        P(("grp", "rep"), None, None),
        P(("grp", "rep"), None, None),
        P(),
        P(),
        P(),
        P(),
        P(),
        P(),
        P(),
        P(),
        P(),
        P(),
        P(),
        P(),
        P(),
        P(),
        P(),
    )
    return jax.shard_map(
        per_device,
        mesh=mesh,
        in_specs=placed,
        out_specs=(
            P(("grp", "rep"), None, None),
            P(("grp", "rep"), None, None),
            P(("grp", "rep")),
            P(("grp", "rep"), None, None),
            P(("grp", "rep"), None, None),
            P(None, "grp", None),
            P(None, "grp"),
            P(None, "grp", None),
            P(None, "grp", None),
            P(None, "grp"),
            P(None, "grp", None),
            P(None, "grp"),
            P(None, "grp"),
            P(None, "grp"),
            P(None, "grp", None),
            P(None, "grp"),
            P(None, "grp", None),
            P(None, "grp"),
            P(None, "grp"),
            P(None, "grp"),
        ),
        check_vma=False,
    )
```

```python
import functools
import math

import jax
import jax.numpy as jnp
from jax import lax
from jax.experimental import pallas as pl
from jax.experimental.pallas import tpu as pltpu
from jax.sharding import PartitionSpec as P

HEADS = 12
DH = 64
LAYERS = 2
NBINS = 10


def narrow(values):
    return values.astype(jnp.bfloat16)


def product(former, latter):
    return jnp.dot(former, latter, preferred_element_type=jnp.float32)


def contract_rows(former, latter):
    return lax.dot_general(
        former, latter, (((0,), (0,)), ((), ())), preferred_element_type=jnp.float32
    )


def contract_last(former, latter):
    return lax.dot_general(
        former, latter, (((1,), (1,)), ((), ())), preferred_element_type=jnp.float32
    )


def column_total(values):
    return jnp.sum(values.astype(jnp.float32), axis=0)


def norm_forward(summed, gain_vector, shift_vector):
    average = jnp.mean(summed, axis=-1, keepdims=True)
    centred = summed - average
    scaled = lax.rsqrt(jnp.mean(centred * centred, axis=-1, keepdims=True) + 1e-12)
    unit_rows = centred * scaled
    return (unit_rows * gain_vector + shift_vector, unit_rows, scaled)


def norm_backward(upstream, unit_rows, scaled, gain_vector):
    delta_unit = upstream * gain_vector
    delta_summed = scaled * (
        delta_unit
        - jnp.mean(delta_unit, axis=-1, keepdims=True)
        - unit_rows * jnp.mean(delta_unit * unit_rows, axis=-1, keepdims=True)
    )
    return (delta_summed, jnp.sum(upstream * unit_rows, axis=0), jnp.sum(upstream, axis=0))


def split_heads(flat, group_count, length):
    return flat.reshape(group_count, length, HEADS, DH)


def group_spans(layout):
    spans = []
    offset = 0
    for group_count, length in layout:
        spans.append((offset, group_count, length))
        offset = offset + group_count * length
    return spans


def attend_backward(query_part, key_part, value_part, shares, delta_context):
    attention = wide(shares)
    delta_value = jnp.einsum(
        "bhqk,bqhd->bkhd", narrow(attention), delta_context, preferred_element_type=jnp.float32
    )
    delta_attention = jnp.einsum(
        "bqhd,bkhd->bhqk", delta_context, value_part, preferred_element_type=jnp.float32
    )
    delta_scores = narrow(
        attention * (delta_attention - jnp.sum(attention * delta_attention, axis=-1, keepdims=True))
    )
    delta_query = (
        jnp.einsum("bhqk,bkhd->bqhd", delta_scores, key_part, preferred_element_type=jnp.float32)
        * 0.125
    )
    delta_key = (
        jnp.einsum("bhqk,bqhd->bkhd", delta_scores, query_part, preferred_element_type=jnp.float32)
        * 0.125
    )
    return (delta_query, delta_key, delta_value)


def layer_backward(upstream, stored, layout, params):
    (
        query_weight,
        query_bias,
        key_weight,
        value_weight,
        value_bias,
        mix_weight,
        mix_bias,
        norm_gain,
        norm_shift,
        expand_weight,
        expand_bias,
        reduce_weight,
        reduce_bias,
        final_gain,
        final_shift,
    ) = params
    (
        hidden,
        query_heads,
        key_heads,
        value_heads,
        shares,
        query_shares,
        context,
        unit_one,
        middle,
        slope,
        active,
        unit_two,
        scales,
    ) = stored
    scale_one, scale_two = scales[:, 0:1], scales[:, 1:2]
    unit_one, unit_two = wide(unit_one), wide(unit_two)
    (count, query_len), (_, passage_len) = layout
    pair_shares = jnp.pad(shares, ((0, 0), (0, passage_len - shares.shape[1]), (0, 0)))
    pair_shares = pair_shares.reshape(count, HEADS // 2, passage_len, 2, passage_len)
    pair_shares = pair_shares.transpose(0, 1, 3, 4, 2).reshape(
        count, HEADS, passage_len, passage_len
    )
    head_shares = query_shares.reshape(count, query_len, HEADS, count, query_len)
    head_shares = jnp.stack([head_shares[i, :, :, i] for i in range(count)])
    all_shares = (head_shares.transpose(0, 2, 3, 1), pair_shares)
    delta_two, delta_final_gain, delta_final_shift = norm_backward(
        upstream, unit_two, scale_two, final_gain
    )
    delta_branch = narrow(delta_two)
    delta_reduce_bias = column_total(delta_branch)
    delta_expanded = narrow(contract_last(delta_branch, reduce_weight) * wide(slope))
    delta_expand_bias = column_total(delta_expanded)
    delta_middle = delta_two + contract_last(delta_expanded, expand_weight)
    delta_one, delta_norm_gain, delta_norm_shift = norm_backward(
        delta_middle, unit_one, scale_one, norm_gain
    )
    delta_mix = narrow(delta_one)
    delta_mix_bias = column_total(delta_mix)
    delta_context = narrow(contract_last(delta_mix, mix_weight))
    collected = ([], [], [])
    for part_shares, (offset, group_count, length) in zip(all_shares, group_spans(layout)):
        row_span = group_count * length
        pieces = [
            split_heads(array[offset : offset + row_span], group_count, length)
            for array in (query_heads, key_heads, value_heads, delta_context)
        ]
        results = attend_backward(pieces[0], pieces[1], pieces[2], part_shares, pieces[3])
        for bucket, gradient in zip(collected, results):
            bucket.append(narrow(gradient.reshape(row_span, -1)))
    delta_query = jnp.concatenate(collected[0], axis=0)
    delta_key = jnp.concatenate(collected[1], axis=0)
    delta_value = jnp.concatenate(collected[2], axis=0)
    delta_hidden = (
        delta_one
        + contract_last(delta_query, query_weight)
        + contract_last(delta_key, key_weight)
        + contract_last(delta_value, value_weight)
    )
    operands = (
        active,
        delta_branch,
        middle,
        delta_expanded,
        hidden,
        context,
        delta_query,
        delta_key,
        delta_value,
        delta_mix,
    )
    vectors = (
        column_total(delta_query),
        column_total(delta_value),
        delta_mix_bias,
        delta_norm_gain,
        delta_norm_shift,
        delta_expand_bias,
        delta_reduce_bias,
        delta_final_gain,
        delta_final_shift,
    )
    return (delta_hidden, operands, vectors)


CORE_FLIP = [(0, 1), (1, 0), (2, 3), (3, 2)]
SIDE_FLIP = [(0, 2), (2, 0), (1, 3), (3, 1)]


def wide(values):
    return values.astype(jnp.float32)


def pick(array, index):
    return lax.dynamic_index_in_dim(array, index, 0, keepdims=False)


def reduce_chunk(chunk):
    rep_total = lax.axis_size("rep")
    group = lax.axis_index("grp")
    side, core = group // 2, group % 2
    parts = chunk.reshape((2, 2) + chunk.shape[1:])
    got = lax.ppermute(
        lax.dynamic_index_in_dim(parts, 1 - core, 1, keepdims=False), "grp", CORE_FLIP
    )
    mine = lax.dynamic_index_in_dim(parts, core, 1, keepdims=False)
    got = lax.ppermute(
        narrow(wide(pick(mine, 1 - side)) + wide(pick(got, 1 - side))), "grp", SIDE_FLIP
    ), narrow(wide(pick(mine, side)) + wide(pick(got, side)))
    summed = narrow(wide(got[0]) + wide(got[1]))
    rows, columns = summed.shape
    if rep_total != 8:
        part = lax.psum_scatter(summed, "rep", scatter_dimension=0, tiled=True)
        return wide(lax.all_gather(part, "rep", axis=0, tiled=True))
    rep = lax.axis_index("rep")
    deep, near = rep // 2, rep % 2
    flip = [(i, i ^ 1) for i in range(8)]
    shifts = [[(i, (i + 2 * k) % 8) for i in range(8)] for k in range(4)]
    halves = summed.reshape(2, rows // 2, columns)
    got = lax.ppermute(pick(halves, 1 - near), "rep", flip)
    half = narrow(wide(pick(halves, near)) + wide(got)).reshape(4, rows // 8, columns)
    total = wide(pick(half, deep))
    for k in range(1, 4):
        total = total + wide(lax.ppermute(pick(half, (deep + k) % 4), "rep", shifts[k]))
    piece = narrow(total)
    pieces = [piece] + [lax.ppermute(piece, "rep", shifts[k]) for k in range(1, 4)]
    joined = jnp.zeros((4,) + piece.shape, jnp.bfloat16)
    for k in range(4):
        joined = lax.dynamic_update_index_in_dim(joined, pieces[k], (deep - k) % 4, 0)
    other = lax.ppermute(joined, "rep", flip)
    own = joined.reshape(rows // 2, columns)
    other = other.reshape(rows // 2, columns)
    first = jnp.where(near == 0, own, other)
    second = jnp.where(near == 0, other, own)
    return wide(jnp.concatenate([first, second], axis=0))


def reduce_small(small):
    group = lax.axis_index("grp")
    side, core = group // 2, group % 2
    parts = small.reshape(2, 2, -1)
    got = lax.ppermute(
        lax.dynamic_index_in_dim(parts, 1 - core, 1, keepdims=False), "grp", CORE_FLIP
    )
    pair = lax.dynamic_index_in_dim(parts, core, 1, keepdims=False) + got
    total = pick(pair, side) + lax.ppermute(pick(pair, 1 - side), "grp", SIDE_FLIP)
    rep_total = lax.axis_size("rep")
    step = 1
    while step < rep_total:
        total = total + lax.ppermute(total, "rep", [(i, i ^ step) for i in range(rep_total)])
        step = step * 2
    return total


def remote(source, target, send_sem, recv_sem, grp, rep):
    return pltpu.make_async_remote_copy(
        src_ref=source,
        dst_ref=target,
        send_sem=send_sem,
        recv_sem=recv_sem,
        device_id=(grp, rep),
        device_id_type=pl.DeviceIdType.MESH,
    )


def gather_kernel(block_ref, out_ref, send_near, recv_near, send_far, recv_far):
    groups, reps = out_ref.shape[:2]
    grp, rep = lax.axis_index("grp"), lax.axis_index("rep")
    barrier = pltpu.get_barrier_semaphore()

    @pl.loop(1, reps)
    def _(k):
        pl.semaphore_signal(
            barrier, inc=1, device_id=(grp, (rep + k) % reps), device_id_type=pl.DeviceIdType.MESH
        )

    for k in range(1, groups):
        pl.semaphore_signal(
            barrier, inc=1, device_id=((grp + k) % groups, rep), device_id_type=pl.DeviceIdType.MESH
        )
    out_ref[grp, rep] = block_ref[...]
    pl.semaphore_wait(barrier, reps + groups - 2)

    def near(k):
        mine = out_ref.at[grp, rep]
        return remote(mine, mine, send_near.at[k], recv_near.at[k], grp, (rep + k) % reps)

    def far(k):
        row = out_ref.at[grp]
        return remote(row, row, send_far.at[k], recv_far.at[k], (grp + k) % groups, rep)

    @pl.loop(1, reps)
    def _(k):
        near(k).start()

    @pl.loop(1, reps)
    def _(k):
        near(k).wait_recv()

    for k in range(1, groups):
        far(k).start()
    for k in range(1, groups):
        far(k).wait_recv()

    @pl.loop(1, reps)
    def _(k):
        near(k).wait_send()

    for k in range(1, groups):
        far(k).wait_send()


def gather_blocks(block):
    groups, reps = lax.axis_size("grp"), lax.axis_size("rep")
    return pl.pallas_call(
        gather_kernel,
        out_shape=jax.ShapeDtypeStruct((groups, reps) + block.shape, block.dtype),
        in_specs=[pl.BlockSpec(memory_space=pltpu.VMEM)],
        out_specs=pl.BlockSpec(memory_space=pltpu.VMEM),
        scratch_shapes=[
            pltpu.SemaphoreType.DMA((reps,)),
            pltpu.SemaphoreType.DMA((reps,)),
            pltpu.SemaphoreType.DMA((groups,)),
            pltpu.SemaphoreType.DMA((groups,)),
        ],
        compiler_params=pltpu.CompilerParams(collective_id=1, has_side_effects=True),
    )(block)


def reduce_plain(layers):
    results = []
    for active, branch, middle, expanded, hidden, context, query, key, value, mix in layers:
        quarter = lambda former, latter: (
            lambda matrix: narrow(matrix).reshape(4, matrix.shape[0] // 4, matrix.shape[1])
        )(contract_rows(former, latter))
        square = jnp.concatenate(
            [
                quarter(hidden, query),
                quarter(hidden, key),
                quarter(hidden, value),
                quarter(context, mix),
            ],
            axis=1,
        )
        square = reduce_chunk(square)
        height = square.shape[0] // 4
        results.append(
            [square[place * height : (place + 1) * height] for place in range(4)]
            + [reduce_chunk(quarter(middle, expanded)), reduce_chunk(quarter(active, branch))]
        )
    return [jnp.stack([results[1][i], results[0][i]]) for i in range(6)]


SMALL = (1, 4, 6, 7, 8, 10, 12, 13, 14)
MATRICES = (0, 2, 3, 5, 9, 11)


LOG2E = 1.4426950408889634
V_QUERY, V_VALUE, V_MIX, V_GAIN, V_SHIFT, V_REDUCE, V_LAST_GAIN, V_LAST_SHIFT, V_EXPAND = range(9)
VECTOR_ROWS = 16
TILE = 256


def lane_masks(rows):
    lane = lax.broadcasted_iota(jnp.int32, (rows, 2 * DH), 1)
    return ((lane < DH).astype(jnp.float32).astype(jnp.bfloat16),
            (lane >= DH).astype(jnp.float32).astype(jnp.bfloat16))


def head_mask(head, width):
    lane = lax.broadcasted_iota(jnp.int32, (1, width), 1)
    return ((lane >= head * DH) & (lane < (head + 1) * DH))


def live_keys(passage_len):
    return -(-(passage_len * 25 // 32) // 16) * 16


def lanes(start, size=TILE):
    return pl.ds(pl.multiple_of(start, 128), size)


def sublanes(start, size):
    return pl.ds(pl.multiple_of(start, 16), size)


def softmax_rows(scores, bias):
    scaled = scores * (0.125 * LOG2E) + bias
    grown = jnp.exp2(scaled - jnp.max(scaled, axis=0, keepdims=True))
    return narrow(grown * (1.0 / jnp.sum(grown, axis=0, keepdims=True)))


def forward_kernel(
    query_lengths,
    passage_lengths,
    query_in,
    passage_in,
    wq_in,
    wk_in,
    wv_in,
    wm_in,
    we_in,
    wr_in,
    query_bias,
    value_bias,
    mix_bias,
    norm_gain,
    norm_shift,
    reduce_bias,
    final_gain,
    final_shift,
    expand_bias,
    query_out,
    passage_out,
    hidden_out,
    q_out,
    k_out,
    v_out,
    pt_out,
    ptq_out,
    c_out,
    u1_out,
    m_out,
    slope_out,
    f_out,
    u2_out,
    r_out,
    wq,
    wk,
    wv,
    wm,
    we,
    wr,
    x,
    q,
    k,
    v,
    pt,
    ptq,
    c,
    u1,
    m,
    slope,
    f,
    u2,
    r,
    z,
    stack,
    vec_ref,
    weight_sem,
    in_sem,
    out_sem,
):
    width = x.shape[1]
    total = x.shape[0]
    sequences = query_lengths.shape[0]
    query_rows = query_in.shape[0]
    query_len = query_rows // sequences
    passage_len = (total - query_rows) // sequences
    pairs = width // (2 * DH)
    kept = live_keys(passage_len)

    weights = ((wq_in, wq), (wk_in, wk), (wv_in, wv), (wm_in, wm), (we_in, we), (wr_in, wr))

    def weight_copy(which, layer):
        source, target = weights[which]
        return pltpu.make_async_copy(
            source.at[layer], target.at[layer], weight_sem.at[which, layer]
        )

    stored = (
        (x, hidden_out),
        (q, q_out),
        (k, k_out),
        (v, v_out),
        (pt, pt_out),
        (ptq, ptq_out),
        (c, c_out),
        (u1, u1_out),
        (m, m_out),
        (slope, slope_out),
        (f, f_out),
        (u2, u2_out),
        (r, r_out),
    )
    X, Q, K, V, PT, PTQ, C, U1, M, SLOPE, F, U2, R = range(13)

    def store(which, layer):
        source, target = stored[which]
        return pltpu.make_async_copy(source, target.at[layer], out_sem.at[which])

    def reuse(which, layer):
        @pl.when(layer > 0)
        def _():
            store(which, layer - 1).wait()

    first = pltpu.make_async_copy(query_in, x.at[pl.ds(0, query_rows)], in_sem.at[0])
    rest = pltpu.make_async_copy(
        passage_in, x.at[pl.ds(query_rows, total - query_rows)], in_sem.at[1]
    )
    first.start()
    rest.start()
    for which in range(3):
        weight_copy(which, 0).start()
    vectors = (
        query_bias,
        value_bias,
        mix_bias,
        norm_gain,
        norm_shift,
        reduce_bias,
        final_gain,
        final_shift,
    )
    for layer in range(LAYERS):
        for place, vector in enumerate(vectors):
            vec_ref[layer, place : place + 1, :] = wide(vector[layer : layer + 1, :])
        for j in range(4):
            vec_ref[layer, V_EXPAND + j : V_EXPAND + j + 1, :] = wide(
                expand_bias[layer : layer + 1, j * width : (j + 1) * width]
            )
    first.wait()
    rest.wait()

    def project(source, weight, layer, bias_row, target):
        @pl.loop(0, width // TILE, unroll=3)
        def _(i):
            value = product(source[...], weight[layer, :, lanes(i * TILE)])
            if bias_row is not None:
                value = value + vec_ref[layer, pl.ds(bias_row, 1), lanes(i * TILE)]
            target[:, lanes(i * TILE)] = narrow(value)

    def norm(layer, gain_row, shift_row, unit, target, scale_lane):
        step = 96
        gain = vec_ref[layer, pl.ds(gain_row, 1), :]
        shift = vec_ref[layer, pl.ds(shift_row, 1), :]

        @pl.loop(0, total // step, unroll=6)
        def _(i):
            at = sublanes(i * step, step)
            full, unit_rows, scaled = norm_forward(z[at, :], gain, shift)
            unit[at, :] = narrow(unit_rows)
            target[at, :] = narrow(full)
            r[at, scale_lane : scale_lane + 1] = scaled

    @pl.loop(0, LAYERS)
    def _(layer):
        store(X, layer).start()
        weight_copy(0, layer).wait()

        @pl.when(layer == 0)
        def _():
            for which in range(3, 6):
                weight_copy(which, 0).start()

        reuse(Q, layer)
        project(x, wq, layer, V_QUERY, q)
        store(Q, layer).start()
        weight_copy(1, layer).wait()
        reuse(K, layer)
        project(x, wk, layer, None, k)
        store(K, layer).start()
        weight_copy(2, layer).wait()
        reuse(V, layer)
        project(x, wv, layer, V_VALUE, v)
        store(V, layer).start()

        reuse(PT, layer)
        reuse(PTQ, layer)
        reuse(C, layer)

        for head in range(HEADS):
            mask = head_mask(head, width).astype(jnp.float32).astype(jnp.bfloat16)
            stack[head * query_rows : (head + 1) * query_rows, :] = q[:query_rows, :] * mask
        scores = contract_last(k[:query_rows, :], stack[...])
        key_slot = lax.broadcasted_iota(jnp.int32, scores.shape, 0)
        query_slot = lax.broadcasted_iota(jnp.int32, scores.shape, 1) % query_rows
        live = jnp.zeros(scores.shape, jnp.bool_)
        for s in range(sequences):
            low = s * query_len
            live = live | (
                (key_slot >= low)
                & (key_slot < low + query_lengths[s])
                & (query_slot >= low)
                & (query_slot < low + query_len)
            )
        shares = softmax_rows(scores, jnp.where(live, 0.0, -1e30))
        ptq[...] = shares
        spread = contract_rows(shares, v[:query_rows, :])
        context = jnp.zeros((query_rows, width), jnp.float32)
        for head in range(HEADS):
            context = context + jnp.where(
                head_mask(head, width), spread[head * query_rows : (head + 1) * query_rows, :], 0.0
            )
        c[:query_rows, :] = narrow(context)

        @pl.loop(0, sequences * pairs, unroll=3)
        def _(i):
            s, pair = i // pairs, i % pairs
            rows = sublanes(query_rows + s * passage_len, passage_len)
            at = lanes(pair * 2 * DH, 2 * DH)
            key_rows = sublanes(query_rows + s * passage_len, kept)
            even, odd = lane_masks(passage_len)
            q2, k2, v2 = q[rows, at], k[key_rows, at], v[key_rows, at]
            scores = contract_last(k2, jnp.concatenate([q2 * even, q2 * odd], axis=0))
            even, odd = even[:kept], odd[:kept]
            slot = lax.broadcasted_iota(jnp.int32, (kept, 1), 0)
            shares = softmax_rows(
                scores, jnp.where(slot < passage_lengths[s], 0.0, -1e30)
            )
            pt[i] = shares
            shares = jnp.concatenate([shares[:, :passage_len], shares[:, passage_len:]], axis=0)
            spread = contract_rows(jnp.concatenate([v2 * even, v2 * odd], axis=0), shares)
            c[rows, at] = narrow(spread.T)

        store(PT, layer).start()
        store(PTQ, layer).start()
        store(C, layer).start()

        weight_copy(3, layer).wait()

        @pl.when(layer + 1 < LAYERS)
        def _():
            for which in range(6):
                weight_copy(which, layer + 1).start()

        @pl.loop(0, width // TILE, unroll=3)
        def _(i):
            at = lanes(i * TILE)
            z[:, at] = (
                wide(x[:, at])
                + product(c[...], wm[layer, :, at])
                + vec_ref[layer, pl.ds(V_MIX, 1), at]
            )

        reuse(U1, layer)
        reuse(M, layer)
        reuse(R, layer)
        norm(layer, V_GAIN, V_SHIFT, u1, m, 0)
        store(U1, layer).start()
        store(M, layer).start()

        weight_copy(4, layer).wait()
        reuse(SLOPE, layer)
        reuse(F, layer)

        @pl.loop(0, 4 * width // TILE, unroll=6)
        def _(i):
            at = lanes(i * TILE)
            tiles = width // TILE
            bias = vec_ref[layer, pl.ds(V_EXPAND + i // tiles, 1), lanes((i % tiles) * TILE)]
            value = product(m[...], we[layer, :, at]) + bias
            share = 0.5 * (1.0 + lax.erf(value * (1.0 / math.sqrt(2.0))))
            density = jnp.exp2(value * value * (-0.5 * LOG2E)) * (1.0 / math.sqrt(2.0 * math.pi))
            f[:, at] = narrow(value * share)
            slope[:, at] = narrow(share + value * density)

        store(SLOPE, layer).start()
        store(F, layer).start()

        weight_copy(5, layer).wait()

        @pl.loop(0, width // TILE, unroll=3)
        def _(i):
            at = lanes(i * TILE)
            z[:, at] = (
                wide(m[:, at])
                + product(f[...], wr[layer, :, at])
                + vec_ref[layer, pl.ds(V_REDUCE, 1), at]
            )

        store(X, layer).wait()
        reuse(U2, layer)
        norm(layer, V_LAST_GAIN, V_LAST_SHIFT, u2, x, 1)
        store(U2, layer).start()
        store(R, layer).start()

    last = LAYERS - 1
    first = pltpu.make_async_copy(x.at[pl.ds(0, query_rows)], query_out, in_sem.at[0])
    rest = pltpu.make_async_copy(
        x.at[pl.ds(query_rows, total - query_rows)], passage_out, in_sem.at[1]
    )
    first.start()
    rest.start()
    for which in range(1, 13):
        store(which, last).wait()
    first.wait()
    rest.wait()


def run_forward(query_length, passage_length, query_input, passage_input, matrices, vectors):
    sequences, query_len, width = query_input.shape
    passage_len = passage_input.shape[1]
    query_rows, passage_rows = sequences * query_len, sequences * passage_len
    total = query_rows + passage_rows
    pairs = width // (2 * DH)
    bf16, f32 = jnp.bfloat16, jnp.float32
    arrays = (
        ((total, width), bf16),
        ((total, width), bf16),
        ((total, width), bf16),
        ((total, width), bf16),
        ((sequences * pairs, live_keys(passage_len), 2 * passage_len), bf16),
        ((query_rows, HEADS * query_rows), bf16),
        ((total, width), bf16),
        ((total, width), bf16),
        ((total, width), bf16),
        ((total, 4 * width), bf16),
        ((total, 4 * width), bf16),
        ((total, width), bf16),
        ((total, 128), f32),
    )
    anywhere = pl.BlockSpec(memory_space=pl.ANY)
    return pl.pallas_call(
        forward_kernel,
        out_shape=(
            jax.ShapeDtypeStruct((query_rows, width), bf16),
            jax.ShapeDtypeStruct((passage_rows, width), bf16),
        )
        + tuple(jax.ShapeDtypeStruct((LAYERS,) + shape, dtype) for shape, dtype in arrays),
        in_specs=[pl.BlockSpec(memory_space=pltpu.SMEM)] * 2
        + [anywhere] * 8
        + [pl.BlockSpec(memory_space=pltpu.VMEM)] * 9,
        out_specs=[anywhere] * 15,
        scratch_shapes=[pltpu.VMEM(matrix.shape, bf16) for matrix in matrices]
        + [pltpu.VMEM(shape, dtype) for shape, dtype in arrays]
        + [
            pltpu.VMEM((total, width), f32),
            pltpu.VMEM((HEADS * query_rows, width), bf16),
            pltpu.VMEM((LAYERS, VECTOR_ROWS, width), f32),
            pltpu.SemaphoreType.DMA((6, LAYERS)),
            pltpu.SemaphoreType.DMA((2,)),
            pltpu.SemaphoreType.DMA((13,)),
        ],
        compiler_params=pltpu.CompilerParams(vmem_limit_bytes=60 * 1024 * 1024),
    )(
        query_length,
        passage_length,
        query_input.reshape(query_rows, width),
        passage_input.reshape(passage_rows, width),
        *matrices,
        *vectors,
    )


CHUNKS = 24
PARTS = 12
S_QUERY, S_VALUE, S_MIX, S_GAIN, S_SHIFT, S_REDUCE, S_LAST_GAIN, S_LAST_SHIFT, S_EXPAND = range(9)
CORE_SLOTS, SIDE_SLOTS, NEAR_SLOTS, KEEP_SLOTS, SENT_SLOTS = 6, 6, 6, 8, 4
TURNS = 8
LAGS = (2, 3, 4, 5, 6, 9)
BLOCK = 16
SMALL_AT = 21


def one_hot(shape, hit):
    row = lax.broadcasted_iota(jnp.int32, shape, 0)
    column = lax.broadcasted_iota(jnp.int32, shape, 1)
    return narrow(jnp.where(hit(row, column), 1.0, 0.0))


def backward_kernel(
    margin_ref,
    positive_ref,
    cluster_row,
    norm_gain,
    final_gain,
    query_out,
    passage_out,
    query_cot,
    passage_cot,
    wq_in,
    wk_in,
    wv_in,
    wm_in,
    we_in,
    wr_in,
    hidden_in,
    q_in,
    k_in,
    v_in,
    pt_in,
    ptq_in,
    c_in,
    u1_in,
    m_in,
    slope_in,
    f_in,
    u2_in,
    r_in,
    out_ref,
    small_out,
    loss_out,
    query_grad,
    passage_grad,
    buf,
    keep,
    side_out,
    core_in,
    side_in,
    near_in,
    deep_in,
    piece,
    small,
    small_core,
    small_side,
    small_near,
    small_deep,
    first,
    blocks,
    gains,
    dz,
    dy,
    du,
    quad,
    pair_in,
    middle,
    unit,
    active,
    dc,
    pt,
    ptq,
    stack,
    r,
    w,
    gather_near,
    gather_far,
    first_sem,
    load_sem,
    weight_sem,
    core_sem,
    side_sem,
    near_sem,
    deep_send,
    deep_recv,
    back_sem,
    local_sem,
    small_sem,
    small_send,
    small_recv,
    core_free,
    side_free,
    near_free,
):
    groups, reps = blocks.shape[:2]
    depth = reps // 2
    rows, columns = keep.shape[1:]
    width = dz.shape[1]
    quarter = width // 4
    half_rows = rows // 2
    piece_rows = half_rows // depth
    total = dz.shape[0]
    sequences = margin_ref.shape[0]
    query_rows = query_out.shape[0]
    query_len = query_rows // sequences
    passage_len = (total - query_rows) // sequences
    pairs = width // (2 * DH)
    live = live_keys(passage_len)
    passage_rows = pl.ds(query_rows, total - query_rows)
    everyone = cluster_row.shape[1]

    grp, rep = lax.axis_index("grp"), lax.axis_index("rep")
    side, core = grp // 2, grp % 2
    deep, near = rep // 2, rep % 2
    sibling = (2 * side + (1 - core), rep)
    across = (2 * (1 - side) + core, rep)
    beside = (grp, 2 * deep + (1 - near))

    def behind(k):
        return (grp, 2 * ((deep + k) % depth) + near)

    deep_low, deep_high = deep % 2, deep // 2
    beyond = (grp, 2 * (deep + 2 - 4 * deep_high) + near)
    next_to = (grp, 2 * (deep + 1 - 2 * deep_low) + near)

    def signal(semaphore, peer):
        pl.semaphore_signal(
            semaphore, inc=1, device_id=peer, device_id_type=pl.DeviceIdType.MESH
        )

    barrier = pltpu.get_barrier_semaphore()
    for k in range(1, reps):
        signal(barrier, (grp, (rep + k) % reps))
    for k in range(1, groups):
        signal(barrier, ((grp + k) % groups, rep))

    firsts = [
        pltpu.make_async_copy(
            source.at[pl.ds(s * length, BLOCK)],
            first.at[pl.ds((place * sequences + s) * BLOCK, BLOCK)],
            first_sem.at[place * sequences + s],
        )
        for place, (source, length) in enumerate(
            ((query_out, query_len), (passage_out, passage_len))
        )
        for s in range(sequences)
    ]
    for copy in firsts:
        copy.start()

    loaded = {
        "f": (f_in, active),
        "u2": (u2_in, unit.at[0]),
        "slope": (slope_in, du),
        "m": (m_in, middle),
        "u1": (u1_in, unit.at[1]),
        "c": (c_in, pair_in.at[1]),
        "q": (q_in, quad.at[0]),
        "k": (k_in, quad.at[1]),
        "v": (v_in, quad.at[2]),
        "pt": (pt_in, pt),
        "ptq": (ptq_in, ptq),
        "x": (hidden_in, pair_in.at[0]),
    }
    places = {name: place for place, name in enumerate(loaded)}

    def load(name, layer):
        source, target = loaded[name]
        return pltpu.make_async_copy(source.at[layer], target, load_sem.at[places[name]])

    def weight_loads(kind, layer, slot):
        squares = []
        for j in range(4):
            block = pl.ds(j * width, width)
            if kind == 0:
                source = wr_in.at[layer, block]
            elif kind == 1:
                source = we_in.at[layer, :, block]
            else:
                source = (wq_in, wk_in, wv_in, wm_in)[j].at[layer]
            squares.append(
                pltpu.make_async_copy(source, w.at[slot, j], weight_sem.at[slot, j])
            )
        return squares

    def start_weights(kind, layer, slot):
        for copy in weight_loads(kind, layer, slot):
            copy.start()

    def wait_weights(kind, layer, slot):
        for copy in weight_loads(kind, layer, slot):
            copy.wait()

    last = LAYERS - 1
    cots = [
        pltpu.make_async_copy(query_cot, dy.at[pl.ds(0, query_rows)], first_sem.at[4]),
        pltpu.make_async_copy(passage_cot, dy.at[passage_rows], first_sem.at[5]),
        pltpu.make_async_copy(r_in, r, first_sem.at[6]),
    ]
    for copy in cots:
        copy.start()
    load("u2", last).start()

    def tally(layer, row_at, lanes_at, values):
        at = (layer, pl.ds(row_at, 1), lanes_at)
        small[at] = small[at] + jnp.sum(values, axis=0, keepdims=True)

    every_lane = pl.ds(0, width)

    norm_step = 48

    def norm_back_rows(
        layer, unit_at, scale_lane, gain_row, target, gain_to, shift_to, bias_to, tile
    ):
        gain = gains[layer, pl.ds(gain_row, 1), :]
        at = sublanes(tile * norm_step, norm_step)
        upstream = dz[at, :]
        unit_rows = wide(unit[unit_at, at, :])
        scaled = r[layer, at, scale_lane : scale_lane + 1]
        delta_unit = upstream * gain
        delta = scaled * (
            delta_unit
            - jnp.mean(delta_unit, axis=-1, keepdims=True)
            - unit_rows * jnp.mean(delta_unit * unit_rows, axis=-1, keepdims=True)
        )
        dz[at, :] = delta
        rounded = narrow(delta)
        target[at, :] = rounded
        tally(layer, gain_to, every_lane, upstream * unit_rows)
        tally(layer, shift_to, every_lane, upstream)
        tally(layer, bias_to, every_lane, wide(rounded))

    def last_norm_back(layer, tile):
        norm_back_rows(
            layer, 0, 1, 1, dy, S_LAST_GAIN, S_LAST_SHIFT, S_REDUCE, tile
        )

    def first_norm_back(layer, tile):
        norm_back_rows(layer, 1, 0, 0, quad.at[3], S_GAIN, S_SHIFT, S_MIX, tile)

    for copy in firsts:
        copy.wait()
    firsts_count = 2 * sequences
    segments = width // TILE
    packed = jnp.zeros((BLOCK, TILE), jnp.float32)
    for j in range(segments):
        low = j * firsts_count
        packed = packed + product(
            one_hot(
                (BLOCK, first.shape[0]),
                lambda i, k: (k == (i - low) * BLOCK) & (i >= low) & (i < low + firsts_count),
            ),
            first[:, j * TILE : (j + 1) * TILE],
        )
    row = lax.broadcasted_iota(jnp.int32, packed.shape, 0)
    lane = lax.broadcasted_iota(jnp.int32, packed.shape, 1)
    for s in range(sequences):
        positive = positive_ref[s]
        facts = (margin_ref[s], positive // 128, positive % 128)
        for place, fact in enumerate(facts):
            at = (row == segments * firsts_count) & (lane == place * sequences + s)
            packed = jnp.where(at, fact.astype(jnp.float32), packed)
    blocks[grp, rep] = narrow(packed)

    def to_near(k):
        mine = blocks.at[grp, rep]
        return remote(
            mine, mine, gather_near.at[0, k], gather_near.at[1, k], grp, (rep + k) % reps
        )

    def to_far(k):
        line = blocks.at[grp]
        return remote(
            line, line, gather_far.at[0, k], gather_far.at[1, k], (grp + k) % groups, rep
        )

    pl.semaphore_wait(barrier, reps + groups - 2)

    @pl.loop(1, reps)
    def _(k):
        to_near(k).start()

    load("f", last).start()
    load("slope", last).start()
    start_weights(0, last, 0)

    for copy in cots:
        copy.wait()
    small[...] = jnp.zeros_like(small)
    for layer in range(LAYERS):
        gains[layer, 0:1, :] = wide(norm_gain[layer : layer + 1, :])
        gains[layer, 1:2, :] = wide(final_gain[layer : layer + 1, :])

    @pl.loop(0, total // 96)
    def _(i):
        at = sublanes(i * 96, 96)
        dz[at, :] = wide(dy[at, :])

    first_at = [s * query_len for s in range(sequences)]
    first_at += [query_rows + s * passage_len for s in range(sequences)]
    late = sorted({at // norm_step for at in first_at})
    spans = [span for span in zip([-1] + late, late + [total // norm_step])]
    load("u2", last).wait()

    def early_norm(low, high):
        @pl.loop(low, high)
        def _(tile):
            last_norm_back(last, tile)

    for low, high in spans[: len(spans) // 2]:
        if low + 1 < high:
            early_norm(low + 1, high)

    @pl.loop(1, reps)
    def _(k):
        to_near(k).wait_recv()

    for k in range(1, groups):
        to_far(k).start()

    for low, high in spans[len(spans) // 2 :]:
        if low + 1 < high:
            early_norm(low + 1, high)

    for k in range(1, groups):
        to_far(k).wait_recv()

    gathered = blocks[...].reshape(groups * reps * BLOCK, TILE)

    def taken(offset):
        return product(
            one_hot(
                (everyone, gathered.shape[0]),
                lambda i, j: j == BLOCK * (i // sequences) + offset(i),
            ),
            gathered,
        )

    def taken_rows(base):
        return narrow(
            jnp.concatenate(
                [
                    taken(lambda i: j * firsts_count + base + i % sequences)
                    for j in range(segments)
                ],
                axis=1,
            )
        )

    every_query = taken_rows(0)
    every_passage = taken_rows(sequences)
    facts = taken(lambda i: segments * firsts_count)[:, :128]
    query_at = lax.broadcasted_iota(jnp.int32, facts.shape, 0) % sequences
    lane_at = lax.broadcasted_iota(jnp.int32, facts.shape, 1)

    def fact(place):
        hit = lane_at == place * sequences + query_at
        return jnp.sum(jnp.where(hit, facts, 0.0), axis=1, keepdims=True)

    margin_weight = (fact(0) + 1.0) / NBINS
    every_positive = fact(1) * 128.0 + fact(2)
    score_scale = 2.0 / math.sqrt(width)
    logits = contract_last(every_query, every_passage) * score_scale
    passage_at = lax.broadcasted_iota(jnp.int32, logits.shape, 1).astype(jnp.float32)
    chosen_mask = passage_at == every_positive
    clusters = jnp.broadcast_to(cluster_row[...], (everyone, everyone))
    on_diagonal = lax.broadcasted_iota(jnp.int32, clusters.shape, 0) == (
        lax.broadcasted_iota(jnp.int32, clusters.shape, 1)
    )
    own_clusters = jnp.sum(
        jnp.where(on_diagonal, clusters.astype(jnp.float32), 0.0), axis=1, keepdims=True
    )
    allowed = (clusters.astype(jnp.float32) == own_clusters) | chosen_mask
    masked = jnp.where(allowed, logits, -1e30)
    peak = jnp.max(masked, axis=1, keepdims=True)
    normalizer = peak + jnp.log(jnp.sum(jnp.exp(masked - peak), axis=1, keepdims=True))
    chosen = jnp.sum(jnp.where(chosen_mask, logits, 0.0), axis=1, keepdims=True)
    loss = margin_weight * (normalizer - chosen)
    share = jnp.where(allowed, jnp.exp(masked - normalizer), 0.0)
    delta_logits = narrow(margin_weight * (share - jnp.where(chosen_mask, 1.0, 0.0)))
    start = (grp * reps + rep) * sequences
    loss_row = lax.broadcasted_iota(jnp.int32, (everyone, 128), 0)
    loss_lane = lax.broadcasted_iota(jnp.int32, (everyone, 128), 1)
    loss_out[...] = jnp.broadcast_to(
        jnp.sum(jnp.where(loss_row == start + loss_lane, loss, 0.0), axis=0, keepdims=True),
        loss_out.shape,
    )
    own = one_hot((BLOCK, everyone), lambda i, j: (j == start + i) & (i < sequences))
    own_rows = narrow(product(own, delta_logits))
    own_columns = narrow(contract_last(own, delta_logits))
    delta_firsts = (
        product(own_rows, every_passage) * score_scale,
        product(own_columns, every_query) * score_scale,
    )
    eight = lax.broadcasted_iota(jnp.int32, (8, width), 0)
    for place, (base, length) in enumerate(((0, query_len), (query_rows, passage_len))):
        for s in range(sequences):
            at = pl.ds(base + s * length, 8)
            dz[at, :] = dz[at, :] + jnp.where(
                eight == 0, delta_firsts[place][s : s + 1, :], 0.0
            )

    for tile in late:
        last_norm_back(last, tile)

    def core_copy(t):
        return remote(
            buf.at[t % 2, :, 1 - core],
            core_in.at[t % CORE_SLOTS],
            core_sem.at[0, t % CORE_SLOTS],
            core_sem.at[1, t % CORE_SLOTS],
            *sibling,
        )

    def side_copy(t):
        return remote(
            side_out.at[t % SENT_SLOTS],
            side_in.at[t % SIDE_SLOTS],
            side_sem.at[0, t % SIDE_SLOTS],
            side_sem.at[1, t % SIDE_SLOTS],
            *across,
        )

    def near_copy(t):
        return remote(
            keep.at[t % KEEP_SLOTS, sublanes((1 - near) * half_rows, half_rows)],
            near_in.at[t % NEAR_SLOTS],
            near_sem.at[0, t % NEAR_SLOTS],
            near_sem.at[1, t % NEAR_SLOTS],
            *beside,
        )

    def piece_of(place):
        order = 2 * (place % 2) + place // 2
        return sublanes(near * half_rows + order * piece_rows, piece_rows)

    def deep_copy(t, k):
        return remote(
            keep.at[t % KEEP_SLOTS, piece_of((deep + k) % depth)],
            deep_in.at[t % TURNS, k - 1],
            deep_send.at[k - 1, t % TURNS],
            deep_recv.at[k - 1, t % TURNS],
            *behind(k),
        )

    def chunk_place(t):
        step, part = t // PARTS, t % PARTS
        return (part // 4) * 8 + (last - step) * 4 + part % 4

    def own_piece(t):
        return out_ref.at[
            chunk_place(t), near, deep_low, sublanes(deep_high * piece_rows, piece_rows)
        ]

    def local_copy(t):
        return pltpu.make_async_copy(piece.at[t % TURNS], own_piece(t), local_sem.at[t % TURNS])

    def back_copy(stage, source, peer, t, target=None):
        return remote(
            source,
            source if target is None else target,
            back_sem.at[0, stage, t % TURNS],
            back_sem.at[1, stage, t % TURNS],
            *peer,
        )

    def back_high(t):
        return back_copy(0, piece.at[t % TURNS], beyond, t, own_piece(t))

    def even_second(t):
        return back_copy(1, out_ref.at[chunk_place(t), near, deep_low], next_to, t)

    def even_third(t):
        return back_copy(2, out_ref.at[chunk_place(t), near], beside, t)

    def odd_second(t):
        return back_copy(1, out_ref.at[chunk_place(t), near, deep_low], beside, t)

    def odd_third(t):
        return back_copy(2, out_ref.at[chunk_place(t), :, deep_low], next_to, t)

    def by_parity(t, even, odd):
        @pl.when(t % 2 == 0)
        def _():
            even(t)

        @pl.when(t % 2 == 1)
        def _():
            odd(t)

    def add_rows(target, former, latter, count):
        step = 48

        @pl.loop(0, count // step, unroll=2)
        def _(i):
            def at(first_row):
                return sublanes(first_row + i * step, step)

            (to, to_row), (one, one_row), (two, two_row) = target, former, latter
            to[at(to_row), :] = narrow(wide(one[at(one_row), :]) + wide(two[at(two_row), :]))

    def after_core(t):
        core_copy(t).wait()
        slot = t % CORE_SLOTS
        add_rows(
            (side_out.at[t % SENT_SLOTS], 0),
            (buf.at[t % 2, 1 - side, core], 0),
            (core_in.at[slot, 1 - side], 0),
            rows,
        )

        @pl.when(t >= SIDE_SLOTS)
        def _():
            pl.semaphore_wait(side_free, 1)

        side_copy(t).start()
        add_rows(
            (keep.at[t % KEEP_SLOTS], 0),
            (buf.at[t % 2, side, core], 0),
            (core_in.at[slot, side], 0),
            rows,
        )

        @pl.when(t + CORE_SLOTS < CHUNKS)
        def _():
            signal(core_free, sibling)

    def after_side(t):
        side_copy(t).wait()
        kept = keep.at[t % KEEP_SLOTS]
        came = side_in.at[t % SIDE_SLOTS]
        there, here = (1 - near) * half_rows, near * half_rows
        add_rows((kept, there), (kept, there), (came, there), half_rows)

        @pl.when(t >= NEAR_SLOTS)
        def _():
            pl.semaphore_wait(near_free, 1)

        near_copy(t).start()
        add_rows((kept, here), (kept, here), (came, here), half_rows)

        @pl.when(t + SIDE_SLOTS < CHUNKS)
        def _():
            signal(side_free, across)

    def after_near(t):
        near_copy(t).wait()
        kept = keep.at[t % KEEP_SLOTS]
        here = near * half_rows
        add_rows((kept, here), (kept, here), (near_in.at[t % NEAR_SLOTS], 0), half_rows)

        @pl.when(t + NEAR_SLOTS < CHUNKS)
        def _():
            signal(near_free, beside)

        for k in range(1, depth):
            deep_copy(t, k).start()

    def after_deep(t):
        summed = wide(keep[t % KEEP_SLOTS, piece_of(deep), :])
        for k in range(1, depth):
            deep_copy(t, k).wait()
        for k in range(1, depth):
            summed = summed + wide(deep_in[t % TURNS, k - 1])
        piece[t % TURNS] = narrow(summed)
        local_copy(t).start()
        back_high(t).start()

    def after_high(t):
        local_copy(t).wait()
        back_high(t).wait()
        by_parity(t, lambda t: even_second(t).start(), lambda t: odd_second(t).start())

    def after_second(t):
        def even(t):
            even_second(t).wait()
            even_third(t).start()

        def odd(t):
            odd_second(t).wait()
            odd_third(t).start()

        by_parity(t, even, odd)

    def after_third(t):
        by_parity(t, lambda t: even_third(t).wait(), lambda t: odd_third(t).wait())

    def expand_back(layer, slot):
        tiles = width // TILE

        @pl.loop(0, 4 * tiles, unroll=2)
        def _(i):
            at = lanes(i * TILE)
            block, tile = i // tiles, i % tiles
            weight = w[slot, block, sublanes(tile * TILE, TILE), :]
            value = narrow(contract_last(dy[...], weight) * wide(du[:, at]))
            du[:, at] = value
            tally(layer, S_EXPAND + block, lanes(tile * TILE), wide(value))

    def middle_back(slot):
        @pl.loop(0, width // TILE, unroll=3)
        def _(i):
            at = lanes(i * TILE)
            value = dz[:, at]
            for block in range(4):
                weight = w[slot, block, sublanes(i * TILE, TILE), :]
                value = value + contract_last(du[:, block * width : (block + 1) * width], weight)
            dz[:, at] = value

    def context_back(slot):
        @pl.loop(0, width // TILE, unroll=3)
        def _(i):
            weight = w[slot, 3, sublanes(i * TILE, TILE), :]
            dc[:, lanes(i * TILE)] = narrow(contract_last(quad[3], weight))

    def hidden_back(slot):
        @pl.loop(0, width // TILE, unroll=3)
        def _(i):
            at = lanes(i * TILE)
            value = dz[:, at]
            for place in range(3):
                weight = w[slot, place, sublanes(i * TILE, TILE), :]
                value = value + contract_last(quad[place], weight)
            dz[:, at] = value

    def score_back(shares, delta):
        shares = wide(shares)
        weighed = shares * delta
        return narrow(weighed - shares * jnp.sum(weighed, axis=0, keepdims=True))

    def query_attention_back(layer):
        query_span = pl.ds(0, query_rows)
        q2, k2, v2 = quad[0, query_span, :], quad[1, query_span, :], quad[2, query_span, :]

        def fill(rows_of):
            for head in range(HEADS):
                mask = narrow(jnp.where(head_mask(head, width), 1.0, 0.0))
                stack[head * query_rows : (head + 1) * query_rows, :] = rows_of * mask

        fill(dc[query_span, :])
        delta_value = narrow(product(ptq[...], stack[...]))
        delta_scores = score_back(ptq[...], contract_last(v2, stack[...]))
        fill(q2)
        delta_key = narrow(product(delta_scores, stack[...]) * 0.125)
        stack[...] = narrow(contract_rows(delta_scores, k2) * 0.125)
        delta_query = jnp.zeros((query_rows, width), jnp.float32)
        for head in range(HEADS):
            delta_query = delta_query + jnp.where(
                head_mask(head, width),
                wide(stack[head * query_rows : (head + 1) * query_rows, :]),
                0.0,
            )
        delta_query = narrow(delta_query)
        quad[0, query_span, :] = delta_query
        quad[1, query_span, :] = delta_key
        quad[2, query_span, :] = delta_value
        tally(layer, S_QUERY, every_lane, wide(delta_query))
        tally(layer, S_VALUE, every_lane, wide(delta_value))

    def passage_attention_back(layer, low, high):
        @pl.loop(low, high, unroll=2)
        def _(i):
            s, pair = i // pairs, i % pairs
            at_rows = sublanes(query_rows + s * passage_len, passage_len)
            at = lanes(pair * 2 * DH, 2 * DH)
            live_rows = sublanes(query_rows + s * passage_len, live)
            dead_rows = sublanes(query_rows + s * passage_len + live, passage_len - live)
            even, odd = lane_masks(passage_len)
            q2, k2, v2 = quad[0, at_rows, at], quad[1, live_rows, at], quad[2, live_rows, at]
            d2 = dc[at_rows, at]
            shares = pt[i]
            deltas = jnp.concatenate([d2 * even, d2 * odd], axis=0)
            delta_value = narrow(product(shares, deltas))
            delta_scores = score_back(shares, contract_last(v2, deltas))
            queries = jnp.concatenate([q2 * even, q2 * odd], axis=0)
            delta_key = narrow(product(delta_scores, queries) * 0.125)
            keys = jnp.concatenate([k2 * even[:live], k2 * odd[:live]], axis=0)
            piled = jnp.concatenate(
                [delta_scores[:, :passage_len], delta_scores[:, passage_len:]], axis=0
            )
            delta_query = narrow((contract_rows(keys, piled) * 0.125).T)
            quad[0, at_rows, at] = delta_query
            quad[1, live_rows, at] = delta_key
            quad[2, live_rows, at] = delta_value
            nothing = jnp.zeros((passage_len - live, 2 * DH), jnp.bfloat16)
            quad[1, dead_rows, at] = nothing
            quad[2, dead_rows, at] = nothing
            tally(layer, S_QUERY, at, wide(delta_query))
            tally(layer, S_VALUE, at, wide(delta_value))

    def make_terms(t, part):
        pair, half = (part % 4) // 2, lanes((part % 2) * columns, columns)

        @pl.when(part < 4)
        def _():
            @pl.loop(0, 4, unroll=2)
            def _(i):
                taller = active[:, lanes(i * width + pair * rows, rows)]
                buf[t % 2, i // 2, i % 2] = narrow(contract_rows(taller, dy[:, half]))

        def split(i, terms):
            place = sublanes((i // 2) * quarter, quarter)
            terms = narrow(terms)
            buf[t % 2, i % 2, 0, place, :] = terms[:quarter]
            buf[t % 2, i % 2, 1, place, :] = terms[quarter:]

        def two_quarters(i):
            return lanes((i % 2) * 2 * quarter, 2 * quarter)

        @pl.when((part >= 4) & (part < 8))
        def _():
            @pl.loop(0, 4, unroll=2)
            def _(i):
                wider = du[:, lanes((2 * pair + i // 2) * width + (part % 2) * columns, columns)]
                split(i, contract_rows(middle[:, two_quarters(i)], wider))

        @pl.when(part >= 8)
        def _():
            @pl.loop(0, 4, unroll=2)
            def _(i):
                which = 2 * pair + i // 2
                split(
                    i,
                    contract_rows(
                        pair_in[which // 3, :, two_quarters(i)], quad[which, :, half]
                    ),
                )

        @pl.when(t >= CORE_SLOTS)
        def _():
            pl.semaphore_wait(core_free, 1)

        core_copy(t).start()

    def small_move(place, target, peer):
        return remote(
            small, target, small_sem.at[2 * place], small_sem.at[2 * place + 1], *peer
        )

    def small_to_deep(k):
        line = small_deep.at[deep]
        return remote(line, line, small_send.at[k - 1], small_recv.at[k - 1], *behind(k))

    def gradients_out():
        return (
            pltpu.make_async_copy(dz.at[pl.ds(0, query_rows)], query_grad, first_sem.at[4]),
            pltpu.make_async_copy(dz.at[passage_rows], passage_grad, first_sem.at[5]),
        )

    @pl.loop(0, CHUNKS + LAGS[-1])
    def _(t):
        step, part = t // PARTS, t % PARTS
        layer = last - step
        slot = (3 * step) % 2
        busy = t < CHUNKS
        more = busy & (step < LAYERS - 1)

        @pl.when((t > 0) & (t <= CHUNKS))
        def _():
            after_core(t - 1)

        @pl.when(busy & (part == 0))
        def _():
            @pl.when(step > 0)
            def _():
                load("u2", layer).wait()

                @pl.loop(0, total // norm_step)
                def _(tile):
                    last_norm_back(layer, tile)

            load("f", layer).wait()

            @pl.when(step == 0)
            def _():
                start_weights(1, layer, 1)

        for at, names in ((1, ("u1",)), (2, ("q", "k", "v", "ptq")), (3, ("pt", "m")), (5, ("c", "x"))):

            @pl.when(busy & (part == at))
            def _():
                for name in names:
                    load(name, layer).start()

        @pl.when(busy & (part == 4))
        def _():
            load("m", layer).wait()

        @pl.when(busy & (part == 8))
        def _():
            for name in ("c", "x"):
                load(name, layer).wait()

        @pl.when(busy)
        def _():
            make_terms(t, part)

        @pl.when(busy & (part == 1))
        def _():
            @pl.when(more)
            def _():
                load("u2", layer - 1).start()

            load("slope", layer).wait()
            wait_weights(0, layer, slot)
            expand_back(layer, slot)
            start_weights(2, layer, slot)

        @pl.when(busy & (part == 2))
        def _():
            wait_weights(1, layer, 1 - slot)
            middle_back(1 - slot)

            @pl.when(more)
            def _():
                start_weights(0, layer - 1, 1 - slot)

        @pl.when(busy & (part == 3))
        def _():
            load("u1", layer).wait()

            @pl.loop(0, total // norm_step, unroll=2)
            def _(tile):
                first_norm_back(layer, tile)

            wait_weights(2, layer, slot)
            context_back(slot)

            @pl.when(more)
            def _():
                load("f", layer - 1).start()

        @pl.when(busy & (part == 4))
        def _():
            for name in ("q", "k", "v", "pt", "ptq"):
                load(name, layer).wait()
            query_attention_back(layer)

        passages = sequences * pairs

        @pl.when(busy & (part == 5))
        def _():
            passage_attention_back(layer, 0, passages // 3)

        @pl.when(busy & (part == 6))
        def _():
            passage_attention_back(layer, passages // 3, 2 * passages // 3)

        @pl.when(busy & (part == 7))
        def _():
            passage_attention_back(layer, 2 * passages // 3, passages)

        @pl.when(busy & (part == 8))
        def _():
            @pl.when(more)
            def _():
                load("slope", layer - 1).start()

            hidden_back(slot)

            @pl.when(more)
            def _():
                start_weights(1, layer - 1, slot)

            @pl.when(step == LAYERS - 1)
            def _():
                for copy in gradients_out():
                    copy.start()

        for lag, stage in zip(LAGS, (after_side, after_near, after_deep, after_high, after_second, after_third)):

            @pl.when((t >= lag) & (t < CHUNKS + lag))
            def _():
                stage(t - lag)

        for place, (target, peer, came) in enumerate(
            (
                (small_core, sibling, small_core),
                (small_side, across, small_side),
                (small_near, beside, small_near),
            )
        ):

            @pl.when(t == SMALL_AT + place)
            def _():
                small_move(place, target, peer).start()

            @pl.when(t == SMALL_AT + 1 + place)
            def _():
                small_move(place, target, peer).wait()
                small[...] = small[...] + came[...]

        @pl.when(t == SMALL_AT + 3)
        def _():
            small_deep[deep] = small[...]
            for k in range(1, depth):
                small_to_deep(k).start()

        @pl.when(t == SMALL_AT + 5)
        def _():
            for k in range(1, depth):
                small_to_deep(k).wait()
            summed = small_deep[0]
            for k in range(1, depth):
                summed = summed + small_deep[k]
            small_out[...] = summed

    for copy in gradients_out():
        copy.wait()

    @pl.loop(1, reps)
    def _(k):
        to_near(k).wait_send()

    for k in range(1, groups):
        to_far(k).wait_send()


def run_backward(
    margin_bin,
    positive_index,
    cluster_index,
    norm_gain,
    final_gain,
    query_output,
    passage_output,
    query_cotangent,
    passage_cotangent,
    matrices,
    stored,
):
    query_rows, width = query_output.shape
    passage_rows = passage_output.shape[0]
    total = query_rows + passage_rows
    sequences = margin_bin.shape[0]
    everyone = cluster_index.shape[0]
    groups, reps = lax.axis_size("grp"), lax.axis_size("rep")
    depth = reps // 2
    rows = width // 2
    piece_rows = rows // 2 // depth
    bf16, f32 = jnp.bfloat16, jnp.float32
    dma = pltpu.SemaphoreType.DMA
    anywhere = pl.BlockSpec(memory_space=pl.ANY)
    vmem = pl.BlockSpec(memory_space=pltpu.VMEM)
    smem = pl.BlockSpec(memory_space=pltpu.SMEM)
    small_shape = (LAYERS, 16, width)
    pt_shape, ptq_shape = stored[4].shape[1:], stored[5].shape[1:]
    columns = width // 2
    return pl.pallas_call(
        backward_kernel,
        out_shape=(
            jax.ShapeDtypeStruct((CHUNKS, 2, 2, rows // 4, columns), bf16),
            jax.ShapeDtypeStruct(small_shape, f32),
            jax.ShapeDtypeStruct((8, 128), f32),
            jax.ShapeDtypeStruct((query_rows, width), f32),
            jax.ShapeDtypeStruct((passage_rows, width), f32),
        ),
        in_specs=[smem, smem, vmem, vmem, vmem] + [anywhere] * 23,
        out_specs=(anywhere, vmem, vmem, anywhere, anywhere),
        scratch_shapes=[
            pltpu.VMEM((2, 2, 2, rows, columns), bf16),
            pltpu.VMEM((KEEP_SLOTS, rows, columns), bf16),
            pltpu.VMEM((SENT_SLOTS, rows, columns), bf16),
            pltpu.VMEM((CORE_SLOTS, 2, rows, columns), bf16),
            pltpu.VMEM((SIDE_SLOTS, rows, columns), bf16),
            pltpu.VMEM((NEAR_SLOTS, rows // 2, columns), bf16),
            pltpu.VMEM((TURNS, depth - 1, piece_rows, columns), bf16),
            pltpu.VMEM((TURNS, piece_rows, columns), bf16),
            pltpu.VMEM(small_shape, f32),
            pltpu.VMEM(small_shape, f32),
            pltpu.VMEM(small_shape, f32),
            pltpu.VMEM(small_shape, f32),
            pltpu.VMEM((depth,) + small_shape, f32),
            pltpu.VMEM((2 * sequences * BLOCK, width), bf16),
            pltpu.VMEM((groups, reps, BLOCK, TILE), bf16),
            pltpu.VMEM((LAYERS, 8, width), f32),
            pltpu.VMEM((total, width), f32),
            pltpu.VMEM((total, width), bf16),
            pltpu.VMEM((total, 4 * width), bf16),
            pltpu.VMEM((4, total, width), bf16),
            pltpu.VMEM((2, total, width), bf16),
            pltpu.VMEM((total, width), bf16),
            pltpu.VMEM((2, total, width), bf16),
            pltpu.VMEM((total, 4 * width), bf16),
            pltpu.VMEM((total, width), bf16),
            pltpu.VMEM(pt_shape, bf16),
            pltpu.VMEM(ptq_shape, bf16),
            pltpu.VMEM((HEADS * query_rows, width), bf16),
            pltpu.VMEM((LAYERS, total, 128), f32),
            pltpu.VMEM((2, 4, width, width), bf16),
            dma((2, reps)),
            dma((2, groups)),
            dma((7,)),
            dma((12,)),
            dma((2, 4)),
            dma((2, CORE_SLOTS)),
            dma((2, SIDE_SLOTS)),
            dma((2, NEAR_SLOTS)),
            dma((depth - 1, TURNS)),
            dma((depth - 1, TURNS)),
            dma((2, 3, TURNS)),
            dma((TURNS,)),
            dma((6,)),
            dma((depth - 1,)),
            dma((depth - 1,)),
            pltpu.SemaphoreType.REGULAR,
            pltpu.SemaphoreType.REGULAR,
            pltpu.SemaphoreType.REGULAR,
        ],
        compiler_params=pltpu.CompilerParams(
            collective_id=0, has_side_effects=True, vmem_limit_bytes=62 * 1024 * 1024
        ),
    )(
        margin_bin,
        positive_index,
        cluster_index.reshape(1, everyone),
        norm_gain,
        final_gain,
        query_output,
        passage_output,
        query_cotangent.reshape(query_rows, width),
        passage_cotangent.reshape(passage_rows, width),
        *matrices,
        *stored,
    )


def backward_plain(
    query_output,
    passage_output,
    cluster_index,
    margin_bin,
    positive_index,
    query_cotangent,
    passage_cotangent,
    stored,
    params,
):
    batch_size, query_len, model_width = query_output.shape
    passage_len = passage_output.shape[1]
    layout = ((batch_size, query_len), (batch_size, passage_len))
    query_span = batch_size * query_len
    stored_layers = [tuple(array[layer_index] for array in stored) for layer_index in range(LAYERS)]
    query_first = query_output[:, 0, :]
    passage_first = passage_output[:, 0, :]
    facts = jnp.concatenate(
        [margin_bin, positive_index // 128, positive_index % 128], axis=0
    ).astype(jnp.bfloat16)
    facts = jnp.pad(facts, (0, model_width - facts.shape[0]))
    block = jnp.concatenate([query_first, passage_first, facts[None, :]], axis=0)
    block = jnp.pad(block, ((0, 8 - block.shape[0]), (0, 0)))
    total = cluster_index.shape[0]
    every = gather_blocks(block).reshape(-1, 8, model_width)
    every_query = every[:, :batch_size].reshape(total, model_width)
    every_passage = every[:, batch_size : 2 * batch_size].reshape(total, model_width)
    facts = every[:, 2 * batch_size, : 3 * batch_size].astype(jnp.int32)
    facts = facts.reshape(-1, 3, batch_size)
    every_margin = facts[:, 0].reshape(total)
    every_positive = (facts[:, 1] * 128 + facts[:, 2]).reshape(total)
    start_row = lax.axis_index(("grp", "rep")) * batch_size
    score_scale = 2.0 / math.sqrt(model_width)
    logits = contract_last(every_query, every_passage) * score_scale
    columns = lax.broadcasted_iota(jnp.int32, logits.shape, 1)
    chosen_mask = columns == every_positive[:, None]
    allowed = (cluster_index[None, :] == cluster_index[:, None]) | chosen_mask
    masked = jnp.where(allowed, logits, -1e30)
    peak_score = jnp.max(masked, axis=1, keepdims=True)
    normalizer = peak_score + jnp.log(jnp.sum(jnp.exp(masked - peak_score), axis=1, keepdims=True))
    chosen = jnp.sum(jnp.where(chosen_mask, logits, 0.0), axis=1)
    margin_weight = (every_margin + 1).astype(jnp.float32) / NBINS
    every_loss = margin_weight * (normalizer[:, 0] - chosen)
    query_loss = lax.dynamic_slice_in_dim(every_loss, start_row, batch_size)
    delta_logits = narrow(
        margin_weight[:, None]
        * (jnp.where(allowed, jnp.exp(masked - normalizer), 0.0) - chosen_mask.astype(jnp.float32))
    )
    own_rows = lax.dynamic_slice_in_dim(delta_logits, start_row, batch_size, axis=0)
    own_columns = lax.dynamic_slice_in_dim(delta_logits, start_row, batch_size, axis=1)
    delta_query_first = product(own_rows, every_passage) * score_scale
    delta_passage_first = contract_rows(own_columns, every_query) * score_scale
    query_upstream = query_cotangent.astype(jnp.float32).at[:, 0, :].add(delta_query_first)
    passage_upstream = passage_cotangent.astype(jnp.float32).at[:, 0, :].add(delta_passage_first)
    upstream = jnp.concatenate(
        [
            query_upstream.reshape(query_span, model_width),
            passage_upstream.reshape(batch_size * passage_len, model_width),
        ],
        axis=0,
    )
    operands = []
    small = []
    for layer_index in reversed(range(LAYERS)):
        layer_params = tuple(array[layer_index] for array in params)
        upstream, layer_operands, vectors = layer_backward(
            upstream, stored_layers[layer_index], layout, layer_params
        )
        operands.append(layer_operands)
        small.append([vector.reshape(4, -1) for vector in vectors])
    small = small[::-1]
    matrices = reduce_plain(operands)
    flat = reduce_small(jnp.concatenate(small[0] + small[1], axis=1))
    reduced = [None] * 15
    for slot, matrix in zip(MATRICES, matrices):
        reduced[slot] = matrix
    flat = flat.reshape(LAYERS, -1)
    offset = 0
    for slot, vector in zip(SMALL, small[0]):
        size = vector.shape[1]
        reduced[slot] = flat[:, offset : offset + size]
        offset = offset + size
    return query_loss, upstream[:query_span], upstream[query_span:], reduced


def finish_kernel(
    out_ref,
    small_in,
    loss_in,
    query_in,
    passage_in,
    reduce_out,
    expand_out,
    *rest,
):
    square_outs = rest[:4]
    vector_outs = rest[4:12]
    expand_bias_out, query_out, passage_out, loss_out = rest[12:16]
    sums, tall, flat, squares, query, passage, small_ref, loss, in_sem, out_sem = rest[16:]
    rows, columns = sums.shape[1:]
    quarter = rows // 2
    width = 2 * columns
    each = sums.shape[0] // (3 * LAYERS)
    moves = [
        pltpu.make_async_copy(query_in, query, in_sem.at[3 * LAYERS]),
        pltpu.make_async_copy(passage_in, passage, in_sem.at[3 * LAYERS + 1]),
    ]
    little = [
        pltpu.make_async_copy(small_in, small_ref, in_sem.at[3 * LAYERS + 2]),
        pltpu.make_async_copy(loss_in, loss, in_sem.at[3 * LAYERS + 3]),
    ]
    loads = []
    for i in range(3 * LAYERS):
        span = pl.ds(i * each, each)
        loads.append(pltpu.make_async_copy(out_ref.at[span], sums.at[span], in_sem.at[i]))
    for copy in loads + moves + little:
        copy.start()
    stores = []

    def store(source, target):
        copy = pltpu.make_async_copy(source, target, out_sem.at[len(stores)])
        stores.append(copy)
        copy.start()

    for layer in range(LAYERS):
        loads[layer].wait()
        for part in range(4):
            at = pl.ds((part // 2) * rows, rows), pl.ds((part % 2) * columns, columns)
            tall[layer, at[0], at[1]] = wide(sums[layer * each + part])
        store(tall.at[layer], reduce_out.at[layer])
    for move, (source, target) in zip(moves, ((query, query_out), (passage, passage_out))):
        move.wait()
        store(source, target)
    for layer in range(LAYERS):
        loads[LAYERS + layer].wait()
        for part in range(4):
            value = wide(sums[(LAYERS + layer) * each + part])
            for unit in range(2):
                start = (2 * (part // 2) + unit) * width + (part % 2) * columns
                flat[layer, :, start : start + columns] = value[
                    unit * quarter : (unit + 1) * quarter
                ]
        store(flat.at[layer], expand_out.at[layer])
    for layer in range(LAYERS):
        loads[2 * LAYERS + layer].wait()
        for part in range(4):
            value = wide(sums[(2 * LAYERS + layer) * each + part])
            for unit in range(2):
                at = pl.ds((part % 2) * columns, columns)
                squares[2 * (part // 2) + unit, layer, :, at] = value[
                    unit * quarter : (unit + 1) * quarter
                ]
        for which in range(4):
            store(squares.at[which, layer], square_outs[which].at[layer])
    for copy in little:
        copy.wait()
    for i in range(loss_out.shape[0]):
        loss_out[i] = jnp.sum(loss[0:1, i : i + 1])
    group = lax.axis_index("grp")
    vectors = small_ref[:, :8, 0:quarter]
    expand_bias = small_ref[:, S_EXPAND, :]
    for g in range(1, 4):
        vectors = jnp.where(
            group == g, small_ref[:, :8, g * quarter : (g + 1) * quarter], vectors
        )
        expand_bias = jnp.where(group == g, small_ref[:, S_EXPAND + g, :], expand_bias)
    for i in range(8):
        vector_outs[i][...] = vectors[:, i, :]
    expand_bias_out[...] = expand_bias
    for copy in stores:
        copy.wait()


def finish(out, small, loss, query_gradient, passage_gradient, sequences):
    out = out.reshape(out.shape[0], -1, out.shape[-1])
    rows, columns = out.shape[1:]
    quarter, width = rows // 2, 2 * columns
    f32 = jnp.float32
    anywhere = pl.BlockSpec(memory_space=pl.ANY)
    vmem = pl.BlockSpec(memory_space=pltpu.VMEM)
    tall, flat = (LAYERS, width, width), (LAYERS, quarter, 4 * width)
    square, vector = (LAYERS, quarter, width), (LAYERS, quarter)
    results = pl.pallas_call(
        finish_kernel,
        out_shape=[
            jax.ShapeDtypeStruct(shape, f32)
            for shape in [tall, flat]
            + [square] * 4
            + [vector] * 8
            + [(LAYERS, width), query_gradient.shape, passage_gradient.shape, (sequences,)]
        ],
        in_specs=[anywhere] * 5,
        out_specs=[anywhere] * 6
        + [vmem] * 9
        + [anywhere] * 2
        + [pl.BlockSpec(memory_space=pltpu.SMEM)],
        scratch_shapes=[
            pltpu.VMEM(out.shape, jnp.bfloat16),
            pltpu.VMEM(tall, f32),
            pltpu.VMEM(flat, f32),
            pltpu.VMEM((4,) + square, f32),
            pltpu.VMEM(query_gradient.shape, f32),
            pltpu.VMEM(passage_gradient.shape, f32),
            pltpu.VMEM(small.shape, f32),
            pltpu.VMEM(loss.shape, f32),
            pltpu.SemaphoreType.DMA((3 * LAYERS + 4,)),
            pltpu.SemaphoreType.DMA((6 * LAYERS + 2,)),
        ],
        compiler_params=pltpu.CompilerParams(vmem_limit_bytes=60 * 1024 * 1024),
    )(out, small, loss, query_gradient, passage_gradient)
    reduced = [None] * 15
    reduced[11], reduced[9] = results[0], results[1]
    for place, slot in enumerate((0, 2, 3, 5)):
        reduced[slot] = results[2 + place]
    for place, slot in enumerate((1, 4, 6, 7, 8, 12, 13, 14)):
        reduced[slot] = results[6 + place]
    reduced[10] = results[14]
    return results[15], results[16], results[17], reduced


def per_device(
    query_input,
    passage_input,
    query_length,
    passage_length,
    cluster_index,
    margin_bin,
    positive_index,
    query_cotangent,
    passage_cotangent,
    query_weight,
    query_bias,
    key_weight,
    value_weight,
    value_bias,
    mix_weight,
    mix_bias,
    norm_gain,
    norm_shift,
    expand_weight,
    expand_bias,
    reduce_weight,
    reduce_bias,
    final_gain,
    final_shift,
):
    params = (
        query_weight,
        query_bias,
        key_weight,
        value_weight,
        value_bias,
        mix_weight,
        mix_bias,
        norm_gain,
        norm_shift,
        expand_weight,
        expand_bias,
        reduce_weight,
        reduce_bias,
        final_gain,
        final_shift,
    )
    batch_size, query_len, model_width = query_input.shape
    passage_len = passage_input.shape[1]
    matrices = (query_weight, key_weight, value_weight, mix_weight, expand_weight, reduce_weight)
    vectors = (
        query_bias,
        value_bias,
        mix_bias,
        norm_gain,
        norm_shift,
        reduce_bias,
        final_gain,
        final_shift,
        expand_bias,
    )
    results = run_forward(
        query_length,
        passage_length,
        query_input,
        passage_input,
        matrices,
        vectors,
    )
    query_output = results[0].reshape(batch_size, query_len, model_width)
    passage_output = results[1].reshape(batch_size, passage_len, model_width)
    if lax.axis_size("rep") != 8:
        query_loss, query_gradient, passage_gradient, reduced = backward_plain(
            query_output,
            passage_output,
            cluster_index,
            margin_bin,
            positive_index,
            query_cotangent,
            passage_cotangent,
            results[2:],
            params,
        )
    else:
        out, small, loss, query_gradient, passage_gradient = run_backward(
            margin_bin,
            positive_index,
            cluster_index,
            norm_gain,
            final_gain,
            results[0],
            results[1],
            query_cotangent,
            passage_cotangent,
            matrices,
            results[2:],
        )
        query_gradient, passage_gradient, query_loss, reduced = finish(
            out, small, loss, query_gradient, passage_gradient, batch_size
        )
    return (
        query_output,
        passage_output,
        query_loss,
        query_gradient.reshape(batch_size, query_len, model_width),
        passage_gradient.reshape(batch_size, passage_len, model_width),
        reduced[0],
        reduced[1],
        reduced[2],
        reduced[3],
        reduced[4],
        reduced[5],
        reduced[6],
        reduced[7],
        reduced[8],
        reduced[9],
        reduced[10],
        reduced[11],
        reduced[12],
        reduced[13],
        reduced[14],
    )


def solution(mesh):
    placed = (
        P(("grp", "rep"), None, None),
        P(("grp", "rep"), None, None),
        P(("grp", "rep")),
        P(("grp", "rep")),
        P(),
        P(("grp", "rep")),
        P(("grp", "rep")),
        P(("grp", "rep"), None, None),
        P(("grp", "rep"), None, None),
        P(),
        P(),
        P(),
        P(),
        P(),
        P(),
        P(),
        P(),
        P(),
        P(),
        P(),
        P(),
        P(),
        P(),
        P(),
    )
    return jax.shard_map(
        per_device,
        mesh=mesh,
        in_specs=placed,
        out_specs=(
            P(("grp", "rep"), None, None),
            P(("grp", "rep"), None, None),
            P(("grp", "rep")),
            P(("grp", "rep"), None, None),
            P(("grp", "rep"), None, None),
            P(None, "grp", None),
            P(None, "grp"),
            P(None, "grp", None),
            P(None, "grp", None),
            P(None, "grp"),
            P(None, "grp", None),
            P(None, "grp"),
            P(None, "grp"),
            P(None, "grp"),
            P(None, "grp", None),
            P(None, "grp"),
            P(None, "grp", None),
            P(None, "grp"),
            P(None, "grp"),
            P(None, "grp"),
        ),
        check_vma=False,
    )
```
